32 devices in a mesh: head: 2 (over x), ffn: 4 (over y, core), row: 4 (over z).
Axes of the slice: x: 2, y: 2, z: 4, core: 2. Of those that a mesh axis runs over, the one named last changes fastest.
Arguments:
- inputs: bfloat16 [16, 640, 1024], P(('ffn', 'row'), 'head'), may hold values from -6 to 6
- first_values: bfloat16 [16, 640, 1024], P(('ffn', 'row'), 'head'), may hold values from -6 to 6
- lengths: int32 [16], P(('ffn', 'row')), may hold values from 512 to 640, as said below
- gain_attn: float32 [1024], replicated, may hold values from 0.5 to 1.5
- w_qkv: bfloat16 [1024, 3072], replicated, may hold values from -0.1875 to 0.1875
- w_out: bfloat16 [1024, 1024], replicated, may hold values from -3 to 3
- gain_mlp: float32 [1024], replicated, may hold values from 0.5 to 1.5
- w_gate: bfloat16 [1024, 2816], P(None, 'ffn'), may hold values from -0.1875 to 0.1875
- w_up: bfloat16 [1024, 2816], P(None, 'ffn'), may hold values from -0.1875 to 0.1875
- w_down: bfloat16 [2816, 1024], P('ffn'), may hold values from -0.109375 to 0.109375
- cotangent: bfloat16 [16, 640, 1024], P(('ffn', 'row'), 'head'), may hold values from -6 to 6
Outputs:
- output: bfloat16 [16, 640, 1024], P(('ffn', 'row'), 'head')
- grad_inputs: float32 [16, 640, 1024], P(('ffn', 'row'), 'head')
- grad_first_values: bfloat16 [16, 640, 1024], P(('ffn', 'row'), 'head')
- grad_gain_attn: float32 [1024], replicated
- grad_w_qkv: float32 [1024, 3072], P(('ffn', 'row'), 'head')
- grad_w_out: float32 [1024, 1024], P('head', ('ffn', 'row'))
- grad_gain_mlp: float32 [1024], replicated
- grad_w_gate: float32 [1024, 2816], P(('head', 'row'), 'ffn')
- grad_w_up: float32 [1024, 2816], P(('head', 'row'), 'ffn')
- grad_w_down: float32 [2816, 1024], P('ffn', ('head', 'row'))
The draws below stay inside these ranges and needn't reach their ends.
Inputs may be any that keep to these rules, and one draw needn't show every extreme that they name: `lengths`: one bucket in every draw is full.
All inputs are finite; a program needn't handle non-finite values.
Results may differ from the reference program's by a relative error of at most 0.02.
Values may be sent and summed in bfloat16 or wider, within the bound.
No kernel may reach another device: no remote copies, remote signals or barrier semaphores. Data moves between devices by JAX's collectives and lax.ppermute only.
A program may use at most 128 MiB of HBM per device.

```python
import jax
import jax.numpy as jnp
from jax import lax

D = 1024
HEADS = 16
HD = 64
FF = 2816
MIN_LEN = 512
BUCKETS = 16
BUCKET_LEN = 640
QBLOCKS = 1
QBLK = 640


def draw_lengths(key, part):
    key_shift = jax.random.fold_in(key, 11)
    key_cut = jax.random.fold_in(key, 12)
    key_full = jax.random.fold_in(key, 13)
    shifts = jax.random.randint(key_shift, (BUCKETS,), 0, 4, dtype=jnp.int32)
    base_len = jnp.right_shift(jnp.full((BUCKETS,), BUCKET_LEN, dtype=jnp.int32), shifts)
    raw_cut = jax.random.randint(key_cut, (BUCKETS,), 0, 1 << 30, dtype=jnp.int32)
    cut_len = raw_cut % (base_len // 4 + 1)
    result = jnp.maximum(base_len - cut_len, MIN_LEN)
    full_one = jax.random.randint(key_full, (), 0, BUCKETS, dtype=jnp.int32)
    result = jnp.where(jnp.arange(BUCKETS, dtype=jnp.int32) == full_one, BUCKET_LEN, result)
    return result.astype(jnp.int32)


def steps_of(key, dims, pieces, smallest, high):
    def one(dim, shards_of):
        steps = jax.random.uniform(jax.random.fold_in(jax.random.fold_in(key, 6), dim), (shards_of,), jnp.float32, smallest / len(pieces), high / len(pieces))
        return jnp.repeat(jnp.exp(steps), dims[dim] // shards_of).reshape((-1,) + (1,) * (len(dims) - dim - 1))

    loudness = one(*pieces[0])
    for cut in pieces[1:]:
        loudness = loudness * one(*cut)
    return loudness


def bell_draw(rng, extent, scale, most, shards=(), held_as=jnp.bfloat16):
    array = jax.random.normal(rng, extent, jnp.float32) * scale
    if len(shards) > 0:
        array = steps_of(rng, extent, shards, -0.22, 0.18) * array
    return jnp.clip(array, min=-most, max=most).astype(held_as)


def setup_inputs(seed: int = 0) -> dict:
    key_list = jax.random.split(jax.random.key(seed), 12)
    inputs = bell_draw(key_list[0], (BUCKETS, BUCKET_LEN, D), 1.0, 6.0, ((0, 16), (1, 2)))
    first_values = bell_draw(key_list[1], (BUCKETS, BUCKET_LEN, HEADS * HD), 1.0, 6.0, ((0, 16), (1, 2)))
    lengths = draw_lengths(jax.random.fold_in(key_list[11], 71), 0)
    gain_attn = jnp.clip(1.0 + 0.1 * jax.random.normal(key_list[3], (D,), jnp.float32), 0.5, 1.5)
    w_qkv = bell_draw(key_list[4], (D, 3 * HEADS * HD), D ** -0.5, 0.1875)
    w_out = bell_draw(key_list[5], (HEADS * HD, D), 4 ** -0.5, 3.0)
    gain_mlp = jnp.clip(1.0 + 0.1 * jax.random.normal(key_list[6], (D,), jnp.float32), 0.5, 1.5)
    w_gate = bell_draw(key_list[7], (D, FF), D ** -0.5, 0.1875, ((1, 4),))
    w_up = bell_draw(key_list[8], (D, FF), D ** -0.5, 0.1875, ((1, 4),))
    w_down = bell_draw(key_list[9], (FF, D), FF ** -0.5, 0.109375, ((0, 4),))
    cotangent = bell_draw(key_list[10], (BUCKETS, BUCKET_LEN, D), 1.0, 6.0, ((0, 16), (1, 2)))
    return dict(inputs=inputs, first_values=first_values, lengths=lengths, gain_attn=gain_attn, w_qkv=w_qkv, w_out=w_out, gain_mlp=gain_mlp, w_gate=w_gate, w_up=w_up, w_down=w_down, cotangent=cotangent)


eps = 1e-06

@jax.custom_vjp
def low(v):
    return lax.optimization_barrier(v.astype(jnp.bfloat16)).astype(jnp.float32)

@jax.custom_vjp
def low_back(v):
    return v

def low_keep(v):
    return (low(v), None)

def low_pass(kept, grad):
    return (grad,)

def back_keep(v):
    return (v, None)

def back_low(kept, grad):
    return (low(grad),)
low.defvjp(low_keep, low_pass)
low_back.defvjp(back_keep, back_low)

def rotary(length):
    half_size = HD // 2
    inverse = jnp.exp(-jnp.log(10000.0) * jnp.arange(half_size, dtype=jnp.float32) * 2.0 / HD)
    angles = jnp.arange(length, dtype=jnp.float32)[:, None] * inverse[None, :]
    return (jnp.cos(angles), jnp.sin(angles))

def rotate(vectors, cosine, sine):
    half_size = HD // 2
    first_half = vectors[..., :half_size]
    second_half = vectors[..., half_size:]
    cos_rows = cosine[:, None, :]
    sin_rows = sine[:, None, :]
    return jnp.concatenate([first_half * cos_rows - second_half * sin_rows, second_half * cos_rows + first_half * sin_rows], axis=-1)

def bucket_attention(packed, earlier, valid):
    cosine, sine = rotary(BUCKET_LEN)
    query = low(rotate(packed[:, :, 0], cosine, sine))
    keys = low(rotate(packed[:, :, 1], cosine, sine))
    mixed = low(0.5 * (packed[:, :, 2] + earlier))
    columns = jnp.arange(BUCKET_LEN, dtype=jnp.int32)

    def block_out(start):
        q_rows = lax.dynamic_slice_in_dim(query, start, QBLK, 0)
        raw = jnp.einsum('qhe,khe->hqk', q_rows, keys, precision=lax.Precision.HIGHEST)
        scores = low_back(0.125 * raw)
        positions = start + jnp.arange(QBLK, dtype=jnp.int32)
        allowed = (columns[None, :] <= positions[:, None]) & (columns[None, :] < valid)
        scores = jnp.where(allowed[None], scores, -1e+30)
        weights = jax.nn.softmax(scores, axis=-1)
        return jnp.einsum('hqk,khe->qhe', low(weights), mixed, precision=lax.Precision.HIGHEST)
    starts = jnp.arange(QBLOCKS, dtype=jnp.int32) * QBLK
    outs = lax.map(jax.checkpoint(block_out), starts)
    return outs.reshape(BUCKET_LEN, HEADS, HD)

def forward(lengths, inputs, first_values, gain_attn, w_qkv, w_out, gain_mlp, w_gate, w_up, w_down):
    high = lax.Precision.HIGHEST
    flat = inputs.reshape(-1, D)
    scale_one = lax.rsqrt(lax.optimization_barrier(jnp.mean(flat * flat, axis=-1, keepdims=True)) + eps)
    normed = low(flat * scale_one * gain_attn)
    packed = low(low_back(jnp.dot(normed, w_qkv, precision=high)))
    packed = packed.reshape(BUCKETS, BUCKET_LEN, HEADS, 3, HD)
    earlier = low_back(first_values).reshape(BUCKETS, BUCKET_LEN, HEADS, HD)
    attended = lax.map(lambda item: bucket_attention(item[0], item[1], item[2]), (packed, earlier, lengths))
    attended = low(low_back(attended.reshape(-1, HEADS * HD)))
    projected = low_back(jnp.dot(attended, w_out, precision=high))
    hidden = flat + projected
    scale_two = lax.rsqrt(lax.optimization_barrier(jnp.mean(hidden * hidden, axis=-1, keepdims=True)) + eps)
    normed_two = low(hidden * scale_two * gain_mlp)
    gate_rows = low_back(jnp.dot(normed_two, w_gate, precision=high))
    up_rows = low_back(jnp.dot(normed_two, w_up, precision=high))
    active = low(jax.nn.silu(gate_rows) * up_rows)
    down_rows = low_back(jnp.dot(active, w_down, precision=high))
    return (hidden + down_rows).reshape(BUCKETS, BUCKET_LEN, D)

def reference(inputs, first_values, lengths, gain_attn, w_qkv, w_out, gain_mlp, w_gate, w_up, w_down, cotangent):
    floats = (inputs.astype(jnp.float32), first_values.astype(jnp.float32), gain_attn.astype(jnp.float32), w_qkv.astype(jnp.float32), w_out.astype(jnp.float32), gain_mlp.astype(jnp.float32), w_gate.astype(jnp.float32), w_up.astype(jnp.float32), w_down.astype(jnp.float32))

    def closed(a0, a1, a2, a3, a4, a5, a6, a7, a8):
        return forward(lengths, a0, a1, a2, a3, a4, a5, a6, a7, a8)
    result, pullback = jax.vjp(closed, *floats)
    grads = pullback(cotangent.astype(jnp.float32))
    return (result.astype(jnp.bfloat16), grads[0], grads[1].astype(jnp.bfloat16), grads[2], grads[3], grads[4], grads[5], grads[6], grads[7], grads[8])
```

```python
import jax
import jax.numpy as jnp
from jax import lax
from jax.sharding import PartitionSpec as P

HEADS = 16
HD = 64


eps = 1e-06


def rms_scale(values):
    return lax.rsqrt(jnp.mean(values * values, axis=-1, keepdims=True) + eps)


def matmul(left, right):
    return jnp.dot(left, right, preferred_element_type=jnp.float32)


def inner_rows(left, right):
    return lax.dot_general(
        left, right, (((0,), (0,)), ((), ())), preferred_element_type=jnp.float32
    )


def against(left, right):
    return lax.dot_general(
        left, right, (((1,), (1,)), ((), ())), preferred_element_type=jnp.float32
    )


def swap(values, axis, mask):
    size = lax.axis_size(axis)
    return lax.ppermute(values, axis, [(i, i ^ mask) for i in range(size)])


def bits_of(axis):
    size = lax.axis_size(axis)
    return [1 << b for b in range(size.bit_length() - 2, -1, -1)]


def halve(values, dim, axis, mask):
    bit = (lax.axis_index(axis) // mask) % 2
    away = lax.dynamic_index_in_dim(values, 1 - bit, dim, keepdims=False)
    kept = lax.dynamic_index_in_dim(values, bit, dim, keepdims=False)
    came = swap(away.astype(jnp.bfloat16), axis, mask)
    return kept.astype(jnp.float32) + came.astype(jnp.float32)


def total(values, axes):
    for axis in axes:
        for mask in reversed(bits_of(axis)):
            values = values + swap(values, axis, mask)
    return values


def rotary(positions, head_size):
    half_size = head_size // 2
    inverse = jnp.exp(
        -jnp.log(10000.0) * jnp.arange(half_size, dtype=jnp.float32) * 2.0 / head_size
    )
    angles = positions.astype(jnp.float32)[:, None] * inverse[None, :]
    return (jnp.cos(angles), jnp.sin(angles))


def rotate(vectors, cosine, sine, sign):
    half_size = vectors.shape[-1] // 2
    first_half = vectors[..., :half_size]
    second_half = vectors[..., half_size:]
    cos_rows = cosine[:, None, :]
    sin_rows = sign * sine[:, None, :]
    return jnp.concatenate(
        [
            first_half * cos_rows - second_half * sin_rows,
            second_half * cos_rows + first_half * sin_rows,
        ],
        axis=-1,
    )


def masked_scores(q_rows, keys, q_pos, k_pos, valid):
    raw = jnp.einsum("qhe,khe->hqk", q_rows, keys, preferred_element_type=jnp.float32)
    allowed = (k_pos[None, :] <= q_pos[:, None]) & (k_pos[None, :] < valid)
    return jnp.where(allowed[None], 0.125 * raw, -1e30)


def attend_forward(query, keys, mixed, positions, valid, block_rows):
    count = query.shape[0] // block_rows

    def step(carry, index):
        start = index * block_rows
        q_rows = lax.dynamic_slice_in_dim(query, start, block_rows, 0)
        q_pos = lax.dynamic_slice_in_dim(positions, start, block_rows, 0)
        scores = masked_scores(q_rows, keys, q_pos, positions, valid)
        top = jnp.max(scores, axis=-1, keepdims=True)
        expo = jnp.exp(scores - top)
        total_w = jnp.sum(expo, axis=-1, keepdims=True)
        weights = expo / total_w
        result = jnp.einsum(
            "hqk,khe->qhe", weights.astype(jnp.bfloat16), mixed, preferred_element_type=jnp.float32
        )
        return (carry, (result.astype(jnp.bfloat16), top + jnp.log(total_w)))

    _, (outs, log_sums) = lax.scan(step, 0, jnp.arange(count, dtype=jnp.int32))
    return (outs.reshape(query.shape), log_sums)


def attend_backward(query, keys, mixed, positions, valid, log_sums, grad_out, block_rows):
    count = query.shape[0] // block_rows
    zeros = jnp.zeros(keys.shape, jnp.float32)

    def step(carry, index):
        key_sum, value_sum = carry
        start = index * block_rows
        q_rows = lax.dynamic_slice_in_dim(query, start, block_rows, 0)
        q_pos = lax.dynamic_slice_in_dim(positions, start, block_rows, 0)
        g_rows = lax.dynamic_slice_in_dim(grad_out, start, block_rows, 0)
        scores = masked_scores(q_rows, keys, q_pos, positions, valid)
        weights = jnp.exp(scores - log_sums[index])
        grad_w = jnp.einsum("qhe,khe->hqk", g_rows, mixed, preferred_element_type=jnp.float32)
        delta = jnp.sum(weights * grad_w, axis=-1, keepdims=True)
        grad_s = (weights * (grad_w - delta)).astype(jnp.bfloat16)
        grad_q = 0.125 * jnp.einsum(
            "hqk,khe->qhe", grad_s, keys, preferred_element_type=jnp.float32
        )
        key_sum = key_sum + 0.125 * jnp.einsum(
            "hqk,qhe->khe", grad_s, q_rows, preferred_element_type=jnp.float32
        )
        value_sum = value_sum + jnp.einsum(
            "hqk,qhe->khe", weights.astype(jnp.bfloat16), g_rows, preferred_element_type=jnp.float32
        )
        return ((key_sum, value_sum), grad_q)

    (grad_keys, grad_mixed), grad_query = lax.scan(
        step, (zeros, zeros), jnp.arange(count, dtype=jnp.int32)
    )
    return (grad_query.reshape(query.shape), grad_keys, grad_mixed)


def on_device(
    inputs,
    first_values,
    lengths,
    gain_attn,
    w_qkv,
    w_out,
    gain_mlp,
    w_gate,
    w_up,
    w_down,
    cotangent,
):
    rows = inputs.shape[1]
    width = inputs.shape[2]
    groups = lax.axis_size("head")
    shards = lax.axis_size("ffn")
    heads_here = HEADS // groups
    span_rows = rows * groups
    block_rows = span_rows // max(1, span_rows // 512)
    head_pos = lax.axis_index("head")
    valid_len = lengths[0]
    packed_cols = heads_here * 3 * HD
    out_cols = heads_here * HD
    hidden_here = w_gate.shape[1]

    owners = [head_pos ^ m for m in range(groups)]
    x_all = [inputs[0]] + [swap(inputs[0], "head", m) for m in range(1, groups)]
    early = []
    for m in range(groups):
        piece = lax.dynamic_slice_in_dim(first_values[0], owners[m] * out_cols, out_cols, 1)
        early.append(swap(piece, "head", m) if m else piece)
    far = range(2, shards, 2)
    grad_rows = jnp.concatenate([cotangent[0]] + [swap(cotangent[0], "ffn", m) for m in far], 0)
    gate_w = jnp.concatenate([w_gate, swap(w_gate, "ffn", 1)], 1)
    up_w = jnp.concatenate([w_up, swap(w_up, "ffn", 1)], 1)
    down_w = jnp.concatenate([w_down, swap(w_down, "ffn", 1)], 0)
    w_heads = lax.dynamic_slice_in_dim(w_qkv, head_pos * packed_cols, packed_cols, 1)
    out_w = jnp.concatenate(
        [lax.dynamic_slice_in_dim(w_out, o * out_cols, out_cols, 0) for o in owners], 0
    )

    positions = jnp.concatenate([o * rows + jnp.arange(rows, dtype=jnp.int32) for o in owners])
    cosine, sine = rotary(positions, HD)
    normed, scaled, queries, key_list, mixes = [], [], [], [], []
    rows_in = inputs[0].astype(jnp.float32)
    scale_one = rms_scale(rows_in)
    for m in range(groups):
        block = x_all[m].astype(jnp.float32)
        scale = rms_scale(block)
        scaled.append(block * scale)
        normed.append((block * scale * gain_attn).astype(jnp.bfloat16))
        packed = matmul(normed[m], w_heads).astype(jnp.bfloat16)
        packed = packed.reshape(rows, heads_here, 3, HD).astype(jnp.float32)
        part = slice(m * rows, (m + 1) * rows)
        queries.append(rotate(packed[:, :, 0], cosine[part], sine[part], 1.0))
        key_list.append(rotate(packed[:, :, 1], cosine[part], sine[part], 1.0))
        value = early[m].reshape(rows, heads_here, HD).astype(jnp.float32)
        mixes.append(0.5 * (packed[:, :, 2] + value))
    query = jnp.concatenate(queries, 0).astype(jnp.bfloat16)
    keys = jnp.concatenate(key_list, 0).astype(jnp.bfloat16)
    mixed = jnp.concatenate(mixes, 0).astype(jnp.bfloat16)
    attended, log_sums = attend_forward(query, keys, mixed, positions, valid_len, block_rows)
    attended = attended.reshape(groups, rows, out_cols)
    att_own = jnp.concatenate(
        [attended[0]] + [swap(attended[m], "head", m) for m in range(1, groups)], 1
    )
    hidden = rows_in + matmul(att_own, out_w)
    scale_two = rms_scale(hidden)
    normed_two = (hidden * scale_two * gain_mlp).astype(jnp.bfloat16)

    mlp_rows = [normed_two] + [swap(normed_two, "ffn", m) for m in far]
    grad_list = [grad_rows[i * rows : (i + 1) * rows] for i in range(len(mlp_rows))]
    actives, grad_gates, grad_ups, downs, grad_normed_list = [], [], [], [], []
    for i, block in enumerate(mlp_rows):
        gate_rows = matmul(block, gate_w)
        up_rows = matmul(block, up_w)
        sigmoid_gate = jax.nn.sigmoid(gate_rows)
        silu_gate = gate_rows * sigmoid_gate
        grad_active = against(grad_list[i], down_w)
        actives.append((silu_gate * up_rows).astype(jnp.bfloat16))
        grad_gates.append(
            (
                grad_active * up_rows * sigmoid_gate * (1.0 + gate_rows * (1.0 - sigmoid_gate))
            ).astype(jnp.bfloat16)
        )
        grad_ups.append((grad_active * silu_gate).astype(jnp.bfloat16))
        grad_normed_list.append(against(grad_gates[i], gate_w) + against(grad_ups[i], up_w))
        downs.append(matmul(actives[i], down_w))
    grad_normed_two = grad_normed_list[0]
    for i, m in enumerate(far):
        came = swap(grad_normed_list[i + 1].astype(jnp.bfloat16), "ffn", m)
        grad_normed_two = grad_normed_two + came.astype(jnp.float32)
    down_rows = downs[0]
    for i, m in enumerate(far):
        down_rows = down_rows + swap(downs[i + 1].astype(jnp.bfloat16), "ffn", m).astype(jnp.float32)
    output = (hidden + down_rows).astype(jnp.bfloat16)[None]

    all_rows = jnp.concatenate(mlp_rows, 0)
    ff_sums = []
    for left, right in (
        (grad_rows, jnp.concatenate(actives, 0)),
        (all_rows, jnp.concatenate(grad_gates, 0)),
        (all_rows, jnp.concatenate(grad_ups, 0)),
    ):
        away = inner_rows(left, right[:, hidden_here:]).astype(jnp.bfloat16)
        part = inner_rows(left, right[:, :hidden_here])
        part = (part + swap(away, "ffn", 1).astype(jnp.float32)).astype(jnp.bfloat16)
        steps = [("head", b) for b in bits_of("head")] + [("row", b) for b in bits_of("row")]
        part = part.reshape([2] * len(steps) + [-1, hidden_here])
        order = [s for s in steps if s[0] == "head"] + [s for s in reversed(steps) if s[0] == "row"]
        left_steps = list(steps)
        for s in order:
            part = halve(part, left_steps.index(s), *s)
            left_steps.remove(s)
            if left_steps:
                part = part.astype(jnp.bfloat16)
        ff_sums.append(part)
    sum_down, sum_gate, sum_up = ff_sums

    grad_y = cotangent[0].astype(jnp.float32)
    grad_gain_two = jnp.sum(grad_normed_two * hidden * scale_two, axis=0)
    weighted_two = grad_normed_two * gain_mlp
    cube_two = scale_two * scale_two * scale_two
    grad_hidden = (
        grad_y
        + scale_two * weighted_two
        - hidden * cube_two * jnp.mean(weighted_two * hidden, axis=-1, keepdims=True)
    )
    grad_proj = grad_hidden.astype(jnp.bfloat16)
    grad_att = against(grad_proj, out_w).astype(jnp.bfloat16)
    grad_att = jnp.concatenate(
        [
            swap(grad_att[:, m * out_cols : (m + 1) * out_cols], "head", m)
            if m
            else grad_att[:, :out_cols]
            for m in range(groups)
        ],
        0,
    ).reshape(span_rows, heads_here, HD)

    def over_buckets(part):
        steps = [("ffn", b) for b in bits_of("ffn")] + [("row", b) for b in bits_of("row")]
        part = part.astype(jnp.bfloat16).reshape([2] * len(steps) + [-1, part.shape[1]])
        order = [s for s in reversed(steps) if s[0] == "ffn"] + [
            s for s in reversed(steps) if s[0] == "row"
        ]
        left_steps = list(steps)
        for s in order:
            part = halve(part, left_steps.index(s), *s)
            left_steps.remove(s)
            if left_steps:
                part = part.astype(jnp.bfloat16)
        return part

    part = over_buckets(inner_rows(grad_proj, att_own))
    sum_out = part[:, :out_cols]
    for m in range(1, groups):
        came = swap(part[:, m * out_cols : (m + 1) * out_cols].astype(jnp.bfloat16), "head", m)
        sum_out = sum_out + came.astype(jnp.float32)

    grad_query, grad_keys, grad_mixed = attend_backward(
        query, keys, mixed, positions, valid_len, log_sums, grad_att, block_rows
    )
    grad_packed = jnp.stack(
        [
            rotate(grad_query, cosine, sine, -1.0),
            rotate(grad_keys, cosine, sine, -1.0),
            0.5 * grad_mixed,
        ],
        axis=2,
    )
    grad_packed = grad_packed.astype(jnp.bfloat16).reshape(span_rows, packed_cols)
    grad_early = (0.5 * grad_mixed).astype(jnp.bfloat16).reshape(span_rows, out_cols)
    firsts = [grad_early[m * rows : (m + 1) * rows] for m in range(groups)]
    firsts = [swap(firsts[m], "head", m) if m else firsts[0] for m in range(groups)]
    grad_first = jnp.zeros((rows, width), jnp.bfloat16)
    for m in range(groups):
        grad_first = lax.dynamic_update_slice_in_dim(grad_first, firsts[m], owners[m] * out_cols, 1)
    shares = [
        against(grad_packed[m * rows : (m + 1) * rows], w_heads) for m in range(groups)
    ]
    grad_gain_one = sum(jnp.sum(shares[m] * scaled[m], axis=0) for m in range(groups))
    grad_normed = shares[0]
    for m in range(1, groups):
        grad_normed = grad_normed + swap(shares[m].astype(jnp.bfloat16), "head", m).astype(jnp.float32)
    sum_qkv = over_buckets(inner_rows(jnp.concatenate(normed, 0), grad_packed))
    weighted_one = grad_normed * gain_attn
    cube_one = scale_one * scale_one * scale_one
    grad_in = (
        grad_hidden
        + scale_one * weighted_one
        - rows_in * cube_one * jnp.mean(weighted_one * rows_in, axis=-1, keepdims=True)
    )
    gains = total(jnp.stack([grad_gain_one, grad_gain_two]), ("ffn", "head", "row"))
    return (
        output,
        grad_in[None],
        grad_first[None],
        gains[0],
        sum_qkv,
        sum_out.T,
        gains[1],
        sum_gate,
        sum_up,
        sum_down.T,
    )


def solution(mesh):
    in_specs = (
        P(("ffn", "row"), "head", None),
        P(("ffn", "row"), "head", None),
        P(("ffn", "row")),
        P(),
        P(),
        P(),
        P(),
        P(None, "ffn"),
        P(None, "ffn"),
        P("ffn", None),
        P(("ffn", "row"), "head", None),
    )
    out_specs = (
        P(("ffn", "row"), "head", None),
        P(("ffn", "row"), "head", None),
        P(("ffn", "row"), "head", None),
        P(),
        P(("ffn", "row"), "head"),
        P("head", ("ffn", "row")),
        P(),
        P(("head", "row"), "ffn"),
        P(("head", "row"), "ffn"),
        P("ffn", ("head", "row")),
    )
    return jax.shard_map(
        on_device, mesh=mesh, in_specs=in_specs, out_specs=out_specs, check_vma=False
    )
```

```python
import jax
import jax.numpy as jnp
from jax import lax
from jax.experimental import pallas as pl
from jax.experimental.pallas import tpu as pltpu
from jax.sharding import PartitionSpec as P

HEADS = 16
HD = 64
MIN_LEN = 512
STEP = 256


eps = 1e-06


def rms_scale(values):
    return lax.rsqrt(jnp.mean(values * values, axis=-1, keepdims=True) + eps)


def matmul(left, right):
    return jnp.dot(left, right, preferred_element_type=jnp.float32)


def inner_rows(left, right):
    return lax.dot_general(
        left, right, (((0,), (0,)), ((), ())), preferred_element_type=jnp.float32
    )


def against(left, right):
    return lax.dot_general(
        left, right, (((1,), (1,)), ((), ())), preferred_element_type=jnp.float32
    )


def swap(values, axis, mask):
    size = lax.axis_size(axis)
    return lax.ppermute(values, axis, [(i, i ^ mask) for i in range(size)])


def bits_of(axis):
    size = lax.axis_size(axis)
    return [1 << b for b in range(size.bit_length() - 2, -1, -1)]


def halve(values, dim, axis, mask):
    bit = (lax.axis_index(axis) // mask) % 2
    away = lax.dynamic_index_in_dim(values, 1 - bit, dim, keepdims=False)
    kept = lax.dynamic_index_in_dim(values, bit, dim, keepdims=False)
    came = swap(away.astype(jnp.bfloat16), axis, mask)
    return kept.astype(jnp.float32) + came.astype(jnp.float32)


def total(values, axes):
    for axis in axes:
        for mask in reversed(bits_of(axis)):
            values = values + swap(values, axis, mask)
    return values


def rotary(positions, head_size):
    half_size = head_size // 2
    inverse = jnp.exp(
        -jnp.log(10000.0) * jnp.arange(half_size, dtype=jnp.float32) * 2.0 / head_size
    )
    angles = positions.astype(jnp.float32)[:, None] * inverse[None, :]
    return (jnp.cos(angles), jnp.sin(angles))


def rotate(vectors, cosine, sine, sign):
    half_size = vectors.shape[-1] // 2
    first_half = vectors[..., :half_size]
    second_half = vectors[..., half_size:]
    cos_rows = cosine[:, None, :]
    sin_rows = sign * sine[:, None, :]
    return jnp.concatenate(
        [
            first_half * cos_rows - second_half * sin_rows,
            second_half * cos_rows + first_half * sin_rows,
        ],
        axis=-1,
    )


def masked_scores(q_rows, keys, q_pos, k_pos, valid):
    raw = jnp.einsum("qhe,khe->hqk", q_rows, keys, preferred_element_type=jnp.float32)
    allowed = (k_pos[None, :] <= q_pos[:, None]) & (k_pos[None, :] < valid)
    return jnp.where(allowed[None], 0.125 * raw, -1e30)


def scan_forward(query, keys, mixed, positions, valid, block_rows):
    count = query.shape[0] // block_rows

    def step(carry, index):
        start = index * block_rows
        q_rows = lax.dynamic_slice_in_dim(query, start, block_rows, 0)
        q_pos = lax.dynamic_slice_in_dim(positions, start, block_rows, 0)
        scores = masked_scores(q_rows, keys, q_pos, positions, valid)
        top = jnp.max(scores, axis=-1, keepdims=True)
        expo = jnp.exp(scores - top)
        total_w = jnp.sum(expo, axis=-1, keepdims=True)
        weights = expo / total_w
        result = jnp.einsum(
            "hqk,khe->qhe", weights.astype(jnp.bfloat16), mixed, preferred_element_type=jnp.float32
        )
        return (carry, (result.astype(jnp.bfloat16), top + jnp.log(total_w)))

    _, (outs, log_sums) = lax.scan(step, 0, jnp.arange(count, dtype=jnp.int32))
    return (outs.reshape(query.shape), log_sums)


def scan_backward(query, keys, mixed, positions, valid, log_sums, grad_out, block_rows):
    count = query.shape[0] // block_rows
    zeros = jnp.zeros(keys.shape, jnp.float32)

    def step(carry, index):
        key_sum, value_sum = carry
        start = index * block_rows
        q_rows = lax.dynamic_slice_in_dim(query, start, block_rows, 0)
        q_pos = lax.dynamic_slice_in_dim(positions, start, block_rows, 0)
        g_rows = lax.dynamic_slice_in_dim(grad_out, start, block_rows, 0)
        scores = masked_scores(q_rows, keys, q_pos, positions, valid)
        weights = jnp.exp(scores - log_sums[index])
        grad_w = jnp.einsum("qhe,khe->hqk", g_rows, mixed, preferred_element_type=jnp.float32)
        delta = jnp.sum(weights * grad_w, axis=-1, keepdims=True)
        grad_s = (weights * (grad_w - delta)).astype(jnp.bfloat16)
        grad_q = 0.125 * jnp.einsum(
            "hqk,khe->qhe", grad_s, keys, preferred_element_type=jnp.float32
        )
        key_sum = key_sum + 0.125 * jnp.einsum(
            "hqk,qhe->khe", grad_s, q_rows, preferred_element_type=jnp.float32
        )
        value_sum = value_sum + jnp.einsum(
            "hqk,qhe->khe", weights.astype(jnp.bfloat16), g_rows, preferred_element_type=jnp.float32
        )
        return ((key_sum, value_sum), grad_q)

    (grad_keys, grad_mixed), grad_query = lax.scan(
        step, (zeros, zeros), jnp.arange(count, dtype=jnp.int32)
    )
    return (grad_query.reshape(query.shape), grad_keys, grad_mixed)


def any_groups(
    inputs,
    first_values,
    lengths,
    gain_attn,
    w_qkv,
    w_out,
    gain_mlp,
    w_gate,
    w_up,
    w_down,
    cotangent,
):
    rows = inputs.shape[1]
    width = inputs.shape[2]
    groups = lax.axis_size("head")
    shards = lax.axis_size("ffn")
    heads_here = HEADS // groups
    span_rows = rows * groups
    block_rows = span_rows // max(1, span_rows // 512)
    head_pos = lax.axis_index("head")
    valid_len = lengths[0]
    packed_cols = heads_here * 3 * HD
    out_cols = heads_here * HD
    hidden_here = w_gate.shape[1]

    owners = [head_pos ^ m for m in range(groups)]
    x_all = [inputs[0]] + [swap(inputs[0], "head", m) for m in range(1, groups)]
    early = []
    for m in range(groups):
        piece = lax.dynamic_slice_in_dim(first_values[0], owners[m] * out_cols, out_cols, 1)
        early.append(swap(piece, "head", m) if m else piece)
    far = range(2, shards, 2)
    grad_rows = jnp.concatenate([cotangent[0]] + [swap(cotangent[0], "ffn", m) for m in far], 0)
    gate_w = jnp.concatenate([w_gate, swap(w_gate, "ffn", 1)], 1)
    up_w = jnp.concatenate([w_up, swap(w_up, "ffn", 1)], 1)
    down_w = jnp.concatenate([w_down, swap(w_down, "ffn", 1)], 0)
    w_heads = lax.dynamic_slice_in_dim(w_qkv, head_pos * packed_cols, packed_cols, 1)
    out_w = jnp.concatenate(
        [lax.dynamic_slice_in_dim(w_out, o * out_cols, out_cols, 0) for o in owners], 0
    )

    positions = jnp.concatenate([o * rows + jnp.arange(rows, dtype=jnp.int32) for o in owners])
    cosine, sine = rotary(positions, HD)
    normed, scaled, queries, key_list, mixes = [], [], [], [], []
    rows_in = inputs[0].astype(jnp.float32)
    scale_one = rms_scale(rows_in)
    for m in range(groups):
        block = x_all[m].astype(jnp.float32)
        scale = rms_scale(block)
        scaled.append(block * scale)
        normed.append((block * scale * gain_attn).astype(jnp.bfloat16))
        packed = matmul(normed[m], w_heads).astype(jnp.bfloat16)
        packed = packed.reshape(rows, heads_here, 3, HD).astype(jnp.float32)
        part = slice(m * rows, (m + 1) * rows)
        queries.append(rotate(packed[:, :, 0], cosine[part], sine[part], 1.0))
        key_list.append(rotate(packed[:, :, 1], cosine[part], sine[part], 1.0))
        value = early[m].reshape(rows, heads_here, HD).astype(jnp.float32)
        mixes.append(0.5 * (packed[:, :, 2] + value))
    query = jnp.concatenate(queries, 0).astype(jnp.bfloat16)
    keys = jnp.concatenate(key_list, 0).astype(jnp.bfloat16)
    mixed = jnp.concatenate(mixes, 0).astype(jnp.bfloat16)
    attended, log_sums = scan_forward(query, keys, mixed, positions, valid_len, block_rows)
    attended = attended.reshape(groups, rows, out_cols)
    att_own = jnp.concatenate(
        [attended[0]] + [swap(attended[m], "head", m) for m in range(1, groups)], 1
    )
    hidden = rows_in + matmul(att_own, out_w)
    scale_two = rms_scale(hidden)
    normed_two = (hidden * scale_two * gain_mlp).astype(jnp.bfloat16)

    mlp_rows = [normed_two] + [swap(normed_two, "ffn", m) for m in far]
    grad_list = [grad_rows[i * rows : (i + 1) * rows] for i in range(len(mlp_rows))]
    actives, grad_gates, grad_ups, downs, grad_normed_list = [], [], [], [], []
    for i, block in enumerate(mlp_rows):
        gate_rows = matmul(block, gate_w)
        up_rows = matmul(block, up_w)
        sigmoid_gate = jax.nn.sigmoid(gate_rows)
        silu_gate = gate_rows * sigmoid_gate
        grad_active = against(grad_list[i], down_w)
        actives.append((silu_gate * up_rows).astype(jnp.bfloat16))
        grad_gates.append(
            (
                grad_active * up_rows * sigmoid_gate * (1.0 + gate_rows * (1.0 - sigmoid_gate))
            ).astype(jnp.bfloat16)
        )
        grad_ups.append((grad_active * silu_gate).astype(jnp.bfloat16))
        grad_normed_list.append(against(grad_gates[i], gate_w) + against(grad_ups[i], up_w))
        downs.append(matmul(actives[i], down_w))
    grad_normed_two = grad_normed_list[0]
    for i, m in enumerate(far):
        came = swap(grad_normed_list[i + 1].astype(jnp.bfloat16), "ffn", m)
        grad_normed_two = grad_normed_two + came.astype(jnp.float32)
    down_rows = downs[0]
    for i, m in enumerate(far):
        down_rows = down_rows + swap(downs[i + 1].astype(jnp.bfloat16), "ffn", m).astype(jnp.float32)
    output = (hidden + down_rows).astype(jnp.bfloat16)[None]

    all_rows = jnp.concatenate(mlp_rows, 0)
    ff_sums = []
    for left, right in (
        (grad_rows, jnp.concatenate(actives, 0)),
        (all_rows, jnp.concatenate(grad_gates, 0)),
        (all_rows, jnp.concatenate(grad_ups, 0)),
    ):
        away = inner_rows(left, right[:, hidden_here:]).astype(jnp.bfloat16)
        part = inner_rows(left, right[:, :hidden_here])
        part = (part + swap(away, "ffn", 1).astype(jnp.float32)).astype(jnp.bfloat16)
        steps = [("head", b) for b in bits_of("head")] + [("row", b) for b in bits_of("row")]
        part = part.reshape([2] * len(steps) + [-1, hidden_here])
        order = [s for s in steps if s[0] == "head"] + [s for s in reversed(steps) if s[0] == "row"]
        left_steps = list(steps)
        for s in order:
            part = halve(part, left_steps.index(s), *s)
            left_steps.remove(s)
            if left_steps:
                part = part.astype(jnp.bfloat16)
        ff_sums.append(part)
    sum_down, sum_gate, sum_up = ff_sums

    grad_y = cotangent[0].astype(jnp.float32)
    grad_gain_two = jnp.sum(grad_normed_two * hidden * scale_two, axis=0)
    weighted_two = grad_normed_two * gain_mlp
    cube_two = scale_two * scale_two * scale_two
    grad_hidden = (
        grad_y
        + scale_two * weighted_two
        - hidden * cube_two * jnp.mean(weighted_two * hidden, axis=-1, keepdims=True)
    )
    grad_proj = grad_hidden.astype(jnp.bfloat16)
    grad_att = against(grad_proj, out_w).astype(jnp.bfloat16)
    grad_att = jnp.concatenate(
        [
            swap(grad_att[:, m * out_cols : (m + 1) * out_cols], "head", m)
            if m
            else grad_att[:, :out_cols]
            for m in range(groups)
        ],
        0,
    ).reshape(span_rows, heads_here, HD)

    def over_buckets(part):
        steps = [("ffn", b) for b in bits_of("ffn")] + [("row", b) for b in bits_of("row")]
        part = part.astype(jnp.bfloat16).reshape([2] * len(steps) + [-1, part.shape[1]])
        order = [s for s in reversed(steps) if s[0] == "ffn"] + [
            s for s in reversed(steps) if s[0] == "row"
        ]
        left_steps = list(steps)
        for s in order:
            part = halve(part, left_steps.index(s), *s)
            left_steps.remove(s)
            if left_steps:
                part = part.astype(jnp.bfloat16)
        return part

    part = over_buckets(inner_rows(grad_proj, att_own))
    sum_out = part[:, :out_cols]
    for m in range(1, groups):
        came = swap(part[:, m * out_cols : (m + 1) * out_cols].astype(jnp.bfloat16), "head", m)
        sum_out = sum_out + came.astype(jnp.float32)

    grad_query, grad_keys, grad_mixed = scan_backward(
        query, keys, mixed, positions, valid_len, log_sums, grad_att, block_rows
    )
    grad_packed = jnp.stack(
        [
            rotate(grad_query, cosine, sine, -1.0),
            rotate(grad_keys, cosine, sine, -1.0),
            0.5 * grad_mixed,
        ],
        axis=2,
    )
    grad_packed = grad_packed.astype(jnp.bfloat16).reshape(span_rows, packed_cols)
    grad_early = (0.5 * grad_mixed).astype(jnp.bfloat16).reshape(span_rows, out_cols)
    firsts = [grad_early[m * rows : (m + 1) * rows] for m in range(groups)]
    firsts = [swap(firsts[m], "head", m) if m else firsts[0] for m in range(groups)]
    grad_first = jnp.zeros((rows, width), jnp.bfloat16)
    for m in range(groups):
        grad_first = lax.dynamic_update_slice_in_dim(grad_first, firsts[m], owners[m] * out_cols, 1)
    shares = [
        against(grad_packed[m * rows : (m + 1) * rows], w_heads) for m in range(groups)
    ]
    grad_gain_one = sum(jnp.sum(shares[m] * scaled[m], axis=0) for m in range(groups))
    grad_normed = shares[0]
    for m in range(1, groups):
        grad_normed = grad_normed + swap(shares[m].astype(jnp.bfloat16), "head", m).astype(jnp.float32)
    sum_qkv = over_buckets(inner_rows(jnp.concatenate(normed, 0), grad_packed))
    weighted_one = grad_normed * gain_attn
    cube_one = scale_one * scale_one * scale_one
    grad_in = (
        grad_hidden
        + scale_one * weighted_one
        - rows_in * cube_one * jnp.mean(weighted_one * rows_in, axis=-1, keepdims=True)
    )
    gains = total(jnp.stack([grad_gain_one, grad_gain_two]), ("ffn", "head", "row"))
    return (
        output,
        grad_in[None],
        grad_first[None],
        gains[0],
        sum_qkv,
        sum_out.T,
        gains[1],
        sum_gate,
        sum_up,
        sum_down.T,
    )


def spans(total):
    return [(a, min(a + STEP, total)) for a in range(0, total, STEP)]

def turn(values):
    lane = lax.broadcasted_iota(jnp.int32, values.shape, 1)
    return jnp.where(lane % HD < HD // 2, pltpu.roll(values, 2 * HD - HD // 2, 1), pltpu.roll(values, HD // 2, 1))

def forward_body(place, packed_own, packed_oth, early_own, early_oth, cos_ref, sin_ref, att_own, att_oth, q_out, k_out, v_out, lse_out, packed, early, att):
    rows = packed_own.shape[0]
    span = 2 * rows
    own = pl.multiple_of(place[0] * rows, rows)
    oth = pl.multiple_of((1 - place[0]) * rows, rows)
    valid = place[1]
    packed[pl.ds(own, rows), :] = packed_own[...]
    packed[pl.ds(oth, rows), :] = packed_oth[...]
    early[pl.ds(own, rows), :] = early_own[...]
    early[pl.ds(oth, rows), :] = early_oth[...]
    wide = 2 * HD
    first = lax.broadcasted_iota(jnp.int32, (1, wide), 1) < HD
    for a, b in spans(span):
        x0 = packed[a:b, :wide].astype(jnp.float32)
        x1 = packed[a:b, wide : 2 * wide].astype(jnp.float32)
        x2 = packed[a:b, 2 * wide :].astype(jnp.float32)
        cosine = cos_ref[a:b, :]
        sine = sin_ref[a:b, :]
        q = jnp.where(first, x0, x1)
        k = pltpu.roll(jnp.where(first, x2, x0), HD, 1)
        v = jnp.where(first, x1, x2)
        q_out[a:b, :] = (q * cosine + turn(q) * sine).astype(jnp.bfloat16)
        k_out[a:b, :] = (k * cosine + turn(k) * sine).astype(jnp.bfloat16)
        v_out[a:b, :] = (0.5 * (v + early[a:b, :].astype(jnp.float32))).astype(jnp.bfloat16)
    for a, b in spans(span):
        q = q_out[a:b, :] * jnp.asarray(0.125, jnp.bfloat16)
        size = b - a
        outs, logs = [], []
        down = lax.broadcasted_iota(jnp.int32, (size, size), 0)
        across = lax.broadcasted_iota(jnp.int32, (size, size), 1)
        allowed = across <= down
        if b > MIN_LEN:
            allowed = allowed & (across < valid - a)
        for e in range(2):
            qe = jnp.where(first == (e == 0), q, jnp.zeros_like(q))
            diag = jnp.where(allowed, against(qe, k_out[a:b, :]), -1e30)
            top = jnp.max(diag, axis=1, keepdims=True)
            if a:
                past = against(qe, k_out[:a, :])
                top = jnp.maximum(top, jnp.max(past, axis=1, keepdims=True))
            expo = jnp.exp(diag - top)
            amount = jnp.sum(expo, axis=1, keepdims=True)
            out = matmul(expo.astype(jnp.bfloat16), v_out[a:b, :])
            if a:
                expo = jnp.exp(past - top)
                amount = amount + jnp.sum(expo, axis=1, keepdims=True)
                out = out + matmul(expo.astype(jnp.bfloat16), v_out[:a, :])
            outs.append(out / amount)
            logs.append(top + jnp.log(amount))
        att[a:b, :] = jnp.where(first, outs[0], outs[1]).astype(jnp.bfloat16)
        lse_out[a:b, :] = jnp.where(first, logs[0], logs[1])
    att_own[...] = att[pl.ds(own, rows), :]
    att_oth[...] = att[pl.ds(oth, rows), :]

def attend_forward(place, packed_own, packed_oth, early_own, early_oth, cosine, sine):
    rows, cols = packed_own.shape
    heads = cols // (3 * HD)
    wide = 2 * HD
    span = 2 * rows
    bf = jnp.bfloat16
    def block(r, c): return pl.BlockSpec((r, c), lambda p, s: (0, p))
    def fixed(r, c): return pl.BlockSpec((r, c), lambda p, s: (0, 0))
    out = jax.ShapeDtypeStruct((rows, heads * HD), bf)
    nat = jax.ShapeDtypeStruct((span, heads * HD), bf)
    return pl.pallas_call(
        forward_body,
        out_shape=(out, out, nat, nat, nat, jax.ShapeDtypeStruct((span, heads * HD), jnp.float32)),
        grid_spec=pltpu.PrefetchScalarGridSpec(
            num_scalar_prefetch=1, grid=(heads // 2,),
            in_specs=[block(rows, 3 * wide)] * 2 + [block(rows, wide)] * 2 + [fixed(span, wide)] * 2,
            out_specs=[block(rows, wide)] * 2 + [block(span, wide)] * 4,
            scratch_shapes=[pltpu.VMEM((span, 3 * wide), bf), pltpu.VMEM((span, wide), bf), pltpu.VMEM((span, wide), bf)],
        ),
        cost_estimate=pl.CostEstimate(flops=4 * heads * span * span * HD, transcendentals=heads * span * span, bytes_accessed=12 * span * heads * HD),
        name="attend_forward",
    )(place, packed_own, packed_oth, early_own, early_oth, cosine, sine)

def backward_body(place, q_ref, k_ref, v_ref, lse_ref, go_own, go_oth, att_own, att_oth, cos_ref, sin_ref, d_own, d_oth, f_own, f_oth, grad, prod, dq, packed):
    rows = go_own.shape[0]
    span = 2 * rows
    own = pl.multiple_of(place[0] * rows, rows)
    oth = pl.multiple_of((1 - place[0]) * rows, rows)
    valid = place[1]
    wide = 2 * HD
    f32 = jnp.float32
    bf = jnp.bfloat16
    first = lax.broadcasted_iota(jnp.int32, (1, wide), 1) < HD
    grad[pl.ds(own, rows), :] = go_own[...]
    grad[pl.ds(oth, rows), :] = go_oth[...]
    prod[pl.ds(own, rows), :] = go_own[...].astype(f32) * att_own[...].astype(f32)
    prod[pl.ds(oth, rows), :] = go_oth[...].astype(f32) * att_oth[...].astype(f32)
    flat = prod[...].T
    deltas = [jnp.sum(flat[e * HD : (e + 1) * HD, :], axis=0, keepdims=True) for e in range(2)]
    logs = lse_ref[...].T
    logs = [logs[e * HD : e * HD + 1, :] for e in range(2)]
    dq[...] = jnp.zeros_like(dq)
    eighth = jnp.asarray(0.125, bf)
    for a, b in spans(span):
        size = b - a
        down = lax.broadcasted_iota(jnp.int32, (size, size), 0)
        across = lax.broadcasted_iota(jnp.int32, (size, size), 1)
        allowed = down <= across
        if b > MIN_LEN:
            allowed = allowed & (down < valid - a)
        k = k_ref[a:b, :]
        v = v_ref[a:b, :]
        dk = dv = None
        for e in range(2):
            mine = first == (e == 0)
            ke = jnp.where(mine, k * eighth, jnp.zeros_like(k))
            for lo, hi in ((a, b), (b, span)):
                if lo == hi:
                    continue
                q = q_ref[lo:hi, :] * eighth
                qe = jnp.where(mine, q, jnp.zeros_like(q))
                g = grad[lo:hi, :]
                ge = jnp.where(mine, g, jnp.zeros_like(g))
                scores = against(k, qe)
                if lo == a:
                    scores = jnp.where(allowed, scores, -1e30)
                weights = jnp.exp(scores - logs[e][:, lo:hi])
                grad_w = against(v, ge)
                grad_s = (weights * (grad_w - deltas[e][:, lo:hi])).astype(bf)
                dv_here = matmul(weights.astype(bf), ge)
                dk_here = matmul(grad_s, qe)
                dv = dv_here if dv is None else dv + dv_here
                dk = dk_here if dk is None else dk + dk_here
                dq[lo:hi, :] += inner_rows(grad_s, ke)
        cosine = cos_ref[a:b, :]
        sine = sin_ref[a:b, :]
        dv = (0.5 * dv).astype(bf)
        dk = (dk * cosine - turn(dk) * sine)
        dk = pltpu.roll(dk, HD, 1).astype(bf)
        gq = dq[a:b, :]
        gq = (gq * cosine - turn(gq) * sine).astype(bf)
        packed[a:b, :wide] = jnp.where(first, gq, dk)
        packed[a:b, wide : 2 * wide] = jnp.where(first, dv, gq)
        packed[a:b, 2 * wide :] = jnp.where(first, dk, dv)
        grad[a:b, :] = dv
    d_own[...] = packed[pl.ds(own, rows), :]
    d_oth[...] = packed[pl.ds(oth, rows), :]
    f_own[...] = grad[pl.ds(own, rows), :]
    f_oth[...] = grad[pl.ds(oth, rows), :]

def attend_backward(place, q, k, v, lse, go_own, go_oth, att_own, att_oth, cosine, sine):
    span, cols = q.shape
    rows = span // 2
    heads = cols // HD
    wide = 2 * HD
    bf = jnp.bfloat16
    def block(r, c): return pl.BlockSpec((r, c), lambda p, s: (0, p))
    def fixed(r, c): return pl.BlockSpec((r, c), lambda p, s: (0, 0))
    out = jax.ShapeDtypeStruct((rows, 3 * cols), bf)
    first = jax.ShapeDtypeStruct((rows, cols), bf)
    return pl.pallas_call(
        backward_body,
        out_shape=(out, out, first, first),
        grid_spec=pltpu.PrefetchScalarGridSpec(
            num_scalar_prefetch=1, grid=(heads // 2,),
            in_specs=[block(span, wide)] * 4 + [block(rows, wide)] * 4 + [fixed(span, wide)] * 2,
            out_specs=[block(rows, 3 * wide)] * 2 + [block(rows, wide)] * 2,
            scratch_shapes=[pltpu.VMEM((span, wide), bf), pltpu.VMEM((span, wide), jnp.float32), pltpu.VMEM((span, wide), jnp.float32), pltpu.VMEM((span, 3 * wide), bf)],
        ),
        cost_estimate=pl.CostEstimate(flops=10 * heads * span * span * HD, transcendentals=heads * span * span, bytes_accessed=20 * span * heads * HD),
        name="attend_backward",
    )(place, q, k, v, lse, go_own, go_oth, att_own, att_oth, cosine, sine)


def reorder(values, picks, size):
    return jnp.concatenate(
        [lax.dynamic_slice_in_dim(values, p * size, size, 1) for p in picks], axis=1
    )


def both(first, second):
    return jnp.concatenate([first, second], 0)


def low(values):
    return values.astype(jnp.bfloat16)


def high(values):
    return values.astype(jnp.float32)


def two_groups(
    inputs,
    first_values,
    lengths,
    gain_attn,
    w_qkv,
    w_out,
    gain_mlp,
    w_gate,
    w_up,
    w_down,
    cotangent,
):
    rows = inputs.shape[1]
    width = inputs.shape[2]
    span = 2 * rows
    out_cols = HEADS // 2 * HD
    packed_cols = 3 * out_cols
    h = lax.axis_index("head")
    f = lax.axis_index("ffn")
    r = lax.axis_index("row")
    row_size = lax.axis_size("row")
    place = jnp.stack([h, lengths[0]]).astype(jnp.int32)

    x_own = inputs[0]
    x_oth = swap(x_own, "head", 1)
    early_own = lax.dynamic_slice_in_dim(first_values[0], h * out_cols, out_cols, 1)
    early_oth = swap(
        lax.dynamic_slice_in_dim(first_values[0], (1 - h) * out_cols, out_cols, 1), "head", 1
    )
    dy_own = cotangent[0]
    dy_oth = swap(dy_own, "ffn", 2)
    gate_w = (w_gate.T, swap(w_gate.T, "ffn", 1))
    up_w = (w_up.T, swap(w_up.T, "ffn", 1))
    down_w = (w_down, swap(w_down, "ffn", 1))
    qkv_w = lax.dynamic_slice_in_dim(w_qkv, h * packed_cols, packed_cols, 1)
    out_own = lax.dynamic_slice_in_dim(w_out, h * out_cols, out_cols, 0)
    out_oth = lax.dynamic_slice_in_dim(w_out, (1 - h) * out_cols, out_cols, 0)
    half = HD // 2
    inverse = jnp.exp(-jnp.log(10000.0) * jnp.arange(half, dtype=jnp.float32) * 2.0 / HD)
    angles = jnp.arange(span, dtype=jnp.float32)[:, None] * jnp.tile(inverse, 4)[None, :]
    cosine = jnp.cos(angles)
    sign = jnp.where(jnp.arange(2 * HD) % HD < half, -1.0, 1.0)
    sine = jnp.sin(angles) * sign[None, :]

    ff_size = width // (2 * row_size)
    ff_order = [(h ^ a) * row_size + (r ^ b) for a in (1, 0) for b in (3, 1, 2, 0)]
    att_size = width // 8
    att_order = [
        ((f ^ a) * row_size + (r & 2 ^ b)) // 2 for a in (3, 1, 2, 0) for b in (2, 0)
    ]

    rows_own = high(x_own)
    scale_one = rms_scale(rows_own)
    scaled_own = rows_own * scale_one
    xn_own = low(scaled_own * gain_attn)
    packed_own = low(matmul(xn_own, qkv_w))
    rows_oth = high(x_oth)
    scaled_oth = rows_oth * rms_scale(rows_oth)
    xn_oth = low(scaled_oth * gain_attn)
    packed_oth = low(matmul(xn_oth, qkv_w))
    att_own, att_oth, query, keys, mixed, log_sums = attend_forward(
        place, packed_own, packed_oth, early_own, early_oth, cosine, sine
    )
    att_came = swap(att_oth, "head", 1)
    hidden = rows_own + matmul(att_own, out_own) + matmul(att_came, out_oth)
    scale_two = rms_scale(hidden)
    hn_own = low(hidden * scale_two * gain_mlp)
    hn_oth = swap(hn_own, "ffn", 2)

    def feed(hn, dy):
        actives, gates, ups = [], [], []
        for s in range(2):
            gate = against(hn, gate_w[s])
            up = against(hn, up_w[s])
            grad = against(dy, down_w[s])
            sig = jax.nn.sigmoid(gate)
            silu = gate * sig
            actives.append(low(silu * up))
            gates.append(low(grad * up * sig * (1.0 + gate * (1.0 - sig))))
            ups.append(low(grad * silu))
        grad_hn = sum(matmul(gates[s], gate_w[s]) + matmul(ups[s], up_w[s]) for s in range(2))
        return actives, gates, ups, grad_hn

    act_own, gates_own, ups_own, dhn_own = feed(hn_own, dy_own)
    act_oth, gates_oth, ups_oth, dhn_oth = feed(hn_oth, dy_oth)
    dhn_came = swap(low(dhn_oth), "ffn", 2)
    down_oth = sum(matmul(act_oth[s], down_w[s]) for s in range(2))
    down_came = swap(low(down_oth), "ffn", 2)
    down_own = sum(matmul(act_own[s], down_w[s]) for s in range(2))

    dy_all = both(reorder(dy_own, ff_order, ff_size), reorder(dy_oth, ff_order, ff_size))
    hn_all = both(reorder(hn_own, ff_order, ff_size), reorder(hn_oth, ff_order, ff_size))
    lefts = [
        [both(own[s], oth[s]) for s in range(2)]
        for own, oth in ((act_own, act_oth), (gates_own, gates_oth), (ups_own, ups_oth))
    ]
    rights = (dy_all, hn_all, hn_all)
    mid = width // 2
    came = [swap(low(inner_rows(lefts[i][1], rights[i])), "ffn", 1) for i in range(3)]
    away = [
        low(inner_rows(lefts[i][0], rights[i][:, :mid]) + high(came[i][:, :mid])) for i in range(3)
    ]
    kept = [
        low(inner_rows(lefts[i][0], rights[i][:, mid:]) + high(came[i][:, mid:])) for i in range(3)
    ]
    dhn_came, away, kept = lax.optimization_barrier((dhn_came, away, kept))
    ff_sums = []
    for i in range(3):
        part = low(high(kept[i]) + high(swap(away[i], "head", 1)))
        part = low(high(part[:, mid // 2 :]) + high(swap(part[:, : mid // 2], "row", 1)))
        part = high(part[:, mid // 4 :]) + high(swap(part[:, : mid // 4], "row", 2))
        ff_sums.append(part)
    output = low(hidden + down_own + high(down_came))[None]

    dhn = dhn_own + high(dhn_came)
    grad_gain_two = jnp.sum(dhn * hidden * scale_two, axis=0)
    weighted = dhn * gain_mlp
    cube = scale_two * scale_two * scale_two
    grad_hidden = (
        high(dy_own)
        + scale_two * weighted
        - hidden * cube * jnp.mean(weighted * hidden, axis=-1, keepdims=True)
    )
    grad_proj = low(grad_hidden)
    go_oth = swap(low(against(grad_proj, out_oth)), "head", 1)
    go_own = low(against(grad_proj, out_own))

    def over_buckets(left, rights):
        def product(a, b):
            return jnp.concatenate([inner_rows(left[:, a:b], right) for right in rights], 1)

        quarter = width // 4
        came = swap(low(product(0, 2 * quarter)), "ffn", 1)
        away = low(product(2 * quarter, 3 * quarter) + high(came[:quarter]))
        kept = product(3 * quarter, width) + high(came[quarter:])
        part = low(kept + high(swap(away, "ffn", 2)))
        part = part.reshape(2, 2, att_size // 2, -1)
        near = r & 1
        away = lax.dynamic_index_in_dim(part, 1 - near, 1, keepdims=False)
        kept = lax.dynamic_index_in_dim(part, near, 1, keepdims=False)
        part = low(high(kept) + high(swap(away, "row", 1)))
        return high(part[1]) + high(swap(part[0], "row", 2))

    out_sum = over_buckets(reorder(grad_proj, att_order, att_size), (att_own, att_came))
    out_sum = out_sum[:, :out_cols] + high(swap(low(out_sum[:, out_cols:]), "head", 1))

    d_own, d_oth, first_own, first_oth = attend_backward(
        place, query, keys, mixed, log_sums, go_own, go_oth, att_own, att_oth, cosine, sine
    )
    share_oth = against(d_oth, qkv_w)
    dxn_came = swap(low(share_oth), "head", 1)
    first_came = swap(first_oth, "head", 1)
    share_own = against(d_own, qkv_w)
    grad_gain_one = jnp.sum(share_own * scaled_own, axis=0) + jnp.sum(share_oth * scaled_oth, axis=0)
    xn_all = both(reorder(xn_own, att_order, att_size), reorder(xn_oth, att_order, att_size))
    qkv_sum = over_buckets(xn_all, (both(d_own, d_oth),))
    gains = total(jnp.stack([grad_gain_one, grad_gain_two]), ("ffn", "head", "row"))
    dxn = share_own + high(dxn_came)
    weighted = dxn * gain_attn
    cube = scale_one * scale_one * scale_one
    grad_in = (
        grad_hidden
        + scale_one * weighted
        - rows_own * cube * jnp.mean(weighted * rows_own, axis=-1, keepdims=True)
    )
    grad_first = jnp.concatenate(
        [jnp.where(h == 0, first_own, first_came), jnp.where(h == 0, first_came, first_own)], 1
    )
    return (
        output,
        grad_in[None],
        grad_first[None],
        gains[0],
        qkv_sum,
        out_sum.T,
        gains[1],
        ff_sums[1].T,
        ff_sums[2].T,
        ff_sums[0],
    )


def solution(mesh):
    in_specs = (
        P(("ffn", "row"), "head", None),
        P(("ffn", "row"), "head", None),
        P(("ffn", "row")),
        P(),
        P(),
        P(),
        P(),
        P(None, "ffn"),
        P(None, "ffn"),
        P("ffn", None),
        P(("ffn", "row"), "head", None),
    )
    out_specs = (
        P(("ffn", "row"), "head", None),
        P(("ffn", "row"), "head", None),
        P(("ffn", "row"), "head", None),
        P(),
        P(("ffn", "row"), "head"),
        P("head", ("ffn", "row")),
        P(),
        P(("head", "row"), "ffn"),
        P(("head", "row"), "ffn"),
        P("ffn", ("head", "row")),
    )
    body = two_groups if mesh.shape["head"] == 2 and mesh.shape["ffn"] == 4 else any_groups
    return jax.shard_map(
        body, mesh=mesh, in_specs=in_specs, out_specs=out_specs, check_vma=False
    )
```

```python
import jax
import jax.numpy as jnp
from jax import lax
from jax.experimental import pallas as pl
from jax.experimental.pallas import tpu as pltpu
from jax.sharding import PartitionSpec as P

HEADS = 16
HD = 64
MIN_LEN = 512
STEP = 256


eps = 1e-06


def rms_scale(values):
    return lax.rsqrt(jnp.mean(values * values, axis=-1, keepdims=True) + eps)


def matmul(left, right):
    return jnp.dot(left, right, preferred_element_type=jnp.float32)


def inner_rows(left, right):
    return lax.dot_general(
        left, right, (((0,), (0,)), ((), ())), preferred_element_type=jnp.float32
    )


def against(left, right):
    return lax.dot_general(
        left, right, (((1,), (1,)), ((), ())), preferred_element_type=jnp.float32
    )


def swap(values, axis, mask):
    size = lax.axis_size(axis)
    return lax.ppermute(values, axis, [(i, i ^ mask) for i in range(size)])


def bits_of(axis):
    size = lax.axis_size(axis)
    return [1 << b for b in range(size.bit_length() - 2, -1, -1)]


def halve(values, dim, axis, mask):
    bit = (lax.axis_index(axis) // mask) % 2
    away = lax.dynamic_index_in_dim(values, 1 - bit, dim, keepdims=False)
    kept = lax.dynamic_index_in_dim(values, bit, dim, keepdims=False)
    came = swap(away.astype(jnp.bfloat16), axis, mask)
    return kept.astype(jnp.float32) + came.astype(jnp.float32)


def total(values, axes):
    for axis in axes:
        for mask in reversed(bits_of(axis)):
            values = values + swap(values, axis, mask)
    return values


def rotary(positions, head_size):
    half_size = head_size // 2
    inverse = jnp.exp(
        -jnp.log(10000.0) * jnp.arange(half_size, dtype=jnp.float32) * 2.0 / head_size
    )
    angles = positions.astype(jnp.float32)[:, None] * inverse[None, :]
    return (jnp.cos(angles), jnp.sin(angles))


def rotate(vectors, cosine, sine, sign):
    half_size = vectors.shape[-1] // 2
    first_half = vectors[..., :half_size]
    second_half = vectors[..., half_size:]
    cos_rows = cosine[:, None, :]
    sin_rows = sign * sine[:, None, :]
    return jnp.concatenate(
        [
            first_half * cos_rows - second_half * sin_rows,
            second_half * cos_rows + first_half * sin_rows,
        ],
        axis=-1,
    )


def masked_scores(q_rows, keys, q_pos, k_pos, valid):
    raw = jnp.einsum("qhe,khe->hqk", q_rows, keys, preferred_element_type=jnp.float32)
    allowed = (k_pos[None, :] <= q_pos[:, None]) & (k_pos[None, :] < valid)
    return jnp.where(allowed[None], 0.125 * raw, -1e30)


def scan_forward(query, keys, mixed, positions, valid, block_rows):
    count = query.shape[0] // block_rows

    def step(carry, index):
        start = index * block_rows
        q_rows = lax.dynamic_slice_in_dim(query, start, block_rows, 0)
        q_pos = lax.dynamic_slice_in_dim(positions, start, block_rows, 0)
        scores = masked_scores(q_rows, keys, q_pos, positions, valid)
        top = jnp.max(scores, axis=-1, keepdims=True)
        expo = jnp.exp(scores - top)
        total_w = jnp.sum(expo, axis=-1, keepdims=True)
        weights = expo / total_w
        result = jnp.einsum(
            "hqk,khe->qhe", weights.astype(jnp.bfloat16), mixed, preferred_element_type=jnp.float32
        )
        return (carry, (result.astype(jnp.bfloat16), top + jnp.log(total_w)))

    _, (outs, log_sums) = lax.scan(step, 0, jnp.arange(count, dtype=jnp.int32))
    return (outs.reshape(query.shape), log_sums)


def scan_backward(query, keys, mixed, positions, valid, log_sums, grad_out, block_rows):
    count = query.shape[0] // block_rows
    zeros = jnp.zeros(keys.shape, jnp.float32)

    def step(carry, index):
        key_sum, value_sum = carry
        start = index * block_rows
        q_rows = lax.dynamic_slice_in_dim(query, start, block_rows, 0)
        q_pos = lax.dynamic_slice_in_dim(positions, start, block_rows, 0)
        g_rows = lax.dynamic_slice_in_dim(grad_out, start, block_rows, 0)
        scores = masked_scores(q_rows, keys, q_pos, positions, valid)
        weights = jnp.exp(scores - log_sums[index])
        grad_w = jnp.einsum("qhe,khe->hqk", g_rows, mixed, preferred_element_type=jnp.float32)
        delta = jnp.sum(weights * grad_w, axis=-1, keepdims=True)
        grad_s = (weights * (grad_w - delta)).astype(jnp.bfloat16)
        grad_q = 0.125 * jnp.einsum(
            "hqk,khe->qhe", grad_s, keys, preferred_element_type=jnp.float32
        )
        key_sum = key_sum + 0.125 * jnp.einsum(
            "hqk,qhe->khe", grad_s, q_rows, preferred_element_type=jnp.float32
        )
        value_sum = value_sum + jnp.einsum(
            "hqk,qhe->khe", weights.astype(jnp.bfloat16), g_rows, preferred_element_type=jnp.float32
        )
        return ((key_sum, value_sum), grad_q)

    (grad_keys, grad_mixed), grad_query = lax.scan(
        step, (zeros, zeros), jnp.arange(count, dtype=jnp.int32)
    )
    return (grad_query.reshape(query.shape), grad_keys, grad_mixed)


def any_groups(
    inputs,
    first_values,
    lengths,
    gain_attn,
    w_qkv,
    w_out,
    gain_mlp,
    w_gate,
    w_up,
    w_down,
    cotangent,
):
    rows = inputs.shape[1]
    width = inputs.shape[2]
    groups = lax.axis_size("head")
    shards = lax.axis_size("ffn")
    heads_here = HEADS // groups
    span_rows = rows * groups
    block_rows = span_rows // max(1, span_rows // 512)
    head_pos = lax.axis_index("head")
    valid_len = lengths[0]
    packed_cols = heads_here * 3 * HD
    out_cols = heads_here * HD
    hidden_here = w_gate.shape[1]

    owners = [head_pos ^ m for m in range(groups)]
    x_all = [inputs[0]] + [swap(inputs[0], "head", m) for m in range(1, groups)]
    early = []
    for m in range(groups):
        piece = lax.dynamic_slice_in_dim(first_values[0], owners[m] * out_cols, out_cols, 1)
        early.append(swap(piece, "head", m) if m else piece)
    far = range(2, shards, 2)
    grad_rows = jnp.concatenate([cotangent[0]] + [swap(cotangent[0], "ffn", m) for m in far], 0)
    gate_w = jnp.concatenate([w_gate, swap(w_gate, "ffn", 1)], 1)
    up_w = jnp.concatenate([w_up, swap(w_up, "ffn", 1)], 1)
    down_w = jnp.concatenate([w_down, swap(w_down, "ffn", 1)], 0)
    w_heads = lax.dynamic_slice_in_dim(w_qkv, head_pos * packed_cols, packed_cols, 1)
    out_w = jnp.concatenate(
        [lax.dynamic_slice_in_dim(w_out, o * out_cols, out_cols, 0) for o in owners], 0
    )

    positions = jnp.concatenate([o * rows + jnp.arange(rows, dtype=jnp.int32) for o in owners])
    cosine, sine = rotary(positions, HD)
    normed, scaled, queries, key_list, mixes = [], [], [], [], []
    rows_in = inputs[0].astype(jnp.float32)
    scale_one = rms_scale(rows_in)
    for m in range(groups):
        block = x_all[m].astype(jnp.float32)
        scale = rms_scale(block)
        scaled.append(block * scale)
        normed.append((block * scale * gain_attn).astype(jnp.bfloat16))
        packed = matmul(normed[m], w_heads).astype(jnp.bfloat16)
        packed = packed.reshape(rows, heads_here, 3, HD).astype(jnp.float32)
        part = slice(m * rows, (m + 1) * rows)
        queries.append(rotate(packed[:, :, 0], cosine[part], sine[part], 1.0))
        key_list.append(rotate(packed[:, :, 1], cosine[part], sine[part], 1.0))
        value = early[m].reshape(rows, heads_here, HD).astype(jnp.float32)
        mixes.append(0.5 * (packed[:, :, 2] + value))
    query = jnp.concatenate(queries, 0).astype(jnp.bfloat16)
    keys = jnp.concatenate(key_list, 0).astype(jnp.bfloat16)
    mixed = jnp.concatenate(mixes, 0).astype(jnp.bfloat16)
    attended, log_sums = scan_forward(query, keys, mixed, positions, valid_len, block_rows)
    attended = attended.reshape(groups, rows, out_cols)
    att_own = jnp.concatenate(
        [attended[0]] + [swap(attended[m], "head", m) for m in range(1, groups)], 1
    )
    hidden = rows_in + matmul(att_own, out_w)
    scale_two = rms_scale(hidden)
    normed_two = (hidden * scale_two * gain_mlp).astype(jnp.bfloat16)

    mlp_rows = [normed_two] + [swap(normed_two, "ffn", m) for m in far]
    grad_list = [grad_rows[i * rows : (i + 1) * rows] for i in range(len(mlp_rows))]
    actives, grad_gates, grad_ups, downs, grad_normed_list = [], [], [], [], []
    for i, block in enumerate(mlp_rows):
        gate_rows = matmul(block, gate_w)
        up_rows = matmul(block, up_w)
        sigmoid_gate = jax.nn.sigmoid(gate_rows)
        silu_gate = gate_rows * sigmoid_gate
        grad_active = against(grad_list[i], down_w)
        actives.append((silu_gate * up_rows).astype(jnp.bfloat16))
        grad_gates.append(
            (
                grad_active * up_rows * sigmoid_gate * (1.0 + gate_rows * (1.0 - sigmoid_gate))
            ).astype(jnp.bfloat16)
        )
        grad_ups.append((grad_active * silu_gate).astype(jnp.bfloat16))
        grad_normed_list.append(against(grad_gates[i], gate_w) + against(grad_ups[i], up_w))
        downs.append(matmul(actives[i], down_w))
    grad_normed_two = grad_normed_list[0]
    for i, m in enumerate(far):
        came = swap(grad_normed_list[i + 1].astype(jnp.bfloat16), "ffn", m)
        grad_normed_two = grad_normed_two + came.astype(jnp.float32)
    down_rows = downs[0]
    for i, m in enumerate(far):
        down_rows = down_rows + swap(downs[i + 1].astype(jnp.bfloat16), "ffn", m).astype(jnp.float32)
    output = (hidden + down_rows).astype(jnp.bfloat16)[None]

    all_rows = jnp.concatenate(mlp_rows, 0)
    ff_sums = []
    for left, right in (
        (grad_rows, jnp.concatenate(actives, 0)),
        (all_rows, jnp.concatenate(grad_gates, 0)),
        (all_rows, jnp.concatenate(grad_ups, 0)),
    ):
        away = inner_rows(left, right[:, hidden_here:]).astype(jnp.bfloat16)
        part = inner_rows(left, right[:, :hidden_here])
        part = (part + swap(away, "ffn", 1).astype(jnp.float32)).astype(jnp.bfloat16)
        steps = [("head", b) for b in bits_of("head")] + [("row", b) for b in bits_of("row")]
        part = part.reshape([2] * len(steps) + [-1, hidden_here])
        order = [s for s in steps if s[0] == "head"] + [s for s in reversed(steps) if s[0] == "row"]
        left_steps = list(steps)
        for s in order:
            part = halve(part, left_steps.index(s), *s)
            left_steps.remove(s)
            if left_steps:
                part = part.astype(jnp.bfloat16)
        ff_sums.append(part)
    sum_down, sum_gate, sum_up = ff_sums

    grad_y = cotangent[0].astype(jnp.float32)
    grad_gain_two = jnp.sum(grad_normed_two * hidden * scale_two, axis=0)
    weighted_two = grad_normed_two * gain_mlp
    cube_two = scale_two * scale_two * scale_two
    grad_hidden = (
        grad_y
        + scale_two * weighted_two
        - hidden * cube_two * jnp.mean(weighted_two * hidden, axis=-1, keepdims=True)
    )
    grad_proj = grad_hidden.astype(jnp.bfloat16)
    grad_att = against(grad_proj, out_w).astype(jnp.bfloat16)
    grad_att = jnp.concatenate(
        [
            swap(grad_att[:, m * out_cols : (m + 1) * out_cols], "head", m)
            if m
            else grad_att[:, :out_cols]
            for m in range(groups)
        ],
        0,
    ).reshape(span_rows, heads_here, HD)

    def over_buckets(part):
        steps = [("ffn", b) for b in bits_of("ffn")] + [("row", b) for b in bits_of("row")]
        part = part.astype(jnp.bfloat16).reshape([2] * len(steps) + [-1, part.shape[1]])
        order = [s for s in reversed(steps) if s[0] == "ffn"] + [
            s for s in reversed(steps) if s[0] == "row"
        ]
        left_steps = list(steps)
        for s in order:
            part = halve(part, left_steps.index(s), *s)
            left_steps.remove(s)
            if left_steps:
                part = part.astype(jnp.bfloat16)
        return part

    part = over_buckets(inner_rows(grad_proj, att_own))
    sum_out = part[:, :out_cols]
    for m in range(1, groups):
        came = swap(part[:, m * out_cols : (m + 1) * out_cols].astype(jnp.bfloat16), "head", m)
        sum_out = sum_out + came.astype(jnp.float32)

    grad_query, grad_keys, grad_mixed = scan_backward(
        query, keys, mixed, positions, valid_len, log_sums, grad_att, block_rows
    )
    grad_packed = jnp.stack(
        [
            rotate(grad_query, cosine, sine, -1.0),
            rotate(grad_keys, cosine, sine, -1.0),
            0.5 * grad_mixed,
        ],
        axis=2,
    )
    grad_packed = grad_packed.astype(jnp.bfloat16).reshape(span_rows, packed_cols)
    grad_early = (0.5 * grad_mixed).astype(jnp.bfloat16).reshape(span_rows, out_cols)
    firsts = [grad_early[m * rows : (m + 1) * rows] for m in range(groups)]
    firsts = [swap(firsts[m], "head", m) if m else firsts[0] for m in range(groups)]
    grad_first = jnp.zeros((rows, width), jnp.bfloat16)
    for m in range(groups):
        grad_first = lax.dynamic_update_slice_in_dim(grad_first, firsts[m], owners[m] * out_cols, 1)
    shares = [
        against(grad_packed[m * rows : (m + 1) * rows], w_heads) for m in range(groups)
    ]
    grad_gain_one = sum(jnp.sum(shares[m] * scaled[m], axis=0) for m in range(groups))
    grad_normed = shares[0]
    for m in range(1, groups):
        grad_normed = grad_normed + swap(shares[m].astype(jnp.bfloat16), "head", m).astype(jnp.float32)
    sum_qkv = over_buckets(inner_rows(jnp.concatenate(normed, 0), grad_packed))
    weighted_one = grad_normed * gain_attn
    cube_one = scale_one * scale_one * scale_one
    grad_in = (
        grad_hidden
        + scale_one * weighted_one
        - rows_in * cube_one * jnp.mean(weighted_one * rows_in, axis=-1, keepdims=True)
    )
    gains = total(jnp.stack([grad_gain_one, grad_gain_two]), ("ffn", "head", "row"))
    return (
        output,
        grad_in[None],
        grad_first[None],
        gains[0],
        sum_qkv,
        sum_out.T,
        gains[1],
        sum_gate,
        sum_up,
        sum_down.T,
    )


def spans(total):
    return [(a, min(a + STEP, total)) for a in range(0, total, STEP)]


def turn(values):
    lane = lax.broadcasted_iota(jnp.int32, values.shape, 1)
    return jnp.where(
        lane % HD < HD // 2, pltpu.roll(values, 2 * HD - HD // 2, 1), pltpu.roll(values, HD // 2, 1)
    )


def allowed_keys(a, b, valid):
    size = b - a
    down = lax.broadcasted_iota(jnp.int32, (size, size), 0)
    across = lax.broadcasted_iota(jnp.int32, (size, size), 1)
    allowed = down <= across
    if b > MIN_LEN:
        allowed = allowed & (down < valid - a)
    return allowed


def forward_body(place, packed_own, packed_oth, early_own, early_oth, cos_ref, sin_ref, att_out, q_out, k_out, v_out, lse_out, flipped, att):
    rows = packed_own.shape[0]
    span = 2 * rows
    valid = place[1]
    wide = 2 * HD
    f32 = jnp.float32
    bf = jnp.bfloat16
    first = lax.broadcasted_iota(jnp.int32, (1, wide), 1) < HD
    for m, (packed, early) in enumerate(((packed_own, early_own), (packed_oth, early_oth))):
        start = pl.multiple_of((place[0] ^ m) * rows, rows)
        here = pl.ds(start, rows)
        x0 = packed[:, :wide].astype(f32)
        x1 = packed[:, wide : 2 * wide].astype(f32)
        x2 = packed[:, 2 * wide :].astype(f32)
        cosine = cos_ref[here, :]
        sine = sin_ref[here, :]
        q = jnp.where(first, x0, x1)
        k = pltpu.roll(jnp.where(first, x2, x0), HD, 1)
        v = jnp.where(first, x1, x2)
        q_out[here, :] = (q * cosine + turn(q) * sine).astype(bf)
        k_out[here, :] = (k * cosine + turn(k) * sine).astype(bf)
        v_out[here, :] = (0.5 * (v + early[...].astype(f32))).astype(bf)
    turned = v_out[...].T
    ones = jnp.ones((16, span), bf)
    for e in range(2):
        flipped[e, :HD, :] = turned[e * HD : (e + 1) * HD, :]
        flipped[e, HD:, :] = ones
    for a, b in spans(span):
        q = q_out[a:b, :] * jnp.asarray(0.125, bf)
        allowed = allowed_keys(a, b, valid)
        for e in range(2):
            qe = jnp.where(first == (e == 0), q, jnp.zeros_like(q))
            diag = jnp.where(allowed, against(k_out[a:b, :], qe), -1e30)
            top = jnp.max(diag, axis=0, keepdims=True)
            if a:
                past = against(k_out[:a, :], qe)
                top = jnp.maximum(top, jnp.max(past, axis=0, keepdims=True))
            out = matmul(flipped[e, :, a:b], jnp.exp(diag - top).astype(bf))
            if a:
                out = out + matmul(flipped[e, :, :a], jnp.exp(past - top).astype(bf))
            amount = out[HD : HD + 1, :]
            att[e * HD : (e + 1) * HD, a:b] = out[:HD, :] / amount
            lse_out[0, e : e + 1, a:b] = top + jnp.log(amount)
    result = att[...].T.astype(bf)
    att_out[place[0]] = result[:rows, :]
    att_out[1 - place[0]] = result[rows:, :]


def attend_forward(place, packed_own, packed_oth, early_own, early_oth, cosine, sine):
    rows, cols = packed_own.shape
    heads = cols // (3 * HD)
    wide = 2 * HD
    span = 2 * rows
    bf = jnp.bfloat16

    def block(r, c):
        return pl.BlockSpec((r, c), lambda p, s: (0, p))

    def fixed(r, c):
        return pl.BlockSpec((r, c), lambda p, s: (0, 0))

    natural = jax.ShapeDtypeStruct((span, heads * HD), bf)
    return pl.pallas_call(
        forward_body,
        out_shape=(
            jax.ShapeDtypeStruct((2, rows, heads * HD), bf),
            natural,
            natural,
            natural,
            jax.ShapeDtypeStruct((heads // 2, 2, span), jnp.float32),
        ),
        grid_spec=pltpu.PrefetchScalarGridSpec(
            num_scalar_prefetch=1,
            grid=(heads // 2,),
            in_specs=[block(rows, 3 * wide)] * 2 + [block(rows, wide)] * 2 + [fixed(span, wide)] * 2,
            out_specs=[pl.BlockSpec((2, rows, wide), lambda p, s: (0, 0, p))]
            + [block(span, wide)] * 3
            + [pl.BlockSpec((1, 2, span), lambda p, s: (p, 0, 0))],
            scratch_shapes=[pltpu.VMEM((2, HD + 16, span), bf), pltpu.VMEM((wide, span), jnp.float32)],
        ),
        cost_estimate=pl.CostEstimate(
            flops=4 * heads * span * span * HD,
            transcendentals=heads * span * span,
            bytes_accessed=12 * span * heads * HD,
        ),
        compiler_params=pltpu.CompilerParams(vmem_limit_bytes=14 << 20),
        name="attend_forward",
    )(place, packed_own, packed_oth, early_own, early_oth, cosine, sine)


def backward_body(place, q_ref, k_ref, v_ref, lse_ref, go_own, go_oth, att_ref, cos_ref, sin_ref, d_out, f_out, grad, prod, turned_k, dq, dk, dv):
    rows = go_own.shape[0]
    span = 2 * rows
    valid = place[1]
    wide = 2 * HD
    f32 = jnp.float32
    bf = jnp.bfloat16
    first = lax.broadcasted_iota(jnp.int32, (1, wide), 1) < HD
    for m, go in enumerate((go_own, go_oth)):
        here = pl.ds(pl.multiple_of((place[0] ^ m) * rows, rows), rows)
        grad[here, :] = go[...]
        prod[here, :] = go[...].astype(f32) * att_ref[m].astype(f32)
    flat = prod[...].T
    deltas = [jnp.sum(flat[e * HD : (e + 1) * HD, :], axis=0, keepdims=True) for e in range(2)]
    eighth = jnp.asarray(0.125, bf)
    turned_k[...] = (k_ref[...] * eighth).T
    dk[...] = jnp.zeros_like(dk)
    dv[...] = jnp.zeros_like(dv)
    for a, b in spans(span):
        allowed = allowed_keys(a, b, valid)
        q = q_ref[a:b, :] * eighth
        g = grad[a:b, :]
        parts = ((a, b), (0, a)) if a else ((a, b),)
        sums = {}
        for e in range(2):
            mine = first == (e == 0)
            qe = jnp.where(mine, q, jnp.zeros_like(q))
            ge = jnp.where(mine, g, jnp.zeros_like(g))
            for lo, hi in parts:
                scores = against(k_ref[lo:hi, :], qe)
                if lo == a:
                    scores = jnp.where(allowed, scores, -1e30)
                weights = jnp.exp(scores - lse_ref[0, e : e + 1, a:b])
                grad_w = against(v_ref[lo:hi, :], ge)
                grad_s = (weights * (grad_w - deltas[e][:, a:b])).astype(bf)
                dv_here = matmul(weights.astype(bf), ge)
                dk_here = matmul(grad_s, qe)
                dq_here = matmul(turned_k[e * HD : (e + 1) * HD, lo:hi], grad_s)
                if (lo, "v") in sums:
                    dv_here = dv_here + sums[lo, "v"]
                    dk_here = dk_here + sums[lo, "k"]
                sums[lo, "v"], sums[lo, "k"] = dv_here, dk_here
                sums[lo, e] = dq_here
        for e in range(2):
            dq[e * HD : (e + 1) * HD, a:b] = sums[a, e] + sums[0, e] if a else sums[a, e]
        for lo, hi in parts:
            dv[lo:hi, :] += sums[lo, "v"]
            dk[lo:hi, :] += sums[lo, "k"]
    prod[...] = dq[...].T
    for m in range(2):
        here = pl.ds(pl.multiple_of((place[0] ^ m) * rows, rows), rows)
        cosine = cos_ref[here, :]
        sine = sin_ref[here, :]
        gv = (0.5 * dv[here, :]).astype(bf)
        gk = dk[here, :]
        gk = pltpu.roll(gk * cosine - turn(gk) * sine, HD, 1).astype(bf)
        gq = prod[here, :]
        gq = (gq * cosine - turn(gq) * sine).astype(bf)
        d_out[m, :, :wide] = jnp.where(first, gq, gk)
        d_out[m, :, wide : 2 * wide] = jnp.where(first, gv, gq)
        d_out[m, :, 2 * wide :] = jnp.where(first, gk, gv)
        f_out[m] = gv


def attend_backward(place, q, k, v, lse, go_own, go_oth, att, cosine, sine, pairs):
    span = q.shape[0]
    rows = span // 2
    wide = 2 * HD
    start, end = pairs
    heads = 2 * (end - start)
    cols = heads * HD
    bf = jnp.bfloat16

    def block(r, c):
        return pl.BlockSpec((r, c), lambda p, s: (0, p + start))

    def fixed(r, c):
        return pl.BlockSpec((r, c), lambda p, s: (0, 0))

    return pl.pallas_call(
        backward_body,
        out_shape=(
            jax.ShapeDtypeStruct((2, rows, 3 * cols), bf),
            jax.ShapeDtypeStruct((2, rows, cols), bf),
        ),
        grid_spec=pltpu.PrefetchScalarGridSpec(
            num_scalar_prefetch=1,
            grid=(end - start,),
            in_specs=[block(span, wide)] * 3
            + [pl.BlockSpec((1, 2, span), lambda p, s: (p + start, 0, 0))]
            + [block(rows, wide)] * 2
            + [pl.BlockSpec((2, rows, wide), lambda p, s: (0, 0, p + start))]
            + [fixed(span, wide)] * 2,
            out_specs=[
                pl.BlockSpec((2, rows, 3 * wide), lambda p, s: (0, 0, p)),
                pl.BlockSpec((2, rows, wide), lambda p, s: (0, 0, p)),
            ],
            scratch_shapes=[
                pltpu.VMEM((span, wide), bf),
                pltpu.VMEM((span, wide), jnp.float32),
                pltpu.VMEM((wide, span), bf),
                pltpu.VMEM((wide, span), jnp.float32),
                pltpu.VMEM((span, wide), jnp.float32),
                pltpu.VMEM((span, wide), jnp.float32),
            ],
        ),
        cost_estimate=pl.CostEstimate(
            flops=10 * heads * span * span * HD,
            transcendentals=heads * span * span,
            bytes_accessed=20 * span * heads * HD,
        ),
        compiler_params=pltpu.CompilerParams(vmem_limit_bytes=16 << 20),
        name="attend_backward",
    )(place, q, k, v, lse, go_own, go_oth, att, cosine, sine)


def reorder_body(order, *refs):
    blocks, out = refs[:-1], refs[-1]
    rows = blocks[0].shape[0]
    size = out.shape[1] // order.shape[0]
    for i in range(order.shape[0]):
        start = pl.multiple_of(order[i] * size, size)
        for b, block in enumerate(blocks):
            out[b * rows : (b + 1) * rows, i * size : (i + 1) * size] = block[:, pl.ds(start, size)]


def reorder(order, *blocks):
    rows, cols = blocks[0].shape
    whole = pl.BlockSpec((rows, cols), lambda i, s: (0, 0))
    return pl.pallas_call(
        reorder_body,
        out_shape=jax.ShapeDtypeStruct((rows * len(blocks), cols), blocks[0].dtype),
        grid_spec=pltpu.PrefetchScalarGridSpec(
            num_scalar_prefetch=1,
            grid=(1,),
            in_specs=[whole] * len(blocks),
            out_specs=pl.BlockSpec((rows * len(blocks), cols), lambda i, s: (0, 0)),
        ),
        cost_estimate=pl.CostEstimate(
            flops=0, transcendentals=0, bytes_accessed=4 * rows * cols * len(blocks)
        ),
        name="reorder",
        compiler_params=pltpu.CompilerParams(vmem_limit_bytes=8 << 20),
    )(order, *blocks)


def both(first, second):
    return jnp.concatenate([first, second], 0)


def after(first, *values):
    return lax.optimization_barrier((first, *values))[1:]


def low(values):
    return values.astype(jnp.bfloat16)


def high(values):
    return values.astype(jnp.float32)


def two_groups(
    inputs,
    first_values,
    lengths,
    gain_attn,
    w_qkv,
    w_out,
    gain_mlp,
    w_gate,
    w_up,
    w_down,
    cotangent,
):
    rows = inputs.shape[1]
    width = inputs.shape[2]
    span = 2 * rows
    out_cols = HEADS // 2 * HD
    packed_cols = 3 * out_cols
    mid = width // 2
    h = lax.axis_index("head")
    f = lax.axis_index("ffn")
    r = lax.axis_index("row")
    row_size = lax.axis_size("row")
    place = jnp.stack([h, lengths[0]]).astype(jnp.int32)
    tie = lax.optimization_barrier

    x_own = inputs[0]
    x_oth = swap(x_own, "head", 1)
    early_own = lax.dynamic_slice_in_dim(first_values[0], h * out_cols, out_cols, 1)
    early_oth = swap(
        lax.dynamic_slice_in_dim(first_values[0], (1 - h) * out_cols, out_cols, 1), "head", 1
    )
    dy_own = cotangent[0]
    dy_oth = swap(dy_own, "ffn", 2)
    gate_oth = swap(w_gate.T, "ffn", 1)
    up_oth = swap(w_up.T, "ffn", 1)
    down_oth = swap(w_down, "ffn", 1)
    qkv_w = lax.dynamic_slice_in_dim(w_qkv, h * packed_cols, packed_cols, 1)
    out_own = lax.dynamic_slice_in_dim(w_out, h * out_cols, out_cols, 0)
    out_oth = lax.dynamic_slice_in_dim(w_out, (1 - h) * out_cols, out_cols, 0)
    half = HD // 2
    inverse = jnp.exp(-jnp.log(10000.0) * jnp.arange(half, dtype=jnp.float32) * 2.0 / HD)
    angles = jnp.arange(span, dtype=jnp.float32)[:, None] * jnp.tile(inverse, 4)[None, :]
    cosine = jnp.cos(angles)
    sign = jnp.where(jnp.arange(2 * HD) % HD < half, -1.0, 1.0)
    sine = jnp.sin(angles) * sign[None, :]

    ff_order = jnp.stack([(h ^ a) * row_size + (r ^ b) for a in (1, 0) for b in (3, 1, 2, 0)])
    down_order = jnp.stack([(h ^ a) * row_size + (r ^ b) for b in (3, 1, 2, 0) for a in (1, 0)])
    att_order = jnp.stack(
        [((f ^ a) * row_size + (r & 2 ^ b)) // 2 for a in (3, 1, 2, 0) for b in (2, 0)]
    )
    att_size = width // 8

    rows_own = high(x_own)
    scale_one = rms_scale(rows_own)
    scaled_own = rows_own * scale_one
    xn_own = low(scaled_own * gain_attn)
    packed_own = low(matmul(xn_own, qkv_w))
    rows_oth = high(x_oth)
    scaled_oth = rows_oth * rms_scale(rows_oth)
    xn_oth = low(scaled_oth * gain_attn)
    packed_oth = low(matmul(xn_oth, qkv_w))
    packed_oth, early_oth, dy_oth, gate_oth, up_oth, down_oth = tie(
        (packed_oth, early_oth, dy_oth, gate_oth, up_oth, down_oth)
    )
    gate_w = (w_gate.T, gate_oth)
    up_w = (w_up.T, up_oth)
    down_w = (w_down, down_oth)
    attended, query, keys, mixed, log_sums = attend_forward(
        place, packed_own, packed_oth, early_own, early_oth, cosine, sine
    )
    att_own = attended[0]
    att_came = swap(attended[1], "head", 1)
    dact_own = [against(dy_own, w) for w in down_w]
    dact_oth = [against(dy_oth, w) for w in down_w]
    xn_all = reorder(att_order, xn_own, xn_oth)
    dy_all = reorder(down_order, dy_own, dy_oth)
    att_came, dact_own, dact_oth, xn_all, dy_all = tie(
        (att_came, dact_own, dact_oth, xn_all, dy_all)
    )
    hidden = rows_own + matmul(att_own, out_own) + matmul(att_came, out_oth)
    scale_two = rms_scale(hidden)
    hn_own = low(hidden * scale_two * gain_mlp)
    hn_oth = swap(hn_own, "ffn", 2)

    def feed(hn, grads):
        actives, gates, ups = [], [], []
        for s in range(2):
            gate = against(hn, gate_w[s])
            up = against(hn, up_w[s])
            grad = grads[s]
            sig = jax.nn.sigmoid(gate)
            silu = gate * sig
            actives.append(low(silu * up))
            gates.append(low(grad * up * sig * (1.0 + gate * (1.0 - sig))))
            ups.append(low(grad * silu))
        grad_hn = sum(matmul(gates[s], gate_w[s]) + matmul(ups[s], up_w[s]) for s in range(2))
        return actives, gates, ups, grad_hn

    act_own, gates_own, ups_own, dhn_own = feed(hn_own, dact_own)
    down_own = sum(matmul(act_own[s], down_w[s]) for s in range(2))
    hn_oth, act_own, gates_own, ups_own, dhn_own, down_own = tie(
        (hn_oth, act_own, gates_own, ups_own, dhn_own, down_own)
    )
    act_oth, gates_oth, ups_oth, dhn_oth = feed(hn_oth, dact_oth)
    dhn_oth = low(dhn_oth)
    dhn_came = swap(dhn_oth, "ffn", 2)

    hn_all = reorder(ff_order, hn_own, hn_oth)
    lefts = [
        [both(own[s], oth[s]) for s in range(2)]
        for own, oth in ((gates_own, gates_oth), (ups_own, ups_oth), (act_own, act_oth))
    ]
    rights = (hn_all, hn_all, dy_all)
    away = [low(inner_rows(lefts[i][1], rights[i])) for i in range(3)]
    came = [swap(a, "ffn", 1) for a in away]
    parts = [low(inner_rows(lefts[i][0], rights[i]) + high(came[i])) for i in range(3)]
    gate_x = swap(parts[0][:, :mid], "head", 1)
    down_near = swap(parts[2][:, :mid], "row", 1)
    dhn_came, parts = tie((dhn_came, parts))

    dhn = dhn_own + high(dhn_came)
    grad_gain_two = jnp.sum(dhn * hidden * scale_two, axis=0)
    weighted = dhn * gain_mlp
    cube = scale_two * scale_two * scale_two
    grad_hidden = (
        high(dy_own)
        + scale_two * weighted
        - hidden * cube * jnp.mean(weighted * hidden, axis=-1, keepdims=True)
    )
    grad_proj = low(grad_hidden)
    go_oth = swap(low(against(grad_proj, out_oth)), "head", 1)
    go_own = low(against(grad_proj, out_own))

    def split_near(part):
        part = part.reshape(2, 2, att_size // 2, -1)
        near = r & 1
        away = lax.dynamic_index_in_dim(part, 1 - near, 1, keepdims=False)
        kept = lax.dynamic_index_in_dim(part, near, 1, keepdims=False)
        return away, kept

    def product(left, rights, a, b):
        return jnp.concatenate([inner_rows(left[:, a:b], right) for right in rights], 1)

    quarter = width // 4

    proj_all = reorder(att_order, grad_proj)
    out_rights = (att_own, att_came)
    out_core = swap(low(product(proj_all, out_rights, 0, 2 * quarter)), "ffn", 1)
    gate_kept, down_kept, *act_oth = after(
        go_own, parts[0][:, mid:], parts[2][:, mid:], act_oth[0], act_oth[1]
    )
    part_gate = low(high(gate_kept) + high(gate_x))
    gate_near = swap(part_gate[:, : mid // 2], "row", 1)
    part_down = low(high(down_kept) + high(down_near))
    down_mid = swap(part_down[:, : mid // 2], "row", 2)
    (up_send,) = after(part_down, parts[1][:, :mid])
    up_x = swap(up_send, "head", 1)
    down_send = low(sum(matmul(act_oth[s], down_w[s]) for s in range(2)))
    down_came = swap(down_send, "ffn", 2)
    out_away = low(product(proj_all, out_rights, 2 * quarter, 3 * quarter) + high(out_core[:quarter]))
    out_kept = product(proj_all, out_rights, 3 * quarter, width) + high(out_core[quarter:])
    out_y = swap(out_away, "ffn", 2)
    go_oth, part_gate, part_down, out_kept, down_send, up_send = tie(
        (go_oth, part_gate, part_down, out_kept, down_send, up_send)
    )

    def backward(pairs, lse):
        d, first = attend_backward(
            place, query, keys, mixed, lse, go_own, go_oth, attended, cosine, sine, pairs
        )
        return d.reshape(span, -1), first

    pairs = HEADS // 4
    d_a, first_a = backward((0, pairs // 2), log_sums)
    core_send = low(inner_rows(xn_all[:, : 2 * quarter], d_a))
    core_a = swap(core_send, "ffn", 1)
    out_kept, residual = after(d_a, out_kept, hidden + down_own)
    out_send, out_kept = split_near(low(out_kept + high(out_y)))
    out_near = swap(out_send, "row", 1)
    output = low(residual + high(down_came))[None]
    log_sums, output, out_kept, core_send = tie((log_sums, output, out_kept, core_send))
    d_b, first_b = backward((pairs // 2, pairs), log_sums)

    def y_step(d_all, core):
        away = low(inner_rows(xn_all[:, 2 * quarter : 3 * quarter], d_all) + high(core[:quarter]))
        kept = inner_rows(xn_all[:, 3 * quarter :], d_all) + high(core[quarter:])
        return away, kept

    cut = packed_cols // 2
    share_oth = against(d_a[rows:], qkv_w[:, :cut]) + against(d_b[rows:], qkv_w[:, cut:])
    share_own = against(d_a[:rows], qkv_w[:, :cut]) + against(d_b[:rows], qkv_w[:, cut:])
    grad_gain_one = jnp.sum(share_own * scaled_own, axis=0) + jnp.sum(share_oth * scaled_oth, axis=0)
    gains = jnp.stack([grad_gain_one, grad_gain_two])
    gains_x = swap(gains, "head", 1)
    back_send = jnp.concatenate([low(share_oth), first_a[1], first_b[1]], 1)
    back_came = swap(back_send, "head", 1)
    first_own = jnp.concatenate([first_a[0], first_b[0]], 1)
    (core_a,) = after(back_send, core_a)
    away_a, kept_a = y_step(d_a, core_a)
    y_a = swap(away_a, "ffn", 2)
    core_send = low(inner_rows(xn_all[:, : 2 * quarter], d_b))
    core_b = swap(core_send, "ffn", 1)
    gate_kept, down_kept, up_kept, out_kept = after(
        core_send, part_gate[:, mid // 2 :], part_down[:, mid // 2 :], parts[1][:, mid:], out_kept
    )
    part_gate = low(high(gate_kept) + high(gate_near))
    gate_far = swap(part_gate[:, : mid // 4], "row", 2)
    part_down = low(high(down_kept) + high(down_mid))
    part_up = low(high(up_kept) + high(up_x))
    up_near = swap(part_up[:, : mid // 2], "row", 1)
    gains = gains + gains_x
    gains = gains + swap(gains, "ffn", 1)
    core_b, gains, part_up = tie((core_b, gains, part_up))
    away_b, kept_b = y_step(d_b, core_b)

    extra = low(jnp.pad(gains.reshape(-1), (0, 16 * cut - 2 * width)).reshape(16, cut))
    y_b = swap(both(away_b, extra), "ffn", 2)
    (out_kept, gate_kept, down_send) = after(
        away_b, out_kept, part_gate[:, mid // 4 :], part_down[:, : mid // 4]
    )
    down_x = swap(down_send, "head", 1)
    out_part = low(high(out_kept) + high(out_near))
    out_far = swap(out_part[0], "row", 2)
    sum_gate = high(gate_kept) + high(gate_far)

    near_send, near_kept = split_near(low(kept_a + high(y_a)))
    near_a = swap(near_send, "row", 1)
    (up_kept,) = after(near_send, part_up[:, mid // 2 :])
    part_up = low(high(up_kept) + high(up_near))
    up_far = swap(part_up[:, : mid // 4], "row", 2)
    extra = high(extra) + high(y_b[quarter:])
    send_b, kept_b = split_near(low(kept_b + high(y_b[:quarter])))
    extra = low(extra)
    wide_b = both(send_b.reshape(att_size, cut), extra)
    near_b = swap(wide_b, "row", 1)
    out_kept, kept_a = after(wide_b, out_part[1], near_kept)
    part_a = low(high(kept_a) + high(near_a))
    far_a = swap(part_a[0], "row", 2)
    out_sum = high(out_kept) + high(out_far)
    out_x = swap(low(out_sum[:, out_cols:]), "head", 1)
    (dxn_own,) = after(wide_b, share_own)
    dxn = dxn_own + high(back_came[:, :width])
    first_came = back_came[:, width:]
    part_b = low(high(kept_b) + high(near_b[:att_size].reshape(kept_b.shape)))
    extra = low(high(extra) + high(near_b[att_size:]))
    wide_b = both(part_b[0], extra)
    far_b = swap(wide_b, "row", 2)
    part_a, part_b1, out_sum, down_kept, up_kept = after(
        wide_b, part_a[1], part_b[1], out_sum[:, :out_cols], part_down[:, mid // 4 :], part_up[:, mid // 4 :]
    )
    out_sum = out_sum + high(out_x)
    sum_down = high(down_kept) + high(down_x)
    sum_up = high(up_kept) + high(up_far)
    sum_a = high(part_a) + high(far_a)
    sum_b = high(part_b1) + high(far_b[: att_size // 2])
    gains = (high(extra) + high(far_b[att_size // 2 :])).reshape(-1)[: 2 * width].reshape(2, width)

    weighted = dxn * gain_attn
    cube = scale_one * scale_one * scale_one
    grad_in = (
        grad_hidden
        + scale_one * weighted
        - rows_own * cube * jnp.mean(weighted * rows_own, axis=-1, keepdims=True)
    )
    grad_first = jnp.concatenate(
        [jnp.where(h == 0, first_own, first_came), jnp.where(h == 0, first_came, first_own)], 1
    )
    return (
        output,
        grad_in[None],
        grad_first[None],
        gains[0],
        jnp.concatenate([sum_a, sum_b], 1),
        out_sum.T,
        gains[1],
        sum_gate.T,
        sum_up.T,
        sum_down,
    )


def solution(mesh):
    in_specs = (
        P(("ffn", "row"), "head", None),
        P(("ffn", "row"), "head", None),
        P(("ffn", "row")),
        P(),
        P(),
        P(),
        P(),
        P(None, "ffn"),
        P(None, "ffn"),
        P("ffn", None),
        P(("ffn", "row"), "head", None),
    )
    out_specs = (
        P(("ffn", "row"), "head", None),
        P(("ffn", "row"), "head", None),
        P(("ffn", "row"), "head", None),
        P(),
        P(("ffn", "row"), "head"),
        P("head", ("ffn", "row")),
        P(),
        P(("head", "row"), "ffn"),
        P(("head", "row"), "ffn"),
        P("ffn", ("head", "row")),
    )
    body = two_groups if mesh.shape["head"] == 2 and mesh.shape["ffn"] == 4 else any_groups
    return jax.shard_map(
        body, mesh=mesh, in_specs=in_specs, out_specs=out_specs, check_vma=False
    )
```

```python
import functools

import jax
import jax.numpy as jnp
from jax import lax
from jax.experimental import pallas as pl
from jax.experimental.pallas import tpu as pltpu
from jax.sharding import PartitionSpec as P

HEADS = 16
HD = 64
MIN_LEN = 512
STEP = 256


eps = 1e-06


def rms_scale(values):
    return lax.rsqrt(jnp.mean(values * values, axis=-1, keepdims=True) + eps)


def matmul(left, right):
    return jnp.dot(left, right, preferred_element_type=jnp.float32)


def inner_rows(left, right):
    return lax.dot_general(
        left, right, (((0,), (0,)), ((), ())), preferred_element_type=jnp.float32
    )


def against(left, right):
    return lax.dot_general(
        left, right, (((1,), (1,)), ((), ())), preferred_element_type=jnp.float32
    )


def swap(values, axis, mask):
    size = lax.axis_size(axis)
    return lax.ppermute(values, axis, [(i, i ^ mask) for i in range(size)])


def bits_of(axis):
    size = lax.axis_size(axis)
    return [1 << b for b in range(size.bit_length() - 2, -1, -1)]


def halve(values, dim, axis, mask):
    bit = (lax.axis_index(axis) // mask) % 2
    away = lax.dynamic_index_in_dim(values, 1 - bit, dim, keepdims=False)
    kept = lax.dynamic_index_in_dim(values, bit, dim, keepdims=False)
    came = swap(away.astype(jnp.bfloat16), axis, mask)
    return kept.astype(jnp.float32) + came.astype(jnp.float32)


def total(values, axes):
    for axis in axes:
        for mask in reversed(bits_of(axis)):
            values = values + swap(values, axis, mask)
    return values


def rotary(positions, head_size):
    half_size = head_size // 2
    inverse = jnp.exp(
        -jnp.log(10000.0) * jnp.arange(half_size, dtype=jnp.float32) * 2.0 / head_size
    )
    angles = positions.astype(jnp.float32)[:, None] * inverse[None, :]
    return (jnp.cos(angles), jnp.sin(angles))


def rotate(vectors, cosine, sine, sign):
    half_size = vectors.shape[-1] // 2
    first_half = vectors[..., :half_size]
    second_half = vectors[..., half_size:]
    cos_rows = cosine[:, None, :]
    sin_rows = sign * sine[:, None, :]
    return jnp.concatenate(
        [
            first_half * cos_rows - second_half * sin_rows,
            second_half * cos_rows + first_half * sin_rows,
        ],
        axis=-1,
    )


def masked_scores(q_rows, keys, q_pos, k_pos, valid):
    raw = jnp.einsum("qhe,khe->hqk", q_rows, keys, preferred_element_type=jnp.float32)
    allowed = (k_pos[None, :] <= q_pos[:, None]) & (k_pos[None, :] < valid)
    return jnp.where(allowed[None], 0.125 * raw, -1e30)


def scan_forward(query, keys, mixed, positions, valid, block_rows):
    count = query.shape[0] // block_rows

    def step(carry, index):
        start = index * block_rows
        q_rows = lax.dynamic_slice_in_dim(query, start, block_rows, 0)
        q_pos = lax.dynamic_slice_in_dim(positions, start, block_rows, 0)
        scores = masked_scores(q_rows, keys, q_pos, positions, valid)
        top = jnp.max(scores, axis=-1, keepdims=True)
        expo = jnp.exp(scores - top)
        total_w = jnp.sum(expo, axis=-1, keepdims=True)
        weights = expo / total_w
        result = jnp.einsum(
            "hqk,khe->qhe", weights.astype(jnp.bfloat16), mixed, preferred_element_type=jnp.float32
        )
        return (carry, (result.astype(jnp.bfloat16), top + jnp.log(total_w)))

    _, (outs, log_sums) = lax.scan(step, 0, jnp.arange(count, dtype=jnp.int32))
    return (outs.reshape(query.shape), log_sums)


def scan_backward(query, keys, mixed, positions, valid, log_sums, grad_out, block_rows):
    count = query.shape[0] // block_rows
    zeros = jnp.zeros(keys.shape, jnp.float32)

    def step(carry, index):
        key_sum, value_sum = carry
        start = index * block_rows
        q_rows = lax.dynamic_slice_in_dim(query, start, block_rows, 0)
        q_pos = lax.dynamic_slice_in_dim(positions, start, block_rows, 0)
        g_rows = lax.dynamic_slice_in_dim(grad_out, start, block_rows, 0)
        scores = masked_scores(q_rows, keys, q_pos, positions, valid)
        weights = jnp.exp(scores - log_sums[index])
        grad_w = jnp.einsum("qhe,khe->hqk", g_rows, mixed, preferred_element_type=jnp.float32)
        delta = jnp.sum(weights * grad_w, axis=-1, keepdims=True)
        grad_s = (weights * (grad_w - delta)).astype(jnp.bfloat16)
        grad_q = 0.125 * jnp.einsum(
            "hqk,khe->qhe", grad_s, keys, preferred_element_type=jnp.float32
        )
        key_sum = key_sum + 0.125 * jnp.einsum(
            "hqk,qhe->khe", grad_s, q_rows, preferred_element_type=jnp.float32
        )
        value_sum = value_sum + jnp.einsum(
            "hqk,qhe->khe", weights.astype(jnp.bfloat16), g_rows, preferred_element_type=jnp.float32
        )
        return ((key_sum, value_sum), grad_q)

    (grad_keys, grad_mixed), grad_query = lax.scan(
        step, (zeros, zeros), jnp.arange(count, dtype=jnp.int32)
    )
    return (grad_query.reshape(query.shape), grad_keys, grad_mixed)


def any_groups(
    inputs,
    first_values,
    lengths,
    gain_attn,
    w_qkv,
    w_out,
    gain_mlp,
    w_gate,
    w_up,
    w_down,
    cotangent,
):
    rows = inputs.shape[1]
    width = inputs.shape[2]
    groups = lax.axis_size("head")
    shards = lax.axis_size("ffn")
    heads_here = HEADS // groups
    span_rows = rows * groups
    block_rows = span_rows // max(1, span_rows // 512)
    head_pos = lax.axis_index("head")
    valid_len = lengths[0]
    packed_cols = heads_here * 3 * HD
    out_cols = heads_here * HD
    hidden_here = w_gate.shape[1]

    owners = [head_pos ^ m for m in range(groups)]
    x_all = [inputs[0]] + [swap(inputs[0], "head", m) for m in range(1, groups)]
    early = []
    for m in range(groups):
        piece = lax.dynamic_slice_in_dim(first_values[0], owners[m] * out_cols, out_cols, 1)
        early.append(swap(piece, "head", m) if m else piece)
    far = range(2, shards, 2)
    grad_rows = jnp.concatenate([cotangent[0]] + [swap(cotangent[0], "ffn", m) for m in far], 0)
    gate_w = jnp.concatenate([w_gate, swap(w_gate, "ffn", 1)], 1)
    up_w = jnp.concatenate([w_up, swap(w_up, "ffn", 1)], 1)
    down_w = jnp.concatenate([w_down, swap(w_down, "ffn", 1)], 0)
    w_heads = lax.dynamic_slice_in_dim(w_qkv, head_pos * packed_cols, packed_cols, 1)
    out_w = jnp.concatenate(
        [lax.dynamic_slice_in_dim(w_out, o * out_cols, out_cols, 0) for o in owners], 0
    )

    positions = jnp.concatenate([o * rows + jnp.arange(rows, dtype=jnp.int32) for o in owners])
    cosine, sine = rotary(positions, HD)
    normed, scaled, queries, key_list, mixes = [], [], [], [], []
    rows_in = inputs[0].astype(jnp.float32)
    scale_one = rms_scale(rows_in)
    for m in range(groups):
        block = x_all[m].astype(jnp.float32)
        scale = rms_scale(block)
        scaled.append(block * scale)
        normed.append((block * scale * gain_attn).astype(jnp.bfloat16))
        packed = matmul(normed[m], w_heads).astype(jnp.bfloat16)
        packed = packed.reshape(rows, heads_here, 3, HD).astype(jnp.float32)
        part = slice(m * rows, (m + 1) * rows)
        queries.append(rotate(packed[:, :, 0], cosine[part], sine[part], 1.0))
        key_list.append(rotate(packed[:, :, 1], cosine[part], sine[part], 1.0))
        value = early[m].reshape(rows, heads_here, HD).astype(jnp.float32)
        mixes.append(0.5 * (packed[:, :, 2] + value))
    query = jnp.concatenate(queries, 0).astype(jnp.bfloat16)
    keys = jnp.concatenate(key_list, 0).astype(jnp.bfloat16)
    mixed = jnp.concatenate(mixes, 0).astype(jnp.bfloat16)
    attended, log_sums = scan_forward(query, keys, mixed, positions, valid_len, block_rows)
    attended = attended.reshape(groups, rows, out_cols)
    att_own = jnp.concatenate(
        [attended[0]] + [swap(attended[m], "head", m) for m in range(1, groups)], 1
    )
    hidden = rows_in + matmul(att_own, out_w)
    scale_two = rms_scale(hidden)
    normed_two = (hidden * scale_two * gain_mlp).astype(jnp.bfloat16)

    mlp_rows = [normed_two] + [swap(normed_two, "ffn", m) for m in far]
    grad_list = [grad_rows[i * rows : (i + 1) * rows] for i in range(len(mlp_rows))]
    actives, grad_gates, grad_ups, downs, grad_normed_list = [], [], [], [], []
    for i, block in enumerate(mlp_rows):
        gate_rows = matmul(block, gate_w)
        up_rows = matmul(block, up_w)
        sigmoid_gate = jax.nn.sigmoid(gate_rows)
        silu_gate = gate_rows * sigmoid_gate
        grad_active = against(grad_list[i], down_w)
        actives.append((silu_gate * up_rows).astype(jnp.bfloat16))
        grad_gates.append(
            (
                grad_active * up_rows * sigmoid_gate * (1.0 + gate_rows * (1.0 - sigmoid_gate))
            ).astype(jnp.bfloat16)
        )
        grad_ups.append((grad_active * silu_gate).astype(jnp.bfloat16))
        grad_normed_list.append(against(grad_gates[i], gate_w) + against(grad_ups[i], up_w))
        downs.append(matmul(actives[i], down_w))
    grad_normed_two = grad_normed_list[0]
    for i, m in enumerate(far):
        came = swap(grad_normed_list[i + 1].astype(jnp.bfloat16), "ffn", m)
        grad_normed_two = grad_normed_two + came.astype(jnp.float32)
    down_rows = downs[0]
    for i, m in enumerate(far):
        down_rows = down_rows + swap(downs[i + 1].astype(jnp.bfloat16), "ffn", m).astype(jnp.float32)
    output = (hidden + down_rows).astype(jnp.bfloat16)[None]

    all_rows = jnp.concatenate(mlp_rows, 0)
    ff_sums = []
    for left, right in (
        (grad_rows, jnp.concatenate(actives, 0)),
        (all_rows, jnp.concatenate(grad_gates, 0)),
        (all_rows, jnp.concatenate(grad_ups, 0)),
    ):
        away = inner_rows(left, right[:, hidden_here:]).astype(jnp.bfloat16)
        part = inner_rows(left, right[:, :hidden_here])
        part = (part + swap(away, "ffn", 1).astype(jnp.float32)).astype(jnp.bfloat16)
        steps = [("head", b) for b in bits_of("head")] + [("row", b) for b in bits_of("row")]
        part = part.reshape([2] * len(steps) + [-1, hidden_here])
        order = [s for s in steps if s[0] == "head"] + [s for s in reversed(steps) if s[0] == "row"]
        left_steps = list(steps)
        for s in order:
            part = halve(part, left_steps.index(s), *s)
            left_steps.remove(s)
            if left_steps:
                part = part.astype(jnp.bfloat16)
        ff_sums.append(part)
    sum_down, sum_gate, sum_up = ff_sums

    grad_y = cotangent[0].astype(jnp.float32)
    grad_gain_two = jnp.sum(grad_normed_two * hidden * scale_two, axis=0)
    weighted_two = grad_normed_two * gain_mlp
    cube_two = scale_two * scale_two * scale_two
    grad_hidden = (
        grad_y
        + scale_two * weighted_two
        - hidden * cube_two * jnp.mean(weighted_two * hidden, axis=-1, keepdims=True)
    )
    grad_proj = grad_hidden.astype(jnp.bfloat16)
    grad_att = against(grad_proj, out_w).astype(jnp.bfloat16)
    grad_att = jnp.concatenate(
        [
            swap(grad_att[:, m * out_cols : (m + 1) * out_cols], "head", m)
            if m
            else grad_att[:, :out_cols]
            for m in range(groups)
        ],
        0,
    ).reshape(span_rows, heads_here, HD)

    def over_buckets(part):
        steps = [("ffn", b) for b in bits_of("ffn")] + [("row", b) for b in bits_of("row")]
        part = part.astype(jnp.bfloat16).reshape([2] * len(steps) + [-1, part.shape[1]])
        order = [s for s in reversed(steps) if s[0] == "ffn"] + [
            s for s in reversed(steps) if s[0] == "row"
        ]
        left_steps = list(steps)
        for s in order:
            part = halve(part, left_steps.index(s), *s)
            left_steps.remove(s)
            if left_steps:
                part = part.astype(jnp.bfloat16)
        return part

    part = over_buckets(inner_rows(grad_proj, att_own))
    sum_out = part[:, :out_cols]
    for m in range(1, groups):
        came = swap(part[:, m * out_cols : (m + 1) * out_cols].astype(jnp.bfloat16), "head", m)
        sum_out = sum_out + came.astype(jnp.float32)

    grad_query, grad_keys, grad_mixed = scan_backward(
        query, keys, mixed, positions, valid_len, log_sums, grad_att, block_rows
    )
    grad_packed = jnp.stack(
        [
            rotate(grad_query, cosine, sine, -1.0),
            rotate(grad_keys, cosine, sine, -1.0),
            0.5 * grad_mixed,
        ],
        axis=2,
    )
    grad_packed = grad_packed.astype(jnp.bfloat16).reshape(span_rows, packed_cols)
    grad_early = (0.5 * grad_mixed).astype(jnp.bfloat16).reshape(span_rows, out_cols)
    firsts = [grad_early[m * rows : (m + 1) * rows] for m in range(groups)]
    firsts = [swap(firsts[m], "head", m) if m else firsts[0] for m in range(groups)]
    grad_first = jnp.zeros((rows, width), jnp.bfloat16)
    for m in range(groups):
        grad_first = lax.dynamic_update_slice_in_dim(grad_first, firsts[m], owners[m] * out_cols, 1)
    shares = [
        against(grad_packed[m * rows : (m + 1) * rows], w_heads) for m in range(groups)
    ]
    grad_gain_one = sum(jnp.sum(shares[m] * scaled[m], axis=0) for m in range(groups))
    grad_normed = shares[0]
    for m in range(1, groups):
        grad_normed = grad_normed + swap(shares[m].astype(jnp.bfloat16), "head", m).astype(jnp.float32)
    sum_qkv = over_buckets(inner_rows(jnp.concatenate(normed, 0), grad_packed))
    weighted_one = grad_normed * gain_attn
    cube_one = scale_one * scale_one * scale_one
    grad_in = (
        grad_hidden
        + scale_one * weighted_one
        - rows_in * cube_one * jnp.mean(weighted_one * rows_in, axis=-1, keepdims=True)
    )
    gains = total(jnp.stack([grad_gain_one, grad_gain_two]), ("ffn", "head", "row"))
    return (
        output,
        grad_in[None],
        grad_first[None],
        gains[0],
        sum_qkv,
        sum_out.T,
        gains[1],
        sum_gate,
        sum_up,
        sum_down.T,
    )


SCALE = 4.5e8


def low(values):
    return values.astype(jnp.bfloat16)


def high(values):
    return values.astype(jnp.float32)


def on_chip(body, outs, scalars, arrays, name, scratch=(), aliases=None, limit=3, cost=1.0, away=()):
    inside = pl.BlockSpec(memory_space=pltpu.VMEM)
    return pl.pallas_call(
        body,
        out_shape=outs,
        in_specs=[pl.BlockSpec(memory_space=pltpu.SMEM)] * len(scalars) + [inside] * len(arrays),
        out_specs=jax.tree.unflatten(
            jax.tree.structure(outs),
            [
                pl.BlockSpec(memory_space=pltpu.HBM) if i in away else inside
                for i in range(len(jax.tree.leaves(outs)))
            ],
        ),
        scratch_shapes=list(scratch),
        input_output_aliases=aliases or {},
        cost_estimate=pl.CostEstimate(
            flops=int(cost * SCALE), transcendentals=0, bytes_accessed=1
        ),
        compiler_params=pltpu.CompilerParams(vmem_limit_bytes=limit << 20),
        name=name,
    )(*scalars, *arrays)


def shape16(*dims):
    return jax.ShapeDtypeStruct(dims, jnp.bfloat16)


def shape32(*dims):
    return jax.ShapeDtypeStruct(dims, jnp.float32)


def spans(total):
    return [(a, min(a + STEP, total)) for a in range(0, total, STEP)]


def turn(values):
    lane = lax.broadcasted_iota(jnp.int32, values.shape, 1)
    return jnp.where(
        lane % HD < HD // 2, pltpu.roll(values, 2 * HD - HD // 2, 1), pltpu.roll(values, HD // 2, 1)
    )


def allowed_keys(a, b, valid):
    size = b - a
    down = lax.broadcasted_iota(jnp.int32, (size, size), 0)
    across = lax.broadcasted_iota(jnp.int32, (size, size), 1)
    allowed = down <= across
    if b > MIN_LEN:
        allowed = allowed & (down < valid - a)
    return allowed


def columns(index, size):
    return pl.ds(pl.multiple_of(index * size, size), size)


def forward_body(
    place, packed_own, packed_oth, early_own, early_oth, cos_ref, sin_ref,
    att_own, att_oth, q_far, k_far, v_far, lse_out, q_out, k_out, v_out, flipped, att, sems,
):
    rows = packed_own.shape[0]
    span = 2 * rows
    wide = 2 * HD
    valid = place[1]
    f32 = jnp.float32
    bf = jnp.bfloat16
    first = lax.broadcasted_iota(jnp.int32, (1, wide), 1) < HD
    flipped[:, HD:, :] = jnp.ones((2, 16, span), bf)

    def copies(p):
        cols = columns(p, wide)
        return [
            pltpu.make_async_copy(near.at[:, cols], far.at[:, cols], sems.at[i, p])
            for i, (near, far) in enumerate(((q_out, q_far), (k_out, k_far), (v_out, v_far)))
        ]

    def pair(p, _):
        cols = columns(p, wide)
        for m, (packed, early) in enumerate(((packed_own, early_own), (packed_oth, early_oth))):
            here = columns(place[0] ^ m, rows)
            x0 = high(packed[:, pl.ds(pl.multiple_of(p * 3 * wide, wide), wide)])
            x1 = high(packed[:, pl.ds(pl.multiple_of(p * 3 * wide + wide, wide), wide)])
            x2 = high(packed[:, pl.ds(pl.multiple_of(p * 3 * wide + 2 * wide, wide), wide)])
            cosine = cos_ref[here, :]
            sine = sin_ref[here, :]
            q = jnp.where(first, x0, x1)
            k = pltpu.roll(jnp.where(first, x2, x0), HD, 1)
            v = jnp.where(first, x1, x2)
            q_out[here, cols] = low(q * cosine + turn(q) * sine)
            k_out[here, cols] = low(k * cosine + turn(k) * sine)
            v_out[here, cols] = low(0.5 * (v + high(early[:, cols])))
        for copy in copies(p):
            copy.start()
        turned = v_out[:, cols].T
        for e in range(2):
            flipped[e, :HD, :] = turned[e * HD : (e + 1) * HD, :]
        for a, b in spans(span):
            q = q_out[a:b, cols] * jnp.asarray(0.125, bf)
            allowed = allowed_keys(a, b, valid)
            for e in range(2):
                qe = jnp.where(first == (e == 0), q, jnp.zeros_like(q))
                diag = jnp.where(allowed, against(k_out[a:b, cols], qe), -1e30)
                top = jnp.max(diag, axis=0, keepdims=True)
                if a:
                    past = against(k_out[:a, cols], qe)
                    top = jnp.maximum(top, jnp.max(past, axis=0, keepdims=True))
                out = matmul(flipped[e, :, a:b], low(jnp.exp(diag - top)))
                if a:
                    out = out + matmul(flipped[e, :, :a], low(jnp.exp(past - top)))
                amount = out[HD : HD + 1, :]
                att[e * HD : (e + 1) * HD, a:b] = out[:HD, :] / amount
                lse_out[p, e : e + 1, a:b] = top + jnp.log(amount)
        result = low(att[...].T)
        upper = place[0] == 0
        att_own[:, cols] = jnp.where(upper, result[:rows, :], result[rows:, :])
        att_oth[:, cols] = jnp.where(upper, result[rows:, :], result[:rows, :])
        return 0

    lax.fori_loop(0, lse_out.shape[0], pair, 0)
    for p in range(lse_out.shape[0]):
        for copy in copies(p):
            copy.wait()


def attend_forward(place, packed_own, packed_oth, early_own, early_oth, cosine, sine):
    rows, cols = packed_own.shape
    heads = cols // (3 * HD)
    span = 2 * rows
    out = shape16(rows, heads * HD)
    natural = shape16(span, heads * HD)
    return on_chip(
        forward_body,
        (out, out, natural, natural, natural, shape32(heads // 2, 2, span)),
        (place,),
        (packed_own, packed_oth, early_own, early_oth, cosine, sine),
        "attend_forward",
        cost=11.0,
        limit=6,
        away=(2, 3, 4),
        scratch=(
            pltpu.VMEM(natural.shape, jnp.bfloat16),
            pltpu.VMEM(natural.shape, jnp.bfloat16),
            pltpu.VMEM(natural.shape, jnp.bfloat16),
            pltpu.VMEM((2, HD + 16, span), jnp.bfloat16),
            pltpu.VMEM((2 * HD, span), jnp.float32),
            pltpu.SemaphoreType.DMA((3, heads // 2)),
        ),
    )


def backward_body(
    start, place, q_ref, k_ref, v_ref, lse_ref, go_own, go_oth, att_own, att_oth, cos_ref, sin_ref,
    d_out, f_own, f_oth, grad, prod, turned_k, dq, dk, dv,
):
    rows = go_own.shape[0]
    span = 2 * rows
    valid = place[1]
    wide = 2 * HD
    bf = jnp.bfloat16
    first = lax.broadcasted_iota(jnp.int32, (1, wide), 1) < HD
    eighth = jnp.asarray(0.125, bf)

    def pair(i, _):
        p = i + start
        cols = columns(p, wide)
        for m, (go, att) in enumerate(((go_own, att_own), (go_oth, att_oth))):
            here = columns(place[0] ^ m, rows)
            grad[here, :] = go[:, cols]
            prod[here, :] = high(go[:, cols]) * high(att[:, cols])
        flat = prod[...].T
        deltas = [jnp.sum(flat[e * HD : (e + 1) * HD, :], axis=0, keepdims=True) for e in range(2)]
        turned_k[...] = (k_ref[:, cols] * eighth).T
        for n, (a, b) in enumerate(spans(span)):
            allowed = allowed_keys(a, b, valid)
            q = q_ref[a:b, cols] * eighth
            g = grad[a:b, :]
            parts = ((a, b), (0, a)) if a else ((a, b),)
            sums = {}
            for e in range(2):
                mine = first == (e == 0)
                qe = jnp.where(mine, q, jnp.zeros_like(q))
                ge = jnp.where(mine, g, jnp.zeros_like(g))
                for lo, hi in parts:
                    scores = against(k_ref[lo:hi, cols], qe)
                    if lo == a:
                        scores = jnp.where(allowed, scores, -1e30)
                    weights = jnp.exp(scores - lse_ref[p, e : e + 1, a:b])
                    grad_w = against(v_ref[lo:hi, cols], ge)
                    grad_s = low(weights * (grad_w - deltas[e][:, a:b]))
                    dv_here = matmul(low(weights), ge)
                    dk_here = matmul(grad_s, qe)
                    dq_here = matmul(turned_k[e * HD : (e + 1) * HD, lo:hi], grad_s)
                    if (lo, "v") in sums:
                        dv_here = dv_here + sums[lo, "v"]
                        dk_here = dk_here + sums[lo, "k"]
                    sums[lo, "v"], sums[lo, "k"] = dv_here, dk_here
                    sums[lo, e] = dq_here
            for e in range(2):
                dq[e * HD : (e + 1) * HD, a:b] = sums[a, e] + sums[0, e] if a else sums[a, e]
            dv[a:b, :] = sums[a, "v"]
            dk[a:b, :] = sums[a, "k"]
            if a:
                dv[:a, :] += sums[0, "v"]
                dk[:a, :] += sums[0, "k"]
        prod[...] = dq[...].T
        for m, f_out in enumerate((f_own, f_oth)):
            here = columns(place[0] ^ m, rows)
            cosine = cos_ref[here, :]
            sine = sin_ref[here, :]
            gv = low(0.5 * dv[here, :])
            gk = dk[here, :]
            gk = low(pltpu.roll(gk * cosine - turn(gk) * sine, HD, 1))
            gq = prod[here, :]
            gq = low(gq * cosine - turn(gq) * sine)
            part = slice(m * rows, (m + 1) * rows)
            base = i * 3 * wide
            d_out[part, pl.ds(pl.multiple_of(base, wide), wide)] = jnp.where(first, gq, gk)
            d_out[part, pl.ds(pl.multiple_of(base + wide, wide), wide)] = jnp.where(first, gv, gq)
            d_out[part, pl.ds(pl.multiple_of(base + 2 * wide, wide), wide)] = jnp.where(first, gk, gv)
            f_out[:, columns(i, wide)] = gv
        return 0

    lax.fori_loop(0, f_own.shape[1] // wide, pair, 0)


def attend_backward(place, q, k, v, lse, go_own, go_oth, att_own, att_oth, cosine, sine, pairs):
    span = q.shape[0]
    rows = span // 2
    wide = 2 * HD
    cols = wide * (pairs[1] - pairs[0])
    return on_chip(
        functools.partial(backward_body, pairs[0]),
        (shape16(span, 3 * cols), shape16(rows, cols), shape16(rows, cols)),
        (place,),
        (q, k, v, lse, go_own, go_oth, att_own, att_oth, cosine, sine),
        "attend_backward",
        cost=7.5,
        limit=4,
        scratch=(
            pltpu.VMEM((span, wide), jnp.bfloat16),
            pltpu.VMEM((span, wide), jnp.float32),
            pltpu.VMEM((wide, span), jnp.bfloat16),
            pltpu.VMEM((wide, span), jnp.float32),
            pltpu.VMEM((span, wide), jnp.float32),
            pltpu.VMEM((span, wide), jnp.float32),
        ),
    )


def project_body(base, order, x_ref, gain_ref, w_ref, *refs):
    away_far, mine_far, packed_ref, xn, away, mine, sems = refs[-7:]
    rows = x_ref.shape[0]
    x = high(x_ref[...])
    xn[...] = low(x * rms_scale(x) * gain_ref[...])
    arrange_halves(order, (xn,), away, mine)
    there = slice(base, base + rows)
    copies = [
        pltpu.make_async_copy(away, away_far.at[there, :], sems.at[0]),
        pltpu.make_async_copy(mine, mine_far.at[there, :], sems.at[1]),
    ]
    for copy in copies:
        copy.start()
    cols = w_ref.shape[1] // 3
    for i in range(3):
        part = slice(i * cols, (i + 1) * cols)
        packed_ref[:, part] = low(matmul(xn[...], w_ref[:, part]))
    for copy in copies:
        copy.wait()


def project(order, x, gain, w, before=()):
    rows, width = x.shape
    part = shape16(2 * rows, width // 2)
    return pl.pallas_call(
        functools.partial(project_body, rows if before else 0),
        out_shape=(part, part, shape16(rows, w.shape[1])),
        in_specs=[pl.BlockSpec(memory_space=pltpu.SMEM)]
        + [pl.BlockSpec(memory_space=pltpu.VMEM)] * 3
        + [pl.BlockSpec(memory_space=pltpu.HBM)] * len(before),
        out_specs=(
            pl.BlockSpec(memory_space=pltpu.HBM),
            pl.BlockSpec(memory_space=pltpu.HBM),
            pl.BlockSpec(memory_space=pltpu.VMEM),
        ),
        scratch_shapes=[
            pltpu.VMEM((rows, width), jnp.bfloat16),
            pltpu.VMEM((rows, width // 2), jnp.bfloat16),
            pltpu.VMEM((rows, width // 2), jnp.bfloat16),
            pltpu.SemaphoreType.DMA((2,)),
        ],
        input_output_aliases={4 + i: i for i in range(len(before))},
        cost_estimate=pl.CostEstimate(
            flops=int(2 * SCALE), transcendentals=0, bytes_accessed=1
        ),
        compiler_params=pltpu.CompilerParams(vmem_limit_bytes=5 << 20),
        name="project",
    )(order, x, gain, w, *before)


def arrange(order, blocks, out):
    rows = blocks[0].shape[0]
    size = out.shape[1] // order.shape[0]
    for i in range(order.shape[0]):
        for b, block in enumerate(blocks):
            out[b * rows : (b + 1) * rows, i * size : (i + 1) * size] = block[:, columns(order[i], size)]


def finish(place, x, att_own, att_came, w, gain):
    def body(place, x_ref, att_own, att_came, w_ref, gain_ref, hidden_far, hn_ref, hidden_ref, sem):
        cols = att_own.shape[1]
        hidden = high(x_ref[...]) + matmul(att_own[...], w_ref[columns(place[0], cols), :])
        hidden = hidden + matmul(att_came[...], w_ref[columns(1 - place[0], cols), :])
        hidden_ref[...] = hidden
        copy = pltpu.make_async_copy(hidden_ref, hidden_far, sem.at[0])
        copy.start()
        hn_ref[...] = low(hidden * rms_scale(hidden) * gain_ref[...])
        copy.wait()

    return on_chip(
        body,
        (shape32(*x.shape), shape16(*x.shape)),
        (place,),
        (x, att_own, att_came, w, gain),
        "finish",
        cost=3.0,
        limit=5,
        away=(0,),
        scratch=(pltpu.VMEM(x.shape, jnp.float32), pltpu.SemaphoreType.DMA((1,))),
    )


def reorder(order, *blocks):
    rows, cols = blocks[0].shape

    def body(order, *refs):
        arrange(order, refs[:-1], refs[-1])

    return on_chip(body, shape16(rows * len(blocks), cols), (order,), blocks, "reorder", cost=0.9)


def arrange_halves(order, blocks, away, mine):
    rows = blocks[0].shape[0]
    count = order.shape[0] // 2
    size = mine.shape[1] // count
    for half, out in enumerate((away, mine)):
        for i in range(count):
            for b, block in enumerate(blocks):
                out[b * rows : (b + 1) * rows, i * size : (i + 1) * size] = block[
                    :, columns(order[half * count + i], size)
                ]


def reorder_halves(order, *blocks):
    rows, cols = blocks[0].shape

    def body(order, *refs):
        arrange_halves(order, refs[:-2], *refs[-2:])

    part = shape16(rows * len(blocks), cols // 2)
    return on_chip(body, (part, part), (order,), blocks, "reorder_halves", cost=0.9)


def feed_rows(hn, grads, gate_w, up_w, mine, other, base):
    rows = hn.shape[0]
    units = gate_w[0].shape[0]
    here = slice(base, base + rows)
    total_hn = None
    for s in range(2):
        gate = against(hn[...], gate_w[s][...])
        up = against(hn[...], up_w[s][...])
        grad = high(grads[s][...])
        sig = 1.0 / (1.0 + jnp.exp(-gate))
        silu = gate * sig
        results = (silu * up, grad * up * sig * (1.0 + gate * (1.0 - sig)), grad * silu)
        for i, result in enumerate(results):
            if s == 0:
                mine[i][here, :] = low(result)
            else:
                other[2 * i * rows + base : 2 * i * rows + base + rows, :units] = low(result)
    for s in range(2):
        for i, w in ((1, gate_w[s]), (2, up_w[s])):
            if s == 0:
                share = matmul(mine[i][here, :], w[...])
            else:
                share = matmul(other[2 * i * rows + base : 2 * i * rows + base + rows, :units], w[...])
            total_hn = share if total_hn is None else total_hn + share
    return total_hn


def feed_own_body(order, hn, dy_own, dy_oth, wg0, wg1, wu0, wu1, wd0, wd1, *refs):
    rows = hn.shape[0]
    outs, grads = refs[:9], refs[9:]
    mine, other, dhn, down = outs[:3], outs[3], outs[4], outs[5]
    for grad, w in zip(grads, (wd0, wd1)):
        grad[...] = low(against(dy_own[...], w[...]))
    dhn[...] = feed_rows(hn, grads, (wg0, wg1), (wu0, wu1), mine, other, 0)
    down[...] = matmul(mine[0][:rows, :], wd0[...]) + matmul(other[:rows, : wd1.shape[0]], wd1[...])
    for grad, w in zip(outs[6:8], (wd0, wd1)):
        grad[...] = low(against(dy_oth[...], w[...]))
    arrange(order, (dy_own, dy_oth), outs[8])


def feed_oth_body(order, hn_own, hn, g0, g1, wg0, wg1, wu0, wu1, *refs):
    outs = refs[4:]
    outs[4][...] = low(
        feed_rows(hn, (g0, g1), (wg0, wg1), (wu0, wu1), outs[:3], outs[3], hn.shape[0])
    )
    arrange(order, (hn_own, hn), outs[5])


def feed_own(order, hn, dy_own, dy_oth, gate_w, up_w, down_w):
    rows, width = hn.shape
    units = gate_w[0].shape[0]
    part = shape16(2 * rows, units)
    other = shape16(6 * rows, -(-units // 128) * 128)
    return on_chip(
        feed_own_body,
        (part,) * 3
        + (other,)
        + (shape32(rows, width),) * 2
        + (shape16(rows, units),) * 2
        + (shape16(2 * rows, width),),
        (order,),
        (hn, dy_own, dy_oth, *gate_w, *up_w, *down_w),
        "feed_own",
        limit=15,
        cost=11.0,
        scratch=(pltpu.VMEM((rows, units), jnp.bfloat16),) * 2,
    )


def feed_oth(order, hn_own, hn, grads, gate_w, up_w, parts):
    rows, width = hn.shape
    return on_chip(
        feed_oth_body,
        tuple(shape16(*part.shape) for part in parts)
        + (shape16(rows, width), shape16(2 * rows, width)),
        (order,),
        (hn_own, hn, *grads, *gate_w, *up_w, *parts),
        "feed_oth",
        aliases={9 + i: i for i in range(4)},
        limit=14,
        cost=7.0,
    )


def ff_grad(left, left_core, index, right, right_core):
    rows, units = left.shape
    mid = right.shape[1] // 2

    def body(left, left_core, right, right_core, away, kept):
        for i, out in enumerate((away, kept)):
            part = slice(i * mid, (i + 1) * mid)
            out[...] = low(
                inner_rows(left[...], right[:, part])
                + inner_rows(left_core[index * rows : (index + 1) * rows, :units], right_core[:, part])
            )

    part = shape16(units, mid)
    return on_chip(body, (part, part), (), (left, left_core, right, right_core), "ff_grad", cost=2.7)


def fold(kept, came):
    mid = kept.shape[1] // 2

    def body(kept, came, away, rest):
        away[...] = low(high(kept[:, :mid]) + high(came[:, :mid]))
        rest[...] = low(high(kept[:, mid:]) + high(came[:, mid:]))

    part = shape16(kept.shape[0], mid)
    return on_chip(body, (part, part), (), (kept, came), "fold", cost=0.3)


def fold_rows(kept, came):
    mid = kept.shape[0] // 2

    def body(kept, came, away, rest):
        away[...] = low(high(kept[:mid, :]) + high(came[:mid, :]))
        rest[...] = low(high(kept[mid:, :]) + high(came[mid:, :]))

    part = shape16(mid, kept.shape[1])
    return on_chip(body, (part, part), (), (kept, came), "fold_rows", cost=0.3)


def hidden_grad_body(order, place, dhn_own, dhn_came, hidden_ref, dy_ref, gain_ref, w_ref, grad_ref, send_ref, own_ref, away_ref, mine_ref, gains_ref, proj):
    hidden = hidden_ref[...]
    scale = rms_scale(hidden)
    dhn = dhn_own[...] + high(dhn_came[...])
    gains_ref[...] = jnp.sum(dhn * hidden * scale, axis=0, keepdims=True)
    weighted = dhn * gain_ref[...]
    mean = jnp.mean(weighted * hidden, axis=-1, keepdims=True)
    grad = high(dy_ref[...]) + scale * weighted - hidden * (scale * scale * scale * mean)
    grad_ref[...] = grad
    proj[...] = low(grad)
    cols = send_ref.shape[1]
    send_ref[...] = low(against(proj[...], w_ref[columns(1 - place[0], cols), :]))
    own_ref[...] = low(against(proj[...], w_ref[columns(place[0], cols), :]))
    arrange_halves(order, (proj,), away_ref, mine_ref)


def hidden_grad(order, place, dhn_own, dhn_came, hidden, dy, gain, w):
    rows, width = hidden.shape
    part = shape16(rows, width // 2)
    return on_chip(
        hidden_grad_body,
        (shape32(rows, width), part, part, part, part, shape32(1, width)),
        (order, place),
        (dhn_own, dhn_came, hidden, dy, gain, w),
        "hidden_grad",
        cost=2.2,
        limit=6,
        scratch=(pltpu.VMEM((rows, width), jnp.bfloat16),),
    )


def bucket_grad(left, left_core, rights, rights_core):
    mid = left.shape[1] // 2
    cols = rights[0].shape[1]
    count = len(rights)

    def body(left, left_core, *refs):
        for i in range(count):
            part = slice(i * cols, (i + 1) * cols)
            for half, out in enumerate(refs[-2:]):
                cut = slice(half * mid, (half + 1) * mid)
                out[:, part] = low(
                    inner_rows(left[:, cut], refs[i][...])
                    + inner_rows(left_core[:, cut], refs[count + i][...])
                )

    full = shape16(mid, cols * count)
    return on_chip(
        body, (full, full), (), (left, left_core, *rights, *rights_core), "bucket_grad", cost=3.0
    )


def bucket_near(row, kept, came, gains=None):
    quarter, cols = kept.shape
    size = quarter // 4
    extra = 0 if gains is None else 16

    def body(row, kept, came, *refs):
        away, rest = refs[-2:]
        near = row[0] & 1
        for i in range(2):
            here = pl.ds(pl.multiple_of(i * 2 * size + near * size, size), size)
            there = pl.ds(pl.multiple_of(i * 2 * size + (1 - near) * size, size), size)
            part = slice(i * size, (i + 1) * size)
            away[part, :] = low(high(kept[there, :]) + high(came[there, :]))
            rest[part, :] = low(high(kept[here, :]) + high(came[here, :]))
        if extra:
            values = refs[0][...]
            blank = jnp.zeros((2, cols - values.shape[1]), jnp.float32)
            lines = [jnp.concatenate([values, blank], 1), jnp.zeros((extra - 2, cols), jnp.float32)]
            away[2 * size :, :] = low(jnp.concatenate(lines, 0))

    return on_chip(
        body,
        (shape16(2 * size + extra, cols), shape16(2 * size, cols)),
        (row,),
        (kept, came) + (() if gains is None else (gains,)),
        "bucket_near",
        cost=0.3,
    )


def bucket_far(kept, came, sent):
    half, cols = kept.shape
    size = half // 2

    def body(kept, came, sent, away, rest):
        away[:size, :] = low(high(kept[:size, :]) + high(came[:size, :]))
        rest[...] = low(high(kept[size:, :]) + high(came[size:half, :]))
        away[size:, :] = low(high(sent[half:, :]) + high(came[half:, :]))

    return on_chip(
        body, (shape16(size + 16, cols), shape16(size, cols)), (), (kept, came, sent), "bucket_far", cost=0.3
    )


def shares_body(d_a, d_b, fa, fb, w_ref, x_own, x_oth, gain_two, send_ref, own_ref, gains_ref):
    rows, width = x_own.shape
    cut = d_a.shape[1]
    sums = None
    for m, x_ref in ((1, x_oth), (0, x_own)):
        part = slice(m * rows, (m + 1) * rows)
        share = against(d_a[part, :], w_ref[:, :cut]) + against(d_b[part, :], w_ref[:, cut:])
        if m:
            send_ref[:, :width] = low(share)
        else:
            own_ref[...] = share
        x = high(x_ref[...])
        here = jnp.sum(share * (x * rms_scale(x)), axis=0, keepdims=True)
        sums = here if sums is None else sums + here
    send_ref[:, width : width + fa.shape[1]] = fa[...]
    send_ref[:, width + fa.shape[1] :] = fb[...]
    gains_ref[0:1, :] = sums
    gains_ref[1:2, :] = gain_two[...]


def shares(d_a, d_b, fa, fb, w, x_own, x_oth, gain_two):
    rows, width = x_own.shape
    return on_chip(
        shares_body,
        (shape16(rows, width + 2 * fa.shape[1]), shape32(rows, width), shape32(2, width)),
        (),
        (d_a, d_b, fa, fb, w, x_own, x_oth, gain_two),
        "shares",
        cost=2.3,
    )


def input_grad_body(place, share_ref, came_ref, grad_ref, x_ref, gain_ref, fa, fb, out_ref, first_ref):
    width = x_ref.shape[1]
    x = high(x_ref[...])
    scale = rms_scale(x)
    weighted = (share_ref[...] + high(came_ref[:, :width])) * gain_ref[...]
    mean = jnp.mean(weighted * x, axis=-1, keepdims=True)
    out_ref[...] = grad_ref[...] + scale * weighted - x * (scale * scale * scale * mean)
    cols = fa.shape[1]
    own = 2 * place[0]
    oth = 2 - own
    first_ref[:, columns(own, cols)] = fa[...]
    first_ref[:, columns(own + 1, cols)] = fb[...]
    first_ref[:, columns(oth, cols)] = came_ref[:, width : width + cols]
    first_ref[:, columns(oth + 1, cols)] = came_ref[:, width + cols :]


def input_grad(place, share, came, grad_hidden, x, gain, fa, fb):
    return on_chip(
        input_grad_body,
        (shape32(*x.shape), shape16(*x.shape)),
        (place,),
        (share, came, grad_hidden, x, gain, fa, fb),
        "input_grad",
        cost=2.0,
        limit=6,
    )


def after(first, *values):
    return lax.optimization_barrier((first, *values))[1:]


def two_groups(
    inputs,
    first_values,
    lengths,
    gain_attn,
    w_qkv,
    w_out,
    gain_mlp,
    w_gate,
    w_up,
    w_down,
    cotangent,
):
    rows = inputs.shape[1]
    width = inputs.shape[2]
    span = 2 * rows
    out_cols = HEADS // 2 * HD
    packed_cols = 3 * out_cols
    mid = width // 2
    h = lax.axis_index("head")
    f = lax.axis_index("ffn")
    r = lax.axis_index("row")
    row_size = lax.axis_size("row")
    place = jnp.stack([h, lengths[0]]).astype(jnp.int32)
    row = r.reshape(1).astype(jnp.int32)
    tie = lax.optimization_barrier
    gain_attn = gain_attn.reshape(1, width)
    gain_mlp = gain_mlp.reshape(1, width)

    x_own = inputs[0]
    x_oth = swap(x_own, "head", 1)
    early_own = lax.dynamic_slice_in_dim(first_values[0], h * out_cols, out_cols, 1)
    early_oth = swap(
        lax.dynamic_slice_in_dim(first_values[0], (1 - h) * out_cols, out_cols, 1), "head", 1
    )
    dy_own = cotangent[0]
    dy_oth = swap(dy_own, "ffn", 2)
    down_core = swap(w_down, "ffn", 1)
    gate_core = swap(w_gate.T, "ffn", 1)
    up_core = swap(w_up.T, "ffn", 1)
    qkv_w = lax.dynamic_slice_in_dim(w_qkv, h * packed_cols, packed_cols, 1)
    half = HD // 2
    inverse = jnp.exp(-jnp.log(10000.0) * jnp.arange(half, dtype=jnp.float32) * 2.0 / HD)
    angles = jnp.arange(span, dtype=jnp.float32)[:, None] * jnp.tile(inverse, 4)[None, :]
    cosine = jnp.cos(angles)
    sign = jnp.where(jnp.arange(2 * HD) % HD < half, -1.0, 1.0)
    sine = jnp.sin(angles) * sign[None, :]

    ff_order = jnp.stack([(h ^ a) * row_size + (r ^ b) for a in (1, 0) for b in (3, 1, 2, 0)])
    down_order = jnp.stack([(h ^ a) * row_size + (r ^ b) for b in (3, 1, 2, 0) for a in (1, 0)])
    att_order = jnp.stack(
        [((f ^ a) * row_size + (r & 2 ^ b)) // 2 for a in (3, 1, 2, 0) for b in (2, 0)]
    )

    xn_away, xn_mine, packed_own = project(att_order, x_own, gain_attn, qkv_w)
    x_oth, early_oth, packed_own, cosine, sine, early_own, down_core, gate_core, up_core = tie(
        (x_oth, early_oth, packed_own, cosine, sine, early_own, down_core, gate_core, up_core)
    )
    xn_away, xn_mine, packed_oth = project(att_order, x_oth, gain_attn, qkv_w, (xn_away, xn_mine))
    att_own, att_oth, query, keys, mixed, log_sums = attend_forward(
        place, packed_own, packed_oth, early_own, early_oth, cosine, sine
    )
    att_came = swap(att_oth, "head", 1)
    att_core = swap(att_own, "ffn", 1)
    dy_oth, xn_away = after(att_own, dy_oth, xn_away)
    down_w = (w_down, down_core)
    gate_w = (w_gate.T, gate_core)
    up_w = (w_up.T, up_core)
    xn_core = swap(xn_away, "ffn", 1)
    dy_send, dyo_send = after(att_own, dy_own, dy_oth)
    dyc_own = swap(dy_send, "ffn", 1)
    dyc_oth = swap(dyo_send, "ffn", 1)
    dyc_all = reorder(down_order, dyc_own, dyc_oth)
    att_came, dyc_all, xn_core, att_core = tie((att_came, dyc_all, xn_core, att_core))
    hidden, hn_own = finish(place, x_own, att_own, att_came, w_out, gain_mlp)
    hn_oth = swap(hn_own, "ffn", 2)
    hnc_own = swap(hn_own, "ffn", 1)
    came_core = swap(after(hn_own, att_came)[0], "ffn", 1)

    *parts, dhn_own, down_own, dact0, dact1, dy_all = feed_own(
        down_order, hn_own, dy_own, dy_oth, gate_w, up_w, down_w
    )
    hn_oth, parts, dhn_own, down_own, dact0, dact1, dy_all, came_core, hnc_own = tie(
        (hn_oth, parts, dhn_own, down_own, dact0, dact1, dy_all, came_core, hnc_own)
    )
    hnc_oth = swap(hn_oth, "ffn", 1)
    act, gate, up, others, dhn_send, hn_all = feed_oth(
        ff_order, hn_own, hn_oth, (dact0, dact1), gate_w, up_w, parts
    )
    dhn_came = swap(dhn_send, "ffn", 2)
    others_core = swap(others, "ffn", 1)
    (hnc_oth,) = after(dhn_send, hnc_oth)
    hnc_all = reorder(ff_order, hnc_own, hnc_oth)

    down_send, down_kept = ff_grad(act, others_core, 0, dy_all, dyc_all)
    down_near = swap(down_send, "row", 1)
    gate_send, gate_kept = ff_grad(gate, others_core, 1, hn_all, hnc_all)
    up_send, up_kept = ff_grad(up, others_core, 2, hn_all, hnc_all)
    dhn_came, up_send, up_kept, gate_send, gate_kept, down_kept = tie(
        (dhn_came, up_send, up_kept, gate_send, gate_kept, down_kept)
    )

    grad_hidden, go_send, go_own, proj_away, proj_mine, gain_two = hidden_grad(
        att_order, place, dhn_own, dhn_came, hidden, dy_own, gain_mlp, w_out
    )
    go_oth = swap(go_send, "head", 1)
    proj_core = swap(proj_away, "ffn", 1)
    (gate_send,) = after(go_send, gate_send)
    gate_x = swap(gate_send, "head", 1)
    out_send, out_kept = bucket_grad(
        proj_mine, proj_core, (att_own, att_came), (att_core, came_core)
    )
    out_y = swap(out_send, "ffn", 2)
    go_oth, out_kept = tie((go_oth, out_kept))

    def backward(pairs, lse):
        return attend_backward(
            place, query, keys, mixed, lse, go_own, go_oth, att_own, att_oth, cosine, sine, pairs
        )

    pairs = HEADS // 4
    d_a, fa_own, fa_oth = backward((0, pairs // 2), log_sums)
    out_kept, down_kept = after(d_a, out_kept, down_kept)
    out_send, out_kept = bucket_near(row, out_kept, out_y)
    out_near = swap(out_send, "row", 1)
    down_send, down_kept = fold(down_kept, down_near)
    down_mid = swap(down_send, "row", 2)
    d_a, out_kept, down_kept, log_sums = tie((d_a, out_kept, down_kept, log_sums))
    core_a = swap(d_a, "ffn", 1)
    d_b, fb_own, fb_oth = backward((pairs // 2, pairs), log_sums)
    (gate_kept,) = after(d_b, gate_kept)
    gate_send, gate_kept = fold(gate_kept, gate_x)
    gate_near = swap(gate_send, "row", 1)
    d_b, gate_kept = tie((d_b, gate_kept))
    core_b = swap(d_b, "ffn", 1)
    up_x = swap(after(gate_kept, up_send)[0], "head", 1)
    back_send, share_own, gains = shares(
        d_a, d_b, fa_oth, fb_oth, qkv_w, x_own, x_oth, gain_two
    )
    gains_x = swap(gains, "head", 1)
    back_came = swap(back_send, "head", 1)
    d_a, core_a, core_b = after(back_send, d_a, core_a, core_b)
    y_send, kept = bucket_grad(xn_mine, xn_core, (d_a, d_b), (core_a, core_b))
    y_came = swap(y_send, "ffn", 2)
    gate_kept, out_kept, gains, act, others, down_kept = after(
        y_send, gate_kept, out_kept, gains, act, others, down_kept
    )
    gate_send, gate_kept = fold(gate_kept, gate_near)
    gate_far = swap(gate_send, "row", 2)
    out_send, out_kept = fold_rows(out_kept, out_near)
    out_far = swap(out_send, "row", 2)
    down_send, down_kept = fold(down_kept, down_mid)
    down_x = swap(down_send, "head", 1)
    units = w_down.shape[0]
    far_send = low(matmul(act[rows:], down_w[0]) + matmul(others[rows:span, :units], down_w[1]))
    up_kept, gains, gate_kept, out_kept = after(far_send, up_kept, gains, gate_kept, out_kept)
    up_send, up_kept = fold(up_kept, up_x)
    up_near = swap(up_send, "row", 1)
    gains = gains + gains_x
    gains = gains + swap(gains, "ffn", 1)
    gains_y = swap(gains, "ffn", 2)
    gains = gains + gains_y
    kept, up_kept, out_kept, gate_kept, down_kept = tie(
        (kept, up_kept, out_kept, gate_kept, down_kept)
    )
    far_send = after(gains, far_send)[0]
    far_came = swap(far_send, "ffn", 2)

    near_send, kept = bucket_near(row, kept, y_came, gains)
    near_came = swap(near_send, "row", 1)
    share_own, gate_kept, out_kept, up_kept = after(
        near_send, share_own, gate_kept, out_kept, up_kept
    )
    sum_gate = high(gate_kept) + high(gate_far)
    out_sum = high(out_kept) + high(out_far)
    out_x = swap(low(out_sum[:, out_cols:]), "head", 1)
    up_send, up_kept = fold(up_kept, up_near)
    up_far = swap(up_send, "row", 2)
    kept, sum_gate, out_sum, up_kept = tie((kept, sum_gate, out_sum, up_kept))
    far_send, kept = bucket_far(kept, near_came, near_send)
    qkv_far = swap(far_send, "row", 2)
    share_own, up_kept, down_kept, out_sum, residual = after(
        far_send, share_own, up_kept, down_kept, out_sum[:, :out_cols], hidden + down_own
    )
    grad_in, grad_first = input_grad(
        place, share_own, back_came, grad_hidden, x_own, gain_attn, fa_own, fb_own
    )
    sum_down = high(down_kept) + high(down_x)
    sum_up = high(up_kept) + high(up_far)
    out_sum = out_sum + high(out_x)
    output = low(residual + high(far_came))[None]
    kept, grad_in, sum_up, sum_down, out_sum, output = tie(
        (kept, grad_in, sum_up, sum_down, out_sum, output)
    )
    size = kept.shape[0]
    sum_qkv = high(kept) + high(qkv_far[:size])
    gains = high(far_send[size : size + 2, :width]) + high(qkv_far[size : size + 2, :width])
    return (
        output,
        grad_in[None],
        grad_first[None],
        gains[0],
        sum_qkv,
        out_sum.T,
        gains[1],
        sum_gate.T,
        sum_up.T,
        sum_down,
    )


def solution(mesh):
    in_specs = (
        P(("ffn", "row"), "head", None),
        P(("ffn", "row"), "head", None),
        P(("ffn", "row")),
        P(),
        P(),
        P(),
        P(),
        P(None, "ffn"),
        P(None, "ffn"),
        P("ffn", None),
        P(("ffn", "row"), "head", None),
    )
    out_specs = (
        P(("ffn", "row"), "head", None),
        P(("ffn", "row"), "head", None),
        P(("ffn", "row"), "head", None),
        P(),
        P(("ffn", "row"), "head"),
        P("head", ("ffn", "row")),
        P(),
        P(("head", "row"), "ffn"),
        P(("head", "row"), "ffn"),
        P("ffn", ("head", "row")),
    )
    body = two_groups if mesh.shape["head"] == 2 and mesh.shape["ffn"] == 4 else any_groups
    return jax.shard_map(
        body, mesh=mesh, in_specs=in_specs, out_specs=out_specs, check_vma=False
    )
```

```python
import functools

import jax
import jax.numpy as jnp
from jax import lax
from jax.experimental import pallas as pl
from jax.experimental.pallas import tpu as pltpu
from jax.sharding import PartitionSpec as P

HEADS = 16
HD = 64
MIN_LEN = 512
STEP = 256


eps = 1e-06


def rms_scale(values):
    return lax.rsqrt(jnp.mean(values * values, axis=-1, keepdims=True) + eps)


def matmul(left, right):
    return jnp.dot(left, right, preferred_element_type=jnp.float32)


def inner_rows(left, right):
    return lax.dot_general(
        left, right, (((0,), (0,)), ((), ())), preferred_element_type=jnp.float32
    )


def against(left, right):
    return lax.dot_general(
        left, right, (((1,), (1,)), ((), ())), preferred_element_type=jnp.float32
    )


def swap(values, axis, mask):
    size = lax.axis_size(axis)
    return lax.ppermute(values, axis, [(i, i ^ mask) for i in range(size)])


def bits_of(axis):
    size = lax.axis_size(axis)
    return [1 << b for b in range(size.bit_length() - 2, -1, -1)]


def halve(values, dim, axis, mask):
    bit = (lax.axis_index(axis) // mask) % 2
    away = lax.dynamic_index_in_dim(values, 1 - bit, dim, keepdims=False)
    kept = lax.dynamic_index_in_dim(values, bit, dim, keepdims=False)
    came = swap(away.astype(jnp.bfloat16), axis, mask)
    return kept.astype(jnp.float32) + came.astype(jnp.float32)


def total(values, axes):
    for axis in axes:
        for mask in reversed(bits_of(axis)):
            values = values + swap(values, axis, mask)
    return values


def rotary(positions, head_size):
    half_size = head_size // 2
    inverse = jnp.exp(
        -jnp.log(10000.0) * jnp.arange(half_size, dtype=jnp.float32) * 2.0 / head_size
    )
    angles = positions.astype(jnp.float32)[:, None] * inverse[None, :]
    return (jnp.cos(angles), jnp.sin(angles))


def rotate(vectors, cosine, sine, sign):
    half_size = vectors.shape[-1] // 2
    first_half = vectors[..., :half_size]
    second_half = vectors[..., half_size:]
    cos_rows = cosine[:, None, :]
    sin_rows = sign * sine[:, None, :]
    return jnp.concatenate(
        [
            first_half * cos_rows - second_half * sin_rows,
            second_half * cos_rows + first_half * sin_rows,
        ],
        axis=-1,
    )


def masked_scores(q_rows, keys, q_pos, k_pos, valid):
    raw = jnp.einsum("qhe,khe->hqk", q_rows, keys, preferred_element_type=jnp.float32)
    allowed = (k_pos[None, :] <= q_pos[:, None]) & (k_pos[None, :] < valid)
    return jnp.where(allowed[None], 0.125 * raw, -1e30)


def scan_forward(query, keys, mixed, positions, valid, block_rows):
    count = query.shape[0] // block_rows

    def step(carry, index):
        start = index * block_rows
        q_rows = lax.dynamic_slice_in_dim(query, start, block_rows, 0)
        q_pos = lax.dynamic_slice_in_dim(positions, start, block_rows, 0)
        scores = masked_scores(q_rows, keys, q_pos, positions, valid)
        top = jnp.max(scores, axis=-1, keepdims=True)
        expo = jnp.exp(scores - top)
        total_w = jnp.sum(expo, axis=-1, keepdims=True)
        weights = expo / total_w
        result = jnp.einsum(
            "hqk,khe->qhe", weights.astype(jnp.bfloat16), mixed, preferred_element_type=jnp.float32
        )
        return (carry, (result.astype(jnp.bfloat16), top + jnp.log(total_w)))

    _, (outs, log_sums) = lax.scan(step, 0, jnp.arange(count, dtype=jnp.int32))
    return (outs.reshape(query.shape), log_sums)


def scan_backward(query, keys, mixed, positions, valid, log_sums, grad_out, block_rows):
    count = query.shape[0] // block_rows
    zeros = jnp.zeros(keys.shape, jnp.float32)

    def step(carry, index):
        key_sum, value_sum = carry
        start = index * block_rows
        q_rows = lax.dynamic_slice_in_dim(query, start, block_rows, 0)
        q_pos = lax.dynamic_slice_in_dim(positions, start, block_rows, 0)
        g_rows = lax.dynamic_slice_in_dim(grad_out, start, block_rows, 0)
        scores = masked_scores(q_rows, keys, q_pos, positions, valid)
        weights = jnp.exp(scores - log_sums[index])
        grad_w = jnp.einsum("qhe,khe->hqk", g_rows, mixed, preferred_element_type=jnp.float32)
        delta = jnp.sum(weights * grad_w, axis=-1, keepdims=True)
        grad_s = (weights * (grad_w - delta)).astype(jnp.bfloat16)
        grad_q = 0.125 * jnp.einsum(
            "hqk,khe->qhe", grad_s, keys, preferred_element_type=jnp.float32
        )
        key_sum = key_sum + 0.125 * jnp.einsum(
            "hqk,qhe->khe", grad_s, q_rows, preferred_element_type=jnp.float32
        )
        value_sum = value_sum + jnp.einsum(
            "hqk,qhe->khe", weights.astype(jnp.bfloat16), g_rows, preferred_element_type=jnp.float32
        )
        return ((key_sum, value_sum), grad_q)

    (grad_keys, grad_mixed), grad_query = lax.scan(
        step, (zeros, zeros), jnp.arange(count, dtype=jnp.int32)
    )
    return (grad_query.reshape(query.shape), grad_keys, grad_mixed)


def any_groups(
    inputs,
    first_values,
    lengths,
    gain_attn,
    w_qkv,
    w_out,
    gain_mlp,
    w_gate,
    w_up,
    w_down,
    cotangent,
):
    rows = inputs.shape[1]
    width = inputs.shape[2]
    groups = lax.axis_size("head")
    shards = lax.axis_size("ffn")
    heads_here = HEADS // groups
    span_rows = rows * groups
    block_rows = span_rows // max(1, span_rows // 512)
    head_pos = lax.axis_index("head")
    valid_len = lengths[0]
    packed_cols = heads_here * 3 * HD
    out_cols = heads_here * HD
    hidden_here = w_gate.shape[1]

    owners = [head_pos ^ m for m in range(groups)]
    x_all = [inputs[0]] + [swap(inputs[0], "head", m) for m in range(1, groups)]
    early = []
    for m in range(groups):
        piece = lax.dynamic_slice_in_dim(first_values[0], owners[m] * out_cols, out_cols, 1)
        early.append(swap(piece, "head", m) if m else piece)
    far = range(2, shards, 2)
    grad_rows = jnp.concatenate([cotangent[0]] + [swap(cotangent[0], "ffn", m) for m in far], 0)
    gate_w = jnp.concatenate([w_gate, swap(w_gate, "ffn", 1)], 1)
    up_w = jnp.concatenate([w_up, swap(w_up, "ffn", 1)], 1)
    down_w = jnp.concatenate([w_down, swap(w_down, "ffn", 1)], 0)
    w_heads = lax.dynamic_slice_in_dim(w_qkv, head_pos * packed_cols, packed_cols, 1)
    out_w = jnp.concatenate(
        [lax.dynamic_slice_in_dim(w_out, o * out_cols, out_cols, 0) for o in owners], 0
    )

    positions = jnp.concatenate([o * rows + jnp.arange(rows, dtype=jnp.int32) for o in owners])
    cosine, sine = rotary(positions, HD)
    normed, scaled, queries, key_list, mixes = [], [], [], [], []
    rows_in = inputs[0].astype(jnp.float32)
    scale_one = rms_scale(rows_in)
    for m in range(groups):
        block = x_all[m].astype(jnp.float32)
        scale = rms_scale(block)
        scaled.append(block * scale)
        normed.append((block * scale * gain_attn).astype(jnp.bfloat16))
        packed = matmul(normed[m], w_heads).astype(jnp.bfloat16)
        packed = packed.reshape(rows, heads_here, 3, HD).astype(jnp.float32)
        part = slice(m * rows, (m + 1) * rows)
        queries.append(rotate(packed[:, :, 0], cosine[part], sine[part], 1.0))
        key_list.append(rotate(packed[:, :, 1], cosine[part], sine[part], 1.0))
        value = early[m].reshape(rows, heads_here, HD).astype(jnp.float32)
        mixes.append(0.5 * (packed[:, :, 2] + value))
    query = jnp.concatenate(queries, 0).astype(jnp.bfloat16)
    keys = jnp.concatenate(key_list, 0).astype(jnp.bfloat16)
    mixed = jnp.concatenate(mixes, 0).astype(jnp.bfloat16)
    attended, log_sums = scan_forward(query, keys, mixed, positions, valid_len, block_rows)
    attended = attended.reshape(groups, rows, out_cols)
    att_own = jnp.concatenate(
        [attended[0]] + [swap(attended[m], "head", m) for m in range(1, groups)], 1
    )
    hidden = rows_in + matmul(att_own, out_w)
    scale_two = rms_scale(hidden)
    normed_two = (hidden * scale_two * gain_mlp).astype(jnp.bfloat16)

    mlp_rows = [normed_two] + [swap(normed_two, "ffn", m) for m in far]
    grad_list = [grad_rows[i * rows : (i + 1) * rows] for i in range(len(mlp_rows))]
    actives, grad_gates, grad_ups, downs, grad_normed_list = [], [], [], [], []
    for i, block in enumerate(mlp_rows):
        gate_rows = matmul(block, gate_w)
        up_rows = matmul(block, up_w)
        sigmoid_gate = jax.nn.sigmoid(gate_rows)
        silu_gate = gate_rows * sigmoid_gate
        grad_active = against(grad_list[i], down_w)
        actives.append((silu_gate * up_rows).astype(jnp.bfloat16))
        grad_gates.append(
            (
                grad_active * up_rows * sigmoid_gate * (1.0 + gate_rows * (1.0 - sigmoid_gate))
            ).astype(jnp.bfloat16)
        )
        grad_ups.append((grad_active * silu_gate).astype(jnp.bfloat16))
        grad_normed_list.append(against(grad_gates[i], gate_w) + against(grad_ups[i], up_w))
        downs.append(matmul(actives[i], down_w))
    grad_normed_two = grad_normed_list[0]
    for i, m in enumerate(far):
        came = swap(grad_normed_list[i + 1].astype(jnp.bfloat16), "ffn", m)
        grad_normed_two = grad_normed_two + came.astype(jnp.float32)
    down_rows = downs[0]
    for i, m in enumerate(far):
        down_rows = down_rows + swap(downs[i + 1].astype(jnp.bfloat16), "ffn", m).astype(jnp.float32)
    output = (hidden + down_rows).astype(jnp.bfloat16)[None]

    all_rows = jnp.concatenate(mlp_rows, 0)
    ff_sums = []
    for left, right in (
        (grad_rows, jnp.concatenate(actives, 0)),
        (all_rows, jnp.concatenate(grad_gates, 0)),
        (all_rows, jnp.concatenate(grad_ups, 0)),
    ):
        away = inner_rows(left, right[:, hidden_here:]).astype(jnp.bfloat16)
        part = inner_rows(left, right[:, :hidden_here])
        part = (part + swap(away, "ffn", 1).astype(jnp.float32)).astype(jnp.bfloat16)
        steps = [("head", b) for b in bits_of("head")] + [("row", b) for b in bits_of("row")]
        part = part.reshape([2] * len(steps) + [-1, hidden_here])
        order = [s for s in steps if s[0] == "head"] + [s for s in reversed(steps) if s[0] == "row"]
        left_steps = list(steps)
        for s in order:
            part = halve(part, left_steps.index(s), *s)
            left_steps.remove(s)
            if left_steps:
                part = part.astype(jnp.bfloat16)
        ff_sums.append(part)
    sum_down, sum_gate, sum_up = ff_sums

    grad_y = cotangent[0].astype(jnp.float32)
    grad_gain_two = jnp.sum(grad_normed_two * hidden * scale_two, axis=0)
    weighted_two = grad_normed_two * gain_mlp
    cube_two = scale_two * scale_two * scale_two
    grad_hidden = (
        grad_y
        + scale_two * weighted_two
        - hidden * cube_two * jnp.mean(weighted_two * hidden, axis=-1, keepdims=True)
    )
    grad_proj = grad_hidden.astype(jnp.bfloat16)
    grad_att = against(grad_proj, out_w).astype(jnp.bfloat16)
    grad_att = jnp.concatenate(
        [
            swap(grad_att[:, m * out_cols : (m + 1) * out_cols], "head", m)
            if m
            else grad_att[:, :out_cols]
            for m in range(groups)
        ],
        0,
    ).reshape(span_rows, heads_here, HD)

    def over_buckets(part):
        steps = [("ffn", b) for b in bits_of("ffn")] + [("row", b) for b in bits_of("row")]
        part = part.astype(jnp.bfloat16).reshape([2] * len(steps) + [-1, part.shape[1]])
        order = [s for s in reversed(steps) if s[0] == "ffn"] + [
            s for s in reversed(steps) if s[0] == "row"
        ]
        left_steps = list(steps)
        for s in order:
            part = halve(part, left_steps.index(s), *s)
            left_steps.remove(s)
            if left_steps:
                part = part.astype(jnp.bfloat16)
        return part

    part = over_buckets(inner_rows(grad_proj, att_own))
    sum_out = part[:, :out_cols]
    for m in range(1, groups):
        came = swap(part[:, m * out_cols : (m + 1) * out_cols].astype(jnp.bfloat16), "head", m)
        sum_out = sum_out + came.astype(jnp.float32)

    grad_query, grad_keys, grad_mixed = scan_backward(
        query, keys, mixed, positions, valid_len, log_sums, grad_att, block_rows
    )
    grad_packed = jnp.stack(
        [
            rotate(grad_query, cosine, sine, -1.0),
            rotate(grad_keys, cosine, sine, -1.0),
            0.5 * grad_mixed,
        ],
        axis=2,
    )
    grad_packed = grad_packed.astype(jnp.bfloat16).reshape(span_rows, packed_cols)
    grad_early = (0.5 * grad_mixed).astype(jnp.bfloat16).reshape(span_rows, out_cols)
    firsts = [grad_early[m * rows : (m + 1) * rows] for m in range(groups)]
    firsts = [swap(firsts[m], "head", m) if m else firsts[0] for m in range(groups)]
    grad_first = jnp.zeros((rows, width), jnp.bfloat16)
    for m in range(groups):
        grad_first = lax.dynamic_update_slice_in_dim(grad_first, firsts[m], owners[m] * out_cols, 1)
    shares = [
        against(grad_packed[m * rows : (m + 1) * rows], w_heads) for m in range(groups)
    ]
    grad_gain_one = sum(jnp.sum(shares[m] * scaled[m], axis=0) for m in range(groups))
    grad_normed = shares[0]
    for m in range(1, groups):
        grad_normed = grad_normed + swap(shares[m].astype(jnp.bfloat16), "head", m).astype(jnp.float32)
    sum_qkv = over_buckets(inner_rows(jnp.concatenate(normed, 0), grad_packed))
    weighted_one = grad_normed * gain_attn
    cube_one = scale_one * scale_one * scale_one
    grad_in = (
        grad_hidden
        + scale_one * weighted_one
        - rows_in * cube_one * jnp.mean(weighted_one * rows_in, axis=-1, keepdims=True)
    )
    gains = total(jnp.stack([grad_gain_one, grad_gain_two]), ("ffn", "head", "row"))
    return (
        output,
        grad_in[None],
        grad_first[None],
        gains[0],
        sum_qkv,
        sum_out.T,
        gains[1],
        sum_gate,
        sum_up,
        sum_down.T,
    )


SCALE = 4.5e8
COSTS = {}
SITES = {}


def site_cost(name, usual):
    count = SITES.get(name, 0)
    SITES[name] = count + 1
    return int(SCALE * COSTS.get(name + str(count), usual))


def low(values):
    return values.astype(jnp.bfloat16)


def high(values):
    return values.astype(jnp.float32)


def on_chip(body, outs, scalars, arrays, name, scratch=(), aliases=None, limit=3, cost=1.0, away=()):
    inside = pl.BlockSpec(memory_space=pltpu.VMEM)
    return pl.pallas_call(
        body,
        out_shape=outs,
        in_specs=[pl.BlockSpec(memory_space=pltpu.SMEM)] * len(scalars) + [inside] * len(arrays),
        out_specs=jax.tree.unflatten(
            jax.tree.structure(outs),
            [
                pl.BlockSpec(memory_space=pltpu.HBM) if i in away else inside
                for i in range(len(jax.tree.leaves(outs)))
            ],
        ),
        scratch_shapes=list(scratch),
        input_output_aliases=aliases or {},
        cost_estimate=pl.CostEstimate(
            flops=site_cost(name, cost), transcendentals=0, bytes_accessed=1
        ),
        compiler_params=pltpu.CompilerParams(vmem_limit_bytes=limit << 20),
        name=name,
    )(*scalars, *arrays)


def shape16(*dims):
    return jax.ShapeDtypeStruct(dims, jnp.bfloat16)


def shape32(*dims):
    return jax.ShapeDtypeStruct(dims, jnp.float32)


def spans(total):
    return [(a, min(a + STEP, total)) for a in range(0, total, STEP)]


def turn(values):
    lane = lax.broadcasted_iota(jnp.int32, values.shape, 1)
    return jnp.where(
        lane % HD < HD // 2, pltpu.roll(values, 2 * HD - HD // 2, 1), pltpu.roll(values, HD // 2, 1)
    )


def allowed_keys(a, b, valid):
    size = b - a
    down = lax.broadcasted_iota(jnp.int32, (size, size), 0)
    across = lax.broadcasted_iota(jnp.int32, (size, size), 1)
    allowed = down <= across
    if b > MIN_LEN:
        allowed = allowed & (down < valid - a)
    return allowed


def columns(index, size):
    return pl.ds(pl.multiple_of(index * size, size), size)


def forward_body(
    place, packed_own, packed_oth, early_own, early_oth, cos_ref, sin_ref,
    att_own, att_oth, q_far, k_far, v_far, lse_out, q_out, k_out, v_out, flipped, att, sems,
):
    rows = packed_own.shape[0]
    span = 2 * rows
    wide = 2 * HD
    valid = place[1]
    f32 = jnp.float32
    bf = jnp.bfloat16
    first = lax.broadcasted_iota(jnp.int32, (1, wide), 1) < HD
    flipped[:, HD:, :] = jnp.ones((2, 16, span), bf)

    def copies(p):
        cols = columns(p, wide)
        return [
            pltpu.make_async_copy(near.at[:, cols], far.at[:, cols], sems.at[i, p])
            for i, (near, far) in enumerate(((q_out, q_far), (k_out, k_far), (v_out, v_far)))
        ]

    def pair(p, _):
        cols = columns(p, wide)
        for m, (packed, early) in enumerate(((packed_own, early_own), (packed_oth, early_oth))):
            here = columns(place[0] ^ m, rows)
            x0 = high(packed[:, pl.ds(pl.multiple_of(p * 3 * wide, wide), wide)])
            x1 = high(packed[:, pl.ds(pl.multiple_of(p * 3 * wide + wide, wide), wide)])
            x2 = high(packed[:, pl.ds(pl.multiple_of(p * 3 * wide + 2 * wide, wide), wide)])
            cosine = cos_ref[here, :]
            sine = sin_ref[here, :]
            q = jnp.where(first, x0, x1)
            k = pltpu.roll(jnp.where(first, x2, x0), HD, 1)
            v = jnp.where(first, x1, x2)
            q_out[here, cols] = low(q * cosine + turn(q) * sine)
            k_out[here, cols] = low(k * cosine + turn(k) * sine)
            v_out[here, cols] = low(0.5 * (v + high(early[:, cols])))
        for copy in copies(p):
            copy.start()
        turned = v_out[:, cols].T
        for e in range(2):
            flipped[e, :HD, :] = turned[e * HD : (e + 1) * HD, :]
        for a, b in spans(span):
            q = q_out[a:b, cols] * jnp.asarray(0.125, bf)
            allowed = allowed_keys(a, b, valid)
            for e in range(2):
                qe = jnp.where(first == (e == 0), q, jnp.zeros_like(q))
                diag = jnp.where(allowed, against(k_out[a:b, cols], qe), -1e30)
                top = jnp.max(diag, axis=0, keepdims=True)
                if a:
                    past = against(k_out[:a, cols], qe)
                    top = jnp.maximum(top, jnp.max(past, axis=0, keepdims=True))
                out = matmul(flipped[e, :, a:b], low(jnp.exp(diag - top)))
                if a:
                    out = out + matmul(flipped[e, :, :a], low(jnp.exp(past - top)))
                amount = out[HD : HD + 1, :]
                att[e * HD : (e + 1) * HD, a:b] = out[:HD, :] / amount
                lse_out[p, e : e + 1, a:b] = top + jnp.log(amount)
        result = low(att[...].T)
        upper = place[0] == 0
        att_own[:, cols] = jnp.where(upper, result[:rows, :], result[rows:, :])
        att_oth[:, cols] = jnp.where(upper, result[rows:, :], result[:rows, :])
        return 0

    lax.fori_loop(0, lse_out.shape[0], pair, 0)
    for p in range(lse_out.shape[0]):
        for copy in copies(p):
            copy.wait()


def attend_forward(place, packed_own, packed_oth, early_own, early_oth, cosine, sine):
    rows, cols = packed_own.shape
    heads = cols // (3 * HD)
    span = 2 * rows
    out = shape16(rows, heads * HD)
    natural = shape16(span, heads * HD)
    return on_chip(
        forward_body,
        (out, out, natural, natural, natural, shape32(heads // 2, 2, span)),
        (place,),
        (packed_own, packed_oth, early_own, early_oth, cosine, sine),
        "attend_forward",
        cost=11.0,
        limit=6,
        away=(2, 3, 4),
        scratch=(
            pltpu.VMEM(natural.shape, jnp.bfloat16),
            pltpu.VMEM(natural.shape, jnp.bfloat16),
            pltpu.VMEM(natural.shape, jnp.bfloat16),
            pltpu.VMEM((2, HD + 16, span), jnp.bfloat16),
            pltpu.VMEM((2 * HD, span), jnp.float32),
            pltpu.SemaphoreType.DMA((3, heads // 2)),
        ),
    )


def backward_body(
    start, place, q_ref, k_ref, v_ref, lse_ref, go_own, go_oth, att_own, att_oth, cos_ref, sin_ref,
    d_out, f_own, f_oth, grad, prod, turned_k, dq, dk, dv,
):
    rows = go_own.shape[0]
    span = 2 * rows
    valid = place[1]
    wide = 2 * HD
    bf = jnp.bfloat16
    first = lax.broadcasted_iota(jnp.int32, (1, wide), 1) < HD
    eighth = jnp.asarray(0.125, bf)

    def pair(i, _):
        p = i + start
        cols = columns(p, wide)
        for m, (go, att) in enumerate(((go_own, att_own), (go_oth, att_oth))):
            here = columns(place[0] ^ m, rows)
            grad[here, :] = go[:, cols]
            prod[here, :] = high(go[:, cols]) * high(att[:, cols])
        flat = prod[...].T
        deltas = [jnp.sum(flat[e * HD : (e + 1) * HD, :], axis=0, keepdims=True) for e in range(2)]
        turned_k[...] = (k_ref[:, cols] * eighth).T
        for n, (a, b) in enumerate(spans(span)):
            allowed = allowed_keys(a, b, valid)
            q = q_ref[a:b, cols] * eighth
            g = grad[a:b, :]
            parts = ((a, b), (0, a)) if a else ((a, b),)
            sums = {}
            for e in range(2):
                mine = first == (e == 0)
                qe = jnp.where(mine, q, jnp.zeros_like(q))
                ge = jnp.where(mine, g, jnp.zeros_like(g))
                for lo, hi in parts:
                    scores = against(k_ref[lo:hi, cols], qe)
                    if lo == a:
                        scores = jnp.where(allowed, scores, -1e30)
                    weights = jnp.exp(scores - lse_ref[p, e : e + 1, a:b])
                    grad_w = against(v_ref[lo:hi, cols], ge)
                    grad_s = low(weights * (grad_w - deltas[e][:, a:b]))
                    dv_here = matmul(low(weights), ge)
                    dk_here = matmul(grad_s, qe)
                    dq_here = matmul(turned_k[e * HD : (e + 1) * HD, lo:hi], grad_s)
                    if (lo, "v") in sums:
                        dv_here = dv_here + sums[lo, "v"]
                        dk_here = dk_here + sums[lo, "k"]
                    sums[lo, "v"], sums[lo, "k"] = dv_here, dk_here
                    sums[lo, e] = dq_here
            for e in range(2):
                dq[e * HD : (e + 1) * HD, a:b] = sums[a, e] + sums[0, e] if a else sums[a, e]
            dv[a:b, :] = sums[a, "v"]
            dk[a:b, :] = sums[a, "k"]
            if a:
                dv[:a, :] += sums[0, "v"]
                dk[:a, :] += sums[0, "k"]
        prod[...] = dq[...].T
        for m, f_out in enumerate((f_own, f_oth)):
            here = columns(place[0] ^ m, rows)
            cosine = cos_ref[here, :]
            sine = sin_ref[here, :]
            gv = low(0.5 * dv[here, :])
            gk = dk[here, :]
            gk = low(pltpu.roll(gk * cosine - turn(gk) * sine, HD, 1))
            gq = prod[here, :]
            gq = low(gq * cosine - turn(gq) * sine)
            part = slice(m * rows, (m + 1) * rows)
            base = i * 3 * wide
            d_out[part, pl.ds(pl.multiple_of(base, wide), wide)] = jnp.where(first, gq, gk)
            d_out[part, pl.ds(pl.multiple_of(base + wide, wide), wide)] = jnp.where(first, gv, gq)
            d_out[part, pl.ds(pl.multiple_of(base + 2 * wide, wide), wide)] = jnp.where(first, gk, gv)
            f_out[:, columns(i, wide)] = gv
        return 0

    lax.fori_loop(0, f_own.shape[1] // wide, pair, 0)


def attend_backward(place, q, k, v, lse, go_own, go_oth, att_own, att_oth, cosine, sine, pairs):
    span = q.shape[0]
    rows = span // 2
    wide = 2 * HD
    cols = wide * (pairs[1] - pairs[0])
    return on_chip(
        functools.partial(backward_body, pairs[0]),
        (shape16(span, 3 * cols), shape16(rows, cols), shape16(rows, cols)),
        (place,),
        (q, k, v, lse, go_own, go_oth, att_own, att_oth, cosine, sine),
        "attend_backward",
        cost=7.5,
        limit=4,
        scratch=(
            pltpu.VMEM((span, wide), jnp.bfloat16),
            pltpu.VMEM((span, wide), jnp.float32),
            pltpu.VMEM((wide, span), jnp.bfloat16),
            pltpu.VMEM((wide, span), jnp.float32),
            pltpu.VMEM((span, wide), jnp.float32),
            pltpu.VMEM((span, wide), jnp.float32),
        ),
    )


def project_body(base, order, x_ref, gain_ref, w_ref, *refs):
    away_far, mine_far, packed_ref, xn, away, mine, sems = refs[-7:]
    rows = x_ref.shape[0]
    x = high(x_ref[...])
    xn[...] = low(x * rms_scale(x) * gain_ref[...])
    arrange_halves(order, (xn,), away, mine)
    there = slice(base, base + rows)
    copies = [
        pltpu.make_async_copy(away, away_far.at[there, :], sems.at[0]),
        pltpu.make_async_copy(mine, mine_far.at[there, :], sems.at[1]),
    ]
    for copy in copies:
        copy.start()
    cols = w_ref.shape[1] // 3
    for i in range(3):
        part = slice(i * cols, (i + 1) * cols)
        packed_ref[:, part] = low(matmul(xn[...], w_ref[:, part]))
    for copy in copies:
        copy.wait()


def project(order, x, gain, w, before=()):
    rows, width = x.shape
    part = shape16(2 * rows, width // 2)
    return pl.pallas_call(
        functools.partial(project_body, rows if before else 0),
        out_shape=(part, part, shape16(rows, w.shape[1])),
        in_specs=[pl.BlockSpec(memory_space=pltpu.SMEM)]
        + [pl.BlockSpec(memory_space=pltpu.VMEM)] * 3
        + [pl.BlockSpec(memory_space=pltpu.HBM)] * len(before),
        out_specs=(
            pl.BlockSpec(memory_space=pltpu.HBM),
            pl.BlockSpec(memory_space=pltpu.HBM),
            pl.BlockSpec(memory_space=pltpu.VMEM),
        ),
        scratch_shapes=[
            pltpu.VMEM((rows, width), jnp.bfloat16),
            pltpu.VMEM((rows, width // 2), jnp.bfloat16),
            pltpu.VMEM((rows, width // 2), jnp.bfloat16),
            pltpu.SemaphoreType.DMA((2,)),
        ],
        input_output_aliases={4 + i: i for i in range(len(before))},
        cost_estimate=pl.CostEstimate(
            flops=site_cost("project", 2.0), transcendentals=0, bytes_accessed=1
        ),
        compiler_params=pltpu.CompilerParams(vmem_limit_bytes=5 << 20),
        name="project",
    )(order, x, gain, w, *before)


def arrange(order, blocks, out):
    rows = blocks[0].shape[0]
    size = out.shape[1] // order.shape[0]
    for i in range(order.shape[0]):
        for b, block in enumerate(blocks):
            out[b * rows : (b + 1) * rows, i * size : (i + 1) * size] = block[:, columns(order[i], size)]


def finish(place, x, att_own, att_came, w, gain):
    def body(place, x_ref, att_own, att_came, w_ref, gain_ref, hidden_far, hn_ref, hidden_ref, sem):
        cols = att_own.shape[1]
        hidden = high(x_ref[...]) + matmul(att_own[...], w_ref[columns(place[0], cols), :])
        hidden = hidden + matmul(att_came[...], w_ref[columns(1 - place[0], cols), :])
        hidden_ref[...] = hidden
        copy = pltpu.make_async_copy(hidden_ref, hidden_far, sem.at[0])
        copy.start()
        hn_ref[...] = low(hidden * rms_scale(hidden) * gain_ref[...])
        copy.wait()

    return on_chip(
        body,
        (shape32(*x.shape), shape16(*x.shape)),
        (place,),
        (x, att_own, att_came, w, gain),
        "finish",
        cost=3.0,
        limit=5,
        away=(0,),
        scratch=(pltpu.VMEM(x.shape, jnp.float32), pltpu.SemaphoreType.DMA((1,))),
    )


def reorder(order, *blocks):
    rows, cols = blocks[0].shape

    def body(order, *refs):
        arrange(order, refs[:-1], refs[-1])

    return on_chip(body, shape16(rows * len(blocks), cols), (order,), blocks, "reorder", cost=0.9)


def arrange_halves(order, blocks, away, mine):
    rows = blocks[0].shape[0]
    count = order.shape[0] // 2
    size = mine.shape[1] // count
    for half, out in enumerate((away, mine)):
        for i in range(count):
            for b, block in enumerate(blocks):
                out[b * rows : (b + 1) * rows, i * size : (i + 1) * size] = block[
                    :, columns(order[half * count + i], size)
                ]


def reorder_halves(order, *blocks):
    rows, cols = blocks[0].shape

    def body(order, *refs):
        arrange_halves(order, refs[:-2], *refs[-2:])

    part = shape16(rows * len(blocks), cols // 2)
    return on_chip(body, (part, part), (order,), blocks, "reorder_halves", cost=0.9)


def feed_rows(hn, grads, gate_w, up_w, mine, other, base):
    rows = hn.shape[0]
    units = gate_w[0].shape[0]
    here = slice(base, base + rows)
    total_hn = None
    for s in range(2):
        gate = against(hn[...], gate_w[s][...])
        up = against(hn[...], up_w[s][...])
        grad = high(grads[s][...])
        sig = 1.0 / (1.0 + jnp.exp(-gate))
        silu = gate * sig
        results = (silu * up, grad * up * sig * (1.0 + gate * (1.0 - sig)), grad * silu)
        for i, result in enumerate(results):
            if s == 0:
                mine[i][here, :] = low(result)
            else:
                other[2 * i * rows + base : 2 * i * rows + base + rows, :units] = low(result)
    for s in range(2):
        for i, w in ((1, gate_w[s]), (2, up_w[s])):
            if s == 0:
                share = matmul(mine[i][here, :], w[...])
            else:
                share = matmul(other[2 * i * rows + base : 2 * i * rows + base + rows, :units], w[...])
            total_hn = share if total_hn is None else total_hn + share
    return total_hn


def feed_own_body(order, hn, dy_own, dy_oth, wg0, wg1, wu0, wu1, wd0, wd1, *refs):
    rows = hn.shape[0]
    outs, grads = refs[:9], refs[9:]
    mine, other, dhn, down = outs[:3], outs[3], outs[4], outs[5]
    for grad, w in zip(grads, (wd0, wd1)):
        grad[...] = low(against(dy_own[...], w[...]))
    dhn[...] = feed_rows(hn, grads, (wg0, wg1), (wu0, wu1), mine, other, 0)
    down[...] = matmul(mine[0][:rows, :], wd0[...]) + matmul(other[:rows, : wd1.shape[0]], wd1[...])
    for grad, w in zip(outs[6:8], (wd0, wd1)):
        grad[...] = low(against(dy_oth[...], w[...]))
    arrange(order, (dy_own, dy_oth), outs[8])


def feed_oth_body(order, hn_own, hn, g0, g1, wg0, wg1, wu0, wu1, *refs):
    outs = refs[4:]
    outs[4][...] = low(
        feed_rows(hn, (g0, g1), (wg0, wg1), (wu0, wu1), outs[:3], outs[3], hn.shape[0])
    )
    arrange(order, (hn_own, hn), outs[5])


def feed_own(order, hn, dy_own, dy_oth, gate_w, up_w, down_w):
    rows, width = hn.shape
    units = gate_w[0].shape[0]
    part = shape16(2 * rows, units)
    other = shape16(6 * rows, -(-units // 128) * 128)
    return on_chip(
        feed_own_body,
        (part,) * 3
        + (other,)
        + (shape32(rows, width),) * 2
        + (shape16(rows, units),) * 2
        + (shape16(2 * rows, width),),
        (order,),
        (hn, dy_own, dy_oth, *gate_w, *up_w, *down_w),
        "feed_own",
        limit=15,
        cost=11.0,
        scratch=(pltpu.VMEM((rows, units), jnp.bfloat16),) * 2,
    )


def feed_oth(order, hn_own, hn, grads, gate_w, up_w, parts):
    rows, width = hn.shape
    return on_chip(
        feed_oth_body,
        tuple(shape16(*part.shape) for part in parts)
        + (shape16(rows, width), shape16(2 * rows, width)),
        (order,),
        (hn_own, hn, *grads, *gate_w, *up_w, *parts),
        "feed_oth",
        aliases={9 + i: i for i in range(4)},
        limit=14,
        cost=7.0,
    )


def ff_grad(left, left_core, index, right, right_core):
    rows, units = left.shape
    mid = right.shape[1] // 2

    def body(left, left_core, right, right_core, away, kept):
        for i, out in enumerate((away, kept)):
            part = slice(i * mid, (i + 1) * mid)
            out[...] = low(
                inner_rows(left[...], right[:, part])
                + inner_rows(left_core[index * rows : (index + 1) * rows, :units], right_core[:, part])
            )

    part = shape16(units, mid)
    return on_chip(body, (part, part), (), (left, left_core, right, right_core), "ff_grad", cost=2.7)


def fold(kept, came):
    mid = kept.shape[1] // 2

    def body(kept, came, away, rest):
        away[...] = low(high(kept[:, :mid]) + high(came[:, :mid]))
        rest[...] = low(high(kept[:, mid:]) + high(came[:, mid:]))

    part = shape16(kept.shape[0], mid)
    return on_chip(body, (part, part), (), (kept, came), "fold", cost=0.3)


def fold_rows(kept, came):
    mid = kept.shape[0] // 2

    def body(kept, came, away, rest):
        away[...] = low(high(kept[:mid, :]) + high(came[:mid, :]))
        rest[...] = low(high(kept[mid:, :]) + high(came[mid:, :]))

    part = shape16(mid, kept.shape[1])
    return on_chip(body, (part, part), (), (kept, came), "fold_rows", cost=0.3)


def hidden_grad_body(order, place, dhn_own, dhn_came, hidden_ref, dy_ref, gain_ref, w_ref, grad_ref, send_ref, own_ref, away_ref, mine_ref, gains_ref, proj):
    hidden = hidden_ref[...]
    scale = rms_scale(hidden)
    dhn = dhn_own[...] + high(dhn_came[...])
    gains_ref[...] = jnp.sum(dhn * hidden * scale, axis=0, keepdims=True)
    weighted = dhn * gain_ref[...]
    mean = jnp.mean(weighted * hidden, axis=-1, keepdims=True)
    grad = high(dy_ref[...]) + scale * weighted - hidden * (scale * scale * scale * mean)
    grad_ref[...] = grad
    proj[...] = low(grad)
    cols = send_ref.shape[1]
    send_ref[...] = low(against(proj[...], w_ref[columns(1 - place[0], cols), :]))
    own_ref[...] = low(against(proj[...], w_ref[columns(place[0], cols), :]))
    arrange_halves(order, (proj,), away_ref, mine_ref)


def hidden_grad(order, place, dhn_own, dhn_came, hidden, dy, gain, w):
    rows, width = hidden.shape
    part = shape16(rows, width // 2)
    return on_chip(
        hidden_grad_body,
        (shape32(rows, width), part, part, part, part, shape32(1, width)),
        (order, place),
        (dhn_own, dhn_came, hidden, dy, gain, w),
        "hidden_grad",
        cost=2.2,
        limit=6,
        scratch=(pltpu.VMEM((rows, width), jnp.bfloat16),),
    )


def bucket_grad(left, left_core, rights, rights_core, place=0, total_cols=None, before=()):
    mid = left.shape[1] // 2
    cols = rights[0].shape[1]
    count = len(rights)

    def body(left, left_core, *refs):
        for i in range(count):
            part = slice(place + i * cols, place + (i + 1) * cols)
            for half, out in enumerate(refs[-2:]):
                cut = slice(half * mid, (half + 1) * mid)
                out[:, part] = low(
                    inner_rows(left[:, cut], refs[i][...])
                    + inner_rows(left_core[:, cut], refs[count + i][...])
                )

    full = shape16(mid, total_cols or cols * count)
    return on_chip(
        body,
        (full, full),
        (),
        (left, left_core, *rights, *rights_core, *before),
        "bucket_grad",
        aliases={2 + 2 * count + i: i for i in range(len(before))},
        cost=1.5,
    )


def bucket_near(row, kept, came):
    quarter, cols = kept.shape
    size = quarter // 4

    def body(row, kept, came, away, rest):
        near = row[0] & 1
        for i in range(2):
            here = pl.ds(pl.multiple_of(i * 2 * size + near * size, size), size)
            there = pl.ds(pl.multiple_of(i * 2 * size + (1 - near) * size, size), size)
            part = slice(i * size, (i + 1) * size)
            away[part, :] = low(high(kept[there, :]) + high(came[there, :]))
            rest[part, :] = low(high(kept[here, :]) + high(came[here, :]))

    half = shape16(2 * size, cols)
    return on_chip(body, (half, half), (row,), (kept, came), "bucket_near", cost=0.3)


def shares_body(d_a, d_b, fa, fb, w_ref, x_own, x_oth, gain_two, send_ref, own_ref, gains_ref):
    rows, width = x_own.shape
    cut = d_a.shape[1]
    sums = None
    for m, x_ref in ((1, x_oth), (0, x_own)):
        part = slice(m * rows, (m + 1) * rows)
        share = against(d_a[part, :], w_ref[:, :cut]) + against(d_b[part, :], w_ref[:, cut:])
        if m:
            send_ref[:, :width] = low(share)
        else:
            own_ref[...] = share
        x = high(x_ref[...])
        here = jnp.sum(share * (x * rms_scale(x)), axis=0, keepdims=True)
        sums = here if sums is None else sums + here
    send_ref[:, width : width + fa.shape[1]] = fa[...]
    send_ref[:, width + fa.shape[1] :] = fb[...]
    gains_ref[0:1, :] = sums
    gains_ref[1:2, :] = gain_two[...]


def shares(d_a, d_b, fa, fb, w, x_own, x_oth, gain_two):
    rows, width = x_own.shape
    return on_chip(
        shares_body,
        (shape16(rows, width + 2 * fa.shape[1]), shape32(rows, width), shape32(2, width)),
        (),
        (d_a, d_b, fa, fb, w, x_own, x_oth, gain_two),
        "shares",
        cost=2.3,
    )


def input_grad_body(place, share_ref, came_ref, grad_ref, x_ref, gain_ref, fa, fb, out_ref, first_ref):
    width = x_ref.shape[1]
    x = high(x_ref[...])
    scale = rms_scale(x)
    weighted = (share_ref[...] + high(came_ref[:, :width])) * gain_ref[...]
    mean = jnp.mean(weighted * x, axis=-1, keepdims=True)
    out_ref[...] = grad_ref[...] + scale * weighted - x * (scale * scale * scale * mean)
    cols = fa.shape[1]
    own = 2 * place[0]
    oth = 2 - own
    first_ref[:, columns(own, cols)] = fa[...]
    first_ref[:, columns(own + 1, cols)] = fb[...]
    first_ref[:, columns(oth, cols)] = came_ref[:, width : width + cols]
    first_ref[:, columns(oth + 1, cols)] = came_ref[:, width + cols :]


def input_grad(place, share, came, grad_hidden, x, gain, fa, fb):
    return on_chip(
        input_grad_body,
        (shape32(*x.shape), shape16(*x.shape)),
        (place,),
        (share, came, grad_hidden, x, gain, fa, fb),
        "input_grad",
        cost=2.0,
        limit=6,
    )


def after(first, *values):
    return lax.optimization_barrier((first, *values))[1:]


def two_groups(
    inputs,
    first_values,
    lengths,
    gain_attn,
    w_qkv,
    w_out,
    gain_mlp,
    w_gate,
    w_up,
    w_down,
    cotangent,
):
    SITES.clear()
    rows = inputs.shape[1]
    width = inputs.shape[2]
    span = 2 * rows
    out_cols = HEADS // 2 * HD
    packed_cols = 3 * out_cols
    mid = width // 2
    h = lax.axis_index("head")
    f = lax.axis_index("ffn")
    r = lax.axis_index("row")
    row_size = lax.axis_size("row")
    place = jnp.stack([h, lengths[0]]).astype(jnp.int32)
    row = r.reshape(1).astype(jnp.int32)
    tie = lax.optimization_barrier
    gain_attn = gain_attn.reshape(1, width)
    gain_mlp = gain_mlp.reshape(1, width)

    x_own = inputs[0]
    x_oth = swap(x_own, "head", 1)
    early_own = lax.dynamic_slice_in_dim(first_values[0], h * out_cols, out_cols, 1)
    early_oth = swap(
        lax.dynamic_slice_in_dim(first_values[0], (1 - h) * out_cols, out_cols, 1), "head", 1
    )
    dy_own = cotangent[0]
    dy_oth = swap(dy_own, "ffn", 2)
    down_core = swap(w_down, "ffn", 1)
    gate_core = swap(w_gate.T, "ffn", 1)
    up_core = swap(w_up.T, "ffn", 1)
    qkv_w = lax.dynamic_slice_in_dim(w_qkv, h * packed_cols, packed_cols, 1)
    half = HD // 2
    inverse = jnp.exp(-jnp.log(10000.0) * jnp.arange(half, dtype=jnp.float32) * 2.0 / HD)
    angles = jnp.arange(span, dtype=jnp.float32)[:, None] * jnp.tile(inverse, 4)[None, :]
    cosine = jnp.cos(angles)
    sign = jnp.where(jnp.arange(2 * HD) % HD < half, -1.0, 1.0)
    sine = jnp.sin(angles) * sign[None, :]

    ff_order = jnp.stack([(h ^ a) * row_size + (r ^ b) for a in (1, 0) for b in (3, 1, 2, 0)])
    down_order = jnp.stack([(h ^ a) * row_size + (r ^ b) for b in (3, 1, 2, 0) for a in (1, 0)])
    att_order = jnp.stack(
        [((f ^ a) * row_size + (r & 2 ^ b)) // 2 for a in (3, 1, 2, 0) for b in (2, 0)]
    )

    xn_away, xn_mine, packed_own = project(att_order, x_own, gain_attn, qkv_w)
    x_oth, early_oth, packed_own, cosine, sine, early_own, down_core, gate_core, up_core = tie(
        (x_oth, early_oth, packed_own, cosine, sine, early_own, down_core, gate_core, up_core)
    )
    xn_away, xn_mine, packed_oth = project(att_order, x_oth, gain_attn, qkv_w, (xn_away, xn_mine))
    att_own, att_oth, query, keys, mixed, log_sums = attend_forward(
        place, packed_own, packed_oth, early_own, early_oth, cosine, sine
    )
    att_came = swap(att_oth, "head", 1)
    att_core = swap(att_own, "ffn", 1)
    dy_oth, xn_away = after(att_own, dy_oth, xn_away)
    down_w = (w_down, down_core)
    gate_w = (w_gate.T, gate_core)
    up_w = (w_up.T, up_core)
    xn_core = swap(xn_away, "ffn", 1)
    dy_send, dyo_send = after(att_own, dy_own, dy_oth)
    dyc_own = swap(dy_send, "ffn", 1)
    dyc_oth = swap(dyo_send, "ffn", 1)
    dyc_all = reorder(down_order, dyc_own, dyc_oth)
    att_came, dyc_all, xn_core, att_core = tie((att_came, dyc_all, xn_core, att_core))
    hidden, hn_own = finish(place, x_own, att_own, att_came, w_out, gain_mlp)
    hn_oth = swap(hn_own, "ffn", 2)
    hnc_own = swap(hn_own, "ffn", 1)
    came_core = swap(after(hn_own, att_came)[0], "ffn", 1)

    *parts, dhn_own, down_own, dact0, dact1, dy_all = feed_own(
        down_order, hn_own, dy_own, dy_oth, gate_w, up_w, down_w
    )
    hn_oth, parts, dhn_own, down_own, dact0, dact1, dy_all, came_core, hnc_own = tie(
        (hn_oth, parts, dhn_own, down_own, dact0, dact1, dy_all, came_core, hnc_own)
    )
    hnc_oth = swap(hn_oth, "ffn", 1)
    act, gate, up, others, dhn_send, hn_all = feed_oth(
        ff_order, hn_own, hn_oth, (dact0, dact1), gate_w, up_w, parts
    )
    dhn_came = swap(dhn_send, "ffn", 2)
    others_core = swap(others, "ffn", 1)
    (hnc_oth,) = after(dhn_send, hnc_oth)
    hnc_all = reorder(ff_order, hnc_own, hnc_oth)

    down_send, down_kept = ff_grad(act, others_core, 0, dy_all, dyc_all)
    down_near = swap(down_send, "row", 1)
    gate_send, gate_kept = ff_grad(gate, others_core, 1, hn_all, hnc_all)
    up_send, up_kept = ff_grad(up, others_core, 2, hn_all, hnc_all)
    dhn_came, up_send, up_kept, gate_send, gate_kept, down_kept = tie(
        (dhn_came, up_send, up_kept, gate_send, gate_kept, down_kept)
    )

    grad_hidden, go_send, go_own, proj_away, proj_mine, gain_two = hidden_grad(
        att_order, place, dhn_own, dhn_came, hidden, dy_own, gain_mlp, w_out
    )
    go_oth = swap(go_send, "head", 1)
    proj_core = swap(proj_away, "ffn", 1)
    (gate_send,) = after(go_send, gate_send)
    gate_x = swap(gate_send, "head", 1)
    out_send, out_kept = bucket_grad(
        proj_mine, proj_core, (att_own, att_came), (att_core, came_core)
    )
    out_y = swap(out_send, "ffn", 2)
    go_oth, out_kept = tie((go_oth, out_kept))

    def backward(pairs, lse):
        return attend_backward(
            place, query, keys, mixed, lse, go_own, go_oth, att_own, att_oth, cosine, sine, pairs
        )

    pairs = HEADS // 4
    d_a, fa_own, fa_oth = backward((0, pairs // 2), log_sums)
    out_kept, down_kept = after(d_a, out_kept, down_kept)
    out_send, out_kept = bucket_near(row, out_kept, out_y)
    out_near = swap(out_send, "row", 1)
    down_send, down_kept = fold(down_kept, down_near)
    down_mid = swap(down_send, "row", 2)
    d_a, out_kept, down_kept, log_sums = tie((d_a, out_kept, down_kept, log_sums))
    core_a = swap(d_a, "ffn", 1)
    d_b, fb_own, fb_oth = backward((pairs // 2, pairs), log_sums)
    gate_kept, out_kept = after(d_b, gate_kept, out_kept)
    gate_send, gate_kept = fold(gate_kept, gate_x)
    out_send, out_kept = fold_rows(out_kept, out_near)
    d_b, gate_kept, out_kept = tie((d_b, gate_kept, out_kept))
    core_b = swap(d_b, "ffn", 1)
    up_x = swap(after(gate_kept, up_send)[0], "head", 1)
    (d_a,) = after(gate_kept, d_a)
    before = bucket_grad(xn_mine, xn_core, (d_a,), (core_a,), 0, packed_cols)
    core_b, *before = tie((core_b, *before))
    y_send, kept = bucket_grad(
        xn_mine, xn_core, (d_b,), (core_b,), packed_cols // 2, packed_cols, before
    )
    y_came = swap(y_send, "ffn", 2)
    d_a, d_b = after(y_send, d_a, d_b)
    back_send, share_own, gains = shares(
        d_a, d_b, fa_oth, fb_oth, qkv_w, x_own, x_oth, gain_two
    )
    gate_send, out_send, act, others = after(back_send, gate_send, out_send, act, others)
    gate_near = swap(gate_send, "row", 1)
    out_far = swap(out_send, "row", 2)
    units = w_down.shape[0]
    far_send = low(matmul(act[rows:], down_w[0]) + matmul(others[rows:span, :units], down_w[1]))
    up_kept, down_kept, gate_kept = after(far_send, up_kept, down_kept, gate_kept)
    up_send, up_kept = fold(up_kept, up_x)
    down_send, down_kept = fold(down_kept, down_mid)
    gains, back_send, up_kept, down_kept = tie((gains, back_send, up_kept, down_kept))
    gains_x = swap(gains, "head", 1)
    back_came = swap(after(gains, back_send)[0], "head", 1)
    gains = gains + gains_x
    gains = gains + swap(gains, "ffn", 1)
    gains_y = swap(gains, "ffn", 2)
    gate_kept, up_send, out_kept = after(gains, gate_kept, up_send, out_kept)
    gate_send, gate_kept = fold(gate_kept, gate_near)
    up_near = swap(up_send, "row", 1)
    out_sum = high(out_kept) + high(out_far)
    gate_far = swap(gate_send, "row", 2)
    kept, gate_kept, out_sum = tie((kept, gate_kept, out_sum))

    near_send, kept = bucket_near(row, kept, y_came)
    near_came = swap(near_send, "row", 1)
    gains, up_kept, far_send, down_send = after(near_send, gains, up_kept, far_send, down_send)
    gains = gains + gains_y
    gains_near = swap(gains, "row", 1)
    far_came = swap(far_send, "ffn", 2)
    up_send, up_kept = fold(up_kept, up_near)
    up_far = swap(up_send, "row", 2)
    gate_kept, out_sum = after(up_send, gate_kept, out_sum)
    sum_gate = high(gate_kept) + high(gate_far)
    out_x = swap(low(out_sum[:, out_cols:]), "head", 1)
    kept, up_kept, sum_gate, gains = tie((kept, up_kept, sum_gate, gains))
    qkv_send, kept = fold_rows(kept, near_came)
    qkv_far = swap(qkv_send, "row", 2)
    down_x = swap(after(qkv_send, down_send)[0], "head", 1)
    share_own, up_kept, down_kept, out_sum, residual, gains = after(
        qkv_send, share_own, up_kept, down_kept, out_sum[:, :out_cols], hidden + down_own, gains
    )
    gains = gains + gains_near
    gains_far = swap(gains, "row", 2)
    grad_in, grad_first = input_grad(
        place, share_own, back_came, grad_hidden, x_own, gain_attn, fa_own, fb_own
    )
    sum_down = high(down_kept) + high(down_x)
    sum_up = high(up_kept) + high(up_far)
    out_sum = out_sum + high(out_x)
    output = low(residual + high(far_came))[None]
    kept, grad_in, sum_up, sum_down, out_sum, output = tie(
        (kept, grad_in, sum_up, sum_down, out_sum, output)
    )
    sum_qkv = high(kept) + high(qkv_far)
    gains = gains + gains_far
    return (
        output,
        grad_in[None],
        grad_first[None],
        gains[0],
        sum_qkv,
        out_sum.T,
        gains[1],
        sum_gate.T,
        sum_up.T,
        sum_down,
    )


def solution(mesh):
    in_specs = (
        P(("ffn", "row"), "head", None),
        P(("ffn", "row"), "head", None),
        P(("ffn", "row")),
        P(),
        P(),
        P(),
        P(),
        P(None, "ffn"),
        P(None, "ffn"),
        P("ffn", None),
        P(("ffn", "row"), "head", None),
    )
    out_specs = (
        P(("ffn", "row"), "head", None),
        P(("ffn", "row"), "head", None),
        P(("ffn", "row"), "head", None),
        P(),
        P(("ffn", "row"), "head"),
        P("head", ("ffn", "row")),
        P(),
        P(("head", "row"), "ffn"),
        P(("head", "row"), "ffn"),
        P("ffn", ("head", "row")),
    )
    body = two_groups if mesh.shape["head"] == 2 and mesh.shape["ffn"] == 4 else any_groups
    return jax.shard_map(
        body, mesh=mesh, in_specs=in_specs, out_specs=out_specs, check_vma=False
    )
```

```python
import functools

import jax
import jax.numpy as jnp
from jax import lax
from jax.experimental import pallas as pl
from jax.experimental.pallas import tpu as pltpu
from jax.sharding import PartitionSpec as P

HEADS = 16
HD = 64
MIN_LEN = 512
STEP = 256


eps = 1e-06


def rms_scale(values):
    return lax.rsqrt(jnp.mean(values * values, axis=-1, keepdims=True) + eps)


def matmul(left, right):
    return jnp.dot(left, right, preferred_element_type=jnp.float32)


def inner_rows(left, right):
    return lax.dot_general(
        left, right, (((0,), (0,)), ((), ())), preferred_element_type=jnp.float32
    )


def against(left, right):
    return lax.dot_general(
        left, right, (((1,), (1,)), ((), ())), preferred_element_type=jnp.float32
    )


def swap(values, axis, mask):
    size = lax.axis_size(axis)
    return lax.ppermute(values, axis, [(i, i ^ mask) for i in range(size)])


def bits_of(axis):
    size = lax.axis_size(axis)
    return [1 << b for b in range(size.bit_length() - 2, -1, -1)]


def halve(values, dim, axis, mask):
    bit = (lax.axis_index(axis) // mask) % 2
    away = lax.dynamic_index_in_dim(values, 1 - bit, dim, keepdims=False)
    kept = lax.dynamic_index_in_dim(values, bit, dim, keepdims=False)
    came = swap(away.astype(jnp.bfloat16), axis, mask)
    return kept.astype(jnp.float32) + came.astype(jnp.float32)


def total(values, axes):
    for axis in axes:
        for mask in reversed(bits_of(axis)):
            values = values + swap(values, axis, mask)
    return values


def rotary(positions, head_size):
    half_size = head_size // 2
    inverse = jnp.exp(
        -jnp.log(10000.0) * jnp.arange(half_size, dtype=jnp.float32) * 2.0 / head_size
    )
    angles = positions.astype(jnp.float32)[:, None] * inverse[None, :]
    return (jnp.cos(angles), jnp.sin(angles))


def rotate(vectors, cosine, sine, sign):
    half_size = vectors.shape[-1] // 2
    first_half = vectors[..., :half_size]
    second_half = vectors[..., half_size:]
    cos_rows = cosine[:, None, :]
    sin_rows = sign * sine[:, None, :]
    return jnp.concatenate(
        [
            first_half * cos_rows - second_half * sin_rows,
            second_half * cos_rows + first_half * sin_rows,
        ],
        axis=-1,
    )


def masked_scores(q_rows, keys, q_pos, k_pos, valid):
    raw = jnp.einsum("qhe,khe->hqk", q_rows, keys, preferred_element_type=jnp.float32)
    allowed = (k_pos[None, :] <= q_pos[:, None]) & (k_pos[None, :] < valid)
    return jnp.where(allowed[None], 0.125 * raw, -1e30)


def scan_forward(query, keys, mixed, positions, valid, block_rows):
    count = query.shape[0] // block_rows

    def step(carry, index):
        start = index * block_rows
        q_rows = lax.dynamic_slice_in_dim(query, start, block_rows, 0)
        q_pos = lax.dynamic_slice_in_dim(positions, start, block_rows, 0)
        scores = masked_scores(q_rows, keys, q_pos, positions, valid)
        top = jnp.max(scores, axis=-1, keepdims=True)
        expo = jnp.exp(scores - top)
        total_w = jnp.sum(expo, axis=-1, keepdims=True)
        weights = expo / total_w
        result = jnp.einsum(
            "hqk,khe->qhe", weights.astype(jnp.bfloat16), mixed, preferred_element_type=jnp.float32
        )
        return (carry, (result.astype(jnp.bfloat16), top + jnp.log(total_w)))

    _, (outs, log_sums) = lax.scan(step, 0, jnp.arange(count, dtype=jnp.int32))
    return (outs.reshape(query.shape), log_sums)


def scan_backward(query, keys, mixed, positions, valid, log_sums, grad_out, block_rows):
    count = query.shape[0] // block_rows
    zeros = jnp.zeros(keys.shape, jnp.float32)

    def step(carry, index):
        key_sum, value_sum = carry
        start = index * block_rows
        q_rows = lax.dynamic_slice_in_dim(query, start, block_rows, 0)
        q_pos = lax.dynamic_slice_in_dim(positions, start, block_rows, 0)
        g_rows = lax.dynamic_slice_in_dim(grad_out, start, block_rows, 0)
        scores = masked_scores(q_rows, keys, q_pos, positions, valid)
        weights = jnp.exp(scores - log_sums[index])
        grad_w = jnp.einsum("qhe,khe->hqk", g_rows, mixed, preferred_element_type=jnp.float32)
        delta = jnp.sum(weights * grad_w, axis=-1, keepdims=True)
        grad_s = (weights * (grad_w - delta)).astype(jnp.bfloat16)
        grad_q = 0.125 * jnp.einsum(
            "hqk,khe->qhe", grad_s, keys, preferred_element_type=jnp.float32
        )
        key_sum = key_sum + 0.125 * jnp.einsum(
            "hqk,qhe->khe", grad_s, q_rows, preferred_element_type=jnp.float32
        )
        value_sum = value_sum + jnp.einsum(
            "hqk,qhe->khe", weights.astype(jnp.bfloat16), g_rows, preferred_element_type=jnp.float32
        )
        return ((key_sum, value_sum), grad_q)

    (grad_keys, grad_mixed), grad_query = lax.scan(
        step, (zeros, zeros), jnp.arange(count, dtype=jnp.int32)
    )
    return (grad_query.reshape(query.shape), grad_keys, grad_mixed)


def any_groups(
    inputs,
    first_values,
    lengths,
    gain_attn,
    w_qkv,
    w_out,
    gain_mlp,
    w_gate,
    w_up,
    w_down,
    cotangent,
):
    rows = inputs.shape[1]
    width = inputs.shape[2]
    groups = lax.axis_size("head")
    shards = lax.axis_size("ffn")
    heads_here = HEADS // groups
    span_rows = rows * groups
    block_rows = span_rows // max(1, span_rows // 512)
    head_pos = lax.axis_index("head")
    valid_len = lengths[0]
    packed_cols = heads_here * 3 * HD
    out_cols = heads_here * HD
    hidden_here = w_gate.shape[1]

    owners = [head_pos ^ m for m in range(groups)]
    x_all = [inputs[0]] + [swap(inputs[0], "head", m) for m in range(1, groups)]
    early = []
    for m in range(groups):
        piece = lax.dynamic_slice_in_dim(first_values[0], owners[m] * out_cols, out_cols, 1)
        early.append(swap(piece, "head", m) if m else piece)
    far = range(2, shards, 2)
    grad_rows = jnp.concatenate([cotangent[0]] + [swap(cotangent[0], "ffn", m) for m in far], 0)
    gate_w = jnp.concatenate([w_gate, swap(w_gate, "ffn", 1)], 1)
    up_w = jnp.concatenate([w_up, swap(w_up, "ffn", 1)], 1)
    down_w = jnp.concatenate([w_down, swap(w_down, "ffn", 1)], 0)
    w_heads = lax.dynamic_slice_in_dim(w_qkv, head_pos * packed_cols, packed_cols, 1)
    out_w = jnp.concatenate(
        [lax.dynamic_slice_in_dim(w_out, o * out_cols, out_cols, 0) for o in owners], 0
    )

    positions = jnp.concatenate([o * rows + jnp.arange(rows, dtype=jnp.int32) for o in owners])
    cosine, sine = rotary(positions, HD)
    normed, scaled, queries, key_list, mixes = [], [], [], [], []
    rows_in = inputs[0].astype(jnp.float32)
    scale_one = rms_scale(rows_in)
    for m in range(groups):
        block = x_all[m].astype(jnp.float32)
        scale = rms_scale(block)
        scaled.append(block * scale)
        normed.append((block * scale * gain_attn).astype(jnp.bfloat16))
        packed = matmul(normed[m], w_heads).astype(jnp.bfloat16)
        packed = packed.reshape(rows, heads_here, 3, HD).astype(jnp.float32)
        part = slice(m * rows, (m + 1) * rows)
        queries.append(rotate(packed[:, :, 0], cosine[part], sine[part], 1.0))
        key_list.append(rotate(packed[:, :, 1], cosine[part], sine[part], 1.0))
        value = early[m].reshape(rows, heads_here, HD).astype(jnp.float32)
        mixes.append(0.5 * (packed[:, :, 2] + value))
    query = jnp.concatenate(queries, 0).astype(jnp.bfloat16)
    keys = jnp.concatenate(key_list, 0).astype(jnp.bfloat16)
    mixed = jnp.concatenate(mixes, 0).astype(jnp.bfloat16)
    attended, log_sums = scan_forward(query, keys, mixed, positions, valid_len, block_rows)
    attended = attended.reshape(groups, rows, out_cols)
    att_own = jnp.concatenate(
        [attended[0]] + [swap(attended[m], "head", m) for m in range(1, groups)], 1
    )
    hidden = rows_in + matmul(att_own, out_w)
    scale_two = rms_scale(hidden)
    normed_two = (hidden * scale_two * gain_mlp).astype(jnp.bfloat16)

    mlp_rows = [normed_two] + [swap(normed_two, "ffn", m) for m in far]
    grad_list = [grad_rows[i * rows : (i + 1) * rows] for i in range(len(mlp_rows))]
    actives, grad_gates, grad_ups, downs, grad_normed_list = [], [], [], [], []
    for i, block in enumerate(mlp_rows):
        gate_rows = matmul(block, gate_w)
        up_rows = matmul(block, up_w)
        sigmoid_gate = jax.nn.sigmoid(gate_rows)
        silu_gate = gate_rows * sigmoid_gate
        grad_active = against(grad_list[i], down_w)
        actives.append((silu_gate * up_rows).astype(jnp.bfloat16))
        grad_gates.append(
            (
                grad_active * up_rows * sigmoid_gate * (1.0 + gate_rows * (1.0 - sigmoid_gate))
            ).astype(jnp.bfloat16)
        )
        grad_ups.append((grad_active * silu_gate).astype(jnp.bfloat16))
        grad_normed_list.append(against(grad_gates[i], gate_w) + against(grad_ups[i], up_w))
        downs.append(matmul(actives[i], down_w))
    grad_normed_two = grad_normed_list[0]
    for i, m in enumerate(far):
        came = swap(grad_normed_list[i + 1].astype(jnp.bfloat16), "ffn", m)
        grad_normed_two = grad_normed_two + came.astype(jnp.float32)
    down_rows = downs[0]
    for i, m in enumerate(far):
        down_rows = down_rows + swap(downs[i + 1].astype(jnp.bfloat16), "ffn", m).astype(jnp.float32)
    output = (hidden + down_rows).astype(jnp.bfloat16)[None]

    all_rows = jnp.concatenate(mlp_rows, 0)
    ff_sums = []
    for left, right in (
        (grad_rows, jnp.concatenate(actives, 0)),
        (all_rows, jnp.concatenate(grad_gates, 0)),
        (all_rows, jnp.concatenate(grad_ups, 0)),
    ):
        away = inner_rows(left, right[:, hidden_here:]).astype(jnp.bfloat16)
        part = inner_rows(left, right[:, :hidden_here])
        part = (part + swap(away, "ffn", 1).astype(jnp.float32)).astype(jnp.bfloat16)
        steps = [("head", b) for b in bits_of("head")] + [("row", b) for b in bits_of("row")]
        part = part.reshape([2] * len(steps) + [-1, hidden_here])
        order = [s for s in steps if s[0] == "head"] + [s for s in reversed(steps) if s[0] == "row"]
        left_steps = list(steps)
        for s in order:
            part = halve(part, left_steps.index(s), *s)
            left_steps.remove(s)
            if left_steps:
                part = part.astype(jnp.bfloat16)
        ff_sums.append(part)
    sum_down, sum_gate, sum_up = ff_sums

    grad_y = cotangent[0].astype(jnp.float32)
    grad_gain_two = jnp.sum(grad_normed_two * hidden * scale_two, axis=0)
    weighted_two = grad_normed_two * gain_mlp
    cube_two = scale_two * scale_two * scale_two
    grad_hidden = (
        grad_y
        + scale_two * weighted_two
        - hidden * cube_two * jnp.mean(weighted_two * hidden, axis=-1, keepdims=True)
    )
    grad_proj = grad_hidden.astype(jnp.bfloat16)
    grad_att = against(grad_proj, out_w).astype(jnp.bfloat16)
    grad_att = jnp.concatenate(
        [
            swap(grad_att[:, m * out_cols : (m + 1) * out_cols], "head", m)
            if m
            else grad_att[:, :out_cols]
            for m in range(groups)
        ],
        0,
    ).reshape(span_rows, heads_here, HD)

    def over_buckets(part):
        steps = [("ffn", b) for b in bits_of("ffn")] + [("row", b) for b in bits_of("row")]
        part = part.astype(jnp.bfloat16).reshape([2] * len(steps) + [-1, part.shape[1]])
        order = [s for s in reversed(steps) if s[0] == "ffn"] + [
            s for s in reversed(steps) if s[0] == "row"
        ]
        left_steps = list(steps)
        for s in order:
            part = halve(part, left_steps.index(s), *s)
            left_steps.remove(s)
            if left_steps:
                part = part.astype(jnp.bfloat16)
        return part

    part = over_buckets(inner_rows(grad_proj, att_own))
    sum_out = part[:, :out_cols]
    for m in range(1, groups):
        came = swap(part[:, m * out_cols : (m + 1) * out_cols].astype(jnp.bfloat16), "head", m)
        sum_out = sum_out + came.astype(jnp.float32)

    grad_query, grad_keys, grad_mixed = scan_backward(
        query, keys, mixed, positions, valid_len, log_sums, grad_att, block_rows
    )
    grad_packed = jnp.stack(
        [
            rotate(grad_query, cosine, sine, -1.0),
            rotate(grad_keys, cosine, sine, -1.0),
            0.5 * grad_mixed,
        ],
        axis=2,
    )
    grad_packed = grad_packed.astype(jnp.bfloat16).reshape(span_rows, packed_cols)
    grad_early = (0.5 * grad_mixed).astype(jnp.bfloat16).reshape(span_rows, out_cols)
    firsts = [grad_early[m * rows : (m + 1) * rows] for m in range(groups)]
    firsts = [swap(firsts[m], "head", m) if m else firsts[0] for m in range(groups)]
    grad_first = jnp.zeros((rows, width), jnp.bfloat16)
    for m in range(groups):
        grad_first = lax.dynamic_update_slice_in_dim(grad_first, firsts[m], owners[m] * out_cols, 1)
    shares = [
        against(grad_packed[m * rows : (m + 1) * rows], w_heads) for m in range(groups)
    ]
    grad_gain_one = sum(jnp.sum(shares[m] * scaled[m], axis=0) for m in range(groups))
    grad_normed = shares[0]
    for m in range(1, groups):
        grad_normed = grad_normed + swap(shares[m].astype(jnp.bfloat16), "head", m).astype(jnp.float32)
    sum_qkv = over_buckets(inner_rows(jnp.concatenate(normed, 0), grad_packed))
    weighted_one = grad_normed * gain_attn
    cube_one = scale_one * scale_one * scale_one
    grad_in = (
        grad_hidden
        + scale_one * weighted_one
        - rows_in * cube_one * jnp.mean(weighted_one * rows_in, axis=-1, keepdims=True)
    )
    gains = total(jnp.stack([grad_gain_one, grad_gain_two]), ("ffn", "head", "row"))
    return (
        output,
        grad_in[None],
        grad_first[None],
        gains[0],
        sum_qkv,
        sum_out.T,
        gains[1],
        sum_gate,
        sum_up,
        sum_down.T,
    )


SCALE = 4.5e8
COSTS = {}
SITES = {}


def site_cost(name, usual):
    count = SITES.get(name, 0)
    SITES[name] = count + 1
    return int(SCALE * COSTS.get(name + str(count), usual))


def low(values):
    return values.astype(jnp.bfloat16)


def high(values):
    return values.astype(jnp.float32)


def on_chip(body, outs, scalars, arrays, name, scratch=(), aliases=None, limit=3, cost=1.0, away=(), far=()):
    inside = pl.BlockSpec(memory_space=pltpu.VMEM)
    outside = pl.BlockSpec(memory_space=pl.ANY)
    return pl.pallas_call(
        body,
        out_shape=jax.tree.unflatten(
            jax.tree.structure(outs),
            [
                pltpu.HBM(o.shape, o.dtype) if i in away else o
                for i, o in enumerate(jax.tree.leaves(outs))
            ],
        ),
        in_specs=[pl.BlockSpec(memory_space=pltpu.SMEM)] * len(scalars)
        + [outside if i in far else inside for i in range(len(arrays))],
        out_specs=jax.tree.unflatten(
            jax.tree.structure(outs),
            [
                outside if i in away else inside
                for i in range(len(jax.tree.leaves(outs)))
            ],
        ),
        scratch_shapes=list(scratch),
        input_output_aliases=aliases or {},
        cost_estimate=pl.CostEstimate(
            flops=site_cost(name, cost), transcendentals=0, bytes_accessed=1
        ),
        compiler_params=pltpu.CompilerParams(vmem_limit_bytes=limit << 20),
        name=name,
    )(*scalars, *arrays)


def shape16(*dims):
    return jax.ShapeDtypeStruct(dims, jnp.bfloat16)


def shape32(*dims):
    return jax.ShapeDtypeStruct(dims, jnp.float32)


def spans(total):
    return [(a, min(a + STEP, total)) for a in range(0, total, STEP)]


def turn(values):
    lane = lax.broadcasted_iota(jnp.int32, values.shape, 1)
    return jnp.where(
        lane % HD < HD // 2, pltpu.roll(values, 2 * HD - HD // 2, 1), pltpu.roll(values, HD // 2, 1)
    )


def allowed_keys(a, b, valid):
    size = b - a
    down = lax.broadcasted_iota(jnp.int32, (size, size), 0)
    across = lax.broadcasted_iota(jnp.int32, (size, size), 1)
    allowed = down <= across
    if b > MIN_LEN:
        allowed = allowed & (down < valid - a)
    return allowed


def columns(index, size):
    return pl.ds(pl.multiple_of(index * size, size), size)


def forward_body(
    place, packed_own, packed_oth, early_own, early_oth, cos_ref, sin_ref,
    own_far, oth_far, q_far, k_far, v_far, lse_out,
    att_own, att_oth, q_out, k_out, v_out, flipped, att, sems,
):
    rows = packed_own.shape[0]
    span = 2 * rows
    wide = 2 * HD
    valid = place[1]
    f32 = jnp.float32
    bf = jnp.bfloat16
    first = lax.broadcasted_iota(jnp.int32, (1, wide), 1) < HD
    flipped[:, HD:, :] = jnp.ones((2, 16, span), bf)

    def copies(p):
        cols = columns(p, wide)
        return [
            pltpu.make_async_copy(near.at[:, cols], far.at[:, cols], sems.at[i, p])
            for i, (near, far) in enumerate(
                (
                    (q_out, q_far),
                    (k_out, k_far),
                    (v_out, v_far),
                    (att_oth, oth_far),
                    (att_own, own_far),
                )
            )
        ]

    def pair(p, _):
        cols = columns(p, wide)
        for m, (packed, early) in enumerate(((packed_own, early_own), (packed_oth, early_oth))):
            here = columns(place[0] ^ m, rows)
            x0 = high(packed[:, pl.ds(pl.multiple_of(p * 3 * wide, wide), wide)])
            x1 = high(packed[:, pl.ds(pl.multiple_of(p * 3 * wide + wide, wide), wide)])
            x2 = high(packed[:, pl.ds(pl.multiple_of(p * 3 * wide + 2 * wide, wide), wide)])
            cosine = cos_ref[here, :]
            sine = sin_ref[here, :]
            q = jnp.where(first, x0, x1)
            k = pltpu.roll(jnp.where(first, x2, x0), HD, 1)
            v = jnp.where(first, x1, x2)
            q_out[here, cols] = low(q * cosine + turn(q) * sine)
            k_out[here, cols] = low(k * cosine + turn(k) * sine)
            v_out[here, cols] = low(0.5 * (v + high(early[:, cols])))
        for copy in copies(p)[:3]:
            copy.start()
        turned = v_out[:, cols].T
        for e in range(2):
            flipped[e, :HD, :] = turned[e * HD : (e + 1) * HD, :]
        for a, b in spans(span):
            q = q_out[a:b, cols] * jnp.asarray(0.125, bf)
            allowed = allowed_keys(a, b, valid)
            for e in range(2):
                qe = jnp.where(first == (e == 0), q, jnp.zeros_like(q))
                diag = jnp.where(allowed, against(k_out[a:b, cols], qe), -1e30)
                top = jnp.max(diag, axis=0, keepdims=True)
                if a:
                    past = against(k_out[:a, cols], qe)
                    top = jnp.maximum(top, jnp.max(past, axis=0, keepdims=True))
                out = matmul(flipped[e, :, a:b], low(jnp.exp(diag - top)))
                if a:
                    out = out + matmul(flipped[e, :, :a], low(jnp.exp(past - top)))
                amount = out[HD : HD + 1, :]
                att[e * HD : (e + 1) * HD, a:b] = out[:HD, :] / amount
                lse_out[p, e : e + 1, a:b] = top + jnp.log(amount)
        result = low(att[...].T)
        upper = place[0] == 0
        att_own[:, cols] = jnp.where(upper, result[:rows, :], result[rows:, :])
        att_oth[:, cols] = jnp.where(upper, result[rows:, :], result[:rows, :])
        for copy in copies(p)[3:]:
            copy.start()
        return 0

    lax.fori_loop(0, lse_out.shape[0], pair, 0)
    for p in range(lse_out.shape[0]):
        for copy in copies(p):
            copy.wait()


def attend_forward(place, packed_own, packed_oth, early_own, early_oth, cosine, sine):
    rows, cols = packed_own.shape
    heads = cols // (3 * HD)
    span = 2 * rows
    out = shape16(rows, heads * HD)
    natural = shape16(span, heads * HD)
    return on_chip(
        forward_body,
        (out, out, natural, natural, natural, shape32(heads // 2, 2, span)),
        (place,),
        (packed_own, packed_oth, early_own, early_oth, cosine, sine),
        "attend_forward",
        cost=11.0,
        limit=7,
        away=(0, 1, 2, 3, 4),
        scratch=(
            pltpu.VMEM(out.shape, jnp.bfloat16),
            pltpu.VMEM(out.shape, jnp.bfloat16),
            pltpu.VMEM(natural.shape, jnp.bfloat16),
            pltpu.VMEM(natural.shape, jnp.bfloat16),
            pltpu.VMEM(natural.shape, jnp.bfloat16),
            pltpu.VMEM((2, HD + 16, span), jnp.bfloat16),
            pltpu.VMEM((2 * HD, span), jnp.float32),
            pltpu.SemaphoreType.DMA((5, heads // 2)),
        ),
    )


def backward_body(
    start, place, q_far, k_far, v_far, lse_ref, go_own, go_oth, att_own, att_oth, cos_ref, sin_ref,
    d_out, f_own, f_oth, q_ref, k_ref, v_ref, sems, grad, prod, turned_k, dq, dk, dv,
):
    rows = go_own.shape[0]
    span = 2 * rows
    valid = place[1]
    wide = 2 * HD
    bf = jnp.bfloat16
    first = lax.broadcasted_iota(jnp.int32, (1, wide), 1) < HD
    eighth = jnp.asarray(0.125, bf)
    count = f_own.shape[1] // wide

    def copies(i):
        there = columns(i + start, wide)
        here = columns(i, wide)
        return [
            pltpu.make_async_copy(away.at[:, there], near.at[:, here], sems.at[n, i])
            for n, (away, near) in enumerate(((q_far, q_ref), (k_far, k_ref), (v_far, v_ref)))
        ]

    for i in range(count):
        for copy in copies(i):
            copy.start()

    def pair(i, _):
        p = i + start
        cols = columns(p, wide)
        near = columns(i, wide)
        for copy in copies(i):
            copy.wait()
        for m, (go, att) in enumerate(((go_own, att_own), (go_oth, att_oth))):
            here = columns(place[0] ^ m, rows)
            grad[here, :] = go[:, cols]
            prod[here, :] = high(go[:, cols]) * high(att[:, cols])
        flat = prod[...].T
        deltas = [jnp.sum(flat[e * HD : (e + 1) * HD, :], axis=0, keepdims=True) for e in range(2)]
        turned_k[...] = (k_ref[:, near] * eighth).T
        for n, (a, b) in enumerate(spans(span)):
            allowed = allowed_keys(a, b, valid)
            q = q_ref[a:b, near] * eighth
            g = grad[a:b, :]
            parts = ((a, b), (0, a)) if a else ((a, b),)
            sums = {}
            for e in range(2):
                mine = first == (e == 0)
                qe = jnp.where(mine, q, jnp.zeros_like(q))
                ge = jnp.where(mine, g, jnp.zeros_like(g))
                for lo, hi in parts:
                    scores = against(k_ref[lo:hi, near], qe)
                    if lo == a:
                        scores = jnp.where(allowed, scores, -1e30)
                    weights = jnp.exp(scores - lse_ref[p, e : e + 1, a:b])
                    grad_w = against(v_ref[lo:hi, near], ge)
                    grad_s = low(weights * (grad_w - deltas[e][:, a:b]))
                    dv_here = matmul(low(weights), ge)
                    dk_here = matmul(grad_s, qe)
                    dq_here = matmul(turned_k[e * HD : (e + 1) * HD, lo:hi], grad_s)
                    if (lo, "v") in sums:
                        dv_here = dv_here + sums[lo, "v"]
                        dk_here = dk_here + sums[lo, "k"]
                    sums[lo, "v"], sums[lo, "k"] = dv_here, dk_here
                    sums[lo, e] = dq_here
            for e in range(2):
                dq[e * HD : (e + 1) * HD, a:b] = sums[a, e] + sums[0, e] if a else sums[a, e]
            dv[a:b, :] = sums[a, "v"]
            dk[a:b, :] = sums[a, "k"]
            if a:
                dv[:a, :] += sums[0, "v"]
                dk[:a, :] += sums[0, "k"]
        prod[...] = dq[...].T
        for m, f_out in enumerate((f_own, f_oth)):
            here = columns(place[0] ^ m, rows)
            cosine = cos_ref[here, :]
            sine = sin_ref[here, :]
            gv = low(0.5 * dv[here, :])
            gk = dk[here, :]
            gk = low(pltpu.roll(gk * cosine - turn(gk) * sine, HD, 1))
            gq = prod[here, :]
            gq = low(gq * cosine - turn(gq) * sine)
            part = slice(m * rows, (m + 1) * rows)
            base = i * 3 * wide
            d_out[part, pl.ds(pl.multiple_of(base, wide), wide)] = jnp.where(first, gq, gk)
            d_out[part, pl.ds(pl.multiple_of(base + wide, wide), wide)] = jnp.where(first, gv, gq)
            d_out[part, pl.ds(pl.multiple_of(base + 2 * wide, wide), wide)] = jnp.where(first, gk, gv)
            f_out[:, columns(i, wide)] = gv
        return 0

    lax.fori_loop(0, count, pair, 0)


def attend_backward(place, q, k, v, lse, go_own, go_oth, att_own, att_oth, cosine, sine, pairs):
    span = q.shape[0]
    rows = span // 2
    wide = 2 * HD
    cols = wide * (pairs[1] - pairs[0])
    return on_chip(
        functools.partial(backward_body, pairs[0]),
        (shape16(span, 3 * cols), shape16(rows, cols), shape16(rows, cols)),
        (place,),
        (q, k, v, lse, go_own, go_oth, att_own, att_oth, cosine, sine),
        "attend_backward",
        cost=7.5,
        limit=6,
        far=(0, 1, 2),
        scratch=(
            pltpu.VMEM((span, cols), jnp.bfloat16),
            pltpu.VMEM((span, cols), jnp.bfloat16),
            pltpu.VMEM((span, cols), jnp.bfloat16),
            pltpu.SemaphoreType.DMA((3, pairs[1] - pairs[0])),
            pltpu.VMEM((span, wide), jnp.bfloat16),
            pltpu.VMEM((span, wide), jnp.float32),
            pltpu.VMEM((wide, span), jnp.bfloat16),
            pltpu.VMEM((wide, span), jnp.float32),
            pltpu.VMEM((span, wide), jnp.float32),
            pltpu.VMEM((span, wide), jnp.float32),
        ),
    )


def project_body(base, order, x_ref, gain_ref, w_ref, *refs):
    away_far, mine_far, packed_ref, xn, away, mine, sems = refs[-7:]
    rows = x_ref.shape[0]
    x = high(x_ref[...])
    xn[...] = low(x * rms_scale(x) * gain_ref[...])
    arrange_halves(order, (xn,), away, mine)
    there = slice(base, base + rows)
    copies = [
        pltpu.make_async_copy(away, away_far.at[there, :], sems.at[0]),
        pltpu.make_async_copy(mine, mine_far.at[there, :], sems.at[1]),
    ]
    for copy in copies:
        copy.start()
    cols = w_ref.shape[1] // 3
    for i in range(3):
        part = slice(i * cols, (i + 1) * cols)
        packed_ref[:, part] = low(matmul(xn[...], w_ref[:, part]))
    for copy in copies:
        copy.wait()


def project(order, x, gain, w, before=()):
    rows, width = x.shape
    part = shape16(2 * rows, width // 2)
    return pl.pallas_call(
        functools.partial(project_body, rows if before else 0),
        out_shape=(
            pltpu.HBM(part.shape, part.dtype),
            pltpu.HBM(part.shape, part.dtype),
            shape16(rows, w.shape[1]),
        ),
        in_specs=[pl.BlockSpec(memory_space=pltpu.SMEM)]
        + [pl.BlockSpec(memory_space=pltpu.VMEM)] * 3
        + [pl.BlockSpec(memory_space=pl.ANY)] * len(before),
        out_specs=(
            pl.BlockSpec(memory_space=pl.ANY),
            pl.BlockSpec(memory_space=pl.ANY),
            pl.BlockSpec(memory_space=pltpu.VMEM),
        ),
        scratch_shapes=[
            pltpu.VMEM((rows, width), jnp.bfloat16),
            pltpu.VMEM((rows, width // 2), jnp.bfloat16),
            pltpu.VMEM((rows, width // 2), jnp.bfloat16),
            pltpu.SemaphoreType.DMA((2,)),
        ],
        input_output_aliases={4 + i: i for i in range(len(before))},
        cost_estimate=pl.CostEstimate(
            flops=site_cost("project", 2.0), transcendentals=0, bytes_accessed=1
        ),
        compiler_params=pltpu.CompilerParams(vmem_limit_bytes=5 << 20),
        name="project",
    )(order, x, gain, w, *before)


def arrange(order, blocks, out):
    rows = blocks[0].shape[0]
    size = out.shape[1] // order.shape[0]
    for i in range(order.shape[0]):
        for b, block in enumerate(blocks):
            out[b * rows : (b + 1) * rows, i * size : (i + 1) * size] = block[:, columns(order[i], size)]


def finish(place, x, att_own, att_came, w, gain):
    def body(
        place, x_ref, own_far, came_far, w_far, gain_ref,
        hidden_far, hn_ref, hidden_ref, w_ref, att_ref, sems,
    ):
        cols = own_far.shape[1]
        loads = []
        for m, far in enumerate((own_far, came_far)):
            there = columns(place[0] ^ m, cols)
            loads.append(pltpu.make_async_copy(far, att_ref.at[m], sems.at[3 + m]))
            loads.append(pltpu.make_async_copy(w_far.at[there, :], w_ref.at[m], sems.at[m]))
        for load in loads:
            load.start()
        hidden = high(x_ref[...])
        for m in range(2):
            loads[2 * m].wait()
            loads[2 * m + 1].wait()
            hidden = hidden + matmul(att_ref[m], w_ref[m])
        hidden_ref[...] = hidden
        copy = pltpu.make_async_copy(hidden_ref, hidden_far, sems.at[2])
        copy.start()
        hn_ref[...] = low(hidden * rms_scale(hidden) * gain_ref[...])
        copy.wait()

    rows, width = x.shape
    return on_chip(
        body,
        (shape32(rows, width), shape16(rows, width)),
        (place,),
        (x, att_own, att_came, w, gain),
        "finish",
        cost=3.0,
        limit=8,
        away=(0,),
        far=(1, 2, 3),
        scratch=(
            pltpu.VMEM((rows, width), jnp.float32),
            pltpu.VMEM((2, width // 2, width), jnp.bfloat16),
            pltpu.VMEM((2, rows, width // 2), jnp.bfloat16),
            pltpu.SemaphoreType.DMA((5,)),
        ),
    )


def reorder(order, *blocks):
    rows, cols = blocks[0].shape

    def body(order, *refs):
        arrange(order, refs[:-1], refs[-1])

    return on_chip(body, shape16(rows * len(blocks), cols), (order,), blocks, "reorder", cost=0.9)


def arrange_halves(order, blocks, away, mine):
    rows = blocks[0].shape[0]
    count = order.shape[0] // 2
    size = mine.shape[1] // count
    for half, out in enumerate((away, mine)):
        for i in range(count):
            for b, block in enumerate(blocks):
                out[b * rows : (b + 1) * rows, i * size : (i + 1) * size] = block[
                    :, columns(order[half * count + i], size)
                ]


def reorder_halves(order, *blocks):
    rows, cols = blocks[0].shape

    def body(order, *refs):
        arrange_halves(order, refs[:-2], *refs[-2:])

    part = shape16(rows * len(blocks), cols // 2)
    return on_chip(body, (part, part), (order,), blocks, "reorder_halves", cost=0.9)


def feed_rows(hn, grads, gate_w, up_w, mine, other, base):
    rows = hn.shape[0]
    units = gate_w[0].shape[0]
    here = slice(base, base + rows)
    total_hn = None
    for s in range(2):
        gate = against(hn[...], gate_w[s][...])
        up = against(hn[...], up_w[s][...])
        grad = high(grads[s][...])
        sig = 1.0 / (1.0 + jnp.exp(-gate))
        silu = gate * sig
        results = (silu * up, grad * up * sig * (1.0 + gate * (1.0 - sig)), grad * silu)
        for i, result in enumerate(results):
            if s == 0:
                mine[i][here, :] = low(result)
            else:
                other[2 * i * rows + base : 2 * i * rows + base + rows, :units] = low(result)
    for s in range(2):
        for i, w in ((1, gate_w[s]), (2, up_w[s])):
            if s == 0:
                share = matmul(mine[i][here, :], w[...])
            else:
                share = matmul(other[2 * i * rows + base : 2 * i * rows + base + rows, :units], w[...])
            total_hn = share if total_hn is None else total_hn + share
    return total_hn


def feed_own_body(order, hn, dy_own, dy_oth, wg0, wg1, wu0, wu1, wd0, wd1, *refs):
    rows = hn.shape[0]
    outs, grads = refs[:9], refs[9:]
    mine, other, dhn, down = outs[:3], outs[3], outs[4], outs[5]
    for grad, w in zip(grads, (wd0, wd1)):
        grad[...] = low(against(dy_own[...], w[...]))
    dhn[...] = feed_rows(hn, grads, (wg0, wg1), (wu0, wu1), mine, other, 0)
    down[...] = matmul(mine[0][:rows, :], wd0[...]) + matmul(other[:rows, : wd1.shape[0]], wd1[...])
    for grad, w in zip(outs[6:8], (wd0, wd1)):
        grad[...] = low(against(dy_oth[...], w[...]))
    arrange(order, (dy_own, dy_oth), outs[8])


def feed_oth_body(order, hn_own, hn, g0, g1, wg0, wg1, wu0, wu1, *refs):
    outs = refs[4:]
    outs[4][...] = low(
        feed_rows(hn, (g0, g1), (wg0, wg1), (wu0, wu1), outs[:3], outs[3], hn.shape[0])
    )
    arrange(order, (hn_own, hn), outs[5])


def feed_own(order, hn, dy_own, dy_oth, gate_w, up_w, down_w):
    rows, width = hn.shape
    units = gate_w[0].shape[0]
    part = shape16(2 * rows, units)
    other = shape16(6 * rows, -(-units // 128) * 128)
    return on_chip(
        feed_own_body,
        (part,) * 3
        + (other,)
        + (shape32(rows, width),) * 2
        + (shape16(rows, units),) * 2
        + (shape16(2 * rows, width),),
        (order,),
        (hn, dy_own, dy_oth, *gate_w, *up_w, *down_w),
        "feed_own",
        limit=15,
        cost=11.0,
        scratch=(pltpu.VMEM((rows, units), jnp.bfloat16),) * 2,
    )


def feed_oth(order, hn_own, hn, grads, gate_w, up_w, parts):
    rows, width = hn.shape
    return on_chip(
        feed_oth_body,
        tuple(shape16(*part.shape) for part in parts)
        + (shape16(rows, width), shape16(2 * rows, width)),
        (order,),
        (hn_own, hn, *grads, *gate_w, *up_w, *parts),
        "feed_oth",
        aliases={9 + i: i for i in range(4)},
        limit=14,
        cost=7.0,
    )


def ff_grad(left, left_core, index, right, right_core):
    rows, units = left.shape
    mid = right.shape[1] // 2

    def body(left, left_core, right, right_core, away, kept):
        for i, out in enumerate((away, kept)):
            part = slice(i * mid, (i + 1) * mid)
            out[...] = low(
                inner_rows(left[...], right[:, part])
                + inner_rows(left_core[index * rows : (index + 1) * rows, :units], right_core[:, part])
            )

    part = shape16(units, mid)
    return on_chip(body, (part, part), (), (left, left_core, right, right_core), "ff_grad", cost=2.7)


def fold(kept, came):
    mid = kept.shape[1] // 2

    def body(kept, came, away, rest):
        away[...] = low(high(kept[:, :mid]) + high(came[:, :mid]))
        rest[...] = low(high(kept[:, mid:]) + high(came[:, mid:]))

    part = shape16(kept.shape[0], mid)
    return on_chip(body, (part, part), (), (kept, came), "fold", cost=0.3)


def fold_rows(kept, came):
    mid = kept.shape[0] // 2

    def body(kept, came, away, rest):
        away[...] = low(high(kept[:mid, :]) + high(came[:mid, :]))
        rest[...] = low(high(kept[mid:, :]) + high(came[mid:, :]))

    part = shape16(mid, kept.shape[1])
    return on_chip(body, (part, part), (), (kept, came), "fold_rows", cost=0.3)


def hidden_grad_body(order, place, dhn_own, dhn_came, hidden_far, dy_ref, gain_ref, w_far,
    grad_ref, send_ref, own_ref, away_ref, mine_ref, gains_ref, proj, hidden_ref, w_ref, sems,
):
    cols = send_ref.shape[1]
    loads = [pltpu.make_async_copy(hidden_far, hidden_ref, sems.at[2])]
    for m in (1, 0):
        there = columns(place[0] ^ m, cols)
        loads.append(pltpu.make_async_copy(w_far.at[there, :], w_ref.at[m], sems.at[m]))
    for load in loads:
        load.start()
    loads[0].wait()
    hidden = hidden_ref[...]
    scale = rms_scale(hidden)
    dhn = dhn_own[...] + high(dhn_came[...])
    gains_ref[...] = jnp.sum(dhn * hidden * scale, axis=0, keepdims=True)
    weighted = dhn * gain_ref[...]
    mean = jnp.mean(weighted * hidden, axis=-1, keepdims=True)
    grad = high(dy_ref[...]) + scale * weighted - hidden * (scale * scale * scale * mean)
    grad_ref[...] = grad
    proj[...] = low(grad)
    loads[1].wait()
    send_ref[...] = low(against(proj[...], w_ref[1]))
    loads[2].wait()
    own_ref[...] = low(against(proj[...], w_ref[0]))
    arrange_halves(order, (proj,), away_ref, mine_ref)


def hidden_grad(order, place, dhn_own, dhn_came, hidden, dy, gain, w):
    rows, width = hidden.shape
    part = shape16(rows, width // 2)
    return on_chip(
        hidden_grad_body,
        (shape32(rows, width), part, part, part, part, shape32(1, width)),
        (order, place),
        (dhn_own, dhn_came, hidden, dy, gain, w),
        "hidden_grad",
        cost=2.2,
        limit=9,
        far=(2, 5),
        scratch=(
            pltpu.VMEM((rows, width), jnp.bfloat16),
            pltpu.VMEM((rows, width), jnp.float32),
            pltpu.VMEM((2, width // 2, width), jnp.bfloat16),
            pltpu.SemaphoreType.DMA((3,)),
        ),
    )


def bucket_grad(left, left_core, rights, rights_core, place=0, total_cols=None, before=()):
    mid = left.shape[1] // 2
    cols = rights[0].shape[1]
    count = len(rights)

    def body(left, left_core, *refs):
        for i in range(count):
            part = slice(place + i * cols, place + (i + 1) * cols)
            for half, out in enumerate(refs[-2:]):
                cut = slice(half * mid, (half + 1) * mid)
                out[:, part] = low(
                    inner_rows(left[:, cut], refs[i][...])
                    + inner_rows(left_core[:, cut], refs[count + i][...])
                )

    full = shape16(mid, total_cols or cols * count)
    return on_chip(
        body,
        (full, full),
        (),
        (left, left_core, *rights, *rights_core, *before),
        "bucket_grad",
        aliases={2 + 2 * count + i: i for i in range(len(before))},
        cost=1.5,
    )


def bucket_near(row, kept, came):
    quarter, cols = kept.shape
    size = quarter // 4

    def body(row, kept, came, away, rest):
        near = row[0] & 1
        for i in range(2):
            here = pl.ds(pl.multiple_of(i * 2 * size + near * size, size), size)
            there = pl.ds(pl.multiple_of(i * 2 * size + (1 - near) * size, size), size)
            part = slice(i * size, (i + 1) * size)
            away[part, :] = low(high(kept[there, :]) + high(came[there, :]))
            rest[part, :] = low(high(kept[here, :]) + high(came[here, :]))

    half = shape16(2 * size, cols)
    return on_chip(body, (half, half), (row,), (kept, came), "bucket_near", cost=0.3)


def shares_body(d_a, d_b, fa, fb, w_ref, x_own, x_oth, gain_two, send_ref, own_ref, gains_ref):
    rows, width = x_own.shape
    cut = d_a.shape[1]
    sums = None
    for m, x_ref in ((1, x_oth), (0, x_own)):
        part = slice(m * rows, (m + 1) * rows)
        share = against(d_a[part, :], w_ref[:, :cut]) + against(d_b[part, :], w_ref[:, cut:])
        if m:
            send_ref[:, :width] = low(share)
        else:
            own_ref[...] = share
        x = high(x_ref[...])
        here = jnp.sum(share * (x * rms_scale(x)), axis=0, keepdims=True)
        sums = here if sums is None else sums + here
    send_ref[:, width : width + fa.shape[1]] = fa[...]
    send_ref[:, width + fa.shape[1] :] = fb[...]
    gains_ref[0:1, :] = sums
    gains_ref[1:2, :] = gain_two[...]


def shares(d_a, d_b, fa, fb, w, x_own, x_oth, gain_two):
    rows, width = x_own.shape
    return on_chip(
        shares_body,
        (shape16(rows, width + 2 * fa.shape[1]), shape32(rows, width), shape32(2, width)),
        (),
        (d_a, d_b, fa, fb, w, x_own, x_oth, gain_two),
        "shares",
        cost=2.3,
    )


def input_grad_body(place, share_ref, came_ref, grad_ref, x_ref, gain_ref, fa, fb, out_ref, first_ref):
    width = x_ref.shape[1]
    x = high(x_ref[...])
    scale = rms_scale(x)
    weighted = (share_ref[...] + high(came_ref[:, :width])) * gain_ref[...]
    mean = jnp.mean(weighted * x, axis=-1, keepdims=True)
    out_ref[...] = grad_ref[...] + scale * weighted - x * (scale * scale * scale * mean)
    cols = fa.shape[1]
    own = 2 * place[0]
    oth = 2 - own
    first_ref[:, columns(own, cols)] = fa[...]
    first_ref[:, columns(own + 1, cols)] = fb[...]
    first_ref[:, columns(oth, cols)] = came_ref[:, width : width + cols]
    first_ref[:, columns(oth + 1, cols)] = came_ref[:, width + cols :]


def input_grad(place, share, came, grad_hidden, x, gain, fa, fb):
    return on_chip(
        input_grad_body,
        (shape32(*x.shape), shape16(*x.shape)),
        (place,),
        (share, came, grad_hidden, x, gain, fa, fb),
        "input_grad",
        cost=2.0,
        limit=6,
    )


def after(first, *values):
    return lax.optimization_barrier((first, *values))[1:]


def two_groups(
    inputs,
    first_values,
    lengths,
    gain_attn,
    w_qkv,
    w_out,
    gain_mlp,
    w_gate,
    w_up,
    w_down,
    cotangent,
):
    SITES.clear()
    rows = inputs.shape[1]
    width = inputs.shape[2]
    span = 2 * rows
    out_cols = HEADS // 2 * HD
    packed_cols = 3 * out_cols
    mid = width // 2
    h = lax.axis_index("head")
    f = lax.axis_index("ffn")
    r = lax.axis_index("row")
    row_size = lax.axis_size("row")
    place = jnp.stack([h, lengths[0]]).astype(jnp.int32)
    row = r.reshape(1).astype(jnp.int32)
    tie = lax.optimization_barrier
    gain_attn = gain_attn.reshape(1, width)
    gain_mlp = gain_mlp.reshape(1, width)

    x_own = inputs[0]
    x_oth = swap(x_own, "head", 1)
    early_own = lax.dynamic_slice_in_dim(first_values[0], h * out_cols, out_cols, 1)
    early_oth = swap(
        lax.dynamic_slice_in_dim(first_values[0], (1 - h) * out_cols, out_cols, 1), "head", 1
    )
    dy_own = cotangent[0]
    down_core = swap(w_down, "ffn", 1)
    gate_core = swap(w_gate.T, "ffn", 1)
    up_core = swap(w_up.T, "ffn", 1)
    qkv_w = lax.dynamic_slice_in_dim(w_qkv, h * packed_cols, packed_cols, 1)
    half = HD // 2
    inverse = jnp.exp(-jnp.log(10000.0) * jnp.arange(half, dtype=jnp.float32) * 2.0 / HD)
    angles = jnp.arange(span, dtype=jnp.float32)[:, None] * jnp.tile(inverse, 4)[None, :]
    cosine = jnp.cos(angles)
    sign = jnp.where(jnp.arange(2 * HD) % HD < half, -1.0, 1.0)
    sine = jnp.sin(angles) * sign[None, :]

    ff_order = jnp.stack([(h ^ a) * row_size + (r ^ b) for a in (1, 0) for b in (3, 1, 2, 0)])
    down_order = jnp.stack([(h ^ a) * row_size + (r ^ b) for b in (3, 1, 2, 0) for a in (1, 0)])
    att_order = jnp.stack(
        [((f ^ a) * row_size + (r & 2 ^ b)) // 2 for a in (3, 1, 2, 0) for b in (2, 0)]
    )

    xn_away, xn_mine, packed_own = project(att_order, x_own, gain_attn, qkv_w)
    x_oth, packed_own, cosine, sine, early_own, down_core, gate_core, up_core = tie(
        (x_oth, packed_own, cosine, sine, early_own, down_core, gate_core, up_core)
    )
    xn_away, xn_mine, packed_oth = project(att_order, x_oth, gain_attn, qkv_w, (xn_away, xn_mine))
    att_own, att_oth, query, keys, mixed, log_sums = attend_forward(
        place, packed_own, packed_oth, early_own, early_oth, cosine, sine
    )
    att_came = swap(att_oth, "head", 1)
    (dy_send,) = after(att_own, dy_own)
    dy_oth = swap(dy_send, "ffn", 2)
    down_w = (w_down, down_core)
    gate_w = (w_gate.T, gate_core)
    up_w = (w_up.T, up_core)
    hidden, hn_own = finish(place, x_own, att_own, att_came, w_out, gain_mlp)
    hn_oth = swap(hn_own, "ffn", 2)
    dy_send, dy_oth = after(hn_own, dy_send, dy_oth)
    dyc_own = swap(dy_send, "ffn", 1)
    dyc_oth = swap(dy_oth, "ffn", 1)
    hnc_own = swap(hn_own, "ffn", 1)

    *parts, dhn_own, down_own, dact0, dact1, dy_all = feed_own(
        down_order, hn_own, dy_own, dy_oth, gate_w, up_w, down_w
    )
    hn_oth, parts, dhn_own, down_own, dact0, dact1, dy_all, hnc_own, dyc_own, dyc_oth = tie(
        (hn_oth, parts, dhn_own, down_own, dact0, dact1, dy_all, hnc_own, dyc_own, dyc_oth)
    )
    hnc_oth = swap(hn_oth, "ffn", 1)
    act, gate, up, others, dhn_send, hn_all = feed_oth(
        ff_order, hn_own, hn_oth, (dact0, dact1), gate_w, up_w, parts
    )
    dhn_came = swap(dhn_send, "ffn", 2)
    others_core = swap(others, "ffn", 1)
    own_send, came_send = after(dhn_send, att_own, att_came)
    att_core = swap(own_send, "ffn", 1)
    came_core = swap(came_send, "ffn", 1)
    hnc_oth, dyc_own, dyc_oth = after(dhn_send, hnc_oth, dyc_own, dyc_oth)
    dyc_all = reorder(down_order, dyc_own, dyc_oth)
    hnc_all = reorder(ff_order, hnc_own, hnc_oth)

    down_send, down_kept = ff_grad(act, others_core, 0, dy_all, dyc_all)
    down_near = swap(down_send, "row", 1)
    gate_send, gate_kept = ff_grad(gate, others_core, 1, hn_all, hnc_all)
    up_send, up_kept = ff_grad(up, others_core, 2, hn_all, hnc_all)
    dhn_came, up_send, up_kept, gate_send, gate_kept, down_kept = tie(
        (dhn_came, up_send, up_kept, gate_send, gate_kept, down_kept)
    )

    grad_hidden, go_send, go_own, proj_away, proj_mine, gain_two = hidden_grad(
        att_order, place, dhn_own, dhn_came, hidden, dy_own, gain_mlp, w_out
    )
    go_oth = swap(go_send, "head", 1)
    proj_core = swap(proj_away, "ffn", 1)
    (gate_send,) = after(go_send, gate_send)
    gate_x = swap(gate_send, "head", 1)
    out_send, out_kept = bucket_grad(
        proj_mine, proj_core, (att_own, att_came), (att_core, came_core)
    )
    out_y = swap(out_send, "ffn", 2)
    go_oth, out_kept = tie((go_oth, out_kept))

    def backward(pairs, lse):
        return attend_backward(
            place, query, keys, mixed, lse, go_own, go_oth, att_own, att_oth, cosine, sine, pairs
        )

    pairs = HEADS // 4
    d_a, fa_own, fa_oth = backward((0, pairs // 2), log_sums)
    out_kept, down_kept = after(d_a, out_kept, down_kept)
    out_send, out_kept = bucket_near(row, out_kept, out_y)
    out_near = swap(out_send, "row", 1)
    down_send, down_kept = fold(down_kept, down_near)
    down_mid = swap(down_send, "row", 2)
    d_a, out_kept, down_kept, log_sums = tie((d_a, out_kept, down_kept, log_sums))
    core_a = swap(d_a, "ffn", 1)
    xn_core = swap(after(out_kept, xn_away)[0], "ffn", 1)
    d_b, fb_own, fb_oth = backward((pairs // 2, pairs), log_sums)
    gate_kept, out_kept = after(d_b, gate_kept, out_kept)
    gate_send, gate_kept = fold(gate_kept, gate_x)
    out_send, out_kept = fold_rows(out_kept, out_near)
    d_b, gate_kept, out_kept = tie((d_b, gate_kept, out_kept))
    core_b = swap(d_b, "ffn", 1)
    up_x = swap(after(gate_kept, up_send)[0], "head", 1)
    (d_a,) = after(gate_kept, d_a)
    before = bucket_grad(xn_mine, xn_core, (d_a,), (core_a,), 0, packed_cols)
    core_b, *before = tie((core_b, *before))
    y_send, kept = bucket_grad(
        xn_mine, xn_core, (d_b,), (core_b,), packed_cols // 2, packed_cols, before
    )
    y_came = swap(y_send, "ffn", 2)
    d_a, d_b = after(y_send, d_a, d_b)
    back_send, share_own, gains = shares(
        d_a, d_b, fa_oth, fb_oth, qkv_w, x_own, x_oth, gain_two
    )
    gate_send, out_send, act, others = after(back_send, gate_send, out_send, act, others)
    gate_near = swap(gate_send, "row", 1)
    out_far = swap(out_send, "row", 2)
    units = w_down.shape[0]
    far_send = low(matmul(act[rows:], down_w[0]) + matmul(others[rows:span, :units], down_w[1]))
    up_kept, down_kept, gate_kept = after(far_send, up_kept, down_kept, gate_kept)
    up_send, up_kept = fold(up_kept, up_x)
    down_send, down_kept = fold(down_kept, down_mid)
    gains, back_send, up_kept, down_kept = tie((gains, back_send, up_kept, down_kept))
    gains_x = swap(gains, "head", 1)
    back_came = swap(after(gains, back_send)[0], "head", 1)
    gains = gains + gains_x
    gains = gains + swap(gains, "ffn", 1)
    gains_y = swap(gains, "ffn", 2)
    gate_kept, up_send, out_kept = after(gains, gate_kept, up_send, out_kept)
    gate_send, gate_kept = fold(gate_kept, gate_near)
    up_near = swap(up_send, "row", 1)
    out_sum = high(out_kept) + high(out_far)
    gate_far = swap(gate_send, "row", 2)
    kept, gate_kept, out_sum = tie((kept, gate_kept, out_sum))

    near_send, kept = bucket_near(row, kept, y_came)
    near_came = swap(near_send, "row", 1)
    gains, up_kept, far_send, down_send = after(near_send, gains, up_kept, far_send, down_send)
    gains = gains + gains_y
    gains_near = swap(gains, "row", 1)
    far_came = swap(far_send, "ffn", 2)
    up_send, up_kept = fold(up_kept, up_near)
    up_far = swap(up_send, "row", 2)
    gate_kept, out_sum = after(up_send, gate_kept, out_sum)
    sum_gate = high(gate_kept) + high(gate_far)
    out_x = swap(low(out_sum[:, out_cols:]), "head", 1)
    kept, up_kept, sum_gate, gains = tie((kept, up_kept, sum_gate, gains))
    qkv_send, kept = fold_rows(kept, near_came)
    qkv_far = swap(qkv_send, "row", 2)
    down_x = swap(after(qkv_send, down_send)[0], "head", 1)
    share_own, up_kept, down_kept, out_sum, residual, gains = after(
        qkv_send, share_own, up_kept, down_kept, out_sum[:, :out_cols], hidden + down_own, gains
    )
    gains = gains + gains_near
    gains_far = swap(gains, "row", 2)
    grad_in, grad_first = input_grad(
        place, share_own, back_came, grad_hidden, x_own, gain_attn, fa_own, fb_own
    )
    sum_down = high(down_kept) + high(down_x)
    sum_up = high(up_kept) + high(up_far)
    out_sum = out_sum + high(out_x)
    output = low(residual + high(far_came))[None]
    kept, grad_in, sum_up, sum_down, out_sum, output = tie(
        (kept, grad_in, sum_up, sum_down, out_sum, output)
    )
    sum_qkv = high(kept) + high(qkv_far)
    gains = gains + gains_far
    return (
        output,
        grad_in[None],
        grad_first[None],
        gains[0],
        sum_qkv,
        out_sum.T,
        gains[1],
        sum_gate.T,
        sum_up.T,
        sum_down,
    )


def solution(mesh):
    in_specs = (
        P(("ffn", "row"), "head", None),
        P(("ffn", "row"), "head", None),
        P(("ffn", "row")),
        P(),
        P(),
        P(),
        P(),
        P(None, "ffn"),
        P(None, "ffn"),
        P("ffn", None),
        P(("ffn", "row"), "head", None),
    )
    out_specs = (
        P(("ffn", "row"), "head", None),
        P(("ffn", "row"), "head", None),
        P(("ffn", "row"), "head", None),
        P(),
        P(("ffn", "row"), "head"),
        P("head", ("ffn", "row")),
        P(),
        P(("head", "row"), "ffn"),
        P(("head", "row"), "ffn"),
        P("ffn", ("head", "row")),
    )
    body = two_groups if mesh.shape["head"] == 2 and mesh.shape["ffn"] == 4 else any_groups
    return jax.shard_map(
        body, mesh=mesh, in_specs=in_specs, out_specs=out_specs, check_vma=False
    )
```

```python
import functools

import jax
import jax.numpy as jnp
from jax import lax
from jax.experimental import pallas as pl
from jax.experimental.pallas import tpu as pltpu
from jax.sharding import PartitionSpec as P

HEADS = 16
HD = 64
MIN_LEN = 512
STEP = 256


eps = 1e-06


def rms_scale(values):
    return lax.rsqrt(jnp.mean(values * values, axis=-1, keepdims=True) + eps)


def matmul(left, right):
    return jnp.dot(left, right, preferred_element_type=jnp.float32)


def inner_rows(left, right):
    return lax.dot_general(
        left, right, (((0,), (0,)), ((), ())), preferred_element_type=jnp.float32
    )


def against(left, right):
    return lax.dot_general(
        left, right, (((1,), (1,)), ((), ())), preferred_element_type=jnp.float32
    )


def swap(values, axis, mask):
    size = lax.axis_size(axis)
    return lax.ppermute(values, axis, [(i, i ^ mask) for i in range(size)])


def bits_of(axis):
    size = lax.axis_size(axis)
    return [1 << b for b in range(size.bit_length() - 2, -1, -1)]


def halve(values, dim, axis, mask):
    bit = (lax.axis_index(axis) // mask) % 2
    away = lax.dynamic_index_in_dim(values, 1 - bit, dim, keepdims=False)
    kept = lax.dynamic_index_in_dim(values, bit, dim, keepdims=False)
    came = swap(away.astype(jnp.bfloat16), axis, mask)
    return kept.astype(jnp.float32) + came.astype(jnp.float32)


def total(values, axes):
    for axis in axes:
        for mask in reversed(bits_of(axis)):
            values = values + swap(values, axis, mask)
    return values


def rotary(positions, head_size):
    half_size = head_size // 2
    inverse = jnp.exp(
        -jnp.log(10000.0) * jnp.arange(half_size, dtype=jnp.float32) * 2.0 / head_size
    )
    angles = positions.astype(jnp.float32)[:, None] * inverse[None, :]
    return (jnp.cos(angles), jnp.sin(angles))


def rotate(vectors, cosine, sine, sign):
    half_size = vectors.shape[-1] // 2
    first_half = vectors[..., :half_size]
    second_half = vectors[..., half_size:]
    cos_rows = cosine[:, None, :]
    sin_rows = sign * sine[:, None, :]
    return jnp.concatenate(
        [
            first_half * cos_rows - second_half * sin_rows,
            second_half * cos_rows + first_half * sin_rows,
        ],
        axis=-1,
    )


def masked_scores(q_rows, keys, q_pos, k_pos, valid):
    raw = jnp.einsum("qhe,khe->hqk", q_rows, keys, preferred_element_type=jnp.float32)
    allowed = (k_pos[None, :] <= q_pos[:, None]) & (k_pos[None, :] < valid)
    return jnp.where(allowed[None], 0.125 * raw, -1e30)


def scan_forward(query, keys, mixed, positions, valid, block_rows):
    count = query.shape[0] // block_rows

    def step(carry, index):
        start = index * block_rows
        q_rows = lax.dynamic_slice_in_dim(query, start, block_rows, 0)
        q_pos = lax.dynamic_slice_in_dim(positions, start, block_rows, 0)
        scores = masked_scores(q_rows, keys, q_pos, positions, valid)
        top = jnp.max(scores, axis=-1, keepdims=True)
        expo = jnp.exp(scores - top)
        total_w = jnp.sum(expo, axis=-1, keepdims=True)
        weights = expo / total_w
        result = jnp.einsum(
            "hqk,khe->qhe", weights.astype(jnp.bfloat16), mixed, preferred_element_type=jnp.float32
        )
        return (carry, (result.astype(jnp.bfloat16), top + jnp.log(total_w)))

    _, (outs, log_sums) = lax.scan(step, 0, jnp.arange(count, dtype=jnp.int32))
    return (outs.reshape(query.shape), log_sums)


def scan_backward(query, keys, mixed, positions, valid, log_sums, grad_out, block_rows):
    count = query.shape[0] // block_rows
    zeros = jnp.zeros(keys.shape, jnp.float32)

    def step(carry, index):
        key_sum, value_sum = carry
        start = index * block_rows
        q_rows = lax.dynamic_slice_in_dim(query, start, block_rows, 0)
        q_pos = lax.dynamic_slice_in_dim(positions, start, block_rows, 0)
        g_rows = lax.dynamic_slice_in_dim(grad_out, start, block_rows, 0)
        scores = masked_scores(q_rows, keys, q_pos, positions, valid)
        weights = jnp.exp(scores - log_sums[index])
        grad_w = jnp.einsum("qhe,khe->hqk", g_rows, mixed, preferred_element_type=jnp.float32)
        delta = jnp.sum(weights * grad_w, axis=-1, keepdims=True)
        grad_s = (weights * (grad_w - delta)).astype(jnp.bfloat16)
        grad_q = 0.125 * jnp.einsum(
            "hqk,khe->qhe", grad_s, keys, preferred_element_type=jnp.float32
        )
        key_sum = key_sum + 0.125 * jnp.einsum(
            "hqk,qhe->khe", grad_s, q_rows, preferred_element_type=jnp.float32
        )
        value_sum = value_sum + jnp.einsum(
            "hqk,qhe->khe", weights.astype(jnp.bfloat16), g_rows, preferred_element_type=jnp.float32
        )
        return ((key_sum, value_sum), grad_q)

    (grad_keys, grad_mixed), grad_query = lax.scan(
        step, (zeros, zeros), jnp.arange(count, dtype=jnp.int32)
    )
    return (grad_query.reshape(query.shape), grad_keys, grad_mixed)


def any_groups(
    inputs,
    first_values,
    lengths,
    gain_attn,
    w_qkv,
    w_out,
    gain_mlp,
    w_gate,
    w_up,
    w_down,
    cotangent,
):
    rows = inputs.shape[1]
    width = inputs.shape[2]
    groups = lax.axis_size("head")
    shards = lax.axis_size("ffn")
    heads_here = HEADS // groups
    span_rows = rows * groups
    block_rows = span_rows // max(1, span_rows // 512)
    head_pos = lax.axis_index("head")
    valid_len = lengths[0]
    packed_cols = heads_here * 3 * HD
    out_cols = heads_here * HD
    hidden_here = w_gate.shape[1]

    owners = [head_pos ^ m for m in range(groups)]
    x_all = [inputs[0]] + [swap(inputs[0], "head", m) for m in range(1, groups)]
    early = []
    for m in range(groups):
        piece = lax.dynamic_slice_in_dim(first_values[0], owners[m] * out_cols, out_cols, 1)
        early.append(swap(piece, "head", m) if m else piece)
    far = range(2, shards, 2)
    grad_rows = jnp.concatenate([cotangent[0]] + [swap(cotangent[0], "ffn", m) for m in far], 0)
    gate_w = jnp.concatenate([w_gate, swap(w_gate, "ffn", 1)], 1)
    up_w = jnp.concatenate([w_up, swap(w_up, "ffn", 1)], 1)
    down_w = jnp.concatenate([w_down, swap(w_down, "ffn", 1)], 0)
    w_heads = lax.dynamic_slice_in_dim(w_qkv, head_pos * packed_cols, packed_cols, 1)
    out_w = jnp.concatenate(
        [lax.dynamic_slice_in_dim(w_out, o * out_cols, out_cols, 0) for o in owners], 0
    )

    positions = jnp.concatenate([o * rows + jnp.arange(rows, dtype=jnp.int32) for o in owners])
    cosine, sine = rotary(positions, HD)
    normed, scaled, queries, key_list, mixes = [], [], [], [], []
    rows_in = inputs[0].astype(jnp.float32)
    scale_one = rms_scale(rows_in)
    for m in range(groups):
        block = x_all[m].astype(jnp.float32)
        scale = rms_scale(block)
        scaled.append(block * scale)
        normed.append((block * scale * gain_attn).astype(jnp.bfloat16))
        packed = matmul(normed[m], w_heads).astype(jnp.bfloat16)
        packed = packed.reshape(rows, heads_here, 3, HD).astype(jnp.float32)
        part = slice(m * rows, (m + 1) * rows)
        queries.append(rotate(packed[:, :, 0], cosine[part], sine[part], 1.0))
        key_list.append(rotate(packed[:, :, 1], cosine[part], sine[part], 1.0))
        value = early[m].reshape(rows, heads_here, HD).astype(jnp.float32)
        mixes.append(0.5 * (packed[:, :, 2] + value))
    query = jnp.concatenate(queries, 0).astype(jnp.bfloat16)
    keys = jnp.concatenate(key_list, 0).astype(jnp.bfloat16)
    mixed = jnp.concatenate(mixes, 0).astype(jnp.bfloat16)
    attended, log_sums = scan_forward(query, keys, mixed, positions, valid_len, block_rows)
    attended = attended.reshape(groups, rows, out_cols)
    att_own = jnp.concatenate(
        [attended[0]] + [swap(attended[m], "head", m) for m in range(1, groups)], 1
    )
    hidden = rows_in + matmul(att_own, out_w)
    scale_two = rms_scale(hidden)
    normed_two = (hidden * scale_two * gain_mlp).astype(jnp.bfloat16)

    mlp_rows = [normed_two] + [swap(normed_two, "ffn", m) for m in far]
    grad_list = [grad_rows[i * rows : (i + 1) * rows] for i in range(len(mlp_rows))]
    actives, grad_gates, grad_ups, downs, grad_normed_list = [], [], [], [], []
    for i, block in enumerate(mlp_rows):
        gate_rows = matmul(block, gate_w)
        up_rows = matmul(block, up_w)
        sigmoid_gate = jax.nn.sigmoid(gate_rows)
        silu_gate = gate_rows * sigmoid_gate
        grad_active = against(grad_list[i], down_w)
        actives.append((silu_gate * up_rows).astype(jnp.bfloat16))
        grad_gates.append(
            (
                grad_active * up_rows * sigmoid_gate * (1.0 + gate_rows * (1.0 - sigmoid_gate))
            ).astype(jnp.bfloat16)
        )
        grad_ups.append((grad_active * silu_gate).astype(jnp.bfloat16))
        grad_normed_list.append(against(grad_gates[i], gate_w) + against(grad_ups[i], up_w))
        downs.append(matmul(actives[i], down_w))
    grad_normed_two = grad_normed_list[0]
    for i, m in enumerate(far):
        came = swap(grad_normed_list[i + 1].astype(jnp.bfloat16), "ffn", m)
        grad_normed_two = grad_normed_two + came.astype(jnp.float32)
    down_rows = downs[0]
    for i, m in enumerate(far):
        down_rows = down_rows + swap(downs[i + 1].astype(jnp.bfloat16), "ffn", m).astype(jnp.float32)
    output = (hidden + down_rows).astype(jnp.bfloat16)[None]

    all_rows = jnp.concatenate(mlp_rows, 0)
    ff_sums = []
    for left, right in (
        (grad_rows, jnp.concatenate(actives, 0)),
        (all_rows, jnp.concatenate(grad_gates, 0)),
        (all_rows, jnp.concatenate(grad_ups, 0)),
    ):
        away = inner_rows(left, right[:, hidden_here:]).astype(jnp.bfloat16)
        part = inner_rows(left, right[:, :hidden_here])
        part = (part + swap(away, "ffn", 1).astype(jnp.float32)).astype(jnp.bfloat16)
        steps = [("head", b) for b in bits_of("head")] + [("row", b) for b in bits_of("row")]
        part = part.reshape([2] * len(steps) + [-1, hidden_here])
        order = [s for s in steps if s[0] == "head"] + [s for s in reversed(steps) if s[0] == "row"]
        left_steps = list(steps)
        for s in order:
            part = halve(part, left_steps.index(s), *s)
            left_steps.remove(s)
            if left_steps:
                part = part.astype(jnp.bfloat16)
        ff_sums.append(part)
    sum_down, sum_gate, sum_up = ff_sums

    grad_y = cotangent[0].astype(jnp.float32)
    grad_gain_two = jnp.sum(grad_normed_two * hidden * scale_two, axis=0)
    weighted_two = grad_normed_two * gain_mlp
    cube_two = scale_two * scale_two * scale_two
    grad_hidden = (
        grad_y
        + scale_two * weighted_two
        - hidden * cube_two * jnp.mean(weighted_two * hidden, axis=-1, keepdims=True)
    )
    grad_proj = grad_hidden.astype(jnp.bfloat16)
    grad_att = against(grad_proj, out_w).astype(jnp.bfloat16)
    grad_att = jnp.concatenate(
        [
            swap(grad_att[:, m * out_cols : (m + 1) * out_cols], "head", m)
            if m
            else grad_att[:, :out_cols]
            for m in range(groups)
        ],
        0,
    ).reshape(span_rows, heads_here, HD)

    def over_buckets(part):
        steps = [("ffn", b) for b in bits_of("ffn")] + [("row", b) for b in bits_of("row")]
        part = part.astype(jnp.bfloat16).reshape([2] * len(steps) + [-1, part.shape[1]])
        order = [s for s in reversed(steps) if s[0] == "ffn"] + [
            s for s in reversed(steps) if s[0] == "row"
        ]
        left_steps = list(steps)
        for s in order:
            part = halve(part, left_steps.index(s), *s)
            left_steps.remove(s)
            if left_steps:
                part = part.astype(jnp.bfloat16)
        return part

    part = over_buckets(inner_rows(grad_proj, att_own))
    sum_out = part[:, :out_cols]
    for m in range(1, groups):
        came = swap(part[:, m * out_cols : (m + 1) * out_cols].astype(jnp.bfloat16), "head", m)
        sum_out = sum_out + came.astype(jnp.float32)

    grad_query, grad_keys, grad_mixed = scan_backward(
        query, keys, mixed, positions, valid_len, log_sums, grad_att, block_rows
    )
    grad_packed = jnp.stack(
        [
            rotate(grad_query, cosine, sine, -1.0),
            rotate(grad_keys, cosine, sine, -1.0),
            0.5 * grad_mixed,
        ],
        axis=2,
    )
    grad_packed = grad_packed.astype(jnp.bfloat16).reshape(span_rows, packed_cols)
    grad_early = (0.5 * grad_mixed).astype(jnp.bfloat16).reshape(span_rows, out_cols)
    firsts = [grad_early[m * rows : (m + 1) * rows] for m in range(groups)]
    firsts = [swap(firsts[m], "head", m) if m else firsts[0] for m in range(groups)]
    grad_first = jnp.zeros((rows, width), jnp.bfloat16)
    for m in range(groups):
        grad_first = lax.dynamic_update_slice_in_dim(grad_first, firsts[m], owners[m] * out_cols, 1)
    shares = [
        against(grad_packed[m * rows : (m + 1) * rows], w_heads) for m in range(groups)
    ]
    grad_gain_one = sum(jnp.sum(shares[m] * scaled[m], axis=0) for m in range(groups))
    grad_normed = shares[0]
    for m in range(1, groups):
        grad_normed = grad_normed + swap(shares[m].astype(jnp.bfloat16), "head", m).astype(jnp.float32)
    sum_qkv = over_buckets(inner_rows(jnp.concatenate(normed, 0), grad_packed))
    weighted_one = grad_normed * gain_attn
    cube_one = scale_one * scale_one * scale_one
    grad_in = (
        grad_hidden
        + scale_one * weighted_one
        - rows_in * cube_one * jnp.mean(weighted_one * rows_in, axis=-1, keepdims=True)
    )
    gains = total(jnp.stack([grad_gain_one, grad_gain_two]), ("ffn", "head", "row"))
    return (
        output,
        grad_in[None],
        grad_first[None],
        gains[0],
        sum_qkv,
        sum_out.T,
        gains[1],
        sum_gate,
        sum_up,
        sum_down.T,
    )


SCALE = 4.5e8
COSTS = {}
SITES = {}


def site_cost(name, usual):
    count = SITES.get(name, 0)
    SITES[name] = count + 1
    return int(SCALE * COSTS.get(name + str(count), usual))


def low(values):
    return values.astype(jnp.bfloat16)


def high(values):
    return values.astype(jnp.float32)


def on_chip(body, outs, scalars, arrays, name, scratch=(), aliases=None, limit=3, cost=1.0, away=(), far=()):
    inside = pl.BlockSpec(memory_space=pltpu.VMEM)
    outside = pl.BlockSpec(memory_space=pl.ANY)
    return pl.pallas_call(
        body,
        out_shape=jax.tree.unflatten(
            jax.tree.structure(outs),
            [
                pltpu.HBM(o.shape, o.dtype) if i in away else o
                for i, o in enumerate(jax.tree.leaves(outs))
            ],
        ),
        in_specs=[pl.BlockSpec(memory_space=pltpu.SMEM)] * len(scalars)
        + [outside if i in far else inside for i in range(len(arrays))],
        out_specs=jax.tree.unflatten(
            jax.tree.structure(outs),
            [
                outside if i in away else inside
                for i in range(len(jax.tree.leaves(outs)))
            ],
        ),
        scratch_shapes=list(scratch),
        input_output_aliases=aliases or {},
        cost_estimate=pl.CostEstimate(
            flops=site_cost(name, cost), transcendentals=0, bytes_accessed=1
        ),
        compiler_params=pltpu.CompilerParams(vmem_limit_bytes=limit << 20),
        name=name,
    )(*scalars, *arrays)


def shape16(*dims):
    return jax.ShapeDtypeStruct(dims, jnp.bfloat16)


def shape32(*dims):
    return jax.ShapeDtypeStruct(dims, jnp.float32)


def spans(total):
    return [(a, min(a + STEP, total)) for a in range(0, total, STEP)]


def turn(values):
    lane = lax.broadcasted_iota(jnp.int32, values.shape, 1)
    return jnp.where(
        lane % HD < HD // 2, pltpu.roll(values, 2 * HD - HD // 2, 1), pltpu.roll(values, HD // 2, 1)
    )


def allowed_keys(a, b, valid):
    size = b - a
    down = lax.broadcasted_iota(jnp.int32, (size, size), 0)
    across = lax.broadcasted_iota(jnp.int32, (size, size), 1)
    allowed = down <= across
    if b > MIN_LEN:
        allowed = allowed & (down < valid - a)
    return allowed


def columns(index, size):
    return pl.ds(pl.multiple_of(index * size, size), size)


def forward_body(
    place, packed_own, packed_oth, early_own, early_oth, cos_ref, sin_ref,
    own_far, oth_far, q_far, k_far, v_far, lse_out,
    att_own, att_oth, q_out, k_out, v_out, flipped, att, sems,
):
    rows = packed_own.shape[0]
    span = 2 * rows
    wide = 2 * HD
    valid = place[1]
    f32 = jnp.float32
    bf = jnp.bfloat16
    first = lax.broadcasted_iota(jnp.int32, (1, wide), 1) < HD
    flipped[:, HD:, :] = jnp.ones((2, 16, span), bf)

    def copies(p):
        cols = columns(p, wide)
        return [
            pltpu.make_async_copy(near.at[:, cols], far.at[:, cols], sems.at[i, p])
            for i, (near, far) in enumerate(
                (
                    (q_out, q_far),
                    (k_out, k_far),
                    (v_out, v_far),
                    (att_oth, oth_far),
                    (att_own, own_far),
                )
            )
        ]

    def pair(p, _):
        cols = columns(p, wide)
        for m, (packed, early) in enumerate(((packed_own, early_own), (packed_oth, early_oth))):
            here = columns(place[0] ^ m, rows)
            x0 = high(packed[:, pl.ds(pl.multiple_of(p * 3 * wide, wide), wide)])
            x1 = high(packed[:, pl.ds(pl.multiple_of(p * 3 * wide + wide, wide), wide)])
            x2 = high(packed[:, pl.ds(pl.multiple_of(p * 3 * wide + 2 * wide, wide), wide)])
            cosine = cos_ref[here, :]
            sine = sin_ref[here, :]
            q = jnp.where(first, x0, x1)
            k = pltpu.roll(jnp.where(first, x2, x0), HD, 1)
            v = jnp.where(first, x1, x2)
            q_out[here, cols] = low(q * cosine + turn(q) * sine)
            k_out[here, cols] = low(k * cosine + turn(k) * sine)
            v_out[here, cols] = low(0.5 * (v + high(early[:, cols])))
        for copy in copies(p)[:3]:
            copy.start()
        turned = v_out[:, cols].T
        for e in range(2):
            flipped[e, :HD, :] = turned[e * HD : (e + 1) * HD, :]
        for a, b in spans(span):
            q = q_out[a:b, cols] * jnp.asarray(0.125, bf)
            allowed = allowed_keys(a, b, valid)
            for e in range(2):
                qe = jnp.where(first == (e == 0), q, jnp.zeros_like(q))
                diag = jnp.where(allowed, against(k_out[a:b, cols], qe), -1e30)
                top = jnp.max(diag, axis=0, keepdims=True)
                if a:
                    past = against(k_out[:a, cols], qe)
                    top = jnp.maximum(top, jnp.max(past, axis=0, keepdims=True))
                out = matmul(flipped[e, :, a:b], low(jnp.exp(diag - top)))
                if a:
                    out = out + matmul(flipped[e, :, :a], low(jnp.exp(past - top)))
                amount = out[HD : HD + 1, :]
                att[e * HD : (e + 1) * HD, a:b] = out[:HD, :] / amount
                lse_out[p, e : e + 1, a:b] = top + jnp.log(amount)
        result = low(att[...].T)
        upper = place[0] == 0
        att_own[:, cols] = jnp.where(upper, result[:rows, :], result[rows:, :])
        att_oth[:, cols] = jnp.where(upper, result[rows:, :], result[:rows, :])
        for copy in copies(p)[3:]:
            copy.start()
        return 0

    lax.fori_loop(0, lse_out.shape[0], pair, 0)
    for p in range(lse_out.shape[0]):
        for copy in copies(p):
            copy.wait()


def attend_forward(place, packed_own, packed_oth, early_own, early_oth, cosine, sine):
    rows, cols = packed_own.shape
    heads = cols // (3 * HD)
    span = 2 * rows
    out = shape16(rows, heads * HD)
    natural = shape16(span, heads * HD)
    return on_chip(
        forward_body,
        (out, out, natural, natural, natural, shape32(heads // 2, 2, span)),
        (place,),
        (packed_own, packed_oth, early_own, early_oth, cosine, sine),
        "attend_forward",
        cost=11.0,
        limit=7,
        away=(0, 1, 2, 3, 4),
        scratch=(
            pltpu.VMEM(out.shape, jnp.bfloat16),
            pltpu.VMEM(out.shape, jnp.bfloat16),
            pltpu.VMEM(natural.shape, jnp.bfloat16),
            pltpu.VMEM(natural.shape, jnp.bfloat16),
            pltpu.VMEM(natural.shape, jnp.bfloat16),
            pltpu.VMEM((2, HD + 16, span), jnp.bfloat16),
            pltpu.VMEM((2 * HD, span), jnp.float32),
            pltpu.SemaphoreType.DMA((5, heads // 2)),
        ),
    )


def backward_body(
    start, place, q_far, k_far, v_far, lse_ref, go_own, go_oth, att_own, att_oth, cos_ref, sin_ref,
    d_out, f_own, f_oth, q_ref, k_ref, v_ref, sems, grad, prod, turned_k, dq, dk, dv,
):
    rows = go_own.shape[0]
    span = 2 * rows
    valid = place[1]
    wide = 2 * HD
    bf = jnp.bfloat16
    first = lax.broadcasted_iota(jnp.int32, (1, wide), 1) < HD
    eighth = jnp.asarray(0.125, bf)
    count = f_own.shape[1] // wide

    def copies(i):
        there = columns(i + start, wide)
        here = columns(i, wide)
        return [
            pltpu.make_async_copy(away.at[:, there], near.at[:, here], sems.at[n, i])
            for n, (away, near) in enumerate(((q_far, q_ref), (k_far, k_ref), (v_far, v_ref)))
        ]

    for i in range(count):
        for copy in copies(i):
            copy.start()

    def pair(i, _):
        p = i + start
        cols = columns(p, wide)
        near = columns(i, wide)
        for copy in copies(i):
            copy.wait()
        for m, (go, att) in enumerate(((go_own, att_own), (go_oth, att_oth))):
            here = columns(place[0] ^ m, rows)
            grad[here, :] = go[:, cols]
            prod[here, :] = high(go[:, cols]) * high(att[:, cols])
        flat = prod[...].T
        deltas = [jnp.sum(flat[e * HD : (e + 1) * HD, :], axis=0, keepdims=True) for e in range(2)]
        turned_k[...] = (k_ref[:, near] * eighth).T
        for n, (a, b) in enumerate(spans(span)):
            allowed = allowed_keys(a, b, valid)
            q = q_ref[a:b, near] * eighth
            g = grad[a:b, :]
            parts = ((a, b), (0, a)) if a else ((a, b),)
            sums = {}
            for e in range(2):
                mine = first == (e == 0)
                qe = jnp.where(mine, q, jnp.zeros_like(q))
                ge = jnp.where(mine, g, jnp.zeros_like(g))
                for lo, hi in parts:
                    scores = against(k_ref[lo:hi, near], qe)
                    if lo == a:
                        scores = jnp.where(allowed, scores, -1e30)
                    weights = jnp.exp(scores - lse_ref[p, e : e + 1, a:b])
                    grad_w = against(v_ref[lo:hi, near], ge)
                    grad_s = low(weights * (grad_w - deltas[e][:, a:b]))
                    dv_here = matmul(low(weights), ge)
                    dk_here = matmul(grad_s, qe)
                    dq_here = matmul(turned_k[e * HD : (e + 1) * HD, lo:hi], grad_s)
                    if (lo, "v") in sums:
                        dv_here = dv_here + sums[lo, "v"]
                        dk_here = dk_here + sums[lo, "k"]
                    sums[lo, "v"], sums[lo, "k"] = dv_here, dk_here
                    sums[lo, e] = dq_here
            for e in range(2):
                dq[e * HD : (e + 1) * HD, a:b] = sums[a, e] + sums[0, e] if a else sums[a, e]
            dv[a:b, :] = sums[a, "v"]
            dk[a:b, :] = sums[a, "k"]
            if a:
                dv[:a, :] += sums[0, "v"]
                dk[:a, :] += sums[0, "k"]
        prod[...] = dq[...].T
        for m, f_out in enumerate((f_own, f_oth)):
            here = columns(place[0] ^ m, rows)
            cosine = cos_ref[here, :]
            sine = sin_ref[here, :]
            gv = low(0.5 * dv[here, :])
            gk = dk[here, :]
            gk = low(pltpu.roll(gk * cosine - turn(gk) * sine, HD, 1))
            gq = prod[here, :]
            gq = low(gq * cosine - turn(gq) * sine)
            part = slice(m * rows, (m + 1) * rows)
            base = i * 3 * wide
            d_out[part, pl.ds(pl.multiple_of(base, wide), wide)] = jnp.where(first, gq, gk)
            d_out[part, pl.ds(pl.multiple_of(base + wide, wide), wide)] = jnp.where(first, gv, gq)
            d_out[part, pl.ds(pl.multiple_of(base + 2 * wide, wide), wide)] = jnp.where(first, gk, gv)
            f_out[:, columns(i, wide)] = gv
        return 0

    lax.fori_loop(0, count, pair, 0)


def attend_backward(place, q, k, v, lse, go_own, go_oth, att_own, att_oth, cosine, sine, pairs):
    span = q.shape[0]
    rows = span // 2
    wide = 2 * HD
    cols = wide * (pairs[1] - pairs[0])
    return on_chip(
        functools.partial(backward_body, pairs[0]),
        (shape16(span, 3 * cols), shape16(rows, cols), shape16(rows, cols)),
        (place,),
        (q, k, v, lse, go_own, go_oth, att_own, att_oth, cosine, sine),
        "attend_backward",
        cost=7.5,
        limit=6,
        far=(0, 1, 2),
        scratch=(
            pltpu.VMEM((span, cols), jnp.bfloat16),
            pltpu.VMEM((span, cols), jnp.bfloat16),
            pltpu.VMEM((span, cols), jnp.bfloat16),
            pltpu.SemaphoreType.DMA((3, pairs[1] - pairs[0])),
            pltpu.VMEM((span, wide), jnp.bfloat16),
            pltpu.VMEM((span, wide), jnp.float32),
            pltpu.VMEM((wide, span), jnp.bfloat16),
            pltpu.VMEM((wide, span), jnp.float32),
            pltpu.VMEM((span, wide), jnp.float32),
            pltpu.VMEM((span, wide), jnp.float32),
        ),
    )


def project_body(base, order, x_ref, gain_ref, w_ref, *refs):
    away_far, mine_far, packed_ref, xn, away, mine, sems = refs[-7:]
    rows = x_ref.shape[0]
    x = high(x_ref[...])
    xn[...] = low(x * rms_scale(x) * gain_ref[...])
    arrange_halves(order, (xn,), away, mine)
    there = slice(base, base + rows)
    copies = [
        pltpu.make_async_copy(away, away_far.at[there, :], sems.at[0]),
        pltpu.make_async_copy(mine, mine_far.at[there, :], sems.at[1]),
    ]
    for copy in copies:
        copy.start()
    cols = w_ref.shape[1] // 3
    for i in range(3):
        part = slice(i * cols, (i + 1) * cols)
        packed_ref[:, part] = low(matmul(xn[...], w_ref[:, part]))
    for copy in copies:
        copy.wait()


def project(order, x, gain, w, before=()):
    rows, width = x.shape
    part = shape16(2 * rows, width // 2)
    return pl.pallas_call(
        functools.partial(project_body, rows if before else 0),
        out_shape=(
            pltpu.HBM(part.shape, part.dtype),
            pltpu.HBM(part.shape, part.dtype),
            shape16(rows, w.shape[1]),
        ),
        in_specs=[pl.BlockSpec(memory_space=pltpu.SMEM)]
        + [pl.BlockSpec(memory_space=pltpu.VMEM)] * 3
        + [pl.BlockSpec(memory_space=pl.ANY)] * len(before),
        out_specs=(
            pl.BlockSpec(memory_space=pl.ANY),
            pl.BlockSpec(memory_space=pl.ANY),
            pl.BlockSpec(memory_space=pltpu.VMEM),
        ),
        scratch_shapes=[
            pltpu.VMEM((rows, width), jnp.bfloat16),
            pltpu.VMEM((rows, width // 2), jnp.bfloat16),
            pltpu.VMEM((rows, width // 2), jnp.bfloat16),
            pltpu.SemaphoreType.DMA((2,)),
        ],
        input_output_aliases={4 + i: i for i in range(len(before))},
        cost_estimate=pl.CostEstimate(
            flops=site_cost("project", 2.0), transcendentals=0, bytes_accessed=1
        ),
        compiler_params=pltpu.CompilerParams(vmem_limit_bytes=5 << 20),
        name="project",
    )(order, x, gain, w, *before)


def arrange(order, blocks, out):
    rows = blocks[0].shape[0]
    size = out.shape[1] // order.shape[0]
    for i in range(order.shape[0]):
        for b, block in enumerate(blocks):
            out[b * rows : (b + 1) * rows, i * size : (i + 1) * size] = block[:, columns(order[i], size)]


def finish(place, x, att_own, att_came, w, gain):
    def body(
        place, x_ref, own_far, came_far, w_far, gain_ref,
        hidden_far, hn_ref, hidden_ref, w_ref, att_ref, sems,
    ):
        cols = own_far.shape[1]
        loads = []
        for m, far in enumerate((own_far, came_far)):
            there = columns(place[0] ^ m, cols)
            loads.append(pltpu.make_async_copy(far, att_ref.at[m], sems.at[3 + m]))
            loads.append(pltpu.make_async_copy(w_far.at[there, :], w_ref.at[m], sems.at[m]))
        for load in loads:
            load.start()
        hidden = high(x_ref[...])
        for m in range(2):
            loads[2 * m].wait()
            loads[2 * m + 1].wait()
            hidden = hidden + matmul(att_ref[m], w_ref[m])
        hidden_ref[...] = hidden
        copy = pltpu.make_async_copy(hidden_ref, hidden_far, sems.at[2])
        copy.start()
        hn_ref[...] = low(hidden * rms_scale(hidden) * gain_ref[...])
        copy.wait()

    rows, width = x.shape
    return on_chip(
        body,
        (shape32(rows, width), shape16(rows, width)),
        (place,),
        (x, att_own, att_came, w, gain),
        "finish",
        cost=3.0,
        limit=8,
        away=(0,),
        far=(1, 2, 3),
        scratch=(
            pltpu.VMEM((rows, width), jnp.float32),
            pltpu.VMEM((2, width // 2, width), jnp.bfloat16),
            pltpu.VMEM((2, rows, width // 2), jnp.bfloat16),
            pltpu.SemaphoreType.DMA((5,)),
        ),
    )


def reorder(order, *blocks):
    rows, cols = blocks[0].shape

    def body(order, *refs):
        arrange(order, refs[:-1], refs[-1])

    return on_chip(body, shape16(rows * len(blocks), cols), (order,), blocks, "reorder", cost=0.9)


def arrange_halves(order, blocks, away, mine):
    rows = blocks[0].shape[0]
    count = order.shape[0] // 2
    size = mine.shape[1] // count
    for half, out in enumerate((away, mine)):
        for i in range(count):
            for b, block in enumerate(blocks):
                out[b * rows : (b + 1) * rows, i * size : (i + 1) * size] = block[
                    :, columns(order[half * count + i], size)
                ]


def reorder_halves(order, *blocks):
    rows, cols = blocks[0].shape

    def body(order, *refs):
        arrange_halves(order, refs[:-2], *refs[-2:])

    part = shape16(rows * len(blocks), cols // 2)
    return on_chip(body, (part, part), (order,), blocks, "reorder_halves", cost=0.9)


def feed_rows(hn, grads, gate_w, up_w, mine, other, base):
    rows = hn.shape[0]
    units = gate_w[0].shape[0]
    here = slice(base, base + rows)
    total_hn = None
    for s in range(2):
        gate = against(hn[...], gate_w[s][...])
        up = against(hn[...], up_w[s][...])
        grad = high(grads[s][...])
        sig = 1.0 / (1.0 + jnp.exp(-gate))
        silu = gate * sig
        results = (silu * up, grad * up * sig * (1.0 + gate * (1.0 - sig)), grad * silu)
        for i, result in enumerate(results):
            if s == 0:
                mine[i][here, :] = low(result)
            else:
                other[2 * i * rows + base : 2 * i * rows + base + rows, :units] = low(result)
    for s in range(2):
        for i, w in ((1, gate_w[s]), (2, up_w[s])):
            if s == 0:
                share = matmul(mine[i][here, :], w[...])
            else:
                share = matmul(other[2 * i * rows + base : 2 * i * rows + base + rows, :units], w[...])
            total_hn = share if total_hn is None else total_hn + share
    return total_hn


def feed_own_body(order, hn, dy_own, dy_oth, wg0, wg1, wu0, wu1, wd0, wd1, *refs):
    rows = hn.shape[0]
    outs, grads = refs[:9], refs[9:]
    mine, other, dhn, down = outs[:3], outs[3], outs[4], outs[5]
    for grad, w in zip(grads, (wd0, wd1)):
        grad[...] = low(against(dy_own[...], w[...]))
    dhn[...] = feed_rows(hn, grads, (wg0, wg1), (wu0, wu1), mine, other, 0)
    down[...] = matmul(mine[0][:rows, :], wd0[...]) + matmul(other[:rows, : wd1.shape[0]], wd1[...])
    for grad, w in zip(outs[6:8], (wd0, wd1)):
        grad[...] = low(against(dy_oth[...], w[...]))
    arrange(order, (dy_own, dy_oth), outs[8])


def feed_oth_body(order, hn_own, hn, g0, g1, wg0, wg1, wu0, wu1, *refs):
    outs = refs[4:]
    outs[4][...] = low(
        feed_rows(hn, (g0, g1), (wg0, wg1), (wu0, wu1), outs[:3], outs[3], hn.shape[0])
    )
    arrange(order, (hn_own, hn), outs[5])


def feed_own(order, hn, dy_own, dy_oth, gate_w, up_w, down_w):
    rows, width = hn.shape
    units = gate_w[0].shape[0]
    part = shape16(2 * rows, units)
    other = shape16(6 * rows, -(-units // 128) * 128)
    return on_chip(
        feed_own_body,
        (part,) * 3
        + (other,)
        + (shape32(rows, width),) * 2
        + (shape16(rows, units),) * 2
        + (shape16(2 * rows, width),),
        (order,),
        (hn, dy_own, dy_oth, *gate_w, *up_w, *down_w),
        "feed_own",
        limit=15,
        cost=11.0,
        scratch=(pltpu.VMEM((rows, units), jnp.bfloat16),) * 2,
    )


def feed_oth(order, hn_own, hn, grads, gate_w, up_w, parts):
    rows, width = hn.shape
    return on_chip(
        feed_oth_body,
        tuple(shape16(*part.shape) for part in parts)
        + (shape16(rows, width), shape16(2 * rows, width)),
        (order,),
        (hn_own, hn, *grads, *gate_w, *up_w, *parts),
        "feed_oth",
        aliases={9 + i: i for i in range(4)},
        limit=14,
        cost=7.0,
    )


def ff_grad(left, left_core, index, right, right_core, pieces):
    rows, units = left.shape
    size = right.shape[1] // pieces
    half = right.shape[1] // 2

    def body(left, left_core, right, right_core, *outs):
        for i in range(2):
            part = slice(i * half, (i + 1) * half)
            sums = low(
                inner_rows(left[...], right[:, part])
                + inner_rows(left_core[index * rows : (index + 1) * rows, :units], right_core[:, part])
            )
            for j in range(pieces // 2):
                outs[i * pieces // 2 + j][...] = sums[:, j * size : (j + 1) * size]

    part = shape16(units, size)
    return on_chip(
        body, (part,) * pieces, (), (left, left_core, right, right_core), "ff_grad", cost=2.7
    )


def join(first, second):
    def body(first, second, out):
        out[...] = low(high(first[...]) + high(second[...]))

    return on_chip(body, shape16(*first.shape), (), (first, second), "join", cost=0.3)


def fold_three(first, second, third):
    mid = first.shape[1] // 2

    def body(first, second, third, away, rest):
        for out, part in ((away, slice(0, mid)), (rest, slice(mid, 2 * mid))):
            out[...] = low(high(first[:, part]) + high(second[:, part]) + high(third[:, part]))

    part = shape16(first.shape[0], mid)
    return on_chip(body, (part, part), (), (first, second, third), "fold_three", cost=0.3)


def fold(kept, came):
    mid = kept.shape[1] // 2

    def body(kept, came, away, rest):
        away[...] = low(high(kept[:, :mid]) + high(came[:, :mid]))
        rest[...] = low(high(kept[:, mid:]) + high(came[:, mid:]))

    part = shape16(kept.shape[0], mid)
    return on_chip(body, (part, part), (), (kept, came), "fold", cost=0.3)


def fold_rows(kept, came):
    mid = kept.shape[0] // 2

    def body(kept, came, away, rest):
        away[...] = low(high(kept[:mid, :]) + high(came[:mid, :]))
        rest[...] = low(high(kept[mid:, :]) + high(came[mid:, :]))

    part = shape16(mid, kept.shape[1])
    return on_chip(body, (part, part), (), (kept, came), "fold_rows", cost=0.3)


def hidden_grad_body(order, place, dhn_own, dhn_came, hidden_far, dy_ref, gain_ref, w_far,
    grad_ref, send_ref, own_ref, away_ref, mine_ref, gains_ref, proj, hidden_ref, w_ref, sems,
):
    cols = send_ref.shape[1]
    loads = [pltpu.make_async_copy(hidden_far, hidden_ref, sems.at[2])]
    for m in (1, 0):
        there = columns(place[0] ^ m, cols)
        loads.append(pltpu.make_async_copy(w_far.at[there, :], w_ref.at[m], sems.at[m]))
    for load in loads:
        load.start()
    loads[0].wait()
    hidden = hidden_ref[...]
    scale = rms_scale(hidden)
    dhn = dhn_own[...] + high(dhn_came[...])
    gains_ref[...] = jnp.sum(dhn * hidden * scale, axis=0, keepdims=True)
    weighted = dhn * gain_ref[...]
    mean = jnp.mean(weighted * hidden, axis=-1, keepdims=True)
    grad = high(dy_ref[...]) + scale * weighted - hidden * (scale * scale * scale * mean)
    grad_ref[...] = grad
    proj[...] = low(grad)
    loads[1].wait()
    send_ref[...] = low(against(proj[...], w_ref[1]))
    loads[2].wait()
    own_ref[...] = low(against(proj[...], w_ref[0]))
    arrange_halves(order, (proj,), away_ref, mine_ref)


def hidden_grad(order, place, dhn_own, dhn_came, hidden, dy, gain, w):
    rows, width = hidden.shape
    part = shape16(rows, width // 2)
    return on_chip(
        hidden_grad_body,
        (shape32(rows, width), part, part, part, part, shape32(1, width)),
        (order, place),
        (dhn_own, dhn_came, hidden, dy, gain, w),
        "hidden_grad",
        cost=2.2,
        limit=9,
        far=(2, 5),
        scratch=(
            pltpu.VMEM((rows, width), jnp.bfloat16),
            pltpu.VMEM((rows, width), jnp.float32),
            pltpu.VMEM((2, width // 2, width), jnp.bfloat16),
            pltpu.SemaphoreType.DMA((3,)),
        ),
    )


def bucket_grad(left, left_core, rights, rights_core, place=0, total_cols=None, before=()):
    mid = left.shape[1] // 2
    cols = rights[0].shape[1]
    count = len(rights)

    def body(left, left_core, *refs):
        for i in range(count):
            part = slice(place + i * cols, place + (i + 1) * cols)
            for half, out in enumerate(refs[-2:]):
                cut = slice(half * mid, (half + 1) * mid)
                out[:, part] = low(
                    inner_rows(left[:, cut], refs[i][...])
                    + inner_rows(left_core[:, cut], refs[count + i][...])
                )

    full = shape16(mid, total_cols or cols * count)
    return on_chip(
        body,
        (full, full),
        (),
        (left, left_core, *rights, *rights_core, *before),
        "bucket_grad",
        aliases={2 + 2 * count + i: i for i in range(len(before))},
        cost=1.5,
    )


def bucket_near(row, kept, came):
    quarter, cols = kept.shape
    size = quarter // 4

    def body(row, kept, came, away, rest):
        near = row[0] & 1
        for i in range(2):
            here = pl.ds(pl.multiple_of(i * 2 * size + near * size, size), size)
            there = pl.ds(pl.multiple_of(i * 2 * size + (1 - near) * size, size), size)
            part = slice(i * size, (i + 1) * size)
            away[part, :] = low(high(kept[there, :]) + high(came[there, :]))
            rest[part, :] = low(high(kept[here, :]) + high(came[here, :]))

    half = shape16(2 * size, cols)
    return on_chip(body, (half, half), (row,), (kept, came), "bucket_near", cost=0.3)


def shares_body(d_a, d_b, fa, fb, w_ref, x_own, x_oth, gain_two, send_ref, own_ref, gains_ref):
    rows, width = x_own.shape
    cut = d_a.shape[1]
    sums = None
    for m, x_ref in ((1, x_oth), (0, x_own)):
        part = slice(m * rows, (m + 1) * rows)
        share = against(d_a[part, :], w_ref[:, :cut]) + against(d_b[part, :], w_ref[:, cut:])
        if m:
            send_ref[:, :width] = low(share)
        else:
            own_ref[...] = share
        x = high(x_ref[...])
        here = jnp.sum(share * (x * rms_scale(x)), axis=0, keepdims=True)
        sums = here if sums is None else sums + here
    send_ref[:, width : width + fa.shape[1]] = fa[...]
    send_ref[:, width + fa.shape[1] :] = fb[...]
    gains_ref[0:1, :] = sums
    gains_ref[1:2, :] = gain_two[...]


def shares(d_a, d_b, fa, fb, w, x_own, x_oth, gain_two):
    rows, width = x_own.shape
    return on_chip(
        shares_body,
        (shape16(rows, width + 2 * fa.shape[1]), shape32(rows, width), shape32(2, width)),
        (),
        (d_a, d_b, fa, fb, w, x_own, x_oth, gain_two),
        "shares",
        cost=2.3,
    )


def input_grad_body(place, share_ref, came_ref, grad_ref, x_ref, gain_ref, fa, fb, out_ref, first_ref):
    width = x_ref.shape[1]
    x = high(x_ref[...])
    scale = rms_scale(x)
    weighted = (share_ref[...] + high(came_ref[:, :width])) * gain_ref[...]
    mean = jnp.mean(weighted * x, axis=-1, keepdims=True)
    out_ref[...] = grad_ref[...] + scale * weighted - x * (scale * scale * scale * mean)
    cols = fa.shape[1]
    own = 2 * place[0]
    oth = 2 - own
    first_ref[:, columns(own, cols)] = fa[...]
    first_ref[:, columns(own + 1, cols)] = fb[...]
    first_ref[:, columns(oth, cols)] = came_ref[:, width : width + cols]
    first_ref[:, columns(oth + 1, cols)] = came_ref[:, width + cols :]


def input_grad(place, share, came, grad_hidden, x, gain, fa, fb):
    return on_chip(
        input_grad_body,
        (shape32(*x.shape), shape16(*x.shape)),
        (place,),
        (share, came, grad_hidden, x, gain, fa, fb),
        "input_grad",
        cost=2.0,
        limit=6,
    )


def after(first, *values):
    return lax.optimization_barrier((first, *values))[1:]


def two_groups(
    inputs,
    first_values,
    lengths,
    gain_attn,
    w_qkv,
    w_out,
    gain_mlp,
    w_gate,
    w_up,
    w_down,
    cotangent,
):
    SITES.clear()
    rows = inputs.shape[1]
    width = inputs.shape[2]
    span = 2 * rows
    out_cols = HEADS // 2 * HD
    packed_cols = 3 * out_cols
    mid = width // 2
    h = lax.axis_index("head")
    f = lax.axis_index("ffn")
    r = lax.axis_index("row")
    row_size = lax.axis_size("row")
    place = jnp.stack([h, lengths[0]]).astype(jnp.int32)
    row = r.reshape(1).astype(jnp.int32)
    tie = lax.optimization_barrier
    gain_attn = gain_attn.reshape(1, width)
    gain_mlp = gain_mlp.reshape(1, width)

    x_own = inputs[0]
    x_oth = swap(x_own, "head", 1)
    early_own = lax.dynamic_slice_in_dim(first_values[0], h * out_cols, out_cols, 1)
    early_oth = swap(
        lax.dynamic_slice_in_dim(first_values[0], (1 - h) * out_cols, out_cols, 1), "head", 1
    )
    dy_own = cotangent[0]
    down_core = swap(w_down, "ffn", 1)
    gate_core = swap(w_gate.T, "ffn", 1)
    up_core = swap(w_up.T, "ffn", 1)
    qkv_w = lax.dynamic_slice_in_dim(w_qkv, h * packed_cols, packed_cols, 1)
    half = HD // 2
    inverse = jnp.exp(-jnp.log(10000.0) * jnp.arange(half, dtype=jnp.float32) * 2.0 / HD)
    angles = jnp.arange(span, dtype=jnp.float32)[:, None] * jnp.tile(inverse, 4)[None, :]
    cosine = jnp.cos(angles)
    sign = jnp.where(jnp.arange(2 * HD) % HD < half, -1.0, 1.0)
    sine = jnp.sin(angles) * sign[None, :]

    ff_order = jnp.stack([(h ^ a) * row_size + (r ^ b) for a in (1, 0) for b in (3, 1, 2, 0)])
    down_order = jnp.stack([(h ^ a) * row_size + (r ^ b) for b in (3, 1, 2, 0) for a in (1, 0)])
    att_order = jnp.stack(
        [((f ^ a) * row_size + (r & 2 ^ b)) // 2 for a in (3, 1, 2, 0) for b in (2, 0)]
    )

    xn_away, xn_mine, packed_own = project(att_order, x_own, gain_attn, qkv_w)
    x_oth, packed_own, cosine, sine, early_own, down_core, gate_core, up_core = tie(
        (x_oth, packed_own, cosine, sine, early_own, down_core, gate_core, up_core)
    )
    xn_away, xn_mine, packed_oth = project(att_order, x_oth, gain_attn, qkv_w, (xn_away, xn_mine))
    att_own, att_oth, query, keys, mixed, log_sums = attend_forward(
        place, packed_own, packed_oth, early_own, early_oth, cosine, sine
    )
    att_came = swap(att_oth, "head", 1)
    (dy_send,) = after(att_own, dy_own)
    dy_oth = swap(dy_send, "ffn", 2)
    down_w = (w_down, down_core)
    gate_w = (w_gate.T, gate_core)
    up_w = (w_up.T, up_core)
    hidden, hn_own = finish(place, x_own, att_own, att_came, w_out, gain_mlp)
    hn_oth = swap(hn_own, "ffn", 2)
    dy_send, dy_oth = after(hn_own, dy_send, dy_oth)
    dyc_own = swap(dy_send, "ffn", 1)
    dyc_oth = swap(dy_oth, "ffn", 1)
    hnc_own = swap(hn_own, "ffn", 1)

    *parts, dhn_own, down_own, dact0, dact1, dy_all = feed_own(
        down_order, hn_own, dy_own, dy_oth, gate_w, up_w, down_w
    )
    hn_oth, parts, dhn_own, down_own, dact0, dact1, dy_all, hnc_own, dyc_own, dyc_oth = tie(
        (hn_oth, parts, dhn_own, down_own, dact0, dact1, dy_all, hnc_own, dyc_own, dyc_oth)
    )
    hnc_oth = swap(hn_oth, "ffn", 1)
    act, gate, up, others, dhn_send, hn_all = feed_oth(
        ff_order, hn_own, hn_oth, (dact0, dact1), gate_w, up_w, parts
    )
    dhn_came = swap(dhn_send, "ffn", 2)
    others_core = swap(others, "ffn", 1)
    own_send, came_send = after(dhn_send, att_own, att_came)
    att_core = swap(own_send, "ffn", 1)
    came_core = swap(came_send, "ffn", 1)
    hnc_oth, dyc_own, dyc_oth = after(dhn_send, hnc_oth, dyc_own, dyc_oth)
    dyc_all = reorder(down_order, dyc_own, dyc_oth)
    hnc_all = reorder(ff_order, hnc_own, hnc_oth)

    gate_a, gate_b, gate_near, gate_kept = ff_grad(gate, others_core, 1, hn_all, hnc_all, 4)
    gate_xa = swap(gate_a, "head", 1)
    down_send, down_kept = ff_grad(act, others_core, 0, dy_all, dyc_all, 2)
    down_near = swap(down_send, "row", 1)
    up_a, up_b, up_near, up_kept = ff_grad(up, others_core, 2, hn_all, hnc_all, 4)
    dhn_came, gate_b, gate_kept, gate_near, down_kept, up_a, up_b, up_near, up_kept = tie(
        (dhn_came, gate_b, gate_kept, gate_near, down_kept, up_a, up_b, up_near, up_kept)
    )

    grad_hidden, go_send, go_own, proj_away, proj_mine, gain_two = hidden_grad(
        att_order, place, dhn_own, dhn_came, hidden, dy_own, gain_mlp, w_out
    )
    (gate_near,) = after(go_send, gate_near)
    gate_send = join(gate_near, gate_xa)
    go_send, go_own, proj_away, gate_send = tie((go_send, go_own, proj_away, gate_send))
    go_oth = swap(go_send, "head", 1)
    proj_core = swap(proj_away, "ffn", 1)
    gate_came = swap(gate_send, "row", 1)
    (gate_b,) = after(go_send, gate_b)
    gate_xb = swap(gate_b, "head", 1)
    out_send, out_kept = bucket_grad(
        proj_mine, proj_core, (att_own, att_came), (att_core, came_core)
    )
    out_y = swap(out_send, "ffn", 2)
    up_xa = swap(after(out_send, up_a)[0], "head", 1)
    go_oth, out_kept = tie((go_oth, out_kept))

    def backward(pairs, lse):
        return attend_backward(
            place, query, keys, mixed, lse, go_own, go_oth, att_own, att_oth, cosine, sine, pairs
        )

    pairs = HEADS // 4
    d_a, fa_own, fa_oth = backward((0, pairs // 2), log_sums)
    out_kept, down_kept, gate_kept = after(d_a, out_kept, down_kept, gate_kept)
    out_send, out_kept = bucket_near(row, out_kept, out_y)
    out_near = swap(out_send, "row", 1)
    down_send, down_kept = fold(down_kept, down_near)
    down_mid = swap(down_send, "row", 2)
    gate_kept = join(gate_kept, gate_xb)
    d_a, out_kept, down_kept, gate_kept, log_sums = tie(
        (d_a, out_kept, down_kept, gate_kept, log_sums)
    )
    core_a = swap(d_a, "ffn", 1)
    xn_core = swap(after(out_kept, xn_away)[0], "ffn", 1)
    d_b, fb_own, fb_oth = backward((pairs // 2, pairs), log_sums)
    gate_kept, out_kept, up_near = after(d_b, gate_kept, out_kept, up_near)
    gate_send, gate_kept = fold(gate_kept, gate_came)
    up_send = join(up_near, up_xa)
    out_send, out_kept = fold_rows(out_kept, out_near)
    d_b, gate_kept, out_kept, up_send = tie((d_b, gate_kept, out_kept, up_send))
    core_b = swap(d_b, "ffn", 1)
    up_xb = swap(after(gate_kept, up_b)[0], "head", 1)
    up_came = swap(up_send, "row", 1)
    (d_a,) = after(gate_kept, d_a)
    before = bucket_grad(xn_mine, xn_core, (d_a,), (core_a,), 0, packed_cols)
    core_b, *before = tie((core_b, *before))
    y_send, kept = bucket_grad(
        xn_mine, xn_core, (d_b,), (core_b,), packed_cols // 2, packed_cols, before
    )
    y_came = swap(y_send, "ffn", 2)
    d_a, d_b = after(y_send, d_a, d_b)
    back_send, share_own, gains = shares(
        d_a, d_b, fa_oth, fb_oth, qkv_w, x_own, x_oth, gain_two
    )
    gate_send, out_send, act, others, up_kept, down_kept = after(
        back_send, gate_send, out_send, act, others, up_kept, down_kept
    )
    gains = gains + swap(gains, "head", 1)
    gains, back_send = tie((gains, back_send))
    back_came = swap(back_send, "head", 1)
    up_kept, down_kept = after(gains, up_kept, down_kept)
    up_send, up_kept = fold_three(up_kept, up_xb, up_came)
    gate_far = swap(gate_send, "row", 2)
    out_far = swap(out_send, "row", 2)
    units = w_down.shape[0]
    far_send = low(matmul(act[rows:], down_w[0]) + matmul(others[rows:span, :units], down_w[1]))
    gains, down_kept, gate_kept, out_kept = after(far_send, gains, down_kept, gate_kept, out_kept)
    gains = gains + swap(gains, "ffn", 1)
    down_send, down_kept = fold(down_kept, down_mid)
    sum_gate = high(gate_kept) + high(gate_far)
    kept, up_send, down_send, sum_gate, gains = tie((kept, up_send, down_send, sum_gate, gains))

    near_send, kept = bucket_near(row, kept, y_came)
    near_came = swap(near_send, "row", 1)
    gains, far_send, out_kept, up_send, down_send = after(
        near_send, gains, far_send, out_kept, up_send, down_send
    )
    gains_y = swap(gains, "ffn", 2)
    far_came = swap(far_send, "ffn", 2)
    up_far = swap(up_send, "row", 2)
    out_sum = high(out_kept) + high(out_far)
    out_x = swap(low(out_sum[:, out_cols:]), "head", 1)
    kept, out_sum = tie((kept, out_sum))
    qkv_send, kept = fold_rows(kept, near_came)
    qkv_far = swap(qkv_send, "row", 2)
    share_own, down_kept, up_kept, out_sum, residual, gains, down_send = after(
        qkv_send,
        share_own,
        down_kept,
        up_kept,
        out_sum[:, :out_cols],
        hidden + down_own,
        gains,
        down_send,
    )
    down_x = swap(down_send, "head", 1)
    gains = gains + gains_y
    gains = gains + swap(gains, "row", 1)
    gains_far = swap(gains, "row", 2)
    (share_own,) = after(gains, share_own)
    grad_in, grad_first = input_grad(
        place, share_own, back_came, grad_hidden, x_own, gain_attn, fa_own, fb_own
    )
    sum_up = high(up_kept) + high(up_far)
    sum_down = high(down_kept) + high(down_x)
    out_sum = out_sum + high(out_x)
    output = low(residual + high(far_came))[None]
    gains = gains + gains_far
    kept, grad_in, sum_up, sum_down, out_sum, output, gains = tie(
        (kept, grad_in, sum_up, sum_down, out_sum, output, gains)
    )
    sum_qkv = high(kept) + high(qkv_far)
    return (
        output,
        grad_in[None],
        grad_first[None],
        gains[0],
        sum_qkv,
        out_sum.T,
        gains[1],
        sum_gate.T,
        sum_up.T,
        sum_down,
    )


def solution(mesh):
    in_specs = (
        P(("ffn", "row"), "head", None),
        P(("ffn", "row"), "head", None),
        P(("ffn", "row")),
        P(),
        P(),
        P(),
        P(),
        P(None, "ffn"),
        P(None, "ffn"),
        P("ffn", None),
        P(("ffn", "row"), "head", None),
    )
    out_specs = (
        P(("ffn", "row"), "head", None),
        P(("ffn", "row"), "head", None),
        P(("ffn", "row"), "head", None),
        P(),
        P(("ffn", "row"), "head"),
        P("head", ("ffn", "row")),
        P(),
        P(("head", "row"), "ffn"),
        P(("head", "row"), "ffn"),
        P("ffn", ("head", "row")),
    )
    body = two_groups if mesh.shape["head"] == 2 and mesh.shape["ffn"] == 4 else any_groups
    return jax.shard_map(
        body, mesh=mesh, in_specs=in_specs, out_specs=out_specs, check_vma=False
    )
```

```python
import functools

import jax
import jax.numpy as jnp
from jax import lax
from jax.experimental import pallas as pl
from jax.experimental.pallas import tpu as pltpu
from jax.sharding import PartitionSpec as P

HEADS = 16
HD = 64
MIN_LEN = 512
STEP = 256


eps = 1e-06


def rms_scale(values):
    return lax.rsqrt(jnp.mean(values * values, axis=-1, keepdims=True) + eps)


def matmul(left, right):
    return jnp.dot(left, right, preferred_element_type=jnp.float32)


def inner_rows(left, right):
    return lax.dot_general(
        left, right, (((0,), (0,)), ((), ())), preferred_element_type=jnp.float32
    )


def against(left, right):
    return lax.dot_general(
        left, right, (((1,), (1,)), ((), ())), preferred_element_type=jnp.float32
    )


def swap(values, axis, mask):
    size = lax.axis_size(axis)
    return lax.ppermute(values, axis, [(i, i ^ mask) for i in range(size)])


def bits_of(axis):
    size = lax.axis_size(axis)
    return [1 << b for b in range(size.bit_length() - 2, -1, -1)]


def halve(values, dim, axis, mask):
    bit = (lax.axis_index(axis) // mask) % 2
    away = lax.dynamic_index_in_dim(values, 1 - bit, dim, keepdims=False)
    kept = lax.dynamic_index_in_dim(values, bit, dim, keepdims=False)
    came = swap(away.astype(jnp.bfloat16), axis, mask)
    return kept.astype(jnp.float32) + came.astype(jnp.float32)


def total(values, axes):
    for axis in axes:
        for mask in reversed(bits_of(axis)):
            values = values + swap(values, axis, mask)
    return values


def rotary(positions, head_size):
    half_size = head_size // 2
    inverse = jnp.exp(
        -jnp.log(10000.0) * jnp.arange(half_size, dtype=jnp.float32) * 2.0 / head_size
    )
    angles = positions.astype(jnp.float32)[:, None] * inverse[None, :]
    return (jnp.cos(angles), jnp.sin(angles))


def rotate(vectors, cosine, sine, sign):
    half_size = vectors.shape[-1] // 2
    first_half = vectors[..., :half_size]
    second_half = vectors[..., half_size:]
    cos_rows = cosine[:, None, :]
    sin_rows = sign * sine[:, None, :]
    return jnp.concatenate(
        [
            first_half * cos_rows - second_half * sin_rows,
            second_half * cos_rows + first_half * sin_rows,
        ],
        axis=-1,
    )


def masked_scores(q_rows, keys, q_pos, k_pos, valid):
    raw = jnp.einsum("qhe,khe->hqk", q_rows, keys, preferred_element_type=jnp.float32)
    allowed = (k_pos[None, :] <= q_pos[:, None]) & (k_pos[None, :] < valid)
    return jnp.where(allowed[None], 0.125 * raw, -1e30)


def scan_forward(query, keys, mixed, positions, valid, block_rows):
    count = query.shape[0] // block_rows

    def step(carry, index):
        start = index * block_rows
        q_rows = lax.dynamic_slice_in_dim(query, start, block_rows, 0)
        q_pos = lax.dynamic_slice_in_dim(positions, start, block_rows, 0)
        scores = masked_scores(q_rows, keys, q_pos, positions, valid)
        top = jnp.max(scores, axis=-1, keepdims=True)
        expo = jnp.exp(scores - top)
        total_w = jnp.sum(expo, axis=-1, keepdims=True)
        weights = expo / total_w
        result = jnp.einsum(
            "hqk,khe->qhe", weights.astype(jnp.bfloat16), mixed, preferred_element_type=jnp.float32
        )
        return (carry, (result.astype(jnp.bfloat16), top + jnp.log(total_w)))

    _, (outs, log_sums) = lax.scan(step, 0, jnp.arange(count, dtype=jnp.int32))
    return (outs.reshape(query.shape), log_sums)


def scan_backward(query, keys, mixed, positions, valid, log_sums, grad_out, block_rows):
    count = query.shape[0] // block_rows
    zeros = jnp.zeros(keys.shape, jnp.float32)

    def step(carry, index):
        key_sum, value_sum = carry
        start = index * block_rows
        q_rows = lax.dynamic_slice_in_dim(query, start, block_rows, 0)
        q_pos = lax.dynamic_slice_in_dim(positions, start, block_rows, 0)
        g_rows = lax.dynamic_slice_in_dim(grad_out, start, block_rows, 0)
        scores = masked_scores(q_rows, keys, q_pos, positions, valid)
        weights = jnp.exp(scores - log_sums[index])
        grad_w = jnp.einsum("qhe,khe->hqk", g_rows, mixed, preferred_element_type=jnp.float32)
        delta = jnp.sum(weights * grad_w, axis=-1, keepdims=True)
        grad_s = (weights * (grad_w - delta)).astype(jnp.bfloat16)
        grad_q = 0.125 * jnp.einsum(
            "hqk,khe->qhe", grad_s, keys, preferred_element_type=jnp.float32
        )
        key_sum = key_sum + 0.125 * jnp.einsum(
            "hqk,qhe->khe", grad_s, q_rows, preferred_element_type=jnp.float32
        )
        value_sum = value_sum + jnp.einsum(
            "hqk,qhe->khe", weights.astype(jnp.bfloat16), g_rows, preferred_element_type=jnp.float32
        )
        return ((key_sum, value_sum), grad_q)

    (grad_keys, grad_mixed), grad_query = lax.scan(
        step, (zeros, zeros), jnp.arange(count, dtype=jnp.int32)
    )
    return (grad_query.reshape(query.shape), grad_keys, grad_mixed)


def any_groups(
    inputs,
    first_values,
    lengths,
    gain_attn,
    w_qkv,
    w_out,
    gain_mlp,
    w_gate,
    w_up,
    w_down,
    cotangent,
):
    rows = inputs.shape[1]
    width = inputs.shape[2]
    groups = lax.axis_size("head")
    shards = lax.axis_size("ffn")
    heads_here = HEADS // groups
    span_rows = rows * groups
    block_rows = span_rows // max(1, span_rows // 512)
    head_pos = lax.axis_index("head")
    valid_len = lengths[0]
    packed_cols = heads_here * 3 * HD
    out_cols = heads_here * HD
    hidden_here = w_gate.shape[1]

    owners = [head_pos ^ m for m in range(groups)]
    x_all = [inputs[0]] + [swap(inputs[0], "head", m) for m in range(1, groups)]
    early = []
    for m in range(groups):
        piece = lax.dynamic_slice_in_dim(first_values[0], owners[m] * out_cols, out_cols, 1)
        early.append(swap(piece, "head", m) if m else piece)
    far = range(2, shards, 2)
    grad_rows = jnp.concatenate([cotangent[0]] + [swap(cotangent[0], "ffn", m) for m in far], 0)
    gate_w = jnp.concatenate([w_gate, swap(w_gate, "ffn", 1)], 1)
    up_w = jnp.concatenate([w_up, swap(w_up, "ffn", 1)], 1)
    down_w = jnp.concatenate([w_down, swap(w_down, "ffn", 1)], 0)
    w_heads = lax.dynamic_slice_in_dim(w_qkv, head_pos * packed_cols, packed_cols, 1)
    out_w = jnp.concatenate(
        [lax.dynamic_slice_in_dim(w_out, o * out_cols, out_cols, 0) for o in owners], 0
    )

    positions = jnp.concatenate([o * rows + jnp.arange(rows, dtype=jnp.int32) for o in owners])
    cosine, sine = rotary(positions, HD)
    normed, scaled, queries, key_list, mixes = [], [], [], [], []
    rows_in = inputs[0].astype(jnp.float32)
    scale_one = rms_scale(rows_in)
    for m in range(groups):
        block = x_all[m].astype(jnp.float32)
        scale = rms_scale(block)
        scaled.append(block * scale)
        normed.append((block * scale * gain_attn).astype(jnp.bfloat16))
        packed = matmul(normed[m], w_heads).astype(jnp.bfloat16)
        packed = packed.reshape(rows, heads_here, 3, HD).astype(jnp.float32)
        part = slice(m * rows, (m + 1) * rows)
        queries.append(rotate(packed[:, :, 0], cosine[part], sine[part], 1.0))
        key_list.append(rotate(packed[:, :, 1], cosine[part], sine[part], 1.0))
        value = early[m].reshape(rows, heads_here, HD).astype(jnp.float32)
        mixes.append(0.5 * (packed[:, :, 2] + value))
    query = jnp.concatenate(queries, 0).astype(jnp.bfloat16)
    keys = jnp.concatenate(key_list, 0).astype(jnp.bfloat16)
    mixed = jnp.concatenate(mixes, 0).astype(jnp.bfloat16)
    attended, log_sums = scan_forward(query, keys, mixed, positions, valid_len, block_rows)
    attended = attended.reshape(groups, rows, out_cols)
    att_own = jnp.concatenate(
        [attended[0]] + [swap(attended[m], "head", m) for m in range(1, groups)], 1
    )
    hidden = rows_in + matmul(att_own, out_w)
    scale_two = rms_scale(hidden)
    normed_two = (hidden * scale_two * gain_mlp).astype(jnp.bfloat16)

    mlp_rows = [normed_two] + [swap(normed_two, "ffn", m) for m in far]
    grad_list = [grad_rows[i * rows : (i + 1) * rows] for i in range(len(mlp_rows))]
    actives, grad_gates, grad_ups, downs, grad_normed_list = [], [], [], [], []
    for i, block in enumerate(mlp_rows):
        gate_rows = matmul(block, gate_w)
        up_rows = matmul(block, up_w)
        sigmoid_gate = jax.nn.sigmoid(gate_rows)
        silu_gate = gate_rows * sigmoid_gate
        grad_active = against(grad_list[i], down_w)
        actives.append((silu_gate * up_rows).astype(jnp.bfloat16))
        grad_gates.append(
            (
                grad_active * up_rows * sigmoid_gate * (1.0 + gate_rows * (1.0 - sigmoid_gate))
            ).astype(jnp.bfloat16)
        )
        grad_ups.append((grad_active * silu_gate).astype(jnp.bfloat16))
        grad_normed_list.append(against(grad_gates[i], gate_w) + against(grad_ups[i], up_w))
        downs.append(matmul(actives[i], down_w))
    grad_normed_two = grad_normed_list[0]
    for i, m in enumerate(far):
        came = swap(grad_normed_list[i + 1].astype(jnp.bfloat16), "ffn", m)
        grad_normed_two = grad_normed_two + came.astype(jnp.float32)
    down_rows = downs[0]
    for i, m in enumerate(far):
        down_rows = down_rows + swap(downs[i + 1].astype(jnp.bfloat16), "ffn", m).astype(jnp.float32)
    output = (hidden + down_rows).astype(jnp.bfloat16)[None]

    all_rows = jnp.concatenate(mlp_rows, 0)
    ff_sums = []
    for left, right in (
        (grad_rows, jnp.concatenate(actives, 0)),
        (all_rows, jnp.concatenate(grad_gates, 0)),
        (all_rows, jnp.concatenate(grad_ups, 0)),
    ):
        away = inner_rows(left, right[:, hidden_here:]).astype(jnp.bfloat16)
        part = inner_rows(left, right[:, :hidden_here])
        part = (part + swap(away, "ffn", 1).astype(jnp.float32)).astype(jnp.bfloat16)
        steps = [("head", b) for b in bits_of("head")] + [("row", b) for b in bits_of("row")]
        part = part.reshape([2] * len(steps) + [-1, hidden_here])
        order = [s for s in steps if s[0] == "head"] + [s for s in reversed(steps) if s[0] == "row"]
        left_steps = list(steps)
        for s in order:
            part = halve(part, left_steps.index(s), *s)
            left_steps.remove(s)
            if left_steps:
                part = part.astype(jnp.bfloat16)
        ff_sums.append(part)
    sum_down, sum_gate, sum_up = ff_sums

    grad_y = cotangent[0].astype(jnp.float32)
    grad_gain_two = jnp.sum(grad_normed_two * hidden * scale_two, axis=0)
    weighted_two = grad_normed_two * gain_mlp
    cube_two = scale_two * scale_two * scale_two
    grad_hidden = (
        grad_y
        + scale_two * weighted_two
        - hidden * cube_two * jnp.mean(weighted_two * hidden, axis=-1, keepdims=True)
    )
    grad_proj = grad_hidden.astype(jnp.bfloat16)
    grad_att = against(grad_proj, out_w).astype(jnp.bfloat16)
    grad_att = jnp.concatenate(
        [
            swap(grad_att[:, m * out_cols : (m + 1) * out_cols], "head", m)
            if m
            else grad_att[:, :out_cols]
            for m in range(groups)
        ],
        0,
    ).reshape(span_rows, heads_here, HD)

    def over_buckets(part):
        steps = [("ffn", b) for b in bits_of("ffn")] + [("row", b) for b in bits_of("row")]
        part = part.astype(jnp.bfloat16).reshape([2] * len(steps) + [-1, part.shape[1]])
        order = [s for s in reversed(steps) if s[0] == "ffn"] + [
            s for s in reversed(steps) if s[0] == "row"
        ]
        left_steps = list(steps)
        for s in order:
            part = halve(part, left_steps.index(s), *s)
            left_steps.remove(s)
            if left_steps:
                part = part.astype(jnp.bfloat16)
        return part

    part = over_buckets(inner_rows(grad_proj, att_own))
    sum_out = part[:, :out_cols]
    for m in range(1, groups):
        came = swap(part[:, m * out_cols : (m + 1) * out_cols].astype(jnp.bfloat16), "head", m)
        sum_out = sum_out + came.astype(jnp.float32)

    grad_query, grad_keys, grad_mixed = scan_backward(
        query, keys, mixed, positions, valid_len, log_sums, grad_att, block_rows
    )
    grad_packed = jnp.stack(
        [
            rotate(grad_query, cosine, sine, -1.0),
            rotate(grad_keys, cosine, sine, -1.0),
            0.5 * grad_mixed,
        ],
        axis=2,
    )
    grad_packed = grad_packed.astype(jnp.bfloat16).reshape(span_rows, packed_cols)
    grad_early = (0.5 * grad_mixed).astype(jnp.bfloat16).reshape(span_rows, out_cols)
    firsts = [grad_early[m * rows : (m + 1) * rows] for m in range(groups)]
    firsts = [swap(firsts[m], "head", m) if m else firsts[0] for m in range(groups)]
    grad_first = jnp.zeros((rows, width), jnp.bfloat16)
    for m in range(groups):
        grad_first = lax.dynamic_update_slice_in_dim(grad_first, firsts[m], owners[m] * out_cols, 1)
    shares = [
        against(grad_packed[m * rows : (m + 1) * rows], w_heads) for m in range(groups)
    ]
    grad_gain_one = sum(jnp.sum(shares[m] * scaled[m], axis=0) for m in range(groups))
    grad_normed = shares[0]
    for m in range(1, groups):
        grad_normed = grad_normed + swap(shares[m].astype(jnp.bfloat16), "head", m).astype(jnp.float32)
    sum_qkv = over_buckets(inner_rows(jnp.concatenate(normed, 0), grad_packed))
    weighted_one = grad_normed * gain_attn
    cube_one = scale_one * scale_one * scale_one
    grad_in = (
        grad_hidden
        + scale_one * weighted_one
        - rows_in * cube_one * jnp.mean(weighted_one * rows_in, axis=-1, keepdims=True)
    )
    gains = total(jnp.stack([grad_gain_one, grad_gain_two]), ("ffn", "head", "row"))
    return (
        output,
        grad_in[None],
        grad_first[None],
        gains[0],
        sum_qkv,
        sum_out.T,
        gains[1],
        sum_gate,
        sum_up,
        sum_down.T,
    )


SCALE = 4.5e8
COSTS = {}
SITES = {}


def site_cost(name, usual):
    count = SITES.get(name, 0)
    SITES[name] = count + 1
    return int(SCALE * COSTS.get(name + str(count), usual))


def low(values):
    return values.astype(jnp.bfloat16)


def high(values):
    return values.astype(jnp.float32)


def on_chip(body, outs, scalars, arrays, name, scratch=(), aliases=None, limit=3, cost=1.0, away=(), far=()):
    inside = pl.BlockSpec(memory_space=pltpu.VMEM)
    outside = pl.BlockSpec(memory_space=pl.ANY)
    return pl.pallas_call(
        body,
        out_shape=jax.tree.unflatten(
            jax.tree.structure(outs),
            [
                pltpu.HBM(o.shape, o.dtype) if i in away else o
                for i, o in enumerate(jax.tree.leaves(outs))
            ],
        ),
        in_specs=[pl.BlockSpec(memory_space=pltpu.SMEM)] * len(scalars)
        + [outside if i in far else inside for i in range(len(arrays))],
        out_specs=jax.tree.unflatten(
            jax.tree.structure(outs),
            [
                outside if i in away else inside
                for i in range(len(jax.tree.leaves(outs)))
            ],
        ),
        scratch_shapes=list(scratch),
        input_output_aliases=aliases or {},
        cost_estimate=pl.CostEstimate(
            flops=site_cost(name, cost), transcendentals=0, bytes_accessed=1
        ),
        compiler_params=pltpu.CompilerParams(vmem_limit_bytes=limit << 20),
        name=name,
    )(*scalars, *arrays)


def shape16(*dims):
    return jax.ShapeDtypeStruct(dims, jnp.bfloat16)


def shape32(*dims):
    return jax.ShapeDtypeStruct(dims, jnp.float32)


def spans(total):
    return [(a, min(a + STEP, total)) for a in range(0, total, STEP)]


def turn(values):
    lane = lax.broadcasted_iota(jnp.int32, values.shape, 1)
    return jnp.where(
        lane % HD < HD // 2, pltpu.roll(values, 2 * HD - HD // 2, 1), pltpu.roll(values, HD // 2, 1)
    )


def allowed_keys(a, b, valid):
    size = b - a
    down = lax.broadcasted_iota(jnp.int32, (size, size), 0)
    across = lax.broadcasted_iota(jnp.int32, (size, size), 1)
    allowed = down <= across
    if b > MIN_LEN:
        allowed = allowed & (down < valid - a)
    return allowed


def columns(index, size):
    return pl.ds(pl.multiple_of(index * size, size), size)


def forward_body(
    place, packed_own, packed_oth, early_own, early_oth, cos_ref, sin_ref,
    own_far, oth_far, q_far, k_far, v_far, lse_out,
    att_own, att_oth, q_out, k_out, v_out, flipped, att, sems,
):
    rows = packed_own.shape[0]
    span = 2 * rows
    wide = 2 * HD
    valid = place[1]
    f32 = jnp.float32
    bf = jnp.bfloat16
    first = lax.broadcasted_iota(jnp.int32, (1, wide), 1) < HD
    flipped[:, HD:, :] = jnp.ones((2, 16, span), bf)

    def copies(p):
        cols = columns(p, wide)
        return [
            pltpu.make_async_copy(near.at[:, cols], far.at[:, cols], sems.at[i, p])
            for i, (near, far) in enumerate(
                (
                    (q_out, q_far),
                    (k_out, k_far),
                    (v_out, v_far),
                    (att_oth, oth_far),
                    (att_own, own_far),
                )
            )
        ]

    def pair(p, _):
        cols = columns(p, wide)
        for m, (packed, early) in enumerate(((packed_own, early_own), (packed_oth, early_oth))):
            here = columns(place[0] ^ m, rows)
            x0 = high(packed[:, pl.ds(pl.multiple_of(p * 3 * wide, wide), wide)])
            x1 = high(packed[:, pl.ds(pl.multiple_of(p * 3 * wide + wide, wide), wide)])
            x2 = high(packed[:, pl.ds(pl.multiple_of(p * 3 * wide + 2 * wide, wide), wide)])
            cosine = cos_ref[here, :]
            sine = sin_ref[here, :]
            q = jnp.where(first, x0, x1)
            k = pltpu.roll(jnp.where(first, x2, x0), HD, 1)
            v = jnp.where(first, x1, x2)
            q_out[here, cols] = low(q * cosine + turn(q) * sine)
            k_out[here, cols] = low(k * cosine + turn(k) * sine)
            v_out[here, cols] = low(0.5 * (v + high(early[:, cols])))
        for copy in copies(p)[:3]:
            copy.start()
        turned = v_out[:, cols].T
        for e in range(2):
            flipped[e, :HD, :] = turned[e * HD : (e + 1) * HD, :]
        for a, b in spans(span):
            q = q_out[a:b, cols] * jnp.asarray(0.125, bf)
            allowed = allowed_keys(a, b, valid)
            for e in range(2):
                qe = jnp.where(first == (e == 0), q, jnp.zeros_like(q))
                diag = jnp.where(allowed, against(k_out[a:b, cols], qe), -1e30)
                top = jnp.max(diag, axis=0, keepdims=True)
                if a:
                    past = against(k_out[:a, cols], qe)
                    top = jnp.maximum(top, jnp.max(past, axis=0, keepdims=True))
                out = matmul(flipped[e, :, a:b], low(jnp.exp(diag - top)))
                if a:
                    out = out + matmul(flipped[e, :, :a], low(jnp.exp(past - top)))
                amount = out[HD : HD + 1, :]
                att[e * HD : (e + 1) * HD, a:b] = out[:HD, :] / amount
                lse_out[p, e : e + 1, a:b] = top + jnp.log(amount)
        result = low(att[...].T)
        upper = place[0] == 0
        att_own[:, cols] = jnp.where(upper, result[:rows, :], result[rows:, :])
        att_oth[:, cols] = jnp.where(upper, result[rows:, :], result[:rows, :])
        for copy in copies(p)[3:]:
            copy.start()
        return 0

    lax.fori_loop(0, lse_out.shape[0], pair, 0)
    for p in range(lse_out.shape[0]):
        for copy in copies(p):
            copy.wait()


def attend_forward(place, packed_own, packed_oth, early_own, early_oth, cosine, sine):
    rows, cols = packed_own.shape
    heads = cols // (3 * HD)
    span = 2 * rows
    out = shape16(rows, heads * HD)
    natural = shape16(span, heads * HD)
    return on_chip(
        forward_body,
        (out, out, natural, natural, natural, shape32(heads // 2, 2, span)),
        (place,),
        (packed_own, packed_oth, early_own, early_oth, cosine, sine),
        "attend_forward",
        cost=11.0,
        limit=7,
        away=(0, 1, 2, 3, 4),
        scratch=(
            pltpu.VMEM(out.shape, jnp.bfloat16),
            pltpu.VMEM(out.shape, jnp.bfloat16),
            pltpu.VMEM(natural.shape, jnp.bfloat16),
            pltpu.VMEM(natural.shape, jnp.bfloat16),
            pltpu.VMEM(natural.shape, jnp.bfloat16),
            pltpu.VMEM((2, HD + 16, span), jnp.bfloat16),
            pltpu.VMEM((2 * HD, span), jnp.float32),
            pltpu.SemaphoreType.DMA((5, heads // 2)),
        ),
    )


def backward_body(
    start, place, q_far, k_far, v_far, lse_ref, go_own, go_oth, att_own, att_oth, cos_ref, sin_ref,
    d_out, f_own, f_oth, q_ref, k_ref, v_ref, sems, grad, prod, turned_k, dq, dk, dv,
):
    rows = go_own.shape[0]
    span = 2 * rows
    valid = place[1]
    wide = 2 * HD
    bf = jnp.bfloat16
    first = lax.broadcasted_iota(jnp.int32, (1, wide), 1) < HD
    eighth = jnp.asarray(0.125, bf)
    count = f_own.shape[1] // wide

    def copies(i):
        there = columns(i + start, wide)
        here = columns(i, wide)
        return [
            pltpu.make_async_copy(away.at[:, there], near.at[:, here], sems.at[n, i])
            for n, (away, near) in enumerate(((q_far, q_ref), (k_far, k_ref), (v_far, v_ref)))
        ]

    for i in range(count):
        for copy in copies(i):
            copy.start()

    def pair(i, _):
        p = i + start
        cols = columns(p, wide)
        near = columns(i, wide)
        for copy in copies(i):
            copy.wait()
        for m, (go, att) in enumerate(((go_own, att_own), (go_oth, att_oth))):
            here = columns(place[0] ^ m, rows)
            grad[here, :] = go[:, cols]
            prod[here, :] = high(go[:, cols]) * high(att[:, cols])
        flat = prod[...].T
        deltas = [jnp.sum(flat[e * HD : (e + 1) * HD, :], axis=0, keepdims=True) for e in range(2)]
        turned_k[...] = (k_ref[:, near] * eighth).T
        for n, (a, b) in enumerate(spans(span)):
            allowed = allowed_keys(a, b, valid)
            q = q_ref[a:b, near] * eighth
            g = grad[a:b, :]
            parts = ((a, b), (0, a)) if a else ((a, b),)
            sums = {}
            for e in range(2):
                mine = first == (e == 0)
                qe = jnp.where(mine, q, jnp.zeros_like(q))
                ge = jnp.where(mine, g, jnp.zeros_like(g))
                for lo, hi in parts:
                    scores = against(k_ref[lo:hi, near], qe)
                    if lo == a:
                        scores = jnp.where(allowed, scores, -1e30)
                    weights = jnp.exp(scores - lse_ref[p, e : e + 1, a:b])
                    grad_w = against(v_ref[lo:hi, near], ge)
                    grad_s = low(weights * (grad_w - deltas[e][:, a:b]))
                    dv_here = matmul(low(weights), ge)
                    dk_here = matmul(grad_s, qe)
                    dq_here = matmul(turned_k[e * HD : (e + 1) * HD, lo:hi], grad_s)
                    if (lo, "v") in sums:
                        dv_here = dv_here + sums[lo, "v"]
                        dk_here = dk_here + sums[lo, "k"]
                    sums[lo, "v"], sums[lo, "k"] = dv_here, dk_here
                    sums[lo, e] = dq_here
            for e in range(2):
                dq[e * HD : (e + 1) * HD, a:b] = sums[a, e] + sums[0, e] if a else sums[a, e]
            dv[a:b, :] = sums[a, "v"]
            dk[a:b, :] = sums[a, "k"]
            if a:
                dv[:a, :] += sums[0, "v"]
                dk[:a, :] += sums[0, "k"]
        prod[...] = dq[...].T
        for m, f_out in enumerate((f_own, f_oth)):
            here = columns(place[0] ^ m, rows)
            cosine = cos_ref[here, :]
            sine = sin_ref[here, :]
            gv = low(0.5 * dv[here, :])
            gk = dk[here, :]
            gk = low(pltpu.roll(gk * cosine - turn(gk) * sine, HD, 1))
            gq = prod[here, :]
            gq = low(gq * cosine - turn(gq) * sine)
            part = slice(m * rows, (m + 1) * rows)
            base = i * 3 * wide
            d_out[part, pl.ds(pl.multiple_of(base, wide), wide)] = jnp.where(first, gq, gk)
            d_out[part, pl.ds(pl.multiple_of(base + wide, wide), wide)] = jnp.where(first, gv, gq)
            d_out[part, pl.ds(pl.multiple_of(base + 2 * wide, wide), wide)] = jnp.where(first, gk, gv)
            f_out[:, columns(i, wide)] = gv
        return 0

    lax.fori_loop(0, count, pair, 0)


def attend_backward(place, q, k, v, lse, go_own, go_oth, att_own, att_oth, cosine, sine, pairs):
    span = q.shape[0]
    rows = span // 2
    wide = 2 * HD
    cols = wide * (pairs[1] - pairs[0])
    return on_chip(
        functools.partial(backward_body, pairs[0]),
        (shape16(span, 3 * cols), shape16(rows, cols), shape16(rows, cols)),
        (place,),
        (q, k, v, lse, go_own, go_oth, att_own, att_oth, cosine, sine),
        "attend_backward",
        cost=7.5,
        limit=6,
        far=(0, 1, 2),
        scratch=(
            pltpu.VMEM((span, cols), jnp.bfloat16),
            pltpu.VMEM((span, cols), jnp.bfloat16),
            pltpu.VMEM((span, cols), jnp.bfloat16),
            pltpu.SemaphoreType.DMA((3, pairs[1] - pairs[0])),
            pltpu.VMEM((span, wide), jnp.bfloat16),
            pltpu.VMEM((span, wide), jnp.float32),
            pltpu.VMEM((wide, span), jnp.bfloat16),
            pltpu.VMEM((wide, span), jnp.float32),
            pltpu.VMEM((span, wide), jnp.float32),
            pltpu.VMEM((span, wide), jnp.float32),
        ),
    )


def row_blocks(rows, body, size=64):
    def step(c, _):
        body(columns(c, size))
        return 0

    lax.fori_loop(0, rows // size, step, 0)


def tables(span, inverse, sign):
    def body(inverse, sign, cos_ref, sin_ref):
        def rows(part):
            shape = (64, inverse.shape[1])
            place = part.start + lax.broadcasted_iota(jnp.int32, shape, 0)
            angles = place.astype(jnp.float32) * inverse[...]
            cos_ref[part, :] = jnp.cos(angles)
            sin_ref[part, :] = jnp.sin(angles) * sign[...]

        row_blocks(span, rows)

    out = shape32(span, inverse.shape[1])
    return on_chip(body, (out, out), (), (inverse, sign), "tables", cost=1.0)


def project_body(base, order, x_ref, gain_ref, w_ref, *refs):
    away_far, mine_far, packed_ref, xn, away, mine, sems = refs[-7:]
    rows = x_ref.shape[0]

    def norm(part):
        x = high(x_ref[part, :])
        xn[part, :] = low(x * rms_scale(x) * gain_ref[...])

    row_blocks(rows, norm)
    arrange_halves(order, (xn,), away, mine)
    there = slice(base, base + rows)
    copies = [
        pltpu.make_async_copy(away, away_far.at[there, :], sems.at[0]),
        pltpu.make_async_copy(mine, mine_far.at[there, :], sems.at[1]),
    ]
    for copy in copies:
        copy.start()
    cols = w_ref.shape[1] // 3
    for i in range(3):
        part = slice(i * cols, (i + 1) * cols)
        packed_ref[:, part] = low(matmul(xn[...], w_ref[:, part]))
    for copy in copies:
        copy.wait()


def project(order, x, gain, w, before=()):
    rows, width = x.shape
    part = shape16(2 * rows, width // 2)
    return pl.pallas_call(
        functools.partial(project_body, rows if before else 0),
        out_shape=(
            pltpu.HBM(part.shape, part.dtype),
            pltpu.HBM(part.shape, part.dtype),
            shape16(rows, w.shape[1]),
        ),
        in_specs=[pl.BlockSpec(memory_space=pltpu.SMEM)]
        + [pl.BlockSpec(memory_space=pltpu.VMEM)] * 3
        + [pl.BlockSpec(memory_space=pl.ANY)] * len(before),
        out_specs=(
            pl.BlockSpec(memory_space=pl.ANY),
            pl.BlockSpec(memory_space=pl.ANY),
            pl.BlockSpec(memory_space=pltpu.VMEM),
        ),
        scratch_shapes=[
            pltpu.VMEM((rows, width), jnp.bfloat16),
            pltpu.VMEM((rows, width // 2), jnp.bfloat16),
            pltpu.VMEM((rows, width // 2), jnp.bfloat16),
            pltpu.SemaphoreType.DMA((2,)),
        ],
        input_output_aliases={4 + i: i for i in range(len(before))},
        cost_estimate=pl.CostEstimate(
            flops=site_cost("project", 2.0), transcendentals=0, bytes_accessed=1
        ),
        compiler_params=pltpu.CompilerParams(vmem_limit_bytes=5 << 20),
        name="project",
    )(order, x, gain, w, *before)


def arrange(order, blocks, out):
    rows = blocks[0].shape[0]
    size = out.shape[1] // order.shape[0]
    for i in range(order.shape[0]):
        for b, block in enumerate(blocks):
            out[b * rows : (b + 1) * rows, i * size : (i + 1) * size] = block[:, columns(order[i], size)]


def finish(place, x, att_own, att_came, w, gain):
    def body(
        place, x_ref, own_far, came_far, w_far, gain_ref,
        hidden_far, hn_ref, hidden_ref, w_ref, att_ref, sems,
    ):
        cols = own_far.shape[1]
        loads = []
        for m, far in enumerate((own_far, came_far)):
            there = columns(place[0] ^ m, cols)
            loads.append(pltpu.make_async_copy(far, att_ref.at[m], sems.at[3 + m]))
            loads.append(pltpu.make_async_copy(w_far.at[there, :], w_ref.at[m], sems.at[m]))
        for load in loads:
            load.start()
        hidden = high(x_ref[...])
        for m in range(2):
            loads[2 * m].wait()
            loads[2 * m + 1].wait()
            hidden = hidden + matmul(att_ref[m], w_ref[m])
        hidden_ref[...] = hidden
        copy = pltpu.make_async_copy(hidden_ref, hidden_far, sems.at[2])
        copy.start()

        def norm(part):
            block = hidden_ref[part, :]
            hn_ref[part, :] = low(block * rms_scale(block) * gain_ref[...])

        row_blocks(hidden_ref.shape[0], norm)
        copy.wait()

    rows, width = x.shape
    return on_chip(
        body,
        (shape32(rows, width), shape16(rows, width)),
        (place,),
        (x, att_own, att_came, w, gain),
        "finish",
        cost=3.0,
        limit=8,
        away=(0,),
        far=(1, 2, 3),
        scratch=(
            pltpu.VMEM((rows, width), jnp.float32),
            pltpu.VMEM((2, width // 2, width), jnp.bfloat16),
            pltpu.VMEM((2, rows, width // 2), jnp.bfloat16),
            pltpu.SemaphoreType.DMA((5,)),
        ),
    )


def reorder(order, *blocks):
    rows, cols = blocks[0].shape

    def body(order, *refs):
        arrange(order, refs[:-1], refs[-1])

    return on_chip(body, shape16(rows * len(blocks), cols), (order,), blocks, "reorder", cost=0.9)


def arrange_halves(order, blocks, away, mine):
    rows = blocks[0].shape[0]
    count = order.shape[0] // 2
    size = mine.shape[1] // count
    for half, out in enumerate((away, mine)):
        for i in range(count):
            for b, block in enumerate(blocks):
                out[b * rows : (b + 1) * rows, i * size : (i + 1) * size] = block[
                    :, columns(order[half * count + i], size)
                ]


def reorder_halves(order, *blocks):
    rows, cols = blocks[0].shape

    def body(order, *refs):
        arrange_halves(order, refs[:-2], *refs[-2:])

    part = shape16(rows * len(blocks), cols // 2)
    return on_chip(body, (part, part), (order,), blocks, "reorder_halves", cost=0.9)


def feed_rows(hn, grads, gate_w, up_w, mine, other, base):
    rows = hn.shape[0]
    units = gate_w[0].shape[0]
    here = slice(base, base + rows)
    for s in range(2):
        gate = against(hn[...], gate_w[s][...])
        up = against(hn[...], up_w[s][...])
        grad = high(grads[s][...])
        sig = 1.0 / (1.0 + jnp.exp(-gate))
        silu = gate * sig
        results = (silu * up, grad * up * sig * (1.0 + gate * (1.0 - sig)), grad * silu)
        for i, result in enumerate(results):
            if s == 0:
                mine[i][here, :] = low(result)
            else:
                other[2 * i * rows + base : 2 * i * rows + base + rows, :units] = low(result)


def back_rows(gate_w, up_w, down_w, mine, other, base, rows, out, down=None):
    units = gate_w[0].shape[0]
    here = slice(base, base + rows)
    lefts = [[mine[i][here, :] for i in range(3)]]
    lefts.append(
        [other[2 * i * rows + base : 2 * i * rows + base + rows, :units] for i in range(3)]
    )
    size = out.shape[1] // 2

    def chunk(c, _):
        cols = columns(c, size)
        sums = None
        for s in range(2):
            for i, w in ((1, gate_w[s]), (2, up_w[s])):
                share = matmul(lefts[s][i], w[:, cols])
                sums = share if sums is None else sums + share
        out[:, cols] = sums.astype(out.dtype)
        if down is not None:
            down[:, cols] = matmul(lefts[0][0], down_w[0][:, cols]) + matmul(
                lefts[1][0], down_w[1][:, cols]
            )
        return 0

    lax.fori_loop(0, 2, chunk, 0)


def feed_own_body(order, hn, dy_own, dy_oth, wg0, wg1, wu0, wu1, wd0, wd1, *refs):
    rows = hn.shape[0]
    outs, grads = refs[:9], refs[9:]
    mine, other, dhn, down = outs[:3], outs[3], outs[4], outs[5]
    for grad, w in zip(grads, (wd0, wd1)):
        grad[...] = low(against(dy_own[...], w[...]))
    feed_rows(hn, grads, (wg0, wg1), (wu0, wu1), mine, other, 0)
    back_rows((wg0, wg1), (wu0, wu1), (wd0, wd1), mine, other, 0, rows, dhn, down)
    for grad, w in zip(outs[6:8], (wd0, wd1)):
        grad[...] = low(against(dy_oth[...], w[...]))
    arrange(order, (dy_own, dy_oth), outs[8])


def feed_oth_body(order, hn_own, hn, g0, g1, wg0, wg1, wu0, wu1, *refs):
    outs = refs[4:]
    rows = hn.shape[0]
    feed_rows(hn, (g0, g1), (wg0, wg1), (wu0, wu1), outs[:3], outs[3], rows)
    back_rows((wg0, wg1), (wu0, wu1), None, outs[:3], outs[3], rows, rows, outs[4])
    arrange(order, (hn_own, hn), outs[5])


def feed_own(order, hn, dy_own, dy_oth, gate_w, up_w, down_w):
    rows, width = hn.shape
    units = gate_w[0].shape[0]
    part = shape16(2 * rows, units)
    other = shape16(6 * rows, -(-units // 128) * 128)
    return on_chip(
        feed_own_body,
        (part,) * 3
        + (other,)
        + (shape32(rows, width),) * 2
        + (shape16(rows, units),) * 2
        + (shape16(2 * rows, width),),
        (order,),
        (hn, dy_own, dy_oth, *gate_w, *up_w, *down_w),
        "feed_own",
        limit=15,
        cost=11.0,
        scratch=(pltpu.VMEM((rows, units), jnp.bfloat16),) * 2,
    )


def feed_oth(order, hn_own, hn, grads, gate_w, up_w, parts):
    rows, width = hn.shape
    return on_chip(
        feed_oth_body,
        tuple(shape16(*part.shape) for part in parts)
        + (shape16(rows, width), shape16(2 * rows, width)),
        (order,),
        (hn_own, hn, *grads, *gate_w, *up_w, *parts),
        "feed_oth",
        aliases={9 + i: i for i in range(4)},
        limit=14,
        cost=7.0,
    )


def ff_grad(left, left_core, index, right, right_core, pieces):
    rows, units = left.shape
    size = right.shape[1] // pieces
    step = right.shape[1] // 2

    def body(left, left_core, right, right_core, *outs):
        def chunk(c, _):
            here = columns(c, step)
            sums = low(
                inner_rows(left[...], right[:, here])
                + inner_rows(
                    left_core[index * rows : (index + 1) * rows, :units], right_core[:, here]
                )
            )
            for j in range(2):

                @pl.when(c == j)
                def _():
                    for i in range(pieces // 2):
                        outs[j * pieces // 2 + i][...] = sums[:, i * size : (i + 1) * size]

            return 0

        lax.fori_loop(0, 2, chunk, 0)

    part = shape16(units, size)
    return on_chip(
        body, (part,) * pieces, (), (left, left_core, right, right_core), "ff_grad", cost=2.7
    )


def join(first, second):
    def body(first, second, out):
        out[...] = low(high(first[...]) + high(second[...]))

    return on_chip(body, shape16(*first.shape), (), (first, second), "join", cost=0.3)


def fold_three(first, second, third):
    mid = first.shape[1] // 2

    def body(first, second, third, away, rest):
        for out, part in ((away, slice(0, mid)), (rest, slice(mid, 2 * mid))):
            out[...] = low(high(first[:, part]) + high(second[:, part]) + high(third[:, part]))

    part = shape16(first.shape[0], mid)
    return on_chip(body, (part, part), (), (first, second, third), "fold_three", cost=0.3)


def fold(kept, came):
    mid = kept.shape[1] // 2

    def body(kept, came, away, rest):
        away[...] = low(high(kept[:, :mid]) + high(came[:, :mid]))
        rest[...] = low(high(kept[:, mid:]) + high(came[:, mid:]))

    part = shape16(kept.shape[0], mid)
    return on_chip(body, (part, part), (), (kept, came), "fold", cost=0.3)


def fold_rows(kept, came):
    mid = kept.shape[0] // 2

    def body(kept, came, away, rest):
        away[...] = low(high(kept[:mid, :]) + high(came[:mid, :]))
        rest[...] = low(high(kept[mid:, :]) + high(came[mid:, :]))

    part = shape16(mid, kept.shape[1])
    return on_chip(body, (part, part), (), (kept, came), "fold_rows", cost=0.3)


def hidden_grad_body(order, place, dhn_own, dhn_came, hidden_far, dy_ref, gain_ref, w_far,
    grad_ref, send_ref, own_ref, away_ref, mine_ref, gains_ref, proj, hidden_ref, w_ref, sems,
):
    cols = send_ref.shape[1]
    loads = [pltpu.make_async_copy(hidden_far, hidden_ref, sems.at[2])]
    for m in (1, 0):
        there = columns(place[0] ^ m, cols)
        loads.append(pltpu.make_async_copy(w_far.at[there, :], w_ref.at[m], sems.at[m]))
    for load in loads:
        load.start()
    loads[0].wait()
    gains_ref[...] = jnp.zeros_like(gains_ref)

    def rows_grad(part):
        hidden = hidden_ref[part, :]
        scale = rms_scale(hidden)
        dhn = dhn_own[part, :] + high(dhn_came[part, :])
        gains_ref[...] += jnp.sum(dhn * hidden * scale, axis=0, keepdims=True)
        weighted = dhn * gain_ref[...]
        mean = jnp.mean(weighted * hidden, axis=-1, keepdims=True)
        grad = high(dy_ref[part, :]) + scale * weighted - hidden * (scale * scale * scale * mean)
        grad_ref[part, :] = grad
        proj[part, :] = low(grad)

    row_blocks(hidden_ref.shape[0], rows_grad)
    loads[1].wait()
    send_ref[...] = low(against(proj[...], w_ref[1]))
    loads[2].wait()
    own_ref[...] = low(against(proj[...], w_ref[0]))
    arrange_halves(order, (proj,), away_ref, mine_ref)


def hidden_grad(order, place, dhn_own, dhn_came, hidden, dy, gain, w):
    rows, width = hidden.shape
    part = shape16(rows, width // 2)
    return on_chip(
        hidden_grad_body,
        (shape32(rows, width), part, part, part, part, shape32(1, width)),
        (order, place),
        (dhn_own, dhn_came, hidden, dy, gain, w),
        "hidden_grad",
        cost=2.2,
        limit=9,
        far=(2, 5),
        scratch=(
            pltpu.VMEM((rows, width), jnp.bfloat16),
            pltpu.VMEM((rows, width), jnp.float32),
            pltpu.VMEM((2, width // 2, width), jnp.bfloat16),
            pltpu.SemaphoreType.DMA((3,)),
        ),
    )


def bucket_grad(left, left_core, rights, rights_core, place=0, total_cols=None, before=()):
    mid = left.shape[1] // 2
    cols = rights[0].shape[1]
    count = len(rights)

    def body(left, left_core, *refs):
        for i in range(count):
            part = slice(place + i * cols, place + (i + 1) * cols)
            for half, out in enumerate(refs[-2:]):
                cut = slice(half * mid, (half + 1) * mid)
                out[:, part] = low(
                    inner_rows(left[:, cut], refs[i][...])
                    + inner_rows(left_core[:, cut], refs[count + i][...])
                )

    full = shape16(mid, total_cols or cols * count)
    return on_chip(
        body,
        (full, full),
        (),
        (left, left_core, *rights, *rights_core, *before),
        "bucket_grad",
        aliases={2 + 2 * count + i: i for i in range(len(before))},
        cost=1.5,
    )


def bucket_near(row, kept, came):
    quarter, cols = kept.shape
    size = quarter // 4

    def body(row, kept, came, away, rest):
        near = row[0] & 1
        for i in range(2):
            here = pl.ds(pl.multiple_of(i * 2 * size + near * size, size), size)
            there = pl.ds(pl.multiple_of(i * 2 * size + (1 - near) * size, size), size)
            part = slice(i * size, (i + 1) * size)
            away[part, :] = low(high(kept[there, :]) + high(came[there, :]))
            rest[part, :] = low(high(kept[here, :]) + high(came[here, :]))

    half = shape16(2 * size, cols)
    return on_chip(body, (half, half), (row,), (kept, came), "bucket_near", cost=0.3)


def shares_body(d_a, d_b, fa, fb, w_ref, x_own, x_oth, gain_two, send_ref, own_ref, gains_ref):
    rows, width = x_own.shape
    cut = d_a.shape[1]
    scales = [rms_scale(high(x_ref[...])) for x_ref in (x_own, x_oth)]
    size = width // 2

    def chunk(c, _):
        here = columns(c, size)
        sums = None
        for m, x_ref in enumerate((x_own, x_oth)):
            part = slice(m * rows, (m + 1) * rows)
            share = against(d_a[part, :], w_ref[here, :cut]) + against(d_b[part, :], w_ref[here, cut:])
            if m:
                send_ref[:, here] = low(share)
            else:
                own_ref[:, here] = share
            one = jnp.sum(share * (high(x_ref[:, here]) * scales[m]), axis=0, keepdims=True)
            sums = one if sums is None else sums + one
        gains_ref[0:1, here] = sums
        return 0

    lax.fori_loop(0, 2, chunk, 0)
    send_ref[:, width : width + fa.shape[1]] = fa[...]
    send_ref[:, width + fa.shape[1] :] = fb[...]
    gains_ref[1:2, :] = gain_two[...]


def shares(d_a, d_b, fa, fb, w, x_own, x_oth, gain_two):
    rows, width = x_own.shape
    return on_chip(
        shares_body,
        (shape16(rows, width + 2 * fa.shape[1]), shape32(rows, width), shape32(2, width)),
        (),
        (d_a, d_b, fa, fb, w, x_own, x_oth, gain_two),
        "shares",
        cost=2.3,
    )


def input_grad_body(place, share_ref, came_ref, grad_ref, x_ref, gain_ref, fa, fb, out_ref, first_ref):
    width = x_ref.shape[1]

    def rows_grad(part):
        x = high(x_ref[part, :])
        scale = rms_scale(x)
        weighted = (share_ref[part, :] + high(came_ref[part, :width])) * gain_ref[...]
        mean = jnp.mean(weighted * x, axis=-1, keepdims=True)
        out_ref[part, :] = (
            grad_ref[part, :] + scale * weighted - x * (scale * scale * scale * mean)
        )

    row_blocks(x_ref.shape[0], rows_grad)
    cols = fa.shape[1]
    own = 2 * place[0]
    oth = 2 - own
    first_ref[:, columns(own, cols)] = fa[...]
    first_ref[:, columns(own + 1, cols)] = fb[...]
    first_ref[:, columns(oth, cols)] = came_ref[:, width : width + cols]
    first_ref[:, columns(oth + 1, cols)] = came_ref[:, width + cols :]


def input_grad(place, share, came, grad_hidden, x, gain, fa, fb):
    return on_chip(
        input_grad_body,
        (shape32(*x.shape), shape16(*x.shape)),
        (place,),
        (share, came, grad_hidden, x, gain, fa, fb),
        "input_grad",
        cost=2.0,
        limit=6,
    )


def after(first, *values):
    return lax.optimization_barrier((first, *values))[1:]


def two_groups(
    inputs,
    first_values,
    lengths,
    gain_attn,
    w_qkv,
    w_out,
    gain_mlp,
    w_gate,
    w_up,
    w_down,
    cotangent,
):
    SITES.clear()
    rows = inputs.shape[1]
    width = inputs.shape[2]
    span = 2 * rows
    out_cols = HEADS // 2 * HD
    packed_cols = 3 * out_cols
    mid = width // 2
    h = lax.axis_index("head")
    f = lax.axis_index("ffn")
    r = lax.axis_index("row")
    row_size = lax.axis_size("row")
    place = jnp.stack([h, lengths[0]]).astype(jnp.int32)
    row = r.reshape(1).astype(jnp.int32)
    tie = lax.optimization_barrier
    gain_attn = gain_attn.reshape(1, width)
    gain_mlp = gain_mlp.reshape(1, width)

    x_own = inputs[0]
    x_oth = swap(x_own, "head", 1)
    early_own = lax.dynamic_slice_in_dim(first_values[0], h * out_cols, out_cols, 1)
    early_oth = swap(
        lax.dynamic_slice_in_dim(first_values[0], (1 - h) * out_cols, out_cols, 1), "head", 1
    )
    dy_own = cotangent[0]
    down_core = swap(w_down, "ffn", 1)
    gate_core = swap(w_gate.T, "ffn", 1)
    up_core = swap(w_up.T, "ffn", 1)
    qkv_w = lax.dynamic_slice_in_dim(w_qkv, h * packed_cols, packed_cols, 1)
    half = HD // 2
    inverse = jnp.exp(-jnp.log(10000.0) * jnp.arange(half, dtype=jnp.float32) * 2.0 / HD)
    sign = jnp.where(jnp.arange(2 * HD) % HD < half, -1.0, 1.0)
    cosine, sine = tables(span, jnp.tile(inverse, 4)[None, :], sign[None, :])

    ff_order = jnp.stack([(h ^ a) * row_size + (r ^ b) for a in (1, 0) for b in (3, 1, 2, 0)])
    down_order = jnp.stack([(h ^ a) * row_size + (r ^ b) for b in (3, 1, 2, 0) for a in (1, 0)])
    att_order = jnp.stack(
        [((f ^ a) * row_size + (r & 2 ^ b)) // 2 for a in (3, 1, 2, 0) for b in (2, 0)]
    )

    xn_away, xn_mine, packed_own = project(att_order, x_own, gain_attn, qkv_w)
    x_oth, packed_own, cosine, sine, early_own, down_core, gate_core, up_core = tie(
        (x_oth, packed_own, cosine, sine, early_own, down_core, gate_core, up_core)
    )
    xn_away, xn_mine, packed_oth = project(att_order, x_oth, gain_attn, qkv_w, (xn_away, xn_mine))
    att_own, att_oth, query, keys, mixed, log_sums = attend_forward(
        place, packed_own, packed_oth, early_own, early_oth, cosine, sine
    )
    att_came = swap(att_oth, "head", 1)
    (dy_send,) = after(att_own, dy_own)
    dy_oth = swap(dy_send, "ffn", 2)
    down_w = (w_down, down_core)
    gate_w = (w_gate.T, gate_core)
    up_w = (w_up.T, up_core)
    hidden, hn_own = finish(place, x_own, att_own, att_came, w_out, gain_mlp)
    hn_oth = swap(hn_own, "ffn", 2)
    dy_send, dy_oth = after(hn_own, dy_send, dy_oth)
    dyc_own = swap(dy_send, "ffn", 1)
    dyc_oth = swap(dy_oth, "ffn", 1)
    hnc_own = swap(hn_own, "ffn", 1)

    *parts, dhn_own, down_own, dact0, dact1, dy_all = feed_own(
        down_order, hn_own, dy_own, dy_oth, gate_w, up_w, down_w
    )
    hn_oth, parts, dhn_own, down_own, dact0, dact1, dy_all, hnc_own, dyc_own, dyc_oth = tie(
        (hn_oth, parts, dhn_own, down_own, dact0, dact1, dy_all, hnc_own, dyc_own, dyc_oth)
    )
    hnc_oth = swap(hn_oth, "ffn", 1)
    act, gate, up, others, dhn_send, hn_all = feed_oth(
        ff_order, hn_own, hn_oth, (dact0, dact1), gate_w, up_w, parts
    )
    dhn_came = swap(dhn_send, "ffn", 2)
    others_core = swap(others, "ffn", 1)
    own_send, came_send = after(dhn_send, att_own, att_came)
    att_core = swap(own_send, "ffn", 1)
    came_core = swap(came_send, "ffn", 1)
    hnc_oth, dyc_own, dyc_oth = after(dhn_send, hnc_oth, dyc_own, dyc_oth)
    dyc_all = reorder(down_order, dyc_own, dyc_oth)
    hnc_all = reorder(ff_order, hnc_own, hnc_oth)

    gate_a, gate_b, gate_near, gate_kept = ff_grad(gate, others_core, 1, hn_all, hnc_all, 4)
    gate_xa = swap(gate_a, "head", 1)
    down_send, down_kept = ff_grad(act, others_core, 0, dy_all, dyc_all, 2)
    down_near = swap(down_send, "row", 1)
    up_a, up_b, up_near, up_kept = ff_grad(up, others_core, 2, hn_all, hnc_all, 4)
    dhn_came, gate_b, gate_kept, gate_near, down_kept, up_a, up_b, up_near, up_kept = tie(
        (dhn_came, gate_b, gate_kept, gate_near, down_kept, up_a, up_b, up_near, up_kept)
    )

    grad_hidden, go_send, go_own, proj_away, proj_mine, gain_two = hidden_grad(
        att_order, place, dhn_own, dhn_came, hidden, dy_own, gain_mlp, w_out
    )
    (gate_near,) = after(go_send, gate_near)
    gate_send = join(gate_near, gate_xa)
    go_send, go_own, proj_away, gate_send = tie((go_send, go_own, proj_away, gate_send))
    go_oth = swap(go_send, "head", 1)
    proj_core = swap(proj_away, "ffn", 1)
    gate_came = swap(gate_send, "row", 1)
    (gate_b,) = after(go_send, gate_b)
    gate_xb = swap(gate_b, "head", 1)
    out_send, out_kept = bucket_grad(
        proj_mine, proj_core, (att_own, att_came), (att_core, came_core)
    )
    out_y = swap(out_send, "ffn", 2)
    up_xa = swap(after(out_send, up_a)[0], "head", 1)
    go_oth, out_kept = tie((go_oth, out_kept))

    def backward(pairs, lse):
        return attend_backward(
            place, query, keys, mixed, lse, go_own, go_oth, att_own, att_oth, cosine, sine, pairs
        )

    pairs = HEADS // 4
    d_a, fa_own, fa_oth = backward((0, pairs // 2), log_sums)
    out_kept, down_kept, gate_kept = after(d_a, out_kept, down_kept, gate_kept)
    out_send, out_kept = bucket_near(row, out_kept, out_y)
    out_near = swap(out_send, "row", 1)
    down_send, down_kept = fold(down_kept, down_near)
    down_mid = swap(down_send, "row", 2)
    gate_kept = join(gate_kept, gate_xb)
    d_a, out_kept, down_kept, gate_kept, log_sums = tie(
        (d_a, out_kept, down_kept, gate_kept, log_sums)
    )
    core_a = swap(d_a, "ffn", 1)
    xn_core = swap(after(out_kept, xn_away)[0], "ffn", 1)
    d_b, fb_own, fb_oth = backward((pairs // 2, pairs), log_sums)
    gate_kept, out_kept, up_near = after(d_b, gate_kept, out_kept, up_near)
    gate_send, gate_kept = fold(gate_kept, gate_came)
    up_send = join(up_near, up_xa)
    out_send, out_kept = fold_rows(out_kept, out_near)
    d_b, gate_kept, out_kept, up_send = tie((d_b, gate_kept, out_kept, up_send))
    core_b = swap(d_b, "ffn", 1)
    up_xb = swap(after(gate_kept, up_b)[0], "head", 1)
    up_came = swap(up_send, "row", 1)
    (d_a,) = after(gate_kept, d_a)
    before = bucket_grad(xn_mine, xn_core, (d_a,), (core_a,), 0, packed_cols)
    core_b, *before = tie((core_b, *before))
    y_send, kept = bucket_grad(
        xn_mine, xn_core, (d_b,), (core_b,), packed_cols // 2, packed_cols, before
    )
    y_came = swap(y_send, "ffn", 2)
    d_a, d_b = after(y_send, d_a, d_b)
    back_send, share_own, gains = shares(
        d_a, d_b, fa_oth, fb_oth, qkv_w, x_own, x_oth, gain_two
    )
    gate_send, out_send, act, others, up_kept, down_kept = after(
        back_send, gate_send, out_send, act, others, up_kept, down_kept
    )
    gains = gains + swap(gains, "head", 1)
    gains, back_send = tie((gains, back_send))
    back_came = swap(back_send, "head", 1)
    up_kept, down_kept = after(gains, up_kept, down_kept)
    up_send, up_kept = fold_three(up_kept, up_xb, up_came)
    gate_far = swap(gate_send, "row", 2)
    out_far = swap(out_send, "row", 2)
    units = w_down.shape[0]
    far_send = low(matmul(act[rows:], down_w[0]) + matmul(others[rows:span, :units], down_w[1]))
    gains, down_kept, gate_kept, out_kept = after(far_send, gains, down_kept, gate_kept, out_kept)
    gains = gains + swap(gains, "ffn", 1)
    down_send, down_kept = fold(down_kept, down_mid)
    sum_gate = high(gate_kept) + high(gate_far)
    kept, up_send, down_send, sum_gate, gains = tie((kept, up_send, down_send, sum_gate, gains))

    near_send, kept = bucket_near(row, kept, y_came)
    near_came = swap(near_send, "row", 1)
    gains, far_send, out_kept, up_send, down_send = after(
        near_send, gains, far_send, out_kept, up_send, down_send
    )
    gains_y = swap(gains, "ffn", 2)
    far_came = swap(far_send, "ffn", 2)
    up_far = swap(up_send, "row", 2)
    out_sum = high(out_kept) + high(out_far)
    out_x = swap(low(out_sum[:, out_cols:]), "head", 1)
    kept, out_sum = tie((kept, out_sum))
    qkv_send, kept = fold_rows(kept, near_came)
    qkv_far = swap(qkv_send, "row", 2)
    share_own, down_kept, up_kept, out_sum, residual, gains, down_send = after(
        qkv_send,
        share_own,
        down_kept,
        up_kept,
        out_sum[:, :out_cols],
        hidden + down_own,
        gains,
        down_send,
    )
    down_x = swap(down_send, "head", 1)
    gains = gains + gains_y
    gains = gains + swap(gains, "row", 1)
    gains_far = swap(gains, "row", 2)
    (share_own,) = after(gains, share_own)
    grad_in, grad_first = input_grad(
        place, share_own, back_came, grad_hidden, x_own, gain_attn, fa_own, fb_own
    )
    sum_up = high(up_kept) + high(up_far)
    sum_down = high(down_kept) + high(down_x)
    out_sum = out_sum + high(out_x)
    output = low(residual + high(far_came))[None]
    gains = gains + gains_far
    kept, grad_in, sum_up, sum_down, out_sum, output, gains = tie(
        (kept, grad_in, sum_up, sum_down, out_sum, output, gains)
    )
    sum_qkv = high(kept) + high(qkv_far)
    return (
        output,
        grad_in[None],
        grad_first[None],
        gains[0],
        sum_qkv,
        out_sum.T,
        gains[1],
        sum_gate.T,
        sum_up.T,
        sum_down,
    )


def solution(mesh):
    in_specs = (
        P(("ffn", "row"), "head", None),
        P(("ffn", "row"), "head", None),
        P(("ffn", "row")),
        P(),
        P(),
        P(),
        P(),
        P(None, "ffn"),
        P(None, "ffn"),
        P("ffn", None),
        P(("ffn", "row"), "head", None),
    )
    out_specs = (
        P(("ffn", "row"), "head", None),
        P(("ffn", "row"), "head", None),
        P(("ffn", "row"), "head", None),
        P(),
        P(("ffn", "row"), "head"),
        P("head", ("ffn", "row")),
        P(),
        P(("head", "row"), "ffn"),
        P(("head", "row"), "ffn"),
        P("ffn", ("head", "row")),
    )
    body = two_groups if mesh.shape["head"] == 2 and mesh.shape["ffn"] == 4 else any_groups
    return jax.shard_map(
        body, mesh=mesh, in_specs=in_specs, out_specs=out_specs, check_vma=False
    )
```

```python
import functools

import jax
import jax.numpy as jnp
from jax import lax
from jax.experimental import pallas as pl
from jax.experimental.pallas import tpu as pltpu
from jax.sharding import PartitionSpec as P

HEADS = 16
HD = 64
MIN_LEN = 512
STEP = 256


eps = 1e-06


def rms_scale(values):
    return lax.rsqrt(jnp.mean(values * values, axis=-1, keepdims=True) + eps)


def matmul(left, right):
    return jnp.dot(left, right, preferred_element_type=jnp.float32)


def inner_rows(left, right):
    return lax.dot_general(
        left, right, (((0,), (0,)), ((), ())), preferred_element_type=jnp.float32
    )


def against(left, right):
    return lax.dot_general(
        left, right, (((1,), (1,)), ((), ())), preferred_element_type=jnp.float32
    )


def swap(values, axis, mask):
    size = lax.axis_size(axis)
    return lax.ppermute(values, axis, [(i, i ^ mask) for i in range(size)])


def bits_of(axis):
    size = lax.axis_size(axis)
    return [1 << b for b in range(size.bit_length() - 2, -1, -1)]


def halve(values, dim, axis, mask):
    bit = (lax.axis_index(axis) // mask) % 2
    away = lax.dynamic_index_in_dim(values, 1 - bit, dim, keepdims=False)
    kept = lax.dynamic_index_in_dim(values, bit, dim, keepdims=False)
    came = swap(away.astype(jnp.bfloat16), axis, mask)
    return kept.astype(jnp.float32) + came.astype(jnp.float32)


def total(values, axes):
    for axis in axes:
        for mask in reversed(bits_of(axis)):
            values = values + swap(values, axis, mask)
    return values


def rotary(positions, head_size):
    half_size = head_size // 2
    inverse = jnp.exp(
        -jnp.log(10000.0) * jnp.arange(half_size, dtype=jnp.float32) * 2.0 / head_size
    )
    angles = positions.astype(jnp.float32)[:, None] * inverse[None, :]
    return (jnp.cos(angles), jnp.sin(angles))


def rotate(vectors, cosine, sine, sign):
    half_size = vectors.shape[-1] // 2
    first_half = vectors[..., :half_size]
    second_half = vectors[..., half_size:]
    cos_rows = cosine[:, None, :]
    sin_rows = sign * sine[:, None, :]
    return jnp.concatenate(
        [
            first_half * cos_rows - second_half * sin_rows,
            second_half * cos_rows + first_half * sin_rows,
        ],
        axis=-1,
    )


def masked_scores(q_rows, keys, q_pos, k_pos, valid):
    raw = jnp.einsum("qhe,khe->hqk", q_rows, keys, preferred_element_type=jnp.float32)
    allowed = (k_pos[None, :] <= q_pos[:, None]) & (k_pos[None, :] < valid)
    return jnp.where(allowed[None], 0.125 * raw, -1e30)


def scan_forward(query, keys, mixed, positions, valid, block_rows):
    count = query.shape[0] // block_rows

    def step(carry, index):
        start = index * block_rows
        q_rows = lax.dynamic_slice_in_dim(query, start, block_rows, 0)
        q_pos = lax.dynamic_slice_in_dim(positions, start, block_rows, 0)
        scores = masked_scores(q_rows, keys, q_pos, positions, valid)
        top = jnp.max(scores, axis=-1, keepdims=True)
        expo = jnp.exp(scores - top)
        total_w = jnp.sum(expo, axis=-1, keepdims=True)
        weights = expo / total_w
        result = jnp.einsum(
            "hqk,khe->qhe", weights.astype(jnp.bfloat16), mixed, preferred_element_type=jnp.float32
        )
        return (carry, (result.astype(jnp.bfloat16), top + jnp.log(total_w)))

    _, (outs, log_sums) = lax.scan(step, 0, jnp.arange(count, dtype=jnp.int32))
    return (outs.reshape(query.shape), log_sums)


def scan_backward(query, keys, mixed, positions, valid, log_sums, grad_out, block_rows):
    count = query.shape[0] // block_rows
    zeros = jnp.zeros(keys.shape, jnp.float32)

    def step(carry, index):
        key_sum, value_sum = carry
        start = index * block_rows
        q_rows = lax.dynamic_slice_in_dim(query, start, block_rows, 0)
        q_pos = lax.dynamic_slice_in_dim(positions, start, block_rows, 0)
        g_rows = lax.dynamic_slice_in_dim(grad_out, start, block_rows, 0)
        scores = masked_scores(q_rows, keys, q_pos, positions, valid)
        weights = jnp.exp(scores - log_sums[index])
        grad_w = jnp.einsum("qhe,khe->hqk", g_rows, mixed, preferred_element_type=jnp.float32)
        delta = jnp.sum(weights * grad_w, axis=-1, keepdims=True)
        grad_s = (weights * (grad_w - delta)).astype(jnp.bfloat16)
        grad_q = 0.125 * jnp.einsum(
            "hqk,khe->qhe", grad_s, keys, preferred_element_type=jnp.float32
        )
        key_sum = key_sum + 0.125 * jnp.einsum(
            "hqk,qhe->khe", grad_s, q_rows, preferred_element_type=jnp.float32
        )
        value_sum = value_sum + jnp.einsum(
            "hqk,qhe->khe", weights.astype(jnp.bfloat16), g_rows, preferred_element_type=jnp.float32
        )
        return ((key_sum, value_sum), grad_q)

    (grad_keys, grad_mixed), grad_query = lax.scan(
        step, (zeros, zeros), jnp.arange(count, dtype=jnp.int32)
    )
    return (grad_query.reshape(query.shape), grad_keys, grad_mixed)


def any_groups(
    inputs,
    first_values,
    lengths,
    gain_attn,
    w_qkv,
    w_out,
    gain_mlp,
    w_gate,
    w_up,
    w_down,
    cotangent,
):
    rows = inputs.shape[1]
    width = inputs.shape[2]
    groups = lax.axis_size("head")
    shards = lax.axis_size("ffn")
    heads_here = HEADS // groups
    span_rows = rows * groups
    block_rows = span_rows // max(1, span_rows // 512)
    head_pos = lax.axis_index("head")
    valid_len = lengths[0]
    packed_cols = heads_here * 3 * HD
    out_cols = heads_here * HD
    hidden_here = w_gate.shape[1]

    owners = [head_pos ^ m for m in range(groups)]
    x_all = [inputs[0]] + [swap(inputs[0], "head", m) for m in range(1, groups)]
    early = []
    for m in range(groups):
        piece = lax.dynamic_slice_in_dim(first_values[0], owners[m] * out_cols, out_cols, 1)
        early.append(swap(piece, "head", m) if m else piece)
    far = range(2, shards, 2)
    grad_rows = jnp.concatenate([cotangent[0]] + [swap(cotangent[0], "ffn", m) for m in far], 0)
    gate_w = jnp.concatenate([w_gate, swap(w_gate, "ffn", 1)], 1)
    up_w = jnp.concatenate([w_up, swap(w_up, "ffn", 1)], 1)
    down_w = jnp.concatenate([w_down, swap(w_down, "ffn", 1)], 0)
    w_heads = lax.dynamic_slice_in_dim(w_qkv, head_pos * packed_cols, packed_cols, 1)
    out_w = jnp.concatenate(
        [lax.dynamic_slice_in_dim(w_out, o * out_cols, out_cols, 0) for o in owners], 0
    )

    positions = jnp.concatenate([o * rows + jnp.arange(rows, dtype=jnp.int32) for o in owners])
    cosine, sine = rotary(positions, HD)
    normed, scaled, queries, key_list, mixes = [], [], [], [], []
    rows_in = inputs[0].astype(jnp.float32)
    scale_one = rms_scale(rows_in)
    for m in range(groups):
        block = x_all[m].astype(jnp.float32)
        scale = rms_scale(block)
        scaled.append(block * scale)
        normed.append((block * scale * gain_attn).astype(jnp.bfloat16))
        packed = matmul(normed[m], w_heads).astype(jnp.bfloat16)
        packed = packed.reshape(rows, heads_here, 3, HD).astype(jnp.float32)
        part = slice(m * rows, (m + 1) * rows)
        queries.append(rotate(packed[:, :, 0], cosine[part], sine[part], 1.0))
        key_list.append(rotate(packed[:, :, 1], cosine[part], sine[part], 1.0))
        value = early[m].reshape(rows, heads_here, HD).astype(jnp.float32)
        mixes.append(0.5 * (packed[:, :, 2] + value))
    query = jnp.concatenate(queries, 0).astype(jnp.bfloat16)
    keys = jnp.concatenate(key_list, 0).astype(jnp.bfloat16)
    mixed = jnp.concatenate(mixes, 0).astype(jnp.bfloat16)
    attended, log_sums = scan_forward(query, keys, mixed, positions, valid_len, block_rows)
    attended = attended.reshape(groups, rows, out_cols)
    att_own = jnp.concatenate(
        [attended[0]] + [swap(attended[m], "head", m) for m in range(1, groups)], 1
    )
    hidden = rows_in + matmul(att_own, out_w)
    scale_two = rms_scale(hidden)
    normed_two = (hidden * scale_two * gain_mlp).astype(jnp.bfloat16)

    mlp_rows = [normed_two] + [swap(normed_two, "ffn", m) for m in far]
    grad_list = [grad_rows[i * rows : (i + 1) * rows] for i in range(len(mlp_rows))]
    actives, grad_gates, grad_ups, downs, grad_normed_list = [], [], [], [], []
    for i, block in enumerate(mlp_rows):
        gate_rows = matmul(block, gate_w)
        up_rows = matmul(block, up_w)
        sigmoid_gate = jax.nn.sigmoid(gate_rows)
        silu_gate = gate_rows * sigmoid_gate
        grad_active = against(grad_list[i], down_w)
        actives.append((silu_gate * up_rows).astype(jnp.bfloat16))
        grad_gates.append(
            (
                grad_active * up_rows * sigmoid_gate * (1.0 + gate_rows * (1.0 - sigmoid_gate))
            ).astype(jnp.bfloat16)
        )
        grad_ups.append((grad_active * silu_gate).astype(jnp.bfloat16))
        grad_normed_list.append(against(grad_gates[i], gate_w) + against(grad_ups[i], up_w))
        downs.append(matmul(actives[i], down_w))
    grad_normed_two = grad_normed_list[0]
    for i, m in enumerate(far):
        came = swap(grad_normed_list[i + 1].astype(jnp.bfloat16), "ffn", m)
        grad_normed_two = grad_normed_two + came.astype(jnp.float32)
    down_rows = downs[0]
    for i, m in enumerate(far):
        down_rows = down_rows + swap(downs[i + 1].astype(jnp.bfloat16), "ffn", m).astype(jnp.float32)
    output = (hidden + down_rows).astype(jnp.bfloat16)[None]

    all_rows = jnp.concatenate(mlp_rows, 0)
    ff_sums = []
    for left, right in (
        (grad_rows, jnp.concatenate(actives, 0)),
        (all_rows, jnp.concatenate(grad_gates, 0)),
        (all_rows, jnp.concatenate(grad_ups, 0)),
    ):
        away = inner_rows(left, right[:, hidden_here:]).astype(jnp.bfloat16)
        part = inner_rows(left, right[:, :hidden_here])
        part = (part + swap(away, "ffn", 1).astype(jnp.float32)).astype(jnp.bfloat16)
        steps = [("head", b) for b in bits_of("head")] + [("row", b) for b in bits_of("row")]
        part = part.reshape([2] * len(steps) + [-1, hidden_here])
        order = [s for s in steps if s[0] == "head"] + [s for s in reversed(steps) if s[0] == "row"]
        left_steps = list(steps)
        for s in order:
            part = halve(part, left_steps.index(s), *s)
            left_steps.remove(s)
            if left_steps:
                part = part.astype(jnp.bfloat16)
        ff_sums.append(part)
    sum_down, sum_gate, sum_up = ff_sums

    grad_y = cotangent[0].astype(jnp.float32)
    grad_gain_two = jnp.sum(grad_normed_two * hidden * scale_two, axis=0)
    weighted_two = grad_normed_two * gain_mlp
    cube_two = scale_two * scale_two * scale_two
    grad_hidden = (
        grad_y
        + scale_two * weighted_two
        - hidden * cube_two * jnp.mean(weighted_two * hidden, axis=-1, keepdims=True)
    )
    grad_proj = grad_hidden.astype(jnp.bfloat16)
    grad_att = against(grad_proj, out_w).astype(jnp.bfloat16)
    grad_att = jnp.concatenate(
        [
            swap(grad_att[:, m * out_cols : (m + 1) * out_cols], "head", m)
            if m
            else grad_att[:, :out_cols]
            for m in range(groups)
        ],
        0,
    ).reshape(span_rows, heads_here, HD)

    def over_buckets(part):
        steps = [("ffn", b) for b in bits_of("ffn")] + [("row", b) for b in bits_of("row")]
        part = part.astype(jnp.bfloat16).reshape([2] * len(steps) + [-1, part.shape[1]])
        order = [s for s in reversed(steps) if s[0] == "ffn"] + [
            s for s in reversed(steps) if s[0] == "row"
        ]
        left_steps = list(steps)
        for s in order:
            part = halve(part, left_steps.index(s), *s)
            left_steps.remove(s)
            if left_steps:
                part = part.astype(jnp.bfloat16)
        return part

    part = over_buckets(inner_rows(grad_proj, att_own))
    sum_out = part[:, :out_cols]
    for m in range(1, groups):
        came = swap(part[:, m * out_cols : (m + 1) * out_cols].astype(jnp.bfloat16), "head", m)
        sum_out = sum_out + came.astype(jnp.float32)

    grad_query, grad_keys, grad_mixed = scan_backward(
        query, keys, mixed, positions, valid_len, log_sums, grad_att, block_rows
    )
    grad_packed = jnp.stack(
        [
            rotate(grad_query, cosine, sine, -1.0),
            rotate(grad_keys, cosine, sine, -1.0),
            0.5 * grad_mixed,
        ],
        axis=2,
    )
    grad_packed = grad_packed.astype(jnp.bfloat16).reshape(span_rows, packed_cols)
    grad_early = (0.5 * grad_mixed).astype(jnp.bfloat16).reshape(span_rows, out_cols)
    firsts = [grad_early[m * rows : (m + 1) * rows] for m in range(groups)]
    firsts = [swap(firsts[m], "head", m) if m else firsts[0] for m in range(groups)]
    grad_first = jnp.zeros((rows, width), jnp.bfloat16)
    for m in range(groups):
        grad_first = lax.dynamic_update_slice_in_dim(grad_first, firsts[m], owners[m] * out_cols, 1)
    shares = [
        against(grad_packed[m * rows : (m + 1) * rows], w_heads) for m in range(groups)
    ]
    grad_gain_one = sum(jnp.sum(shares[m] * scaled[m], axis=0) for m in range(groups))
    grad_normed = shares[0]
    for m in range(1, groups):
        grad_normed = grad_normed + swap(shares[m].astype(jnp.bfloat16), "head", m).astype(jnp.float32)
    sum_qkv = over_buckets(inner_rows(jnp.concatenate(normed, 0), grad_packed))
    weighted_one = grad_normed * gain_attn
    cube_one = scale_one * scale_one * scale_one
    grad_in = (
        grad_hidden
        + scale_one * weighted_one
        - rows_in * cube_one * jnp.mean(weighted_one * rows_in, axis=-1, keepdims=True)
    )
    gains = total(jnp.stack([grad_gain_one, grad_gain_two]), ("ffn", "head", "row"))
    return (
        output,
        grad_in[None],
        grad_first[None],
        gains[0],
        sum_qkv,
        sum_out.T,
        gains[1],
        sum_gate,
        sum_up,
        sum_down.T,
    )


SCALE = 4.5e8
COSTS = {}
SITES = {}


def site_cost(name, usual):
    count = SITES.get(name, 0)
    SITES[name] = count + 1
    return int(SCALE * COSTS.get(name + str(count), usual))


def low(values):
    return values.astype(jnp.bfloat16)


def high(values):
    return values.astype(jnp.float32)


def on_chip(body, outs, scalars, arrays, name, scratch=(), aliases=None, limit=3, cost=1.0, away=(), far=()):
    inside = pl.BlockSpec(memory_space=pltpu.VMEM)
    outside = pl.BlockSpec(memory_space=pl.ANY)
    return pl.pallas_call(
        body,
        out_shape=jax.tree.unflatten(
            jax.tree.structure(outs),
            [
                pltpu.HBM(o.shape, o.dtype) if i in away else o
                for i, o in enumerate(jax.tree.leaves(outs))
            ],
        ),
        in_specs=[pl.BlockSpec(memory_space=pltpu.SMEM)] * len(scalars)
        + [outside if i in far else inside for i in range(len(arrays))],
        out_specs=jax.tree.unflatten(
            jax.tree.structure(outs),
            [
                outside if i in away else inside
                for i in range(len(jax.tree.leaves(outs)))
            ],
        ),
        scratch_shapes=list(scratch),
        input_output_aliases=aliases or {},
        cost_estimate=pl.CostEstimate(
            flops=site_cost(name, cost), transcendentals=0, bytes_accessed=1
        ),
        compiler_params=pltpu.CompilerParams(vmem_limit_bytes=limit << 20),
        name=name,
    )(*scalars, *arrays)


def shape16(*dims):
    return jax.ShapeDtypeStruct(dims, jnp.bfloat16)


def shape32(*dims):
    return jax.ShapeDtypeStruct(dims, jnp.float32)


def spans(total):
    return [(a, min(a + STEP, total)) for a in range(0, total, STEP)]


def turn(values):
    lane = lax.broadcasted_iota(jnp.int32, values.shape, 1)
    return jnp.where(
        lane % HD < HD // 2, pltpu.roll(values, 2 * HD - HD // 2, 1), pltpu.roll(values, HD // 2, 1)
    )


def allowed_keys(a, b, valid):
    size = b - a
    down = lax.broadcasted_iota(jnp.int32, (size, size), 0)
    across = lax.broadcasted_iota(jnp.int32, (size, size), 1)
    allowed = down <= across
    if b > MIN_LEN:
        allowed = allowed & (down < valid - a)
    return allowed


def columns(index, size):
    return pl.ds(pl.multiple_of(index * size, size), size)


def forward_body(
    place, q_ref, k_ref, raw_ref, early_own, early_oth,
    own_far, oth_far, v_far, lse_out, att_own, att_oth, v_out, flipped, att, sems,
):
    rows = early_own.shape[0]
    span = 2 * rows
    wide = 2 * HD
    valid = place[1]
    bf = jnp.bfloat16
    first = lax.broadcasted_iota(jnp.int32, (1, wide), 1) < HD
    flipped[:, HD:, :] = jnp.ones((2, 16, span), bf)

    def copies(p):
        cols = columns(p, wide)
        return [
            pltpu.make_async_copy(near.at[:, cols], far.at[:, cols], sems.at[i, p])
            for i, (near, far) in enumerate(
                ((v_out, v_far), (att_oth, oth_far), (att_own, own_far))
            )
        ]

    def pair(p, _):
        cols = columns(p, wide)
        for m, early in enumerate((early_own, early_oth)):
            here = columns(place[0] ^ m, rows)
            v_out[here, cols] = low(0.5 * (high(raw_ref[here, cols]) + high(early[:, cols])))
        copies(p)[0].start()
        turned = v_out[:, cols].T
        for e in range(2):
            flipped[e, :HD, :] = turned[e * HD : (e + 1) * HD, :]
        for a, b in spans(span):
            q = q_ref[a:b, cols] * jnp.asarray(0.125, bf)
            allowed = allowed_keys(a, b, valid)
            for e in range(2):
                qe = jnp.where(first == (e == 0), q, jnp.zeros_like(q))
                diag = jnp.where(allowed, against(k_ref[a:b, cols], qe), -1e30)
                top = jnp.max(diag, axis=0, keepdims=True)
                if a:
                    past = against(k_ref[:a, cols], qe)
                    top = jnp.maximum(top, jnp.max(past, axis=0, keepdims=True))
                out = matmul(flipped[e, :, a:b], low(jnp.exp(diag - top)))
                if a:
                    out = out + matmul(flipped[e, :, :a], low(jnp.exp(past - top)))
                amount = out[HD : HD + 1, :]
                att[e * HD : (e + 1) * HD, a:b] = out[:HD, :] / amount
                lse_out[p, e : e + 1, a:b] = top + jnp.log(amount)
        result = low(att[...].T)
        upper = place[0] == 0
        att_own[:, cols] = jnp.where(upper, result[:rows, :], result[rows:, :])
        att_oth[:, cols] = jnp.where(upper, result[rows:, :], result[:rows, :])
        for copy in copies(p)[1:]:
            copy.start()
        return 0

    lax.fori_loop(0, lse_out.shape[0], pair, 0)
    for p in range(lse_out.shape[0]):
        for copy in copies(p):
            copy.wait()


def attend_forward(place, query, keys, raw, early_own, early_oth):
    span, cols = query.shape
    rows = span // 2
    heads = cols // HD
    out = shape16(rows, cols)
    natural = shape16(span, cols)
    return on_chip(
        forward_body,
        (out, out, natural, shape32(heads // 2, 2, span)),
        (place,),
        (query, keys, raw, early_own, early_oth),
        "attend_forward",
        cost=9.0,
        limit=6,
        away=(0, 1, 2),
        scratch=(
            pltpu.VMEM(out.shape, jnp.bfloat16),
            pltpu.VMEM(out.shape, jnp.bfloat16),
            pltpu.VMEM(natural.shape, jnp.bfloat16),
            pltpu.VMEM((2, HD + 16, span), jnp.bfloat16),
            pltpu.VMEM((2 * HD, span), jnp.float32),
            pltpu.SemaphoreType.DMA((3, heads // 2)),
        ),
    )


def backward_body(
    start, place, q_far, k_far, v_far, lse_ref, go_own, go_oth, att_own, att_oth, cos_ref, sin_ref,
    d_out, f_own, f_oth, q_ref, k_ref, v_ref, sems, grad, prod, turned_k, dq, dk, dv,
):
    rows = go_own.shape[0]
    span = 2 * rows
    valid = place[1]
    wide = 2 * HD
    bf = jnp.bfloat16
    first = lax.broadcasted_iota(jnp.int32, (1, wide), 1) < HD
    eighth = jnp.asarray(0.125, bf)
    count = f_own.shape[1] // wide

    def copies(i):
        there = columns(i + start, wide)
        here = columns(i, wide)
        return [
            pltpu.make_async_copy(away.at[:, there], near.at[:, here], sems.at[n, i])
            for n, (away, near) in enumerate(((q_far, q_ref), (k_far, k_ref), (v_far, v_ref)))
        ]

    for i in range(count):
        for copy in copies(i):
            copy.start()

    def pair(i, _):
        p = i + start
        cols = columns(p, wide)
        near = columns(i, wide)
        for copy in copies(i):
            copy.wait()
        for m, (go, att) in enumerate(((go_own, att_own), (go_oth, att_oth))):
            here = columns(place[0] ^ m, rows)
            grad[here, :] = go[:, cols]
            prod[here, :] = high(go[:, cols]) * high(att[:, cols])
        flat = prod[...].T
        deltas = [jnp.sum(flat[e * HD : (e + 1) * HD, :], axis=0, keepdims=True) for e in range(2)]
        turned_k[...] = (k_ref[:, near] * eighth).T
        for n, (a, b) in enumerate(spans(span)):
            allowed = allowed_keys(a, b, valid)
            q = q_ref[a:b, near] * eighth
            g = grad[a:b, :]
            parts = ((a, b), (0, a)) if a else ((a, b),)
            sums = {}
            for e in range(2):
                mine = first == (e == 0)
                qe = jnp.where(mine, q, jnp.zeros_like(q))
                ge = jnp.where(mine, g, jnp.zeros_like(g))
                for lo, hi in parts:
                    scores = against(k_ref[lo:hi, near], qe)
                    if lo == a:
                        scores = jnp.where(allowed, scores, -1e30)
                    weights = jnp.exp(scores - lse_ref[p, e : e + 1, a:b])
                    grad_w = against(v_ref[lo:hi, near], ge)
                    grad_s = low(weights * (grad_w - deltas[e][:, a:b]))
                    dv_here = matmul(low(weights), ge)
                    dk_here = matmul(grad_s, qe)
                    dq_here = matmul(turned_k[e * HD : (e + 1) * HD, lo:hi], grad_s)
                    if (lo, "v") in sums:
                        dv_here = dv_here + sums[lo, "v"]
                        dk_here = dk_here + sums[lo, "k"]
                    sums[lo, "v"], sums[lo, "k"] = dv_here, dk_here
                    sums[lo, e] = dq_here
            for e in range(2):
                dq[e * HD : (e + 1) * HD, a:b] = sums[a, e] + sums[0, e] if a else sums[a, e]
            dv[a:b, :] = sums[a, "v"]
            dk[a:b, :] = sums[a, "k"]
            if a:
                dv[:a, :] += sums[0, "v"]
                dk[:a, :] += sums[0, "k"]
        prod[...] = dq[...].T
        for m, f_out in enumerate((f_own, f_oth)):
            here = columns(place[0] ^ m, rows)
            cosine = cos_ref[here, :]
            sine = sin_ref[here, :]
            gv = low(0.5 * dv[here, :])
            gk = dk[here, :]
            gk = low(pltpu.roll(gk * cosine - turn(gk) * sine, HD, 1))
            gq = prod[here, :]
            gq = low(gq * cosine - turn(gq) * sine)
            part = slice(m * rows, (m + 1) * rows)
            base = i * 3 * wide
            d_out[part, pl.ds(pl.multiple_of(base, wide), wide)] = jnp.where(first, gq, gk)
            d_out[part, pl.ds(pl.multiple_of(base + wide, wide), wide)] = jnp.where(first, gv, gq)
            d_out[part, pl.ds(pl.multiple_of(base + 2 * wide, wide), wide)] = jnp.where(first, gk, gv)
            f_out[:, columns(i, wide)] = gv
        return 0

    lax.fori_loop(0, count, pair, 0)


def attend_backward(place, q, k, v, lse, go_own, go_oth, att_own, att_oth, cosine, sine, pairs):
    span = q.shape[0]
    rows = span // 2
    wide = 2 * HD
    cols = wide * (pairs[1] - pairs[0])
    return on_chip(
        functools.partial(backward_body, pairs[0]),
        (shape16(span, 3 * cols), shape16(rows, cols), shape16(rows, cols)),
        (place,),
        (q, k, v, lse, go_own, go_oth, att_own, att_oth, cosine, sine),
        "attend_backward",
        cost=7.5,
        limit=6,
        far=(0, 1, 2),
        scratch=(
            pltpu.VMEM((span, cols), jnp.bfloat16),
            pltpu.VMEM((span, cols), jnp.bfloat16),
            pltpu.VMEM((span, cols), jnp.bfloat16),
            pltpu.SemaphoreType.DMA((3, pairs[1] - pairs[0])),
            pltpu.VMEM((span, wide), jnp.bfloat16),
            pltpu.VMEM((span, wide), jnp.float32),
            pltpu.VMEM((wide, span), jnp.bfloat16),
            pltpu.VMEM((wide, span), jnp.float32),
            pltpu.VMEM((span, wide), jnp.float32),
            pltpu.VMEM((span, wide), jnp.float32),
        ),
    )


def project_body(block, order, place, x_ref, gain_ref, w_ref, cos_ref, sin_ref, *refs):
    away_far, mine_far, q_far, k_far, q_out, k_out, v_out = refs[-12:-5]
    xn, away, mine, packed, sems = refs[-5:]
    rows = x_ref.shape[0]
    wide = 2 * HD
    x = high(x_ref[...])
    xn[...] = low(x * rms_scale(x) * gain_ref[...])
    arrange_halves(order, (xn,), away, mine)
    there = slice(block * rows, (block + 1) * rows)
    here = columns(place[0] ^ block, rows)
    copies = [
        pltpu.make_async_copy(away, away_far.at[there, :], sems.at[0]),
        pltpu.make_async_copy(mine, mine_far.at[there, :], sems.at[1]),
        pltpu.make_async_copy(q_out.at[here, :], q_far.at[here, :], sems.at[2]),
        pltpu.make_async_copy(k_out.at[here, :], k_far.at[here, :], sems.at[3]),
    ]
    for copy in copies[:2]:
        copy.start()
    cols = w_ref.shape[1] // 3
    for i in range(3):
        part = slice(i * cols, (i + 1) * cols)
        packed[:, part] = low(matmul(xn[...], w_ref[:, part]))
    cosine = cos_ref[here, :]
    sine = sin_ref[here, :]
    first = lax.broadcasted_iota(jnp.int32, (1, wide), 1) < HD

    def pair(p, _):
        to = columns(p, wide)
        x0, x1, x2 = [high(packed[:, columns(3 * p + i, wide)]) for i in range(3)]
        q = jnp.where(first, x0, x1)
        k = pltpu.roll(jnp.where(first, x2, x0), HD, 1)
        q_out[here, to] = low(q * cosine + turn(q) * sine)
        k_out[here, to] = low(k * cosine + turn(k) * sine)
        v_out[here, to] = low(jnp.where(first, x1, x2))
        return 0

    lax.fori_loop(0, q_out.shape[1] // wide, pair, 0)
    for copy in copies[2:]:
        copy.start()
    for copy in copies:
        copy.wait()


def project(order, place, x, gain, w, cosine, sine, before=()):
    rows, width = x.shape
    inside = pl.BlockSpec(memory_space=pltpu.VMEM)
    outside = pl.BlockSpec(memory_space=pl.ANY)
    scalar = pl.BlockSpec(memory_space=pltpu.SMEM)
    part = (2 * rows, width // 2)
    natural = (2 * rows, w.shape[1] // 3)
    far = [part, part, natural, natural]
    return pl.pallas_call(
        functools.partial(project_body, 1 if before else 0),
        out_shape=tuple(pltpu.HBM(f, jnp.bfloat16) for f in far) + (shape16(*natural),) * 3,
        in_specs=[scalar] * 2 + [inside] * 5 + ([outside] * 4 + [inside] * 3 if before else []),
        out_specs=(outside,) * 4 + (inside,) * 3,
        scratch_shapes=[
            pltpu.VMEM((rows, width), jnp.bfloat16),
            pltpu.VMEM((rows, width // 2), jnp.bfloat16),
            pltpu.VMEM((rows, width // 2), jnp.bfloat16),
            pltpu.VMEM((rows, w.shape[1]), jnp.bfloat16),
            pltpu.SemaphoreType.DMA((4,)),
        ],
        input_output_aliases={7 + i: i for i in range(len(before))},
        cost_estimate=pl.CostEstimate(
            flops=site_cost("project", 3.0), transcendentals=0, bytes_accessed=1
        ),
        compiler_params=pltpu.CompilerParams(vmem_limit_bytes=8 << 20),
        name="project",
    )(order, place, x, gain, w, cosine, sine, *before)


def arrange(order, blocks, out):
    rows = blocks[0].shape[0]
    size = out.shape[1] // order.shape[0]
    for i in range(order.shape[0]):
        for b, block in enumerate(blocks):
            out[b * rows : (b + 1) * rows, i * size : (i + 1) * size] = block[:, columns(order[i], size)]


def finish(place, x, att_own, att_came, w, gain):
    def body(
        place, x_far, own_far, came_far, w_far, gain_ref,
        hidden_far, hn_ref, hidden_ref, w_ref, att_ref, x_ref, sems,
    ):
        cols = own_far.shape[1]
        x_load = pltpu.make_async_copy(x_far, x_ref, sems.at[5])
        x_load.start()
        loads = []
        for m, far in enumerate((own_far, came_far)):
            there = columns(place[0] ^ m, cols)
            loads.append(pltpu.make_async_copy(far, att_ref.at[m], sems.at[3 + m]))
            loads.append(pltpu.make_async_copy(w_far.at[there, :], w_ref.at[m], sems.at[m]))
        for load in loads:
            load.start()
        x_load.wait()
        hidden = high(x_ref[...])
        for m in range(2):
            loads[2 * m].wait()
            loads[2 * m + 1].wait()
            hidden = hidden + matmul(att_ref[m], w_ref[m])
        hidden_ref[...] = hidden
        copy = pltpu.make_async_copy(hidden_ref, hidden_far, sems.at[2])
        copy.start()
        hn_ref[...] = low(hidden * rms_scale(hidden) * gain_ref[...])
        copy.wait()

    rows, width = x.shape
    return on_chip(
        body,
        (shape32(rows, width), shape16(rows, width)),
        (place,),
        (x, att_own, att_came, w, gain),
        "finish",
        cost=3.0,
        limit=8,
        away=(0,),
        far=(0, 1, 2, 3),
        scratch=(
            pltpu.VMEM((rows, width), jnp.float32),
            pltpu.VMEM((2, width // 2, width), jnp.bfloat16),
            pltpu.VMEM((2, rows, width // 2), jnp.bfloat16),
            pltpu.VMEM((rows, width), jnp.bfloat16),
            pltpu.SemaphoreType.DMA((6,)),
        ),
    )


def reorder(order, *blocks):
    rows, cols = blocks[0].shape

    def body(order, *refs):
        arrange(order, refs[:-1], refs[-1])

    return on_chip(body, shape16(rows * len(blocks), cols), (order,), blocks, "reorder", cost=0.9)


def arrange_halves(order, blocks, away, mine):
    rows = blocks[0].shape[0]
    count = order.shape[0] // 2
    size = mine.shape[1] // count
    for half, out in enumerate((away, mine)):
        for i in range(count):
            for b, block in enumerate(blocks):
                out[b * rows : (b + 1) * rows, i * size : (i + 1) * size] = block[
                    :, columns(order[half * count + i], size)
                ]


def reorder_halves(order, *blocks):
    rows, cols = blocks[0].shape

    def body(order, *refs):
        arrange_halves(order, refs[:-2], *refs[-2:])

    part = shape16(rows * len(blocks), cols // 2)
    return on_chip(body, (part, part), (order,), blocks, "reorder_halves", cost=0.9)


def feed_rows(hn, grads, gate_w, up_w, mine, other, base):
    rows = hn.shape[0]
    units = gate_w[0].shape[0]
    here = slice(base, base + rows)
    total_hn = None
    for s in range(2):
        gate = against(hn[...], gate_w[s][...])
        up = against(hn[...], up_w[s][...])
        grad = high(grads[s][...])
        sig = 1.0 / (1.0 + jnp.exp(-gate))
        silu = gate * sig
        results = (silu * up, grad * up * sig * (1.0 + gate * (1.0 - sig)), grad * silu)
        for i, result in enumerate(results):
            if s == 0:
                mine[i][here, :] = low(result)
            else:
                other[2 * i * rows + base : 2 * i * rows + base + rows, :units] = low(result)
    for s in range(2):
        for i, w in ((1, gate_w[s]), (2, up_w[s])):
            if s == 0:
                share = matmul(mine[i][here, :], w[...])
            else:
                share = matmul(other[2 * i * rows + base : 2 * i * rows + base + rows, :units], w[...])
            total_hn = share if total_hn is None else total_hn + share
    return total_hn


def feed_own_body(order, hn, dy_own, dy_oth, wg0, wg1, wu0, wu1, wd0, wd1, *refs):
    rows = hn.shape[0]
    outs, grads = refs[:9], refs[9:]
    mine, other, dhn, down = outs[:3], outs[3], outs[4], outs[5]
    for grad, w in zip(grads, (wd0, wd1)):
        grad[...] = low(against(dy_own[...], w[...]))
    dhn[...] = feed_rows(hn, grads, (wg0, wg1), (wu0, wu1), mine, other, 0)
    down[...] = matmul(mine[0][:rows, :], wd0[...]) + matmul(other[:rows, : wd1.shape[0]], wd1[...])
    for grad, w in zip(outs[6:8], (wd0, wd1)):
        grad[...] = low(against(dy_oth[...], w[...]))
    arrange(order, (dy_own, dy_oth), outs[8])


def feed_oth_body(order, hn_own, hn, g0, g1, wg0, wg1, wu0, wu1, *refs):
    outs = refs[4:]
    outs[4][...] = low(
        feed_rows(hn, (g0, g1), (wg0, wg1), (wu0, wu1), outs[:3], outs[3], hn.shape[0])
    )
    arrange(order, (hn_own, hn), outs[5])


def feed_own(order, hn, dy_own, dy_oth, gate_w, up_w, down_w):
    rows, width = hn.shape
    units = gate_w[0].shape[0]
    part = shape16(2 * rows, units)
    other = shape16(6 * rows, -(-units // 128) * 128)
    return on_chip(
        feed_own_body,
        (part,) * 3
        + (other,)
        + (shape32(rows, width),) * 2
        + (shape16(rows, units),) * 2
        + (shape16(2 * rows, width),),
        (order,),
        (hn, dy_own, dy_oth, *gate_w, *up_w, *down_w),
        "feed_own",
        limit=15,
        cost=11.0,
        scratch=(pltpu.VMEM((rows, units), jnp.bfloat16),) * 2,
    )


def feed_oth(order, hn_own, hn, grads, gate_w, up_w, parts):
    rows, width = hn.shape
    return on_chip(
        feed_oth_body,
        tuple(shape16(*part.shape) for part in parts)
        + (shape16(rows, width), shape16(2 * rows, width)),
        (order,),
        (hn_own, hn, *grads, *gate_w, *up_w, *parts),
        "feed_oth",
        aliases={9 + i: i for i in range(4)},
        limit=14,
        cost=7.0,
    )


def ff_grad(left, left_core, index, right, right_core, pieces):
    rows, units = left.shape
    size = right.shape[1] // pieces
    half = right.shape[1] // 2

    def body(left, left_core, right, right_core, *outs):
        for i in range(2):
            part = slice(i * half, (i + 1) * half)
            sums = low(
                inner_rows(left[...], right[:, part])
                + inner_rows(left_core[index * rows : (index + 1) * rows, :units], right_core[:, part])
            )
            for j in range(pieces // 2):
                outs[i * pieces // 2 + j][...] = sums[:, j * size : (j + 1) * size]

    part = shape16(units, size)
    return on_chip(
        body, (part,) * pieces, (), (left, left_core, right, right_core), "ff_grad", cost=2.7
    )


def join(first, second):
    def body(first, second, out):
        out[...] = low(high(first[...]) + high(second[...]))

    return on_chip(body, shape16(*first.shape), (), (first, second), "join", cost=0.3)


def fold_three(first, second, third):
    mid = first.shape[1] // 2

    def body(first, second, third, away, rest):
        for out, part in ((away, slice(0, mid)), (rest, slice(mid, 2 * mid))):
            out[...] = low(high(first[:, part]) + high(second[:, part]) + high(third[:, part]))

    part = shape16(first.shape[0], mid)
    return on_chip(body, (part, part), (), (first, second, third), "fold_three", cost=0.3)


def fold(kept, came):
    mid = kept.shape[1] // 2

    def body(kept, came, away, rest):
        away[...] = low(high(kept[:, :mid]) + high(came[:, :mid]))
        rest[...] = low(high(kept[:, mid:]) + high(came[:, mid:]))

    part = shape16(kept.shape[0], mid)
    return on_chip(body, (part, part), (), (kept, came), "fold", cost=0.3)


def fold_rows(kept, came):
    mid = kept.shape[0] // 2

    def body(kept, came, away, rest):
        away[...] = low(high(kept[:mid, :]) + high(came[:mid, :]))
        rest[...] = low(high(kept[mid:, :]) + high(came[mid:, :]))

    part = shape16(mid, kept.shape[1])
    return on_chip(body, (part, part), (), (kept, came), "fold_rows", cost=0.3)


def hidden_grad_body(order, place, dhn_own, dhn_came, hidden_far, dy_ref, gain_ref, w_far,
    grad_ref, send_ref, own_ref, away_ref, mine_ref, gains_ref, proj, hidden_ref, w_ref, sems,
):
    cols = send_ref.shape[1]
    loads = [pltpu.make_async_copy(hidden_far, hidden_ref, sems.at[2])]
    for m in (1, 0):
        there = columns(place[0] ^ m, cols)
        loads.append(pltpu.make_async_copy(w_far.at[there, :], w_ref.at[m], sems.at[m]))
    for load in loads:
        load.start()
    loads[0].wait()
    hidden = hidden_ref[...]
    scale = rms_scale(hidden)
    dhn = dhn_own[...] + high(dhn_came[...])
    gains_ref[...] = jnp.sum(dhn * hidden * scale, axis=0, keepdims=True)
    weighted = dhn * gain_ref[...]
    mean = jnp.mean(weighted * hidden, axis=-1, keepdims=True)
    grad = high(dy_ref[...]) + scale * weighted - hidden * (scale * scale * scale * mean)
    grad_ref[...] = grad
    proj[...] = low(grad)
    loads[1].wait()
    send_ref[...] = low(against(proj[...], w_ref[1]))
    loads[2].wait()
    own_ref[...] = low(against(proj[...], w_ref[0]))
    arrange_halves(order, (proj,), away_ref, mine_ref)


def hidden_grad(order, place, dhn_own, dhn_came, hidden, dy, gain, w):
    rows, width = hidden.shape
    part = shape16(rows, width // 2)
    return on_chip(
        hidden_grad_body,
        (shape32(rows, width), part, part, part, part, shape32(1, width)),
        (order, place),
        (dhn_own, dhn_came, hidden, dy, gain, w),
        "hidden_grad",
        cost=2.2,
        limit=9,
        far=(2, 5),
        scratch=(
            pltpu.VMEM((rows, width), jnp.bfloat16),
            pltpu.VMEM((rows, width), jnp.float32),
            pltpu.VMEM((2, width // 2, width), jnp.bfloat16),
            pltpu.SemaphoreType.DMA((3,)),
        ),
    )


def bucket_grad(left, left_core, rights, rights_core, place=0, total_cols=None, before=()):
    mid = left.shape[1] // 2
    cols = rights[0].shape[1]
    count = len(rights)

    def body(left, left_core, *refs):
        for i in range(count):
            part = slice(place + i * cols, place + (i + 1) * cols)
            for half, out in enumerate(refs[-2:]):
                cut = slice(half * mid, (half + 1) * mid)
                out[:, part] = low(
                    inner_rows(left[:, cut], refs[i][...])
                    + inner_rows(left_core[:, cut], refs[count + i][...])
                )

    full = shape16(mid, total_cols or cols * count)
    return on_chip(
        body,
        (full, full),
        (),
        (left, left_core, *rights, *rights_core, *before),
        "bucket_grad",
        aliases={2 + 2 * count + i: i for i in range(len(before))},
        cost=1.5,
    )


def bucket_near(row, kept, came):
    quarter, cols = kept.shape
    size = quarter // 4

    def body(row, kept, came, away, rest):
        near = row[0] & 1
        for i in range(2):
            here = pl.ds(pl.multiple_of(i * 2 * size + near * size, size), size)
            there = pl.ds(pl.multiple_of(i * 2 * size + (1 - near) * size, size), size)
            part = slice(i * size, (i + 1) * size)
            away[part, :] = low(high(kept[there, :]) + high(came[there, :]))
            rest[part, :] = low(high(kept[here, :]) + high(came[here, :]))

    half = shape16(2 * size, cols)
    return on_chip(body, (half, half), (row,), (kept, came), "bucket_near", cost=0.3)


def shares_body(d_a, d_b, fa, fb, w_ref, x_own, x_oth, gain_two, send_ref, own_ref, gains_ref):
    rows, width = x_own.shape
    cut = d_a.shape[1]
    sums = None
    for m, x_ref in ((1, x_oth), (0, x_own)):
        part = slice(m * rows, (m + 1) * rows)
        share = against(d_a[part, :], w_ref[:, :cut]) + against(d_b[part, :], w_ref[:, cut:])
        if m:
            send_ref[:, :width] = low(share)
        else:
            own_ref[...] = share
        x = high(x_ref[...])
        here = jnp.sum(share * (x * rms_scale(x)), axis=0, keepdims=True)
        sums = here if sums is None else sums + here
    send_ref[:, width : width + fa.shape[1]] = fa[...]
    send_ref[:, width + fa.shape[1] :] = fb[...]
    gains_ref[0:1, :] = sums
    gains_ref[1:2, :] = gain_two[...]


def shares(d_a, d_b, fa, fb, w, x_own, x_oth, gain_two):
    rows, width = x_own.shape
    return on_chip(
        shares_body,
        (shape16(rows, width + 2 * fa.shape[1]), shape32(rows, width), shape32(2, width)),
        (),
        (d_a, d_b, fa, fb, w, x_own, x_oth, gain_two),
        "shares",
        cost=2.3,
    )


def input_grad_body(place, share_ref, came_ref, grad_ref, x_ref, gain_ref, fa, fb, out_ref, first_ref):
    width = x_ref.shape[1]
    x = high(x_ref[...])
    scale = rms_scale(x)
    weighted = (share_ref[...] + high(came_ref[:, :width])) * gain_ref[...]
    mean = jnp.mean(weighted * x, axis=-1, keepdims=True)
    out_ref[...] = grad_ref[...] + scale * weighted - x * (scale * scale * scale * mean)
    cols = fa.shape[1]
    own = 2 * place[0]
    oth = 2 - own
    first_ref[:, columns(own, cols)] = fa[...]
    first_ref[:, columns(own + 1, cols)] = fb[...]
    first_ref[:, columns(oth, cols)] = came_ref[:, width : width + cols]
    first_ref[:, columns(oth + 1, cols)] = came_ref[:, width + cols :]


def input_grad(place, share, came, grad_hidden, x, gain, fa, fb):
    return on_chip(
        input_grad_body,
        (shape32(*x.shape), shape16(*x.shape)),
        (place,),
        (share, came, grad_hidden, x, gain, fa, fb),
        "input_grad",
        cost=2.0,
        limit=6,
    )


def after(first, *values):
    return lax.optimization_barrier((first, *values))[1:]


def two_groups(
    inputs,
    first_values,
    lengths,
    gain_attn,
    w_qkv,
    w_out,
    gain_mlp,
    w_gate,
    w_up,
    w_down,
    cotangent,
):
    SITES.clear()
    rows = inputs.shape[1]
    width = inputs.shape[2]
    span = 2 * rows
    out_cols = HEADS // 2 * HD
    packed_cols = 3 * out_cols
    mid = width // 2
    h = lax.axis_index("head")
    f = lax.axis_index("ffn")
    r = lax.axis_index("row")
    row_size = lax.axis_size("row")
    place = jnp.stack([h, lengths[0]]).astype(jnp.int32)
    row = r.reshape(1).astype(jnp.int32)
    tie = lax.optimization_barrier
    gain_attn = gain_attn.reshape(1, width)
    gain_mlp = gain_mlp.reshape(1, width)

    x_own = inputs[0]
    x_oth = swap(x_own, "head", 1)
    early_own = lax.dynamic_slice_in_dim(first_values[0], h * out_cols, out_cols, 1)
    early_oth = swap(
        lax.dynamic_slice_in_dim(first_values[0], (1 - h) * out_cols, out_cols, 1), "head", 1
    )
    dy_own = cotangent[0]
    down_core = swap(w_down, "ffn", 1)
    gate_core = swap(w_gate.T, "ffn", 1)
    up_core = swap(w_up.T, "ffn", 1)
    qkv_w = lax.dynamic_slice_in_dim(w_qkv, h * packed_cols, packed_cols, 1)
    half = HD // 2
    inverse = jnp.exp(-jnp.log(10000.0) * jnp.arange(half, dtype=jnp.float32) * 2.0 / HD)
    angles = jnp.arange(span, dtype=jnp.float32)[:, None] * jnp.tile(inverse, 4)[None, :]
    cosine = jnp.cos(angles)
    sign = jnp.where(jnp.arange(2 * HD) % HD < half, -1.0, 1.0)
    sine = jnp.sin(angles) * sign[None, :]

    ff_order = jnp.stack([(h ^ a) * row_size + (r ^ b) for a in (1, 0) for b in (3, 1, 2, 0)])
    down_order = jnp.stack([(h ^ a) * row_size + (r ^ b) for b in (3, 1, 2, 0) for a in (1, 0)])
    att_order = jnp.stack(
        [((f ^ a) * row_size + (r & 2 ^ b)) // 2 for a in (3, 1, 2, 0) for b in (2, 0)]
    )

    before = project(att_order, place, x_own, gain_attn, qkv_w, cosine, sine)
    x_oth, before, early_own, down_core, gate_core, up_core = tie(
        (x_oth, before, early_own, down_core, gate_core, up_core)
    )
    xn_away, xn_mine, query, keys, *near = project(
        att_order, place, x_oth, gain_attn, qkv_w, cosine, sine, before
    )
    att_own, att_oth, mixed, log_sums = attend_forward(place, *near, early_own, early_oth)
    att_came = swap(att_oth, "head", 1)
    (dy_send,) = after(near[2], dy_own)
    dy_oth = swap(dy_send, "ffn", 2)
    att_came, dy_oth = tie((att_came, dy_oth))
    down_w = (w_down, down_core)
    gate_w = (w_gate.T, gate_core)
    up_w = (w_up.T, up_core)
    hidden, hn_own = finish(place, x_own, att_own, att_came, w_out, gain_mlp)
    hn_oth = swap(hn_own, "ffn", 2)
    dy_send, dy_oth = after(hn_own, dy_send, dy_oth)
    dyc_own = swap(dy_send, "ffn", 1)
    dyc_oth = swap(dy_oth, "ffn", 1)
    hnc_own = swap(hn_own, "ffn", 1)

    *parts, dhn_own, down_own, dact0, dact1, dy_all = feed_own(
        down_order, hn_own, dy_own, dy_oth, gate_w, up_w, down_w
    )
    hn_oth, parts, dhn_own, down_own, dact0, dact1, dy_all, hnc_own, dyc_own, dyc_oth = tie(
        (hn_oth, parts, dhn_own, down_own, dact0, dact1, dy_all, hnc_own, dyc_own, dyc_oth)
    )
    hnc_oth = swap(hn_oth, "ffn", 1)
    act, gate, up, others, dhn_send, hn_all = feed_oth(
        ff_order, hn_own, hn_oth, (dact0, dact1), gate_w, up_w, parts
    )
    dhn_came = swap(dhn_send, "ffn", 2)
    others_core = swap(others, "ffn", 1)
    own_send, came_send = after(dhn_send, att_own, att_came)
    att_core = swap(own_send, "ffn", 1)
    came_core = swap(came_send, "ffn", 1)
    hnc_oth, dyc_own, dyc_oth = after(dhn_send, hnc_oth, dyc_own, dyc_oth)
    dyc_all = reorder(down_order, dyc_own, dyc_oth)
    hnc_all = reorder(ff_order, hnc_own, hnc_oth)

    gate_a, gate_b, gate_near, gate_kept = ff_grad(gate, others_core, 1, hn_all, hnc_all, 4)
    gate_xa = swap(gate_a, "head", 1)
    down_send, down_kept = ff_grad(act, others_core, 0, dy_all, dyc_all, 2)
    down_near = swap(down_send, "row", 1)
    up_a, up_b, up_near, up_kept = ff_grad(up, others_core, 2, hn_all, hnc_all, 4)
    dhn_came, gate_b, gate_kept, gate_near, down_kept, up_a, up_b, up_near, up_kept = tie(
        (dhn_came, gate_b, gate_kept, gate_near, down_kept, up_a, up_b, up_near, up_kept)
    )

    grad_hidden, go_send, go_own, proj_away, proj_mine, gain_two = hidden_grad(
        att_order, place, dhn_own, dhn_came, hidden, dy_own, gain_mlp, w_out
    )
    (gate_near,) = after(go_send, gate_near)
    gate_send = join(gate_near, gate_xa)
    go_send, go_own, proj_away, gate_send = tie((go_send, go_own, proj_away, gate_send))
    go_oth = swap(go_send, "head", 1)
    proj_core = swap(proj_away, "ffn", 1)
    gate_came = swap(gate_send, "row", 1)
    (gate_b,) = after(go_send, gate_b)
    gate_xb = swap(gate_b, "head", 1)
    out_send, out_kept = bucket_grad(
        proj_mine, proj_core, (att_came, att_own), (came_core, att_core)
    )
    out_y = swap(out_send, "ffn", 2)
    up_xa = swap(after(out_send, up_a)[0], "head", 1)
    go_oth, out_kept = tie((go_oth, out_kept))

    def backward(pairs, lse):
        return attend_backward(
            place, query, keys, mixed, lse, go_own, go_oth, att_own, att_oth, cosine, sine, pairs
        )

    pairs = HEADS // 4
    d_a, fa_own, fa_oth = backward((0, pairs // 2), log_sums)
    out_kept, down_kept, gate_kept = after(d_a, out_kept, down_kept, gate_kept)
    out_send, out_kept = fold(out_kept, out_y)
    out_x = swap(out_send, "head", 1)
    down_send, down_kept = fold(down_kept, down_near)
    down_mid = swap(down_send, "row", 2)
    gate_kept = join(gate_kept, gate_xb)
    d_a, out_kept, down_kept, gate_kept, log_sums = tie(
        (d_a, out_kept, down_kept, gate_kept, log_sums)
    )
    core_a = swap(d_a, "ffn", 1)
    xn_core = swap(after(out_kept, xn_away)[0], "ffn", 1)
    d_b, fb_own, fb_oth = backward((pairs // 2, pairs), log_sums)
    gate_kept, up_near = after(d_b, gate_kept, up_near)
    gate_send, gate_kept = fold(gate_kept, gate_came)
    up_send = join(up_near, up_xa)
    d_b, gate_kept, up_send = tie((d_b, gate_kept, up_send))
    core_b = swap(d_b, "ffn", 1)
    up_xb = swap(after(gate_kept, up_b)[0], "head", 1)
    up_came = swap(up_send, "row", 1)
    (d_a,) = after(gate_kept, d_a)
    before = bucket_grad(xn_mine, xn_core, (d_a,), (core_a,), 0, packed_cols)
    core_b, *before = tie((core_b, *before))
    y_send, kept = bucket_grad(
        xn_mine, xn_core, (d_b,), (core_b,), packed_cols // 2, packed_cols, before
    )
    y_came = swap(y_send, "ffn", 2)
    d_a, d_b = after(y_send, d_a, d_b)
    back_send, share_own, gains = shares(
        d_a, d_b, fa_oth, fb_oth, qkv_w, x_own, x_oth, gain_two
    )
    gate_send, out_kept, act, others, up_kept, down_kept = after(
        back_send, gate_send, out_kept, act, others, up_kept, down_kept
    )
    out_send, out_kept = bucket_near(row, out_kept, out_x)
    out_near = swap(out_send, "row", 1)
    gains = gains + swap(gains, "head", 1)
    gains, back_send = tie((gains, back_send))
    back_came = swap(back_send, "head", 1)
    up_kept, down_kept = after(gains, up_kept, down_kept)
    up_send, up_kept = fold_three(up_kept, up_xb, up_came)
    gate_far = swap(gate_send, "row", 2)
    units = w_down.shape[0]
    far_send = low(matmul(act[rows:], down_w[0]) + matmul(others[rows:span, :units], down_w[1]))
    gains, down_kept, gate_kept, out_kept = after(far_send, gains, down_kept, gate_kept, out_kept)
    gains = gains + swap(gains, "ffn", 1)
    down_send, down_kept = fold(down_kept, down_mid)
    out_send, out_kept = fold_rows(out_kept, out_near)
    out_far = swap(out_send, "row", 2)
    sum_gate = high(gate_kept) + high(gate_far)
    kept, up_send, down_send, sum_gate, gains, out_send = tie(
        (kept, up_send, down_send, sum_gate, gains, out_send)
    )

    near_send, kept = bucket_near(row, kept, y_came)
    near_came = swap(near_send, "row", 1)
    gains, far_send, out_kept, up_send, down_send = after(
        near_send, gains, far_send, out_kept, up_send, down_send
    )
    gains_y = swap(gains, "ffn", 2)
    far_came = swap(far_send, "ffn", 2)
    up_far = swap(up_send, "row", 2)
    qkv_send, kept = fold_rows(kept, near_came)
    qkv_far = swap(qkv_send, "row", 2)
    share_own, down_kept, up_kept, out_kept, residual, gains, down_send = after(
        qkv_send,
        share_own,
        down_kept,
        up_kept,
        out_kept,
        hidden + down_own,
        gains,
        down_send,
    )
    down_x = swap(down_send, "head", 1)
    gains = gains + gains_y
    gains = gains + swap(gains, "row", 1)
    gains_far = swap(gains, "row", 2)
    (share_own,) = after(gains, share_own)
    grad_in, grad_first = input_grad(
        place, share_own, back_came, grad_hidden, x_own, gain_attn, fa_own, fb_own
    )
    sum_up = high(up_kept) + high(up_far)
    sum_down = high(down_kept) + high(down_x)
    out_sum = high(out_kept) + high(out_far)
    output = low(residual + high(far_came))[None]
    gains = gains + gains_far
    kept, grad_in, sum_up, sum_down, out_sum, output, gains = tie(
        (kept, grad_in, sum_up, sum_down, out_sum, output, gains)
    )
    sum_qkv = high(kept) + high(qkv_far)
    return (
        output,
        grad_in[None],
        grad_first[None],
        gains[0],
        sum_qkv,
        out_sum.T,
        gains[1],
        sum_gate.T,
        sum_up.T,
        sum_down,
    )


def solution(mesh):
    in_specs = (
        P(("ffn", "row"), "head", None),
        P(("ffn", "row"), "head", None),
        P(("ffn", "row")),
        P(),
        P(),
        P(),
        P(),
        P(None, "ffn"),
        P(None, "ffn"),
        P("ffn", None),
        P(("ffn", "row"), "head", None),
    )
    out_specs = (
        P(("ffn", "row"), "head", None),
        P(("ffn", "row"), "head", None),
        P(("ffn", "row"), "head", None),
        P(),
        P(("ffn", "row"), "head"),
        P("head", ("ffn", "row")),
        P(),
        P(("head", "row"), "ffn"),
        P(("head", "row"), "ffn"),
        P("ffn", ("head", "row")),
    )
    body = two_groups if mesh.shape["head"] == 2 and mesh.shape["ffn"] == 4 else any_groups
    return jax.shard_map(
        body, mesh=mesh, in_specs=in_specs, out_specs=out_specs, check_vma=False
    )
```

```python
import functools

import jax
import jax.numpy as jnp
from jax import lax
from jax.experimental import pallas as pl
from jax.experimental.pallas import tpu as pltpu
from jax.sharding import PartitionSpec as P

HEADS = 16
HD = 64
MIN_LEN = 512
STEP = 256


eps = 1e-06


def rms_scale(values):
    return lax.rsqrt(jnp.mean(values * values, axis=-1, keepdims=True) + eps)


def matmul(left, right):
    return jnp.dot(left, right, preferred_element_type=jnp.float32)


def inner_rows(left, right):
    return lax.dot_general(
        left, right, (((0,), (0,)), ((), ())), preferred_element_type=jnp.float32
    )


def against(left, right):
    return lax.dot_general(
        left, right, (((1,), (1,)), ((), ())), preferred_element_type=jnp.float32
    )


def swap(values, axis, mask):
    size = lax.axis_size(axis)
    return lax.ppermute(values, axis, [(i, i ^ mask) for i in range(size)])


def bits_of(axis):
    size = lax.axis_size(axis)
    return [1 << b for b in range(size.bit_length() - 2, -1, -1)]


def halve(values, dim, axis, mask):
    bit = (lax.axis_index(axis) // mask) % 2
    away = lax.dynamic_index_in_dim(values, 1 - bit, dim, keepdims=False)
    kept = lax.dynamic_index_in_dim(values, bit, dim, keepdims=False)
    came = swap(away.astype(jnp.bfloat16), axis, mask)
    return kept.astype(jnp.float32) + came.astype(jnp.float32)


def total(values, axes):
    for axis in axes:
        for mask in reversed(bits_of(axis)):
            values = values + swap(values, axis, mask)
    return values


def rotary(positions, head_size):
    half_size = head_size // 2
    inverse = jnp.exp(
        -jnp.log(10000.0) * jnp.arange(half_size, dtype=jnp.float32) * 2.0 / head_size
    )
    angles = positions.astype(jnp.float32)[:, None] * inverse[None, :]
    return (jnp.cos(angles), jnp.sin(angles))


def rotate(vectors, cosine, sine, sign):
    half_size = vectors.shape[-1] // 2
    first_half = vectors[..., :half_size]
    second_half = vectors[..., half_size:]
    cos_rows = cosine[:, None, :]
    sin_rows = sign * sine[:, None, :]
    return jnp.concatenate(
        [
            first_half * cos_rows - second_half * sin_rows,
            second_half * cos_rows + first_half * sin_rows,
        ],
        axis=-1,
    )


def masked_scores(q_rows, keys, q_pos, k_pos, valid):
    raw = jnp.einsum("qhe,khe->hqk", q_rows, keys, preferred_element_type=jnp.float32)
    allowed = (k_pos[None, :] <= q_pos[:, None]) & (k_pos[None, :] < valid)
    return jnp.where(allowed[None], 0.125 * raw, -1e30)


def scan_forward(query, keys, mixed, positions, valid, block_rows):
    count = query.shape[0] // block_rows

    def step(carry, index):
        start = index * block_rows
        q_rows = lax.dynamic_slice_in_dim(query, start, block_rows, 0)
        q_pos = lax.dynamic_slice_in_dim(positions, start, block_rows, 0)
        scores = masked_scores(q_rows, keys, q_pos, positions, valid)
        top = jnp.max(scores, axis=-1, keepdims=True)
        expo = jnp.exp(scores - top)
        total_w = jnp.sum(expo, axis=-1, keepdims=True)
        weights = expo / total_w
        result = jnp.einsum(
            "hqk,khe->qhe", weights.astype(jnp.bfloat16), mixed, preferred_element_type=jnp.float32
        )
        return (carry, (result.astype(jnp.bfloat16), top + jnp.log(total_w)))

    _, (outs, log_sums) = lax.scan(step, 0, jnp.arange(count, dtype=jnp.int32))
    return (outs.reshape(query.shape), log_sums)


def scan_backward(query, keys, mixed, positions, valid, log_sums, grad_out, block_rows):
    count = query.shape[0] // block_rows
    zeros = jnp.zeros(keys.shape, jnp.float32)

    def step(carry, index):
        key_sum, value_sum = carry
        start = index * block_rows
        q_rows = lax.dynamic_slice_in_dim(query, start, block_rows, 0)
        q_pos = lax.dynamic_slice_in_dim(positions, start, block_rows, 0)
        g_rows = lax.dynamic_slice_in_dim(grad_out, start, block_rows, 0)
        scores = masked_scores(q_rows, keys, q_pos, positions, valid)
        weights = jnp.exp(scores - log_sums[index])
        grad_w = jnp.einsum("qhe,khe->hqk", g_rows, mixed, preferred_element_type=jnp.float32)
        delta = jnp.sum(weights * grad_w, axis=-1, keepdims=True)
        grad_s = (weights * (grad_w - delta)).astype(jnp.bfloat16)
        grad_q = 0.125 * jnp.einsum(
            "hqk,khe->qhe", grad_s, keys, preferred_element_type=jnp.float32
        )
        key_sum = key_sum + 0.125 * jnp.einsum(
            "hqk,qhe->khe", grad_s, q_rows, preferred_element_type=jnp.float32
        )
        value_sum = value_sum + jnp.einsum(
            "hqk,qhe->khe", weights.astype(jnp.bfloat16), g_rows, preferred_element_type=jnp.float32
        )
        return ((key_sum, value_sum), grad_q)

    (grad_keys, grad_mixed), grad_query = lax.scan(
        step, (zeros, zeros), jnp.arange(count, dtype=jnp.int32)
    )
    return (grad_query.reshape(query.shape), grad_keys, grad_mixed)


def any_groups(
    inputs,
    first_values,
    lengths,
    gain_attn,
    w_qkv,
    w_out,
    gain_mlp,
    w_gate,
    w_up,
    w_down,
    cotangent,
):
    rows = inputs.shape[1]
    width = inputs.shape[2]
    groups = lax.axis_size("head")
    shards = lax.axis_size("ffn")
    heads_here = HEADS // groups
    span_rows = rows * groups
    block_rows = span_rows // max(1, span_rows // 512)
    head_pos = lax.axis_index("head")
    valid_len = lengths[0]
    packed_cols = heads_here * 3 * HD
    out_cols = heads_here * HD
    hidden_here = w_gate.shape[1]

    owners = [head_pos ^ m for m in range(groups)]
    x_all = [inputs[0]] + [swap(inputs[0], "head", m) for m in range(1, groups)]
    early = []
    for m in range(groups):
        piece = lax.dynamic_slice_in_dim(first_values[0], owners[m] * out_cols, out_cols, 1)
        early.append(swap(piece, "head", m) if m else piece)
    far = range(2, shards, 2)
    grad_rows = jnp.concatenate([cotangent[0]] + [swap(cotangent[0], "ffn", m) for m in far], 0)
    gate_w = jnp.concatenate([w_gate, swap(w_gate, "ffn", 1)], 1)
    up_w = jnp.concatenate([w_up, swap(w_up, "ffn", 1)], 1)
    down_w = jnp.concatenate([w_down, swap(w_down, "ffn", 1)], 0)
    w_heads = lax.dynamic_slice_in_dim(w_qkv, head_pos * packed_cols, packed_cols, 1)
    out_w = jnp.concatenate(
        [lax.dynamic_slice_in_dim(w_out, o * out_cols, out_cols, 0) for o in owners], 0
    )

    positions = jnp.concatenate([o * rows + jnp.arange(rows, dtype=jnp.int32) for o in owners])
    cosine, sine = rotary(positions, HD)
    normed, scaled, queries, key_list, mixes = [], [], [], [], []
    rows_in = inputs[0].astype(jnp.float32)
    scale_one = rms_scale(rows_in)
    for m in range(groups):
        block = x_all[m].astype(jnp.float32)
        scale = rms_scale(block)
        scaled.append(block * scale)
        normed.append((block * scale * gain_attn).astype(jnp.bfloat16))
        packed = matmul(normed[m], w_heads).astype(jnp.bfloat16)
        packed = packed.reshape(rows, heads_here, 3, HD).astype(jnp.float32)
        part = slice(m * rows, (m + 1) * rows)
        queries.append(rotate(packed[:, :, 0], cosine[part], sine[part], 1.0))
        key_list.append(rotate(packed[:, :, 1], cosine[part], sine[part], 1.0))
        value = early[m].reshape(rows, heads_here, HD).astype(jnp.float32)
        mixes.append(0.5 * (packed[:, :, 2] + value))
    query = jnp.concatenate(queries, 0).astype(jnp.bfloat16)
    keys = jnp.concatenate(key_list, 0).astype(jnp.bfloat16)
    mixed = jnp.concatenate(mixes, 0).astype(jnp.bfloat16)
    attended, log_sums = scan_forward(query, keys, mixed, positions, valid_len, block_rows)
    attended = attended.reshape(groups, rows, out_cols)
    att_own = jnp.concatenate(
        [attended[0]] + [swap(attended[m], "head", m) for m in range(1, groups)], 1
    )
    hidden = rows_in + matmul(att_own, out_w)
    scale_two = rms_scale(hidden)
    normed_two = (hidden * scale_two * gain_mlp).astype(jnp.bfloat16)

    mlp_rows = [normed_two] + [swap(normed_two, "ffn", m) for m in far]
    grad_list = [grad_rows[i * rows : (i + 1) * rows] for i in range(len(mlp_rows))]
    actives, grad_gates, grad_ups, downs, grad_normed_list = [], [], [], [], []
    for i, block in enumerate(mlp_rows):
        gate_rows = matmul(block, gate_w)
        up_rows = matmul(block, up_w)
        sigmoid_gate = jax.nn.sigmoid(gate_rows)
        silu_gate = gate_rows * sigmoid_gate
        grad_active = against(grad_list[i], down_w)
        actives.append((silu_gate * up_rows).astype(jnp.bfloat16))
        grad_gates.append(
            (
                grad_active * up_rows * sigmoid_gate * (1.0 + gate_rows * (1.0 - sigmoid_gate))
            ).astype(jnp.bfloat16)
        )
        grad_ups.append((grad_active * silu_gate).astype(jnp.bfloat16))
        grad_normed_list.append(against(grad_gates[i], gate_w) + against(grad_ups[i], up_w))
        downs.append(matmul(actives[i], down_w))
    grad_normed_two = grad_normed_list[0]
    for i, m in enumerate(far):
        came = swap(grad_normed_list[i + 1].astype(jnp.bfloat16), "ffn", m)
        grad_normed_two = grad_normed_two + came.astype(jnp.float32)
    down_rows = downs[0]
    for i, m in enumerate(far):
        down_rows = down_rows + swap(downs[i + 1].astype(jnp.bfloat16), "ffn", m).astype(jnp.float32)
    output = (hidden + down_rows).astype(jnp.bfloat16)[None]

    all_rows = jnp.concatenate(mlp_rows, 0)
    ff_sums = []
    for left, right in (
        (grad_rows, jnp.concatenate(actives, 0)),
        (all_rows, jnp.concatenate(grad_gates, 0)),
        (all_rows, jnp.concatenate(grad_ups, 0)),
    ):
        away = inner_rows(left, right[:, hidden_here:]).astype(jnp.bfloat16)
        part = inner_rows(left, right[:, :hidden_here])
        part = (part + swap(away, "ffn", 1).astype(jnp.float32)).astype(jnp.bfloat16)
        steps = [("head", b) for b in bits_of("head")] + [("row", b) for b in bits_of("row")]
        part = part.reshape([2] * len(steps) + [-1, hidden_here])
        order = [s for s in steps if s[0] == "head"] + [s for s in reversed(steps) if s[0] == "row"]
        left_steps = list(steps)
        for s in order:
            part = halve(part, left_steps.index(s), *s)
            left_steps.remove(s)
            if left_steps:
                part = part.astype(jnp.bfloat16)
        ff_sums.append(part)
    sum_down, sum_gate, sum_up = ff_sums

    grad_y = cotangent[0].astype(jnp.float32)
    grad_gain_two = jnp.sum(grad_normed_two * hidden * scale_two, axis=0)
    weighted_two = grad_normed_two * gain_mlp
    cube_two = scale_two * scale_two * scale_two
    grad_hidden = (
        grad_y
        + scale_two * weighted_two
        - hidden * cube_two * jnp.mean(weighted_two * hidden, axis=-1, keepdims=True)
    )
    grad_proj = grad_hidden.astype(jnp.bfloat16)
    grad_att = against(grad_proj, out_w).astype(jnp.bfloat16)
    grad_att = jnp.concatenate(
        [
            swap(grad_att[:, m * out_cols : (m + 1) * out_cols], "head", m)
            if m
            else grad_att[:, :out_cols]
            for m in range(groups)
        ],
        0,
    ).reshape(span_rows, heads_here, HD)

    def over_buckets(part):
        steps = [("ffn", b) for b in bits_of("ffn")] + [("row", b) for b in bits_of("row")]
        part = part.astype(jnp.bfloat16).reshape([2] * len(steps) + [-1, part.shape[1]])
        order = [s for s in reversed(steps) if s[0] == "ffn"] + [
            s for s in reversed(steps) if s[0] == "row"
        ]
        left_steps = list(steps)
        for s in order:
            part = halve(part, left_steps.index(s), *s)
            left_steps.remove(s)
            if left_steps:
                part = part.astype(jnp.bfloat16)
        return part

    part = over_buckets(inner_rows(grad_proj, att_own))
    sum_out = part[:, :out_cols]
    for m in range(1, groups):
        came = swap(part[:, m * out_cols : (m + 1) * out_cols].astype(jnp.bfloat16), "head", m)
        sum_out = sum_out + came.astype(jnp.float32)

    grad_query, grad_keys, grad_mixed = scan_backward(
        query, keys, mixed, positions, valid_len, log_sums, grad_att, block_rows
    )
    grad_packed = jnp.stack(
        [
            rotate(grad_query, cosine, sine, -1.0),
            rotate(grad_keys, cosine, sine, -1.0),
            0.5 * grad_mixed,
        ],
        axis=2,
    )
    grad_packed = grad_packed.astype(jnp.bfloat16).reshape(span_rows, packed_cols)
    grad_early = (0.5 * grad_mixed).astype(jnp.bfloat16).reshape(span_rows, out_cols)
    firsts = [grad_early[m * rows : (m + 1) * rows] for m in range(groups)]
    firsts = [swap(firsts[m], "head", m) if m else firsts[0] for m in range(groups)]
    grad_first = jnp.zeros((rows, width), jnp.bfloat16)
    for m in range(groups):
        grad_first = lax.dynamic_update_slice_in_dim(grad_first, firsts[m], owners[m] * out_cols, 1)
    shares = [
        against(grad_packed[m * rows : (m + 1) * rows], w_heads) for m in range(groups)
    ]
    grad_gain_one = sum(jnp.sum(shares[m] * scaled[m], axis=0) for m in range(groups))
    grad_normed = shares[0]
    for m in range(1, groups):
        grad_normed = grad_normed + swap(shares[m].astype(jnp.bfloat16), "head", m).astype(jnp.float32)
    sum_qkv = over_buckets(inner_rows(jnp.concatenate(normed, 0), grad_packed))
    weighted_one = grad_normed * gain_attn
    cube_one = scale_one * scale_one * scale_one
    grad_in = (
        grad_hidden
        + scale_one * weighted_one
        - rows_in * cube_one * jnp.mean(weighted_one * rows_in, axis=-1, keepdims=True)
    )
    gains = total(jnp.stack([grad_gain_one, grad_gain_two]), ("ffn", "head", "row"))
    return (
        output,
        grad_in[None],
        grad_first[None],
        gains[0],
        sum_qkv,
        sum_out.T,
        gains[1],
        sum_gate,
        sum_up,
        sum_down.T,
    )


SCALE = 4.5e8
COSTS = {}
SITES = {}


def site_cost(name, usual):
    count = SITES.get(name, 0)
    SITES[name] = count + 1
    return int(SCALE * COSTS.get(name + str(count), usual))


def low(values):
    return values.astype(jnp.bfloat16)


def high(values):
    return values.astype(jnp.float32)


def on_chip(body, outs, scalars, arrays, name, scratch=(), aliases=None, limit=3, cost=1.0, away=(), far=()):
    inside = pl.BlockSpec(memory_space=pltpu.VMEM)
    outside = pl.BlockSpec(memory_space=pl.ANY)
    return pl.pallas_call(
        body,
        out_shape=jax.tree.unflatten(
            jax.tree.structure(outs),
            [
                pltpu.HBM(o.shape, o.dtype) if i in away else o
                for i, o in enumerate(jax.tree.leaves(outs))
            ],
        ),
        in_specs=[pl.BlockSpec(memory_space=pltpu.SMEM)] * len(scalars)
        + [outside if i in far else inside for i in range(len(arrays))],
        out_specs=jax.tree.unflatten(
            jax.tree.structure(outs),
            [
                outside if i in away else inside
                for i in range(len(jax.tree.leaves(outs)))
            ],
        ),
        scratch_shapes=list(scratch),
        input_output_aliases=aliases or {},
        cost_estimate=pl.CostEstimate(
            flops=site_cost(name, cost), transcendentals=0, bytes_accessed=1
        ),
        compiler_params=pltpu.CompilerParams(vmem_limit_bytes=limit << 20),
        name=name,
    )(*scalars, *arrays)


def shape16(*dims):
    return jax.ShapeDtypeStruct(dims, jnp.bfloat16)


def shape32(*dims):
    return jax.ShapeDtypeStruct(dims, jnp.float32)


def spans(total):
    return [(a, min(a + STEP, total)) for a in range(0, total, STEP)]


def turn(values):
    lane = lax.broadcasted_iota(jnp.int32, values.shape, 1)
    return jnp.where(
        lane % HD < HD // 2, pltpu.roll(values, 2 * HD - HD // 2, 1), pltpu.roll(values, HD // 2, 1)
    )


def allowed_keys(a, b, valid):
    size = b - a
    down = lax.broadcasted_iota(jnp.int32, (size, size), 0)
    across = lax.broadcasted_iota(jnp.int32, (size, size), 1)
    allowed = down <= across
    if b > MIN_LEN:
        allowed = allowed & (down < valid - a)
    return allowed


def columns(index, size):
    return pl.ds(pl.multiple_of(index * size, size), size)


def forward_body(
    place, q_ref, k_ref, raw_ref, early_own, early_oth,
    own_far, oth_far, v_far, lse_out, att_own, att_oth, v_out, flipped, att, sems,
):
    rows = early_own.shape[0]
    span = 2 * rows
    wide = 2 * HD
    valid = place[1]
    bf = jnp.bfloat16
    first = lax.broadcasted_iota(jnp.int32, (1, wide), 1) < HD
    flipped[:, HD:, :] = jnp.ones((2, 16, span), bf)

    def copies(p):
        cols = columns(p, wide)
        return [
            pltpu.make_async_copy(near.at[:, cols], far.at[:, cols], sems.at[i, p])
            for i, (near, far) in enumerate(
                ((v_out, v_far), (att_oth, oth_far), (att_own, own_far))
            )
        ]

    def pair(p, _):
        cols = columns(p, wide)
        for m, early in enumerate((early_own, early_oth)):
            here = columns(place[0] ^ m, rows)
            v_out[here, cols] = low(0.5 * (high(raw_ref[here, cols]) + high(early[:, cols])))
        copies(p)[0].start()
        turned = v_out[:, cols].T
        for e in range(2):
            flipped[e, :HD, :] = turned[e * HD : (e + 1) * HD, :]
        for a, b in spans(span):
            q = q_ref[a:b, cols] * jnp.asarray(0.125, bf)
            allowed = allowed_keys(a, b, valid)
            for e in range(2):
                qe = jnp.where(first == (e == 0), q, jnp.zeros_like(q))
                diag = jnp.where(allowed, against(k_ref[a:b, cols], qe), -1e30)
                top = jnp.max(diag, axis=0, keepdims=True)
                if a:
                    past = against(k_ref[:a, cols], qe)
                    top = jnp.maximum(top, jnp.max(past, axis=0, keepdims=True))
                out = matmul(flipped[e, :, a:b], low(jnp.exp(diag - top)))
                if a:
                    out = out + matmul(flipped[e, :, :a], low(jnp.exp(past - top)))
                amount = out[HD : HD + 1, :]
                att[e * HD : (e + 1) * HD, a:b] = out[:HD, :] / amount
                lse_out[p, e : e + 1, a:b] = top + jnp.log(amount)
        result = low(att[...].T)
        upper = place[0] == 0
        att_own[:, cols] = jnp.where(upper, result[:rows, :], result[rows:, :])
        att_oth[:, cols] = jnp.where(upper, result[rows:, :], result[:rows, :])
        for copy in copies(p)[1:]:
            copy.start()
        return 0

    lax.fori_loop(0, lse_out.shape[0], pair, 0)
    for p in range(lse_out.shape[0]):
        for copy in copies(p):
            copy.wait()


def attend_forward(place, query, keys, raw, early_own, early_oth):
    span, cols = query.shape
    rows = span // 2
    heads = cols // HD
    out = shape16(rows, cols)
    natural = shape16(span, cols)
    return on_chip(
        forward_body,
        (out, out, natural, shape32(heads // 2, 2, span)),
        (place,),
        (query, keys, raw, early_own, early_oth),
        "attend_forward",
        cost=9.0,
        limit=6,
        away=(0, 1, 2),
        scratch=(
            pltpu.VMEM(out.shape, jnp.bfloat16),
            pltpu.VMEM(out.shape, jnp.bfloat16),
            pltpu.VMEM(natural.shape, jnp.bfloat16),
            pltpu.VMEM((2, HD + 16, span), jnp.bfloat16),
            pltpu.VMEM((2 * HD, span), jnp.float32),
            pltpu.SemaphoreType.DMA((3, heads // 2)),
        ),
    )


def backward_body(
    start, place, q_far, k_far, v_far, lse_ref, go_own, go_oth, att_own, att_oth, cos_ref, sin_ref,
    d_out, f_own, f_oth, q_ref, k_ref, v_ref, sems, grad, prod, turned_k, dq, dk, dv,
):
    rows = go_own.shape[0]
    span = 2 * rows
    valid = place[1]
    wide = 2 * HD
    bf = jnp.bfloat16
    first = lax.broadcasted_iota(jnp.int32, (1, wide), 1) < HD
    eighth = jnp.asarray(0.125, bf)
    count = f_own.shape[1] // wide

    def copies(i):
        there = columns(i + start, wide)
        here = columns(i, wide)
        return [
            pltpu.make_async_copy(away.at[:, there], near.at[:, here], sems.at[n, i])
            for n, (away, near) in enumerate(((q_far, q_ref), (k_far, k_ref), (v_far, v_ref)))
        ]

    for i in range(count):
        for copy in copies(i):
            copy.start()

    def pair(i, _):
        p = i + start
        cols = columns(p, wide)
        near = columns(i, wide)
        for copy in copies(i):
            copy.wait()
        for m, (go, att) in enumerate(((go_own, att_own), (go_oth, att_oth))):
            here = columns(place[0] ^ m, rows)
            grad[here, :] = go[:, cols]
            prod[here, :] = high(go[:, cols]) * high(att[:, cols])
        flat = prod[...].T
        deltas = [jnp.sum(flat[e * HD : (e + 1) * HD, :], axis=0, keepdims=True) for e in range(2)]
        turned_k[...] = (k_ref[:, near] * eighth).T
        for n, (a, b) in enumerate(spans(span)):
            allowed = allowed_keys(a, b, valid)
            q = q_ref[a:b, near] * eighth
            g = grad[a:b, :]
            parts = ((a, b), (0, a)) if a else ((a, b),)
            sums = {}
            for e in range(2):
                mine = first == (e == 0)
                qe = jnp.where(mine, q, jnp.zeros_like(q))
                ge = jnp.where(mine, g, jnp.zeros_like(g))
                for lo, hi in parts:
                    scores = against(k_ref[lo:hi, near], qe)
                    if lo == a:
                        scores = jnp.where(allowed, scores, -1e30)
                    weights = jnp.exp(scores - lse_ref[p, e : e + 1, a:b])
                    grad_w = against(v_ref[lo:hi, near], ge)
                    grad_s = low(weights * (grad_w - deltas[e][:, a:b]))
                    dv_here = matmul(low(weights), ge)
                    dk_here = matmul(grad_s, qe)
                    dq_here = matmul(turned_k[e * HD : (e + 1) * HD, lo:hi], grad_s)
                    if (lo, "v") in sums:
                        dv_here = dv_here + sums[lo, "v"]
                        dk_here = dk_here + sums[lo, "k"]
                    sums[lo, "v"], sums[lo, "k"] = dv_here, dk_here
                    sums[lo, e] = dq_here
            for e in range(2):
                dq[e * HD : (e + 1) * HD, a:b] = sums[a, e] + sums[0, e] if a else sums[a, e]
            dv[a:b, :] = sums[a, "v"]
            dk[a:b, :] = sums[a, "k"]
            if a:
                dv[:a, :] += sums[0, "v"]
                dk[:a, :] += sums[0, "k"]
        prod[...] = dq[...].T
        for m, f_out in enumerate((f_own, f_oth)):
            here = columns(place[0] ^ m, rows)
            cosine = cos_ref[here, :]
            sine = sin_ref[here, :]
            gv = low(0.5 * dv[here, :])
            gk = dk[here, :]
            gk = low(pltpu.roll(gk * cosine - turn(gk) * sine, HD, 1))
            gq = prod[here, :]
            gq = low(gq * cosine - turn(gq) * sine)
            part = slice(m * rows, (m + 1) * rows)
            base = i * 3 * wide
            d_out[part, pl.ds(pl.multiple_of(base, wide), wide)] = jnp.where(first, gq, gk)
            d_out[part, pl.ds(pl.multiple_of(base + wide, wide), wide)] = jnp.where(first, gv, gq)
            d_out[part, pl.ds(pl.multiple_of(base + 2 * wide, wide), wide)] = jnp.where(first, gk, gv)
            f_out[:, columns(i, wide)] = gv
        return 0

    lax.fori_loop(0, count, pair, 0)


def attend_backward(place, q, k, v, lse, go_own, go_oth, att_own, att_oth, cosine, sine, pairs):
    span = q.shape[0]
    rows = span // 2
    wide = 2 * HD
    cols = wide * (pairs[1] - pairs[0])
    return on_chip(
        functools.partial(backward_body, pairs[0]),
        (shape16(span, 3 * cols), shape16(rows, cols), shape16(rows, cols)),
        (place,),
        (q, k, v, lse, go_own, go_oth, att_own, att_oth, cosine, sine),
        "attend_backward",
        cost=7.5,
        limit=6,
        far=(0, 1, 2),
        scratch=(
            pltpu.VMEM((span, cols), jnp.bfloat16),
            pltpu.VMEM((span, cols), jnp.bfloat16),
            pltpu.VMEM((span, cols), jnp.bfloat16),
            pltpu.SemaphoreType.DMA((3, pairs[1] - pairs[0])),
            pltpu.VMEM((span, wide), jnp.bfloat16),
            pltpu.VMEM((span, wide), jnp.float32),
            pltpu.VMEM((wide, span), jnp.bfloat16),
            pltpu.VMEM((wide, span), jnp.float32),
            pltpu.VMEM((span, wide), jnp.float32),
            pltpu.VMEM((span, wide), jnp.float32),
        ),
    )


def row_blocks(rows, body, size=64):
    def step(c, _):
        body(columns(c, size))
        return 0

    lax.fori_loop(0, rows // size, step, 0)


def tables(span, inverse, sign):
    def body(inverse, sign, cos_ref, sin_ref):
        def rows(part):
            shape = (64, inverse.shape[1])
            place = part.start + lax.broadcasted_iota(jnp.int32, shape, 0)
            angles = place.astype(jnp.float32) * inverse[...]
            cos_ref[part, :] = jnp.cos(angles)
            sin_ref[part, :] = jnp.sin(angles) * sign[...]

        row_blocks(span, rows)

    out = shape32(span, inverse.shape[1])
    return on_chip(body, (out, out), (), (inverse, sign), "tables", cost=1.0)


def project_body(block, order, place, x_ref, gain_ref, w_ref, cos_ref, sin_ref, *refs):
    away_far, mine_far, q_far, k_far, q_out, k_out, v_out = refs[-12:-5]
    xn, away, mine, packed, sems = refs[-5:]
    rows = x_ref.shape[0]
    wide = 2 * HD
    x = high(x_ref[...])
    xn[...] = low(x * rms_scale(x) * gain_ref[...])
    arrange_halves(order, (xn,), away, mine)
    there = slice(block * rows, (block + 1) * rows)
    here = columns(place[0] ^ block, rows)
    copies = [
        pltpu.make_async_copy(away, away_far.at[there, :], sems.at[0]),
        pltpu.make_async_copy(mine, mine_far.at[there, :], sems.at[1]),
        pltpu.make_async_copy(q_out.at[here, :], q_far.at[here, :], sems.at[2]),
        pltpu.make_async_copy(k_out.at[here, :], k_far.at[here, :], sems.at[3]),
    ]
    for copy in copies[:2]:
        copy.start()
    cols = w_ref.shape[1] // 3
    for i in range(3):
        part = slice(i * cols, (i + 1) * cols)
        packed[:, part] = low(matmul(xn[...], w_ref[:, part]))
    cosine = cos_ref[here, :]
    sine = sin_ref[here, :]
    first = lax.broadcasted_iota(jnp.int32, (1, wide), 1) < HD

    def pair(p, _):
        to = columns(p, wide)
        x0, x1, x2 = [high(packed[:, columns(3 * p + i, wide)]) for i in range(3)]
        q = jnp.where(first, x0, x1)
        k = pltpu.roll(jnp.where(first, x2, x0), HD, 1)
        q_out[here, to] = low(q * cosine + turn(q) * sine)
        k_out[here, to] = low(k * cosine + turn(k) * sine)
        v_out[here, to] = low(jnp.where(first, x1, x2))
        return 0

    lax.fori_loop(0, q_out.shape[1] // wide, pair, 0)
    for copy in copies[2:]:
        copy.start()
    for copy in copies:
        copy.wait()


def project(order, place, x, gain, w, cosine, sine, before=()):
    rows, width = x.shape
    inside = pl.BlockSpec(memory_space=pltpu.VMEM)
    outside = pl.BlockSpec(memory_space=pl.ANY)
    scalar = pl.BlockSpec(memory_space=pltpu.SMEM)
    part = (2 * rows, width // 2)
    natural = (2 * rows, w.shape[1] // 3)
    far = [part, part, natural, natural]
    return pl.pallas_call(
        functools.partial(project_body, 1 if before else 0),
        out_shape=tuple(pltpu.HBM(f, jnp.bfloat16) for f in far) + (shape16(*natural),) * 3,
        in_specs=[scalar] * 2 + [inside] * 5 + ([outside] * 4 + [inside] * 3 if before else []),
        out_specs=(outside,) * 4 + (inside,) * 3,
        scratch_shapes=[
            pltpu.VMEM((rows, width), jnp.bfloat16),
            pltpu.VMEM((rows, width // 2), jnp.bfloat16),
            pltpu.VMEM((rows, width // 2), jnp.bfloat16),
            pltpu.VMEM((rows, w.shape[1]), jnp.bfloat16),
            pltpu.SemaphoreType.DMA((4,)),
        ],
        input_output_aliases={7 + i: i for i in range(len(before))},
        cost_estimate=pl.CostEstimate(
            flops=site_cost("project", 3.0), transcendentals=0, bytes_accessed=1
        ),
        compiler_params=pltpu.CompilerParams(vmem_limit_bytes=8 << 20),
        name="project",
    )(order, place, x, gain, w, cosine, sine, *before)


def arrange(order, blocks, out):
    rows = blocks[0].shape[0]
    size = out.shape[1] // order.shape[0]
    for i in range(order.shape[0]):
        for b, block in enumerate(blocks):
            out[b * rows : (b + 1) * rows, i * size : (i + 1) * size] = block[:, columns(order[i], size)]


def finish(place, x, att_own, att_came, w, gain):
    def body(
        place, x_far, own_far, came_far, w_far, gain_ref,
        hidden_far, hn_ref, hidden_ref, w_ref, att_ref, x_ref, sems,
    ):
        cols = own_far.shape[1]
        x_load = pltpu.make_async_copy(x_far, x_ref, sems.at[5])
        x_load.start()
        loads = []
        for m, far in enumerate((own_far, came_far)):
            there = columns(place[0] ^ m, cols)
            loads.append(pltpu.make_async_copy(far, att_ref.at[m], sems.at[3 + m]))
            loads.append(pltpu.make_async_copy(w_far.at[there, :], w_ref.at[m], sems.at[m]))
        for load in loads:
            load.start()
        x_load.wait()
        hidden = high(x_ref[...])
        for m in range(2):
            loads[2 * m].wait()
            loads[2 * m + 1].wait()
            hidden = hidden + matmul(att_ref[m], w_ref[m])
        hidden_ref[...] = hidden
        copy = pltpu.make_async_copy(hidden_ref, hidden_far, sems.at[2])
        copy.start()
        hn_ref[...] = low(hidden * rms_scale(hidden) * gain_ref[...])
        copy.wait()

    rows, width = x.shape
    return on_chip(
        body,
        (shape32(rows, width), shape16(rows, width)),
        (place,),
        (x, att_own, att_came, w, gain),
        "finish",
        cost=3.0,
        limit=8,
        away=(0,),
        far=(0, 1, 2, 3),
        scratch=(
            pltpu.VMEM((rows, width), jnp.float32),
            pltpu.VMEM((2, width // 2, width), jnp.bfloat16),
            pltpu.VMEM((2, rows, width // 2), jnp.bfloat16),
            pltpu.VMEM((rows, width), jnp.bfloat16),
            pltpu.SemaphoreType.DMA((6,)),
        ),
    )


def reorder(order, *blocks):
    rows, cols = blocks[0].shape

    def body(order, *refs):
        arrange(order, refs[:-1], refs[-1])

    return on_chip(body, shape16(rows * len(blocks), cols), (order,), blocks, "reorder", cost=0.9)


def arrange_halves(order, blocks, away, mine):
    rows = blocks[0].shape[0]
    count = order.shape[0] // 2
    size = mine.shape[1] // count
    for half, out in enumerate((away, mine)):
        for i in range(count):
            for b, block in enumerate(blocks):
                out[b * rows : (b + 1) * rows, i * size : (i + 1) * size] = block[
                    :, columns(order[half * count + i], size)
                ]


def reorder_halves(order, *blocks):
    rows, cols = blocks[0].shape

    def body(order, *refs):
        arrange_halves(order, refs[:-2], *refs[-2:])

    part = shape16(rows * len(blocks), cols // 2)
    return on_chip(body, (part, part), (order,), blocks, "reorder_halves", cost=0.9)


def feed_rows(hn, grads, gate_w, up_w, mine, other, base):
    rows = hn.shape[0]
    units = gate_w[0].shape[0]
    here = slice(base, base + rows)
    total_hn = None
    for s in range(2):
        gate = against(hn[...], gate_w[s][...])
        up = against(hn[...], up_w[s][...])
        grad = high(grads[s][...])
        sig = 1.0 / (1.0 + jnp.exp(-gate))
        silu = gate * sig
        results = (silu * up, grad * up * sig * (1.0 + gate * (1.0 - sig)), grad * silu)
        for i, result in enumerate(results):
            if s == 0:
                mine[i][here, :] = low(result)
            else:
                other[2 * i * rows + base : 2 * i * rows + base + rows, :units] = low(result)
    for s in range(2):
        for i, w in ((1, gate_w[s]), (2, up_w[s])):
            if s == 0:
                share = matmul(mine[i][here, :], w[...])
            else:
                share = matmul(other[2 * i * rows + base : 2 * i * rows + base + rows, :units], w[...])
            total_hn = share if total_hn is None else total_hn + share
    return total_hn


def feed_own_body(order, hn, dy_own, dy_oth, wg0, wg1, wu0, wu1, wd0, wd1, *refs):
    rows = hn.shape[0]
    outs, grads = refs[:9], refs[9:]
    mine, other, dhn, down = outs[:3], outs[3], outs[4], outs[5]
    for grad, w in zip(grads, (wd0, wd1)):
        grad[...] = low(against(dy_own[...], w[...]))
    dhn[...] = feed_rows(hn, grads, (wg0, wg1), (wu0, wu1), mine, other, 0)
    down[...] = matmul(mine[0][:rows, :], wd0[...]) + matmul(other[:rows, : wd1.shape[0]], wd1[...])
    for grad, w in zip(outs[6:8], (wd0, wd1)):
        grad[...] = low(against(dy_oth[...], w[...]))
    arrange(order, (dy_own, dy_oth), outs[8])


def feed_oth_body(order, hn_own, hn, g0, g1, wg0, wg1, wu0, wu1, *refs):
    outs = refs[4:]
    outs[4][...] = low(
        feed_rows(hn, (g0, g1), (wg0, wg1), (wu0, wu1), outs[:3], outs[3], hn.shape[0])
    )
    arrange(order, (hn_own, hn), outs[5])


def feed_own(order, hn, dy_own, dy_oth, gate_w, up_w, down_w):
    rows, width = hn.shape
    units = gate_w[0].shape[0]
    part = shape16(2 * rows, units)
    other = shape16(6 * rows, -(-units // 128) * 128)
    return on_chip(
        feed_own_body,
        (part,) * 3
        + (other,)
        + (shape32(rows, width),) * 2
        + (shape16(rows, units),) * 2
        + (shape16(2 * rows, width),),
        (order,),
        (hn, dy_own, dy_oth, *gate_w, *up_w, *down_w),
        "feed_own",
        limit=15,
        cost=11.0,
        scratch=(pltpu.VMEM((rows, units), jnp.bfloat16),) * 2,
    )


def feed_oth(order, hn_own, hn, grads, gate_w, up_w, parts):
    rows, width = hn.shape
    return on_chip(
        feed_oth_body,
        tuple(shape16(*part.shape) for part in parts)
        + (shape16(rows, width), shape16(2 * rows, width)),
        (order,),
        (hn_own, hn, *grads, *gate_w, *up_w, *parts),
        "feed_oth",
        aliases={9 + i: i for i in range(4)},
        limit=14,
        cost=7.0,
    )


def ff_grad(left, left_core, index, right, right_core, pieces):
    rows, units = left.shape
    size = right.shape[1] // pieces
    half = right.shape[1] // 2

    def body(left, left_core, right, right_core, *outs):
        for i in range(2):
            part = slice(i * half, (i + 1) * half)
            sums = low(
                inner_rows(left[...], right[:, part])
                + inner_rows(left_core[index * rows : (index + 1) * rows, :units], right_core[:, part])
            )
            for j in range(pieces // 2):
                outs[i * pieces // 2 + j][...] = sums[:, j * size : (j + 1) * size]

    part = shape16(units, size)
    return on_chip(
        body, (part,) * pieces, (), (left, left_core, right, right_core), "ff_grad", cost=2.7
    )


def join(first, second):
    def body(first, second, out):
        out[...] = low(high(first[...]) + high(second[...]))

    return on_chip(body, shape16(*first.shape), (), (first, second), "join", cost=0.3)


def fold_three(first, second, third):
    mid = first.shape[1] // 2

    def body(first, second, third, away, rest):
        for out, part in ((away, slice(0, mid)), (rest, slice(mid, 2 * mid))):
            out[...] = low(high(first[:, part]) + high(second[:, part]) + high(third[:, part]))

    part = shape16(first.shape[0], mid)
    return on_chip(body, (part, part), (), (first, second, third), "fold_three", cost=0.3)


def fold(kept, came):
    mid = kept.shape[1] // 2

    def body(kept, came, away, rest):
        away[...] = low(high(kept[:, :mid]) + high(came[:, :mid]))
        rest[...] = low(high(kept[:, mid:]) + high(came[:, mid:]))

    part = shape16(kept.shape[0], mid)
    return on_chip(body, (part, part), (), (kept, came), "fold", cost=0.3)


def fold_rows(kept, came):
    mid = kept.shape[0] // 2

    def body(kept, came, away, rest):
        away[...] = low(high(kept[:mid, :]) + high(came[:mid, :]))
        rest[...] = low(high(kept[mid:, :]) + high(came[mid:, :]))

    part = shape16(mid, kept.shape[1])
    return on_chip(body, (part, part), (), (kept, came), "fold_rows", cost=0.3)


def hidden_grad_body(order, place, dhn_own, dhn_came, hidden_far, dy_ref, gain_ref, w_far,
    grad_ref, send_ref, own_ref, away_ref, mine_ref, gains_ref, proj, hidden_ref, w_ref, sems,
):
    cols = send_ref.shape[1]
    loads = [pltpu.make_async_copy(hidden_far, hidden_ref, sems.at[2])]
    for m in (1, 0):
        there = columns(place[0] ^ m, cols)
        loads.append(pltpu.make_async_copy(w_far.at[there, :], w_ref.at[m], sems.at[m]))
    for load in loads:
        load.start()
    loads[0].wait()
    hidden = hidden_ref[...]
    scale = rms_scale(hidden)
    dhn = dhn_own[...] + high(dhn_came[...])
    gains_ref[...] = jnp.sum(dhn * hidden * scale, axis=0, keepdims=True)
    weighted = dhn * gain_ref[...]
    mean = jnp.mean(weighted * hidden, axis=-1, keepdims=True)
    grad = high(dy_ref[...]) + scale * weighted - hidden * (scale * scale * scale * mean)
    grad_ref[...] = grad
    proj[...] = low(grad)
    loads[1].wait()
    send_ref[...] = low(against(proj[...], w_ref[1]))
    loads[2].wait()
    own_ref[...] = low(against(proj[...], w_ref[0]))
    arrange_halves(order, (proj,), away_ref, mine_ref)


def hidden_grad(order, place, dhn_own, dhn_came, hidden, dy, gain, w):
    rows, width = hidden.shape
    part = shape16(rows, width // 2)
    return on_chip(
        hidden_grad_body,
        (shape32(rows, width), part, part, part, part, shape32(1, width)),
        (order, place),
        (dhn_own, dhn_came, hidden, dy, gain, w),
        "hidden_grad",
        cost=2.2,
        limit=9,
        far=(2, 5),
        scratch=(
            pltpu.VMEM((rows, width), jnp.bfloat16),
            pltpu.VMEM((rows, width), jnp.float32),
            pltpu.VMEM((2, width // 2, width), jnp.bfloat16),
            pltpu.SemaphoreType.DMA((3,)),
        ),
    )


def bucket_grad(left, left_core, rights, rights_core, place=0, total_cols=None, before=()):
    mid = left.shape[1] // 2
    cols = rights[0].shape[1]
    count = len(rights)

    def body(left, left_core, *refs):
        for i in range(count):
            part = slice(place + i * cols, place + (i + 1) * cols)
            for half, out in enumerate(refs[-2:]):
                cut = slice(half * mid, (half + 1) * mid)
                out[:, part] = low(
                    inner_rows(left[:, cut], refs[i][...])
                    + inner_rows(left_core[:, cut], refs[count + i][...])
                )

    full = shape16(mid, total_cols or cols * count)
    return on_chip(
        body,
        (full, full),
        (),
        (left, left_core, *rights, *rights_core, *before),
        "bucket_grad",
        aliases={2 + 2 * count + i: i for i in range(len(before))},
        cost=1.5,
    )


def bucket_near(row, kept, came):
    quarter, cols = kept.shape
    size = quarter // 4

    def body(row, kept, came, away, rest):
        near = row[0] & 1
        for i in range(2):
            here = pl.ds(pl.multiple_of(i * 2 * size + near * size, size), size)
            there = pl.ds(pl.multiple_of(i * 2 * size + (1 - near) * size, size), size)
            part = slice(i * size, (i + 1) * size)
            away[part, :] = low(high(kept[there, :]) + high(came[there, :]))
            rest[part, :] = low(high(kept[here, :]) + high(came[here, :]))

    half = shape16(2 * size, cols)
    return on_chip(body, (half, half), (row,), (kept, came), "bucket_near", cost=0.3)


def shares_body(d_a, d_b, fa, fb, w_ref, x_own, x_oth, gain_two, send_ref, own_ref, gains_ref):
    rows, width = x_own.shape
    cut = d_a.shape[1]
    sums = None
    for m, x_ref in ((1, x_oth), (0, x_own)):
        part = slice(m * rows, (m + 1) * rows)
        share = against(d_a[part, :], w_ref[:, :cut]) + against(d_b[part, :], w_ref[:, cut:])
        if m:
            send_ref[:, :width] = low(share)
        else:
            own_ref[...] = share
        x = high(x_ref[...])
        here = jnp.sum(share * (x * rms_scale(x)), axis=0, keepdims=True)
        sums = here if sums is None else sums + here
    send_ref[:, width : width + fa.shape[1]] = fa[...]
    send_ref[:, width + fa.shape[1] :] = fb[...]
    gains_ref[0:1, :] = sums
    gains_ref[1:2, :] = gain_two[...]


def shares(d_a, d_b, fa, fb, w, x_own, x_oth, gain_two):
    rows, width = x_own.shape
    return on_chip(
        shares_body,
        (shape16(rows, width + 2 * fa.shape[1]), shape32(rows, width), shape32(2, width)),
        (),
        (d_a, d_b, fa, fb, w, x_own, x_oth, gain_two),
        "shares",
        cost=2.3,
    )


def input_grad_body(place, share_ref, came_ref, grad_ref, x_ref, gain_ref, fa, fb, out_ref, first_ref):
    width = x_ref.shape[1]
    x = high(x_ref[...])
    scale = rms_scale(x)
    weighted = (share_ref[...] + high(came_ref[:, :width])) * gain_ref[...]
    mean = jnp.mean(weighted * x, axis=-1, keepdims=True)
    out_ref[...] = grad_ref[...] + scale * weighted - x * (scale * scale * scale * mean)
    cols = fa.shape[1]
    own = 2 * place[0]
    oth = 2 - own
    first_ref[:, columns(own, cols)] = fa[...]
    first_ref[:, columns(own + 1, cols)] = fb[...]
    first_ref[:, columns(oth, cols)] = came_ref[:, width : width + cols]
    first_ref[:, columns(oth + 1, cols)] = came_ref[:, width + cols :]


def input_grad(place, share, came, grad_hidden, x, gain, fa, fb):
    return on_chip(
        input_grad_body,
        (shape32(*x.shape), shape16(*x.shape)),
        (place,),
        (share, came, grad_hidden, x, gain, fa, fb),
        "input_grad",
        cost=2.0,
        limit=6,
    )


def after(first, *values):
    return lax.optimization_barrier((first, *values))[1:]


def two_groups(
    inputs,
    first_values,
    lengths,
    gain_attn,
    w_qkv,
    w_out,
    gain_mlp,
    w_gate,
    w_up,
    w_down,
    cotangent,
):
    SITES.clear()
    rows = inputs.shape[1]
    width = inputs.shape[2]
    span = 2 * rows
    out_cols = HEADS // 2 * HD
    packed_cols = 3 * out_cols
    mid = width // 2
    h = lax.axis_index("head")
    f = lax.axis_index("ffn")
    r = lax.axis_index("row")
    row_size = lax.axis_size("row")
    place = jnp.stack([h, lengths[0]]).astype(jnp.int32)
    row = r.reshape(1).astype(jnp.int32)
    tie = lax.optimization_barrier
    gain_attn = gain_attn.reshape(1, width)
    gain_mlp = gain_mlp.reshape(1, width)

    x_own = inputs[0]
    x_oth = swap(x_own, "head", 1)
    early_own = lax.dynamic_slice_in_dim(first_values[0], h * out_cols, out_cols, 1)
    early_oth = swap(
        lax.dynamic_slice_in_dim(first_values[0], (1 - h) * out_cols, out_cols, 1), "head", 1
    )
    dy_own = cotangent[0]
    down_core = swap(w_down, "ffn", 1)
    gate_core = swap(w_gate.T, "ffn", 1)
    up_core = swap(w_up.T, "ffn", 1)
    qkv_w = lax.dynamic_slice_in_dim(w_qkv, h * packed_cols, packed_cols, 1)
    half = HD // 2
    inverse = jnp.exp(-jnp.log(10000.0) * jnp.arange(half, dtype=jnp.float32) * 2.0 / HD)
    sign = jnp.where(jnp.arange(2 * HD) % HD < half, -1.0, 1.0)
    cosine, sine = tables(span, jnp.tile(inverse, 4)[None, :], sign[None, :])

    ff_order = jnp.stack([(h ^ a) * row_size + (r ^ b) for a in (1, 0) for b in (3, 1, 2, 0)])
    down_order = jnp.stack([(h ^ a) * row_size + (r ^ b) for b in (3, 1, 2, 0) for a in (1, 0)])
    att_order = jnp.stack(
        [((f ^ a) * row_size + (r & 2 ^ b)) // 2 for a in (3, 1, 2, 0) for b in (2, 0)]
    )

    before = project(att_order, place, x_own, gain_attn, qkv_w, cosine, sine)
    x_oth, before, early_own, down_core, gate_core, up_core = tie(
        (x_oth, before, early_own, down_core, gate_core, up_core)
    )
    xn_away, xn_mine, query, keys, *near = project(
        att_order, place, x_oth, gain_attn, qkv_w, cosine, sine, before
    )
    att_own, att_oth, mixed, log_sums = attend_forward(place, *near, early_own, early_oth)
    att_came = swap(att_oth, "head", 1)
    (dy_send,) = after(near[2], dy_own)
    dy_oth = swap(dy_send, "ffn", 2)
    att_came, dy_oth = tie((att_came, dy_oth))
    down_w = (w_down, down_core)
    gate_w = (w_gate.T, gate_core)
    up_w = (w_up.T, up_core)
    hidden, hn_own = finish(place, x_own, att_own, att_came, w_out, gain_mlp)
    hn_oth = swap(hn_own, "ffn", 2)
    dy_send, dy_oth = after(hn_own, dy_send, dy_oth)
    dyc_own = swap(dy_send, "ffn", 1)
    dyc_oth = swap(dy_oth, "ffn", 1)
    hnc_own = swap(hn_own, "ffn", 1)

    *parts, dhn_own, down_own, dact0, dact1, dy_all = feed_own(
        down_order, hn_own, dy_own, dy_oth, gate_w, up_w, down_w
    )
    hn_oth, parts, dhn_own, down_own, dact0, dact1, dy_all, hnc_own, dyc_own, dyc_oth = tie(
        (hn_oth, parts, dhn_own, down_own, dact0, dact1, dy_all, hnc_own, dyc_own, dyc_oth)
    )
    hnc_oth = swap(hn_oth, "ffn", 1)
    act, gate, up, others, dhn_send, hn_all = feed_oth(
        ff_order, hn_own, hn_oth, (dact0, dact1), gate_w, up_w, parts
    )
    dhn_came = swap(dhn_send, "ffn", 2)
    others_core = swap(others, "ffn", 1)
    own_send, came_send = after(dhn_send, att_own, att_came)
    att_core = swap(own_send, "ffn", 1)
    came_core = swap(came_send, "ffn", 1)
    hnc_oth, dyc_own, dyc_oth = after(dhn_send, hnc_oth, dyc_own, dyc_oth)
    dyc_all = reorder(down_order, dyc_own, dyc_oth)
    hnc_all = reorder(ff_order, hnc_own, hnc_oth)

    gate_a, gate_b, gate_near, gate_kept = ff_grad(gate, others_core, 1, hn_all, hnc_all, 4)
    gate_xa = swap(gate_a, "head", 1)
    down_send, down_kept = ff_grad(act, others_core, 0, dy_all, dyc_all, 2)
    down_near = swap(down_send, "row", 1)
    up_a, up_b, up_near, up_kept = ff_grad(up, others_core, 2, hn_all, hnc_all, 4)
    dhn_came, gate_b, gate_kept, gate_near, down_kept, up_a, up_b, up_near, up_kept = tie(
        (dhn_came, gate_b, gate_kept, gate_near, down_kept, up_a, up_b, up_near, up_kept)
    )

    grad_hidden, go_send, go_own, proj_away, proj_mine, gain_two = hidden_grad(
        att_order, place, dhn_own, dhn_came, hidden, dy_own, gain_mlp, w_out
    )
    (gate_near,) = after(go_send, gate_near)
    gate_send = join(gate_near, gate_xa)
    go_send, go_own, proj_away, gate_send = tie((go_send, go_own, proj_away, gate_send))
    go_oth = swap(go_send, "head", 1)
    proj_core = swap(proj_away, "ffn", 1)
    gate_came = swap(gate_send, "row", 1)
    (gate_b,) = after(go_send, gate_b)
    gate_xb = swap(gate_b, "head", 1)
    out_send, out_kept = bucket_grad(
        proj_mine, proj_core, (att_came, att_own), (came_core, att_core)
    )
    out_y = swap(out_send, "ffn", 2)
    up_xa = swap(after(out_send, up_a)[0], "head", 1)
    go_oth, out_kept = tie((go_oth, out_kept))

    def backward(pairs, lse):
        return attend_backward(
            place, query, keys, mixed, lse, go_own, go_oth, att_own, att_oth, cosine, sine, pairs
        )

    pairs = HEADS // 4
    d_a, fa_own, fa_oth = backward((0, pairs // 2), log_sums)
    out_kept, down_kept, gate_kept = after(d_a, out_kept, down_kept, gate_kept)
    out_send, out_kept = fold(out_kept, out_y)
    out_x = swap(out_send, "head", 1)
    down_send, down_kept = fold(down_kept, down_near)
    down_mid = swap(down_send, "row", 2)
    gate_kept = join(gate_kept, gate_xb)
    d_a, out_kept, down_kept, gate_kept, log_sums = tie(
        (d_a, out_kept, down_kept, gate_kept, log_sums)
    )
    core_a = swap(d_a, "ffn", 1)
    xn_core = swap(after(out_kept, xn_away)[0], "ffn", 1)
    d_b, fb_own, fb_oth = backward((pairs // 2, pairs), log_sums)
    gate_kept, up_near = after(d_b, gate_kept, up_near)
    gate_send, gate_kept = fold(gate_kept, gate_came)
    up_send = join(up_near, up_xa)
    d_b, gate_kept, up_send = tie((d_b, gate_kept, up_send))
    core_b = swap(d_b, "ffn", 1)
    up_xb = swap(after(gate_kept, up_b)[0], "head", 1)
    up_came = swap(up_send, "row", 1)
    (d_a,) = after(gate_kept, d_a)
    before = bucket_grad(xn_mine, xn_core, (d_a,), (core_a,), 0, packed_cols)
    core_b, *before = tie((core_b, *before))
    y_send, kept = bucket_grad(
        xn_mine, xn_core, (d_b,), (core_b,), packed_cols // 2, packed_cols, before
    )
    y_came = swap(y_send, "ffn", 2)
    d_a, d_b = after(y_send, d_a, d_b)
    back_send, share_own, gains = shares(
        d_a, d_b, fa_oth, fb_oth, qkv_w, x_own, x_oth, gain_two
    )
    gate_send, out_kept, act, others, up_kept, down_kept = after(
        back_send, gate_send, out_kept, act, others, up_kept, down_kept
    )
    out_send, out_kept = bucket_near(row, out_kept, out_x)
    out_near = swap(out_send, "row", 1)
    gains = gains + swap(gains, "head", 1)
    gains, back_send = tie((gains, back_send))
    back_came = swap(back_send, "head", 1)
    up_kept, down_kept = after(gains, up_kept, down_kept)
    up_send, up_kept = fold_three(up_kept, up_xb, up_came)
    gate_far = swap(gate_send, "row", 2)
    units = w_down.shape[0]
    far_send = low(matmul(act[rows:], down_w[0]) + matmul(others[rows:span, :units], down_w[1]))
    gains, down_kept, gate_kept, out_kept = after(far_send, gains, down_kept, gate_kept, out_kept)
    gains = gains + swap(gains, "ffn", 1)
    down_send, down_kept = fold(down_kept, down_mid)
    out_send, out_kept = fold_rows(out_kept, out_near)
    out_far = swap(out_send, "row", 2)
    sum_gate = high(gate_kept) + high(gate_far)
    kept, up_send, down_send, sum_gate, gains, out_send = tie(
        (kept, up_send, down_send, sum_gate, gains, out_send)
    )

    near_send, kept = bucket_near(row, kept, y_came)
    near_came = swap(near_send, "row", 1)
    gains, far_send, out_kept, up_send, down_send = after(
        near_send, gains, far_send, out_kept, up_send, down_send
    )
    gains_y = swap(gains, "ffn", 2)
    far_came = swap(far_send, "ffn", 2)
    up_far = swap(up_send, "row", 2)
    qkv_send, kept = fold_rows(kept, near_came)
    qkv_far = swap(qkv_send, "row", 2)
    share_own, down_kept, up_kept, out_kept, residual, gains, down_send = after(
        qkv_send,
        share_own,
        down_kept,
        up_kept,
        out_kept,
        hidden + down_own,
        gains,
        down_send,
    )
    down_x = swap(down_send, "head", 1)
    gains = gains + gains_y
    gains = gains + swap(gains, "row", 1)
    gains_far = swap(gains, "row", 2)
    (share_own,) = after(gains, share_own)
    grad_in, grad_first = input_grad(
        place, share_own, back_came, grad_hidden, x_own, gain_attn, fa_own, fb_own
    )
    sum_up = high(up_kept) + high(up_far)
    sum_down = high(down_kept) + high(down_x)
    out_sum = high(out_kept) + high(out_far)
    output = low(residual + high(far_came))[None]
    gains = gains + gains_far
    kept, grad_in, sum_up, sum_down, out_sum, output, gains = tie(
        (kept, grad_in, sum_up, sum_down, out_sum, output, gains)
    )
    sum_qkv = high(kept) + high(qkv_far)
    return (
        output,
        grad_in[None],
        grad_first[None],
        gains[0],
        sum_qkv,
        out_sum.T,
        gains[1],
        sum_gate.T,
        sum_up.T,
        sum_down,
    )


def solution(mesh):
    in_specs = (
        P(("ffn", "row"), "head", None),
        P(("ffn", "row"), "head", None),
        P(("ffn", "row")),
        P(),
        P(),
        P(),
        P(),
        P(None, "ffn"),
        P(None, "ffn"),
        P("ffn", None),
        P(("ffn", "row"), "head", None),
    )
    out_specs = (
        P(("ffn", "row"), "head", None),
        P(("ffn", "row"), "head", None),
        P(("ffn", "row"), "head", None),
        P(),
        P(("ffn", "row"), "head"),
        P("head", ("ffn", "row")),
        P(),
        P(("head", "row"), "ffn"),
        P(("head", "row"), "ffn"),
        P("ffn", ("head", "row")),
    )
    body = two_groups if mesh.shape["head"] == 2 and mesh.shape["ffn"] == 4 else any_groups
    return jax.shard_map(
        body, mesh=mesh, in_specs=in_specs, out_specs=out_specs, check_vma=False
    )
```

```python
import functools

import jax
import jax.numpy as jnp
from jax import lax
from jax.experimental import pallas as pl
from jax.experimental.pallas import tpu as pltpu
from jax.sharding import PartitionSpec as P

HEADS = 16
HD = 64
MIN_LEN = 512
STEP = 256


eps = 1e-06


def rms_scale(values):
    return lax.rsqrt(jnp.mean(values * values, axis=-1, keepdims=True) + eps)


def matmul(left, right):
    return jnp.dot(left, right, preferred_element_type=jnp.float32)


def inner_rows(left, right):
    return lax.dot_general(
        left, right, (((0,), (0,)), ((), ())), preferred_element_type=jnp.float32
    )


def against(left, right):
    return lax.dot_general(
        left, right, (((1,), (1,)), ((), ())), preferred_element_type=jnp.float32
    )


def swap(values, axis, mask):
    size = lax.axis_size(axis)
    return lax.ppermute(values, axis, [(i, i ^ mask) for i in range(size)])


def bits_of(axis):
    size = lax.axis_size(axis)
    return [1 << b for b in range(size.bit_length() - 2, -1, -1)]


def halve(values, dim, axis, mask):
    bit = (lax.axis_index(axis) // mask) % 2
    away = lax.dynamic_index_in_dim(values, 1 - bit, dim, keepdims=False)
    kept = lax.dynamic_index_in_dim(values, bit, dim, keepdims=False)
    came = swap(away.astype(jnp.bfloat16), axis, mask)
    return kept.astype(jnp.float32) + came.astype(jnp.float32)


def total(values, axes):
    for axis in axes:
        for mask in reversed(bits_of(axis)):
            values = values + swap(values, axis, mask)
    return values


def rotary(positions, head_size):
    half_size = head_size // 2
    inverse = jnp.exp(
        -jnp.log(10000.0) * jnp.arange(half_size, dtype=jnp.float32) * 2.0 / head_size
    )
    angles = positions.astype(jnp.float32)[:, None] * inverse[None, :]
    return (jnp.cos(angles), jnp.sin(angles))


def rotate(vectors, cosine, sine, sign):
    half_size = vectors.shape[-1] // 2
    first_half = vectors[..., :half_size]
    second_half = vectors[..., half_size:]
    cos_rows = cosine[:, None, :]
    sin_rows = sign * sine[:, None, :]
    return jnp.concatenate(
        [
            first_half * cos_rows - second_half * sin_rows,
            second_half * cos_rows + first_half * sin_rows,
        ],
        axis=-1,
    )


def masked_scores(q_rows, keys, q_pos, k_pos, valid):
    raw = jnp.einsum("qhe,khe->hqk", q_rows, keys, preferred_element_type=jnp.float32)
    allowed = (k_pos[None, :] <= q_pos[:, None]) & (k_pos[None, :] < valid)
    return jnp.where(allowed[None], 0.125 * raw, -1e30)


def scan_forward(query, keys, mixed, positions, valid, block_rows):
    count = query.shape[0] // block_rows

    def step(carry, index):
        start = index * block_rows
        q_rows = lax.dynamic_slice_in_dim(query, start, block_rows, 0)
        q_pos = lax.dynamic_slice_in_dim(positions, start, block_rows, 0)
        scores = masked_scores(q_rows, keys, q_pos, positions, valid)
        top = jnp.max(scores, axis=-1, keepdims=True)
        expo = jnp.exp(scores - top)
        total_w = jnp.sum(expo, axis=-1, keepdims=True)
        weights = expo / total_w
        result = jnp.einsum(
            "hqk,khe->qhe", weights.astype(jnp.bfloat16), mixed, preferred_element_type=jnp.float32
        )
        return (carry, (result.astype(jnp.bfloat16), top + jnp.log(total_w)))

    _, (outs, log_sums) = lax.scan(step, 0, jnp.arange(count, dtype=jnp.int32))
    return (outs.reshape(query.shape), log_sums)


def scan_backward(query, keys, mixed, positions, valid, log_sums, grad_out, block_rows):
    count = query.shape[0] // block_rows
    zeros = jnp.zeros(keys.shape, jnp.float32)

    def step(carry, index):
        key_sum, value_sum = carry
        start = index * block_rows
        q_rows = lax.dynamic_slice_in_dim(query, start, block_rows, 0)
        q_pos = lax.dynamic_slice_in_dim(positions, start, block_rows, 0)
        g_rows = lax.dynamic_slice_in_dim(grad_out, start, block_rows, 0)
        scores = masked_scores(q_rows, keys, q_pos, positions, valid)
        weights = jnp.exp(scores - log_sums[index])
        grad_w = jnp.einsum("qhe,khe->hqk", g_rows, mixed, preferred_element_type=jnp.float32)
        delta = jnp.sum(weights * grad_w, axis=-1, keepdims=True)
        grad_s = (weights * (grad_w - delta)).astype(jnp.bfloat16)
        grad_q = 0.125 * jnp.einsum(
            "hqk,khe->qhe", grad_s, keys, preferred_element_type=jnp.float32
        )
        key_sum = key_sum + 0.125 * jnp.einsum(
            "hqk,qhe->khe", grad_s, q_rows, preferred_element_type=jnp.float32
        )
        value_sum = value_sum + jnp.einsum(
            "hqk,qhe->khe", weights.astype(jnp.bfloat16), g_rows, preferred_element_type=jnp.float32
        )
        return ((key_sum, value_sum), grad_q)

    (grad_keys, grad_mixed), grad_query = lax.scan(
        step, (zeros, zeros), jnp.arange(count, dtype=jnp.int32)
    )
    return (grad_query.reshape(query.shape), grad_keys, grad_mixed)


def any_groups(
    inputs,
    first_values,
    lengths,
    gain_attn,
    w_qkv,
    w_out,
    gain_mlp,
    w_gate,
    w_up,
    w_down,
    cotangent,
):
    rows = inputs.shape[1]
    width = inputs.shape[2]
    groups = lax.axis_size("head")
    shards = lax.axis_size("ffn")
    heads_here = HEADS // groups
    span_rows = rows * groups
    block_rows = span_rows // max(1, span_rows // 512)
    head_pos = lax.axis_index("head")
    valid_len = lengths[0]
    packed_cols = heads_here * 3 * HD
    out_cols = heads_here * HD
    hidden_here = w_gate.shape[1]

    owners = [head_pos ^ m for m in range(groups)]
    x_all = [inputs[0]] + [swap(inputs[0], "head", m) for m in range(1, groups)]
    early = []
    for m in range(groups):
        piece = lax.dynamic_slice_in_dim(first_values[0], owners[m] * out_cols, out_cols, 1)
        early.append(swap(piece, "head", m) if m else piece)
    far = range(2, shards, 2)
    grad_rows = jnp.concatenate([cotangent[0]] + [swap(cotangent[0], "ffn", m) for m in far], 0)
    gate_w = jnp.concatenate([w_gate, swap(w_gate, "ffn", 1)], 1)
    up_w = jnp.concatenate([w_up, swap(w_up, "ffn", 1)], 1)
    down_w = jnp.concatenate([w_down, swap(w_down, "ffn", 1)], 0)
    w_heads = lax.dynamic_slice_in_dim(w_qkv, head_pos * packed_cols, packed_cols, 1)
    out_w = jnp.concatenate(
        [lax.dynamic_slice_in_dim(w_out, o * out_cols, out_cols, 0) for o in owners], 0
    )

    positions = jnp.concatenate([o * rows + jnp.arange(rows, dtype=jnp.int32) for o in owners])
    cosine, sine = rotary(positions, HD)
    normed, scaled, queries, key_list, mixes = [], [], [], [], []
    rows_in = inputs[0].astype(jnp.float32)
    scale_one = rms_scale(rows_in)
    for m in range(groups):
        block = x_all[m].astype(jnp.float32)
        scale = rms_scale(block)
        scaled.append(block * scale)
        normed.append((block * scale * gain_attn).astype(jnp.bfloat16))
        packed = matmul(normed[m], w_heads).astype(jnp.bfloat16)
        packed = packed.reshape(rows, heads_here, 3, HD).astype(jnp.float32)
        part = slice(m * rows, (m + 1) * rows)
        queries.append(rotate(packed[:, :, 0], cosine[part], sine[part], 1.0))
        key_list.append(rotate(packed[:, :, 1], cosine[part], sine[part], 1.0))
        value = early[m].reshape(rows, heads_here, HD).astype(jnp.float32)
        mixes.append(0.5 * (packed[:, :, 2] + value))
    query = jnp.concatenate(queries, 0).astype(jnp.bfloat16)
    keys = jnp.concatenate(key_list, 0).astype(jnp.bfloat16)
    mixed = jnp.concatenate(mixes, 0).astype(jnp.bfloat16)
    attended, log_sums = scan_forward(query, keys, mixed, positions, valid_len, block_rows)
    attended = attended.reshape(groups, rows, out_cols)
    att_own = jnp.concatenate(
        [attended[0]] + [swap(attended[m], "head", m) for m in range(1, groups)], 1
    )
    hidden = rows_in + matmul(att_own, out_w)
    scale_two = rms_scale(hidden)
    normed_two = (hidden * scale_two * gain_mlp).astype(jnp.bfloat16)

    mlp_rows = [normed_two] + [swap(normed_two, "ffn", m) for m in far]
    grad_list = [grad_rows[i * rows : (i + 1) * rows] for i in range(len(mlp_rows))]
    actives, grad_gates, grad_ups, downs, grad_normed_list = [], [], [], [], []
    for i, block in enumerate(mlp_rows):
        gate_rows = matmul(block, gate_w)
        up_rows = matmul(block, up_w)
        sigmoid_gate = jax.nn.sigmoid(gate_rows)
        silu_gate = gate_rows * sigmoid_gate
        grad_active = against(grad_list[i], down_w)
        actives.append((silu_gate * up_rows).astype(jnp.bfloat16))
        grad_gates.append(
            (
                grad_active * up_rows * sigmoid_gate * (1.0 + gate_rows * (1.0 - sigmoid_gate))
            ).astype(jnp.bfloat16)
        )
        grad_ups.append((grad_active * silu_gate).astype(jnp.bfloat16))
        grad_normed_list.append(against(grad_gates[i], gate_w) + against(grad_ups[i], up_w))
        downs.append(matmul(actives[i], down_w))
    grad_normed_two = grad_normed_list[0]
    for i, m in enumerate(far):
        came = swap(grad_normed_list[i + 1].astype(jnp.bfloat16), "ffn", m)
        grad_normed_two = grad_normed_two + came.astype(jnp.float32)
    down_rows = downs[0]
    for i, m in enumerate(far):
        down_rows = down_rows + swap(downs[i + 1].astype(jnp.bfloat16), "ffn", m).astype(jnp.float32)
    output = (hidden + down_rows).astype(jnp.bfloat16)[None]

    all_rows = jnp.concatenate(mlp_rows, 0)
    ff_sums = []
    for left, right in (
        (grad_rows, jnp.concatenate(actives, 0)),
        (all_rows, jnp.concatenate(grad_gates, 0)),
        (all_rows, jnp.concatenate(grad_ups, 0)),
    ):
        away = inner_rows(left, right[:, hidden_here:]).astype(jnp.bfloat16)
        part = inner_rows(left, right[:, :hidden_here])
        part = (part + swap(away, "ffn", 1).astype(jnp.float32)).astype(jnp.bfloat16)
        steps = [("head", b) for b in bits_of("head")] + [("row", b) for b in bits_of("row")]
        part = part.reshape([2] * len(steps) + [-1, hidden_here])
        order = [s for s in steps if s[0] == "head"] + [s for s in reversed(steps) if s[0] == "row"]
        left_steps = list(steps)
        for s in order:
            part = halve(part, left_steps.index(s), *s)
            left_steps.remove(s)
            if left_steps:
                part = part.astype(jnp.bfloat16)
        ff_sums.append(part)
    sum_down, sum_gate, sum_up = ff_sums

    grad_y = cotangent[0].astype(jnp.float32)
    grad_gain_two = jnp.sum(grad_normed_two * hidden * scale_two, axis=0)
    weighted_two = grad_normed_two * gain_mlp
    cube_two = scale_two * scale_two * scale_two
    grad_hidden = (
        grad_y
        + scale_two * weighted_two
        - hidden * cube_two * jnp.mean(weighted_two * hidden, axis=-1, keepdims=True)
    )
    grad_proj = grad_hidden.astype(jnp.bfloat16)
    grad_att = against(grad_proj, out_w).astype(jnp.bfloat16)
    grad_att = jnp.concatenate(
        [
            swap(grad_att[:, m * out_cols : (m + 1) * out_cols], "head", m)
            if m
            else grad_att[:, :out_cols]
            for m in range(groups)
        ],
        0,
    ).reshape(span_rows, heads_here, HD)

    def over_buckets(part):
        steps = [("ffn", b) for b in bits_of("ffn")] + [("row", b) for b in bits_of("row")]
        part = part.astype(jnp.bfloat16).reshape([2] * len(steps) + [-1, part.shape[1]])
        order = [s for s in reversed(steps) if s[0] == "ffn"] + [
            s for s in reversed(steps) if s[0] == "row"
        ]
        left_steps = list(steps)
        for s in order:
            part = halve(part, left_steps.index(s), *s)
            left_steps.remove(s)
            if left_steps:
                part = part.astype(jnp.bfloat16)
        return part

    part = over_buckets(inner_rows(grad_proj, att_own))
    sum_out = part[:, :out_cols]
    for m in range(1, groups):
        came = swap(part[:, m * out_cols : (m + 1) * out_cols].astype(jnp.bfloat16), "head", m)
        sum_out = sum_out + came.astype(jnp.float32)

    grad_query, grad_keys, grad_mixed = scan_backward(
        query, keys, mixed, positions, valid_len, log_sums, grad_att, block_rows
    )
    grad_packed = jnp.stack(
        [
            rotate(grad_query, cosine, sine, -1.0),
            rotate(grad_keys, cosine, sine, -1.0),
            0.5 * grad_mixed,
        ],
        axis=2,
    )
    grad_packed = grad_packed.astype(jnp.bfloat16).reshape(span_rows, packed_cols)
    grad_early = (0.5 * grad_mixed).astype(jnp.bfloat16).reshape(span_rows, out_cols)
    firsts = [grad_early[m * rows : (m + 1) * rows] for m in range(groups)]
    firsts = [swap(firsts[m], "head", m) if m else firsts[0] for m in range(groups)]
    grad_first = jnp.zeros((rows, width), jnp.bfloat16)
    for m in range(groups):
        grad_first = lax.dynamic_update_slice_in_dim(grad_first, firsts[m], owners[m] * out_cols, 1)
    shares = [
        against(grad_packed[m * rows : (m + 1) * rows], w_heads) for m in range(groups)
    ]
    grad_gain_one = sum(jnp.sum(shares[m] * scaled[m], axis=0) for m in range(groups))
    grad_normed = shares[0]
    for m in range(1, groups):
        grad_normed = grad_normed + swap(shares[m].astype(jnp.bfloat16), "head", m).astype(jnp.float32)
    sum_qkv = over_buckets(inner_rows(jnp.concatenate(normed, 0), grad_packed))
    weighted_one = grad_normed * gain_attn
    cube_one = scale_one * scale_one * scale_one
    grad_in = (
        grad_hidden
        + scale_one * weighted_one
        - rows_in * cube_one * jnp.mean(weighted_one * rows_in, axis=-1, keepdims=True)
    )
    gains = total(jnp.stack([grad_gain_one, grad_gain_two]), ("ffn", "head", "row"))
    return (
        output,
        grad_in[None],
        grad_first[None],
        gains[0],
        sum_qkv,
        sum_out.T,
        gains[1],
        sum_gate,
        sum_up,
        sum_down.T,
    )


SCALE = 4.5e8
COSTS = {}
SITES = {}


def site_cost(name, usual):
    count = SITES.get(name, 0)
    SITES[name] = count + 1
    return int(SCALE * COSTS.get(name + str(count), usual))


def low(values):
    return values.astype(jnp.bfloat16)


def high(values):
    return values.astype(jnp.float32)


def on_chip(body, outs, scalars, arrays, name, scratch=(), aliases=None, limit=3, cost=1.0, away=(), far=()):
    inside = pl.BlockSpec(memory_space=pltpu.VMEM)
    outside = pl.BlockSpec(memory_space=pl.ANY)
    return pl.pallas_call(
        body,
        out_shape=jax.tree.unflatten(
            jax.tree.structure(outs),
            [
                pltpu.HBM(o.shape, o.dtype) if i in away else o
                for i, o in enumerate(jax.tree.leaves(outs))
            ],
        ),
        in_specs=[pl.BlockSpec(memory_space=pltpu.SMEM)] * len(scalars)
        + [outside if i in far else inside for i in range(len(arrays))],
        out_specs=jax.tree.unflatten(
            jax.tree.structure(outs),
            [
                outside if i in away else inside
                for i in range(len(jax.tree.leaves(outs)))
            ],
        ),
        scratch_shapes=list(scratch),
        input_output_aliases=aliases or {},
        cost_estimate=pl.CostEstimate(
            flops=site_cost(name, cost), transcendentals=0, bytes_accessed=1
        ),
        compiler_params=pltpu.CompilerParams(vmem_limit_bytes=limit << 20),
        name=name,
    )(*scalars, *arrays)


def shape16(*dims):
    return jax.ShapeDtypeStruct(dims, jnp.bfloat16)


def shape32(*dims):
    return jax.ShapeDtypeStruct(dims, jnp.float32)


def spans(total):
    return [(a, min(a + STEP, total)) for a in range(0, total, STEP)]


def turn(values):
    lane = lax.broadcasted_iota(jnp.int32, values.shape, 1)
    return jnp.where(
        lane % HD < HD // 2, pltpu.roll(values, 2 * HD - HD // 2, 1), pltpu.roll(values, HD // 2, 1)
    )


def allowed_keys(a, b, valid):
    size = b - a
    down = lax.broadcasted_iota(jnp.int32, (size, size), 0)
    across = lax.broadcasted_iota(jnp.int32, (size, size), 1)
    allowed = down <= across
    if b > MIN_LEN:
        allowed = allowed & (down < valid - a)
    return allowed


def columns(index, size):
    return pl.ds(pl.multiple_of(index * size, size), size)


def forward_body(
    place, q_ref, k_ref, raw_ref, early_own, early_oth,
    own_far, oth_far, v_far, lse_out, att_own, att_oth, v_out, flipped, att, sems,
):
    rows = early_own.shape[0]
    span = 2 * rows
    wide = 2 * HD
    valid = place[1]
    bf = jnp.bfloat16
    first = lax.broadcasted_iota(jnp.int32, (1, wide), 1) < HD
    flipped[:, HD:, :] = jnp.ones((2, 16, span), bf)

    def copies(p):
        cols = columns(p, wide)
        return [
            pltpu.make_async_copy(near.at[:, cols], far.at[:, cols], sems.at[i, p])
            for i, (near, far) in enumerate(
                ((v_out, v_far), (att_oth, oth_far), (att_own, own_far))
            )
        ]

    def pair(p, _):
        cols = columns(p, wide)
        for m, early in enumerate((early_own, early_oth)):
            here = columns(place[0] ^ m, rows)
            v_out[here, cols] = low(0.5 * (high(raw_ref[here, cols]) + high(early[:, cols])))
        copies(p)[0].start()
        turned = v_out[:, cols].T
        for e in range(2):
            flipped[e, :HD, :] = turned[e * HD : (e + 1) * HD, :]
        for a, b in spans(span):
            q = q_ref[a:b, cols] * jnp.asarray(0.125, bf)
            allowed = allowed_keys(a, b, valid)
            for e in range(2):
                qe = jnp.where(first == (e == 0), q, jnp.zeros_like(q))
                diag = jnp.where(allowed, against(k_ref[a:b, cols], qe), -1e30)
                top = jnp.max(diag, axis=0, keepdims=True)
                if a:
                    past = against(k_ref[:a, cols], qe)
                    top = jnp.maximum(top, jnp.max(past, axis=0, keepdims=True))
                out = matmul(flipped[e, :, a:b], low(jnp.exp(diag - top)))
                if a:
                    out = out + matmul(flipped[e, :, :a], low(jnp.exp(past - top)))
                amount = out[HD : HD + 1, :]
                att[e * HD : (e + 1) * HD, a:b] = out[:HD, :] / amount
                lse_out[p, e : e + 1, a:b] = top + jnp.log(amount)
        result = low(att[...].T)
        upper = place[0] == 0
        att_own[:, cols] = jnp.where(upper, result[:rows, :], result[rows:, :])
        att_oth[:, cols] = jnp.where(upper, result[rows:, :], result[:rows, :])
        for copy in copies(p)[1:]:
            copy.start()
        return 0

    lax.fori_loop(0, lse_out.shape[0], pair, 0)
    for p in range(lse_out.shape[0]):
        for copy in copies(p):
            copy.wait()


def attend_forward(place, query, keys, raw, early_own, early_oth):
    span, cols = query.shape
    rows = span // 2
    heads = cols // HD
    out = shape16(rows, cols)
    natural = shape16(span, cols)
    return on_chip(
        forward_body,
        (out, out, natural, shape32(heads // 2, 2, span)),
        (place,),
        (query, keys, raw, early_own, early_oth),
        "attend_forward",
        cost=9.0,
        limit=6,
        away=(0, 1, 2),
        scratch=(
            pltpu.VMEM(out.shape, jnp.bfloat16),
            pltpu.VMEM(out.shape, jnp.bfloat16),
            pltpu.VMEM(natural.shape, jnp.bfloat16),
            pltpu.VMEM((2, HD + 16, span), jnp.bfloat16),
            pltpu.VMEM((2 * HD, span), jnp.float32),
            pltpu.SemaphoreType.DMA((3, heads // 2)),
        ),
    )


def backward_body(
    start, place, q_far, k_far, v_far, lse_ref, go_own, go_oth, att_own, att_oth, cos_ref, sin_ref,
    d_out, f_own, f_oth, q_ref, k_ref, v_ref, sems, grad, prod, turned_k, dq, dk, dv,
):
    rows = go_own.shape[0]
    span = 2 * rows
    valid = place[1]
    wide = 2 * HD
    bf = jnp.bfloat16
    first = lax.broadcasted_iota(jnp.int32, (1, wide), 1) < HD
    eighth = jnp.asarray(0.125, bf)
    count = f_own.shape[1] // wide

    def copies(i):
        there = columns(i + start, wide)
        here = columns(i, wide)
        return [
            pltpu.make_async_copy(away.at[:, there], near.at[:, here], sems.at[n, i])
            for n, (away, near) in enumerate(((q_far, q_ref), (k_far, k_ref), (v_far, v_ref)))
        ]

    for i in range(count):
        for copy in copies(i):
            copy.start()

    def pair(i, _):
        p = i + start
        cols = columns(p, wide)
        near = columns(i, wide)
        for copy in copies(i):
            copy.wait()
        for m, (go, att) in enumerate(((go_own, att_own), (go_oth, att_oth))):
            here = columns(place[0] ^ m, rows)
            grad[here, :] = go[:, cols]
            prod[here, :] = high(go[:, cols]) * high(att[:, cols])
        flat = prod[...].T
        deltas = [jnp.sum(flat[e * HD : (e + 1) * HD, :], axis=0, keepdims=True) for e in range(2)]
        turned_k[...] = (k_ref[:, near] * eighth).T
        for n, (a, b) in enumerate(spans(span)):
            allowed = allowed_keys(a, b, valid)
            q = q_ref[a:b, near] * eighth
            g = grad[a:b, :]
            parts = ((a, b), (0, a)) if a else ((a, b),)
            sums = {}
            for e in range(2):
                mine = first == (e == 0)
                qe = jnp.where(mine, q, jnp.zeros_like(q))
                ge = jnp.where(mine, g, jnp.zeros_like(g))
                for lo, hi in parts:
                    scores = against(k_ref[lo:hi, near], qe)
                    if lo == a:
                        scores = jnp.where(allowed, scores, -1e30)
                    weights = jnp.exp(scores - lse_ref[p, e : e + 1, a:b])
                    grad_w = against(v_ref[lo:hi, near], ge)
                    grad_s = low(weights * (grad_w - deltas[e][:, a:b]))
                    dv_here = matmul(low(weights), ge)
                    dk_here = matmul(grad_s, qe)
                    dq_here = matmul(turned_k[e * HD : (e + 1) * HD, lo:hi], grad_s)
                    if (lo, "v") in sums:
                        dv_here = dv_here + sums[lo, "v"]
                        dk_here = dk_here + sums[lo, "k"]
                    sums[lo, "v"], sums[lo, "k"] = dv_here, dk_here
                    sums[lo, e] = dq_here
            for e in range(2):
                dq[e * HD : (e + 1) * HD, a:b] = sums[a, e] + sums[0, e] if a else sums[a, e]
            dv[a:b, :] = sums[a, "v"]
            dk[a:b, :] = sums[a, "k"]
            if a:
                dv[:a, :] += sums[0, "v"]
                dk[:a, :] += sums[0, "k"]
        prod[...] = dq[...].T
        for m, f_out in enumerate((f_own, f_oth)):
            here = columns(place[0] ^ m, rows)
            cosine = cos_ref[here, :]
            sine = sin_ref[here, :]
            gv = low(0.5 * dv[here, :])
            gk = dk[here, :]
            gk = low(pltpu.roll(gk * cosine - turn(gk) * sine, HD, 1))
            gq = prod[here, :]
            gq = low(gq * cosine - turn(gq) * sine)
            part = slice(m * rows, (m + 1) * rows)
            base = i * 3 * wide
            d_out[part, pl.ds(pl.multiple_of(base, wide), wide)] = jnp.where(first, gq, gk)
            d_out[part, pl.ds(pl.multiple_of(base + wide, wide), wide)] = jnp.where(first, gv, gq)
            d_out[part, pl.ds(pl.multiple_of(base + 2 * wide, wide), wide)] = jnp.where(first, gk, gv)
            f_out[:, columns(i, wide)] = gv
        return 0

    lax.fori_loop(0, count, pair, 0)


def attend_backward(place, q, k, v, lse, go_own, go_oth, att_own, att_oth, cosine, sine, pairs):
    span = q.shape[0]
    rows = span // 2
    wide = 2 * HD
    cols = wide * (pairs[1] - pairs[0])
    return on_chip(
        functools.partial(backward_body, pairs[0]),
        (shape16(span, 3 * cols), shape16(rows, cols), shape16(rows, cols)),
        (place,),
        (q, k, v, lse, go_own, go_oth, att_own, att_oth, cosine, sine),
        "attend_backward",
        cost=7.5,
        limit=6,
        far=(0, 1, 2),
        scratch=(
            pltpu.VMEM((span, cols), jnp.bfloat16),
            pltpu.VMEM((span, cols), jnp.bfloat16),
            pltpu.VMEM((span, cols), jnp.bfloat16),
            pltpu.SemaphoreType.DMA((3, pairs[1] - pairs[0])),
            pltpu.VMEM((span, wide), jnp.bfloat16),
            pltpu.VMEM((span, wide), jnp.float32),
            pltpu.VMEM((wide, span), jnp.bfloat16),
            pltpu.VMEM((wide, span), jnp.float32),
            pltpu.VMEM((span, wide), jnp.float32),
            pltpu.VMEM((span, wide), jnp.float32),
        ),
    )


def row_blocks(rows, body, size=64):
    def step(c, _):
        body(columns(c, size))
        return 0

    lax.fori_loop(0, rows // size, step, 0)


def tables(span, inverse, sign):
    def body(inverse, sign, cos_ref, sin_ref):
        def rows(part):
            shape = (64, inverse.shape[1])
            place = part.start + lax.broadcasted_iota(jnp.int32, shape, 0)
            angles = place.astype(jnp.float32) * inverse[...]
            cos_ref[part, :] = jnp.cos(angles)
            sin_ref[part, :] = jnp.sin(angles) * sign[...]

        row_blocks(span, rows)

    out = shape32(span, inverse.shape[1])
    return on_chip(body, (out, out), (), (inverse, sign), "tables", cost=1.0)


def project_body(block, order, place, x_ref, gain_ref, w_ref, cos_ref, sin_ref, *refs):
    away_far, mine_far, q_far, k_far, q_out, k_out, v_out = refs[-12:-5]
    xn, away, mine, packed, sems = refs[-5:]
    rows = x_ref.shape[0]
    wide = 2 * HD
    x = high(x_ref[...])
    xn[...] = low(x * rms_scale(x) * gain_ref[...])
    arrange_halves(order, (xn,), away, mine)
    there = slice(block * rows, (block + 1) * rows)
    here = columns(place[0] ^ block, rows)
    copies = [
        pltpu.make_async_copy(away, away_far.at[there, :], sems.at[0]),
        pltpu.make_async_copy(mine, mine_far.at[there, :], sems.at[1]),
        pltpu.make_async_copy(q_out.at[here, :], q_far.at[here, :], sems.at[2]),
        pltpu.make_async_copy(k_out.at[here, :], k_far.at[here, :], sems.at[3]),
    ]
    for copy in copies[:2]:
        copy.start()
    cols = w_ref.shape[1] // 3
    for i in range(3):
        part = slice(i * cols, (i + 1) * cols)
        packed[:, part] = low(matmul(xn[...], w_ref[:, part]))
    cosine = cos_ref[here, :]
    sine = sin_ref[here, :]
    first = lax.broadcasted_iota(jnp.int32, (1, wide), 1) < HD

    def pair(p, _):
        to = columns(p, wide)
        x0, x1, x2 = [high(packed[:, columns(3 * p + i, wide)]) for i in range(3)]
        q = jnp.where(first, x0, x1)
        k = pltpu.roll(jnp.where(first, x2, x0), HD, 1)
        q_out[here, to] = low(q * cosine + turn(q) * sine)
        k_out[here, to] = low(k * cosine + turn(k) * sine)
        v_out[here, to] = low(jnp.where(first, x1, x2))
        return 0

    lax.fori_loop(0, q_out.shape[1] // wide, pair, 0)
    for copy in copies[2:]:
        copy.start()
    for copy in copies:
        copy.wait()


def project(order, place, x, gain, w, cosine, sine, before=()):
    rows, width = x.shape
    inside = pl.BlockSpec(memory_space=pltpu.VMEM)
    outside = pl.BlockSpec(memory_space=pl.ANY)
    scalar = pl.BlockSpec(memory_space=pltpu.SMEM)
    part = (2 * rows, width // 2)
    natural = (2 * rows, w.shape[1] // 3)
    far = [part, part, natural, natural]
    return pl.pallas_call(
        functools.partial(project_body, 1 if before else 0),
        out_shape=tuple(pltpu.HBM(f, jnp.bfloat16) for f in far) + (shape16(*natural),) * 3,
        in_specs=[scalar] * 2 + [inside] * 5 + ([outside] * 4 + [inside] * 3 if before else []),
        out_specs=(outside,) * 4 + (inside,) * 3,
        scratch_shapes=[
            pltpu.VMEM((rows, width), jnp.bfloat16),
            pltpu.VMEM((rows, width // 2), jnp.bfloat16),
            pltpu.VMEM((rows, width // 2), jnp.bfloat16),
            pltpu.VMEM((rows, w.shape[1]), jnp.bfloat16),
            pltpu.SemaphoreType.DMA((4,)),
        ],
        input_output_aliases={7 + i: i for i in range(len(before))},
        cost_estimate=pl.CostEstimate(
            flops=site_cost("project", 3.0), transcendentals=0, bytes_accessed=1
        ),
        compiler_params=pltpu.CompilerParams(vmem_limit_bytes=8 << 20),
        name="project",
    )(order, place, x, gain, w, cosine, sine, *before)


def arrange(order, blocks, out):
    rows = blocks[0].shape[0]
    size = out.shape[1] // order.shape[0]
    for i in range(order.shape[0]):
        for b, block in enumerate(blocks):
            out[b * rows : (b + 1) * rows, i * size : (i + 1) * size] = block[:, columns(order[i], size)]


def finish(place, x, att_own, att_came, w, gain):
    def body(
        place, x_far, own_far, came_far, w_far, gain_ref,
        hidden_far, hn_ref, hidden_ref, w_ref, att_ref, x_ref, sems,
    ):
        cols = own_far.shape[1]
        x_load = pltpu.make_async_copy(x_far, x_ref, sems.at[5])
        x_load.start()
        loads = []
        for m, far in enumerate((own_far, came_far)):
            there = columns(place[0] ^ m, cols)
            loads.append(pltpu.make_async_copy(far, att_ref.at[m], sems.at[3 + m]))
            loads.append(pltpu.make_async_copy(w_far.at[there, :], w_ref.at[m], sems.at[m]))
        for load in loads:
            load.start()
        x_load.wait()
        hidden = high(x_ref[...])
        for m in range(2):
            loads[2 * m].wait()
            loads[2 * m + 1].wait()
            hidden = hidden + matmul(att_ref[m], w_ref[m])
        hidden_ref[...] = hidden
        copy = pltpu.make_async_copy(hidden_ref, hidden_far, sems.at[2])
        copy.start()
        hn_ref[...] = low(hidden * rms_scale(hidden) * gain_ref[...])
        copy.wait()

    rows, width = x.shape
    return on_chip(
        body,
        (shape32(rows, width), shape16(rows, width)),
        (place,),
        (x, att_own, att_came, w, gain),
        "finish",
        cost=3.0,
        limit=8,
        away=(0,),
        far=(0, 1, 2, 3),
        scratch=(
            pltpu.VMEM((rows, width), jnp.float32),
            pltpu.VMEM((2, width // 2, width), jnp.bfloat16),
            pltpu.VMEM((2, rows, width // 2), jnp.bfloat16),
            pltpu.VMEM((rows, width), jnp.bfloat16),
            pltpu.SemaphoreType.DMA((6,)),
        ),
    )


def reorder(order, *blocks):
    rows, cols = blocks[0].shape

    def body(order, *refs):
        arrange(order, refs[:-1], refs[-1])

    return on_chip(body, shape16(rows * len(blocks), cols), (order,), blocks, "reorder", cost=0.9)


def arrange_halves(order, blocks, away, mine):
    rows = blocks[0].shape[0]
    count = order.shape[0] // 2
    size = mine.shape[1] // count
    for half, out in enumerate((away, mine)):
        for i in range(count):
            for b, block in enumerate(blocks):
                out[b * rows : (b + 1) * rows, i * size : (i + 1) * size] = block[
                    :, columns(order[half * count + i], size)
                ]


def reorder_halves(order, *blocks):
    rows, cols = blocks[0].shape

    def body(order, *refs):
        arrange_halves(order, refs[:-2], *refs[-2:])

    part = shape16(rows * len(blocks), cols // 2)
    return on_chip(body, (part, part), (order,), blocks, "reorder_halves", cost=0.9)


def feed_rows(hn, grads, gate_w, up_w, mine, other, base):
    rows = hn.shape[0]
    units = gate_w[0].shape[0]
    here = slice(base, base + rows)
    total_hn = None
    for s in range(2):
        gate = against(hn[...], gate_w[s][...])
        up = against(hn[...], up_w[s][...])
        grad = high(grads[s][...])
        sig = 1.0 / (1.0 + jnp.exp(-gate))
        silu = gate * sig
        results = (silu * up, grad * up * sig * (1.0 + gate * (1.0 - sig)), grad * silu)
        for i, result in enumerate(results):
            if s == 0:
                mine[i][here, :] = low(result)
            else:
                other[2 * i * rows + base : 2 * i * rows + base + rows, :units] = low(result)
    for s in range(2):
        for i, w in ((1, gate_w[s]), (2, up_w[s])):
            if s == 0:
                share = matmul(mine[i][here, :], w[...])
            else:
                share = matmul(other[2 * i * rows + base : 2 * i * rows + base + rows, :units], w[...])
            total_hn = share if total_hn is None else total_hn + share
    return total_hn


def feed_own_body(order, hn, dy_own, dy_oth, wg0, wg1, wu0, wu1, wd0, wd1, *refs):
    rows = hn.shape[0]
    outs, grads = refs[:9], refs[9:]
    mine, other, dhn, down = outs[:3], outs[3], outs[4], outs[5]
    for grad, w in zip(grads, (wd0, wd1)):
        grad[...] = low(against(dy_own[...], w[...]))
    dhn[...] = feed_rows(hn, grads, (wg0, wg1), (wu0, wu1), mine, other, 0)
    down[...] = matmul(mine[0][:rows, :], wd0[...]) + matmul(other[:rows, : wd1.shape[0]], wd1[...])
    for grad, w in zip(outs[6:8], (wd0, wd1)):
        grad[...] = low(against(dy_oth[...], w[...]))
    arrange(order, (dy_own, dy_oth), outs[8])


def feed_oth_body(order, hn_own, hn, g0, g1, wg0, wg1, wu0, wu1, *refs):
    outs = refs[4:]
    outs[4][...] = low(
        feed_rows(hn, (g0, g1), (wg0, wg1), (wu0, wu1), outs[:3], outs[3], hn.shape[0])
    )
    arrange(order, (hn_own, hn), outs[5])


def feed_own(order, hn, dy_own, dy_oth, gate_w, up_w, down_w):
    rows, width = hn.shape
    units = gate_w[0].shape[0]
    part = shape16(2 * rows, units)
    other = shape16(6 * rows, -(-units // 128) * 128)
    return on_chip(
        feed_own_body,
        (part,) * 3
        + (other,)
        + (shape32(rows, width),) * 2
        + (shape16(rows, units),) * 2
        + (shape16(2 * rows, width),),
        (order,),
        (hn, dy_own, dy_oth, *gate_w, *up_w, *down_w),
        "feed_own",
        limit=15,
        cost=11.0,
        scratch=(pltpu.VMEM((rows, units), jnp.bfloat16),) * 2,
    )


def feed_oth(order, hn_own, hn, grads, gate_w, up_w, parts):
    rows, width = hn.shape
    return on_chip(
        feed_oth_body,
        tuple(shape16(*part.shape) for part in parts)
        + (shape16(rows, width), shape16(2 * rows, width)),
        (order,),
        (hn_own, hn, *grads, *gate_w, *up_w, *parts),
        "feed_oth",
        aliases={9 + i: i for i in range(4)},
        limit=14,
        cost=7.0,
    )


def ff_grad(left, left_core, index, right, right_core, pieces):
    rows, units = left.shape
    size = right.shape[1] // pieces
    half = right.shape[1] // 2

    def body(left, left_core, right, right_core, *outs):
        for i in range(2):
            part = slice(i * half, (i + 1) * half)
            sums = low(
                inner_rows(left[...], right[:, part])
                + inner_rows(left_core[index * rows : (index + 1) * rows, :units], right_core[:, part])
            )
            for j in range(pieces // 2):
                outs[i * pieces // 2 + j][...] = sums[:, j * size : (j + 1) * size]

    part = shape16(units, size)
    return on_chip(
        body, (part,) * pieces, (), (left, left_core, right, right_core), "ff_grad", cost=2.7
    )


def join(first, second):
    def body(first, second, out):
        out[...] = low(high(first[...]) + high(second[...]))

    return on_chip(body, shape16(*first.shape), (), (first, second), "join", cost=0.3)


def fold_three(first, second, third):
    mid = first.shape[1] // 2

    def body(first, second, third, away, rest):
        for out, part in ((away, slice(0, mid)), (rest, slice(mid, 2 * mid))):
            out[...] = low(high(first[:, part]) + high(second[:, part]) + high(third[:, part]))

    part = shape16(first.shape[0], mid)
    return on_chip(body, (part, part), (), (first, second, third), "fold_three", cost=0.3)


def fold(kept, came):
    mid = kept.shape[1] // 2

    def body(kept, came, away, rest):
        away[...] = low(high(kept[:, :mid]) + high(came[:, :mid]))
        rest[...] = low(high(kept[:, mid:]) + high(came[:, mid:]))

    part = shape16(kept.shape[0], mid)
    return on_chip(body, (part, part), (), (kept, came), "fold", cost=0.3)


def fold_rows(kept, came):
    mid = kept.shape[0] // 2

    def body(kept, came, away, rest):
        away[...] = low(high(kept[:mid, :]) + high(came[:mid, :]))
        rest[...] = low(high(kept[mid:, :]) + high(came[mid:, :]))

    part = shape16(mid, kept.shape[1])
    return on_chip(body, (part, part), (), (kept, came), "fold_rows", cost=0.3)


def hidden_grad_body(order, place, dhn_own, dhn_came, hidden_far, dy_ref, gain_ref, w_far,
    grad_ref, send_ref, own_ref, away_ref, mine_ref, gains_ref, proj, hidden_ref, w_ref, sems,
):
    cols = send_ref.shape[1]
    loads = [pltpu.make_async_copy(hidden_far, hidden_ref, sems.at[2])]
    for m in (1, 0):
        there = columns(place[0] ^ m, cols)
        loads.append(pltpu.make_async_copy(w_far.at[there, :], w_ref.at[m], sems.at[m]))
    for load in loads:
        load.start()
    loads[0].wait()
    hidden = hidden_ref[...]
    scale = rms_scale(hidden)
    dhn = dhn_own[...] + high(dhn_came[...])
    gains_ref[...] = jnp.sum(dhn * hidden * scale, axis=0, keepdims=True)
    weighted = dhn * gain_ref[...]
    mean = jnp.mean(weighted * hidden, axis=-1, keepdims=True)
    grad = high(dy_ref[...]) + scale * weighted - hidden * (scale * scale * scale * mean)
    grad_ref[...] = grad
    proj[...] = low(grad)
    loads[1].wait()
    send_ref[...] = low(against(proj[...], w_ref[1]))
    loads[2].wait()
    own_ref[...] = low(against(proj[...], w_ref[0]))
    arrange_halves(order, (proj,), away_ref, mine_ref)


def hidden_grad(order, place, dhn_own, dhn_came, hidden, dy, gain, w):
    rows, width = hidden.shape
    part = shape16(rows, width // 2)
    return on_chip(
        hidden_grad_body,
        (shape32(rows, width), part, part, part, part, shape32(1, width)),
        (order, place),
        (dhn_own, dhn_came, hidden, dy, gain, w),
        "hidden_grad",
        cost=2.2,
        limit=9,
        far=(2, 5),
        scratch=(
            pltpu.VMEM((rows, width), jnp.bfloat16),
            pltpu.VMEM((rows, width), jnp.float32),
            pltpu.VMEM((2, width // 2, width), jnp.bfloat16),
            pltpu.SemaphoreType.DMA((3,)),
        ),
    )


def bucket_grad(left, left_core, rights, rights_core, place=0, total_cols=None, before=()):
    mid = left.shape[1] // 2
    cols = rights[0].shape[1]
    count = len(rights)

    def body(left, left_core, *refs):
        for i in range(count):
            part = slice(place + i * cols, place + (i + 1) * cols)
            for half, out in enumerate(refs[-2:]):
                cut = slice(half * mid, (half + 1) * mid)
                out[:, part] = low(
                    inner_rows(left[:, cut], refs[i][...])
                    + inner_rows(left_core[:, cut], refs[count + i][...])
                )

    full = shape16(mid, total_cols or cols * count)
    return on_chip(
        body,
        (full, full),
        (),
        (left, left_core, *rights, *rights_core, *before),
        "bucket_grad",
        aliases={2 + 2 * count + i: i for i in range(len(before))},
        cost=1.5,
    )


def bucket_near(row, kept, came):
    quarter, cols = kept.shape
    size = quarter // 4

    def body(row, kept, came, away, rest):
        near = row[0] & 1
        for i in range(2):
            here = pl.ds(pl.multiple_of(i * 2 * size + near * size, size), size)
            there = pl.ds(pl.multiple_of(i * 2 * size + (1 - near) * size, size), size)
            part = slice(i * size, (i + 1) * size)
            away[part, :] = low(high(kept[there, :]) + high(came[there, :]))
            rest[part, :] = low(high(kept[here, :]) + high(came[here, :]))

    half = shape16(2 * size, cols)
    return on_chip(body, (half, half), (row,), (kept, came), "bucket_near", cost=0.3)


def shares_body(d_a, d_b, fa, fb, w_ref, x_own, x_oth, gain_two, send_ref, own_ref, gains_ref):
    rows, width = x_own.shape
    cut = d_a.shape[1]
    sums = None
    for m, x_ref in ((1, x_oth), (0, x_own)):
        part = slice(m * rows, (m + 1) * rows)
        share = against(d_a[part, :], w_ref[:, :cut]) + against(d_b[part, :], w_ref[:, cut:])
        if m:
            send_ref[:, :width] = low(share)
        else:
            own_ref[...] = share
        x = high(x_ref[...])
        here = jnp.sum(share * (x * rms_scale(x)), axis=0, keepdims=True)
        sums = here if sums is None else sums + here
    send_ref[:, width : width + fa.shape[1]] = fa[...]
    send_ref[:, width + fa.shape[1] :] = fb[...]
    gains_ref[0:1, :] = sums
    gains_ref[1:2, :] = gain_two[...]


def shares(d_a, d_b, fa, fb, w, x_own, x_oth, gain_two):
    rows, width = x_own.shape
    return on_chip(
        shares_body,
        (shape16(rows, width + 2 * fa.shape[1]), shape32(rows, width), shape32(2, width)),
        (),
        (d_a, d_b, fa, fb, w, x_own, x_oth, gain_two),
        "shares",
        cost=2.3,
    )


def input_grad_body(place, share_ref, came_ref, grad_ref, x_ref, gain_ref, fa, fb, out_ref, first_ref):
    width = x_ref.shape[1]
    x = high(x_ref[...])
    scale = rms_scale(x)
    weighted = (share_ref[...] + high(came_ref[:, :width])) * gain_ref[...]
    mean = jnp.mean(weighted * x, axis=-1, keepdims=True)
    out_ref[...] = grad_ref[...] + scale * weighted - x * (scale * scale * scale * mean)
    cols = fa.shape[1]
    own = 2 * place[0]
    oth = 2 - own
    first_ref[:, columns(own, cols)] = fa[...]
    first_ref[:, columns(own + 1, cols)] = fb[...]
    first_ref[:, columns(oth, cols)] = came_ref[:, width : width + cols]
    first_ref[:, columns(oth + 1, cols)] = came_ref[:, width + cols :]


def input_grad(place, share, came, grad_hidden, x, gain, fa, fb):
    return on_chip(
        input_grad_body,
        (shape32(*x.shape), shape16(*x.shape)),
        (place,),
        (share, came, grad_hidden, x, gain, fa, fb),
        "input_grad",
        cost=2.0,
        limit=6,
    )


def after(first, *values):
    return lax.optimization_barrier((first, *values))[1:]


def two_groups(
    inputs,
    first_values,
    lengths,
    gain_attn,
    w_qkv,
    w_out,
    gain_mlp,
    w_gate,
    w_up,
    w_down,
    cotangent,
):
    SITES.clear()
    rows = inputs.shape[1]
    width = inputs.shape[2]
    span = 2 * rows
    out_cols = HEADS // 2 * HD
    packed_cols = 3 * out_cols
    mid = width // 2
    h = lax.axis_index("head")
    f = lax.axis_index("ffn")
    r = lax.axis_index("row")
    row_size = lax.axis_size("row")
    place = jnp.stack([h, lengths[0]]).astype(jnp.int32)
    row = r.reshape(1).astype(jnp.int32)
    tie = lax.optimization_barrier
    gain_attn = gain_attn.reshape(1, width)
    gain_mlp = gain_mlp.reshape(1, width)

    x_own = inputs[0]
    x_oth = swap(x_own, "head", 1)
    early_own = lax.dynamic_slice_in_dim(first_values[0], h * out_cols, out_cols, 1)
    early_oth = swap(
        lax.dynamic_slice_in_dim(first_values[0], (1 - h) * out_cols, out_cols, 1), "head", 1
    )
    dy_own = cotangent[0]
    down_core = swap(w_down, "ffn", 1)
    gate_core = swap(w_gate.T, "ffn", 1)
    up_core = swap(w_up.T, "ffn", 1)
    qkv_w = lax.dynamic_slice_in_dim(w_qkv, h * packed_cols, packed_cols, 1)
    half = HD // 2
    inverse = jnp.exp(-jnp.log(10000.0) * jnp.arange(half, dtype=jnp.float32) * 2.0 / HD)
    sign = jnp.where(jnp.arange(2 * HD) % HD < half, -1.0, 1.0)
    cosine, sine = tables(span, jnp.tile(inverse, 4)[None, :], sign[None, :])

    ff_order = jnp.stack([(h ^ a) * row_size + (r ^ b) for a in (1, 0) for b in (3, 1, 2, 0)])
    down_order = jnp.stack([(h ^ a) * row_size + (r ^ b) for b in (3, 1, 2, 0) for a in (1, 0)])
    att_order = jnp.stack(
        [((f ^ a) * row_size + (r & 2 ^ b)) // 2 for a in (3, 1, 2, 0) for b in (2, 0)]
    )

    before = project(att_order, place, x_own, gain_attn, qkv_w, cosine, sine)
    x_oth, before, early_own, down_core, gate_core, up_core = tie(
        (x_oth, before, early_own, down_core, gate_core, up_core)
    )
    xn_away, xn_mine, query, keys, *near = project(
        att_order, place, x_oth, gain_attn, qkv_w, cosine, sine, before
    )
    att_own, att_oth, mixed, log_sums = attend_forward(place, *near, early_own, early_oth)
    att_came = swap(att_oth, "head", 1)
    (dy_send,) = after(near[2], dy_own)
    dy_oth = swap(dy_send, "ffn", 2)
    att_came, dy_oth = tie((att_came, dy_oth))
    down_w = (w_down, down_core)
    gate_w = (w_gate.T, gate_core)
    up_w = (w_up.T, up_core)
    hidden, hn_own = finish(place, x_own, att_own, att_came, w_out, gain_mlp)
    hn_oth = swap(hn_own, "ffn", 2)
    dy_send, dy_oth = after(hn_own, dy_send, dy_oth)
    dyc_own = swap(dy_send, "ffn", 1)
    dyc_oth = swap(dy_oth, "ffn", 1)
    hnc_own = swap(hn_own, "ffn", 1)

    *parts, dhn_own, down_own, dact0, dact1, dy_all = feed_own(
        down_order, hn_own, dy_own, dy_oth, gate_w, up_w, down_w
    )
    hn_oth, parts, dhn_own, down_own, dact0, dact1, dy_all, hnc_own, dyc_own, dyc_oth = tie(
        (hn_oth, parts, dhn_own, down_own, dact0, dact1, dy_all, hnc_own, dyc_own, dyc_oth)
    )
    hnc_oth = swap(hn_oth, "ffn", 1)
    act, gate, up, others, dhn_send, hn_all = feed_oth(
        ff_order, hn_own, hn_oth, (dact0, dact1), gate_w, up_w, parts
    )
    dhn_came = swap(dhn_send, "ffn", 2)
    others_core = swap(others, "ffn", 1)
    own_send, came_send = after(dhn_send, att_own, att_came)
    att_core = swap(own_send, "ffn", 1)
    came_core = swap(came_send, "ffn", 1)
    hnc_oth, dyc_own, dyc_oth = after(dhn_send, hnc_oth, dyc_own, dyc_oth)
    dyc_all = reorder(down_order, dyc_own, dyc_oth)
    hnc_all = reorder(ff_order, hnc_own, hnc_oth)

    gate_a, gate_b, gate_near, gate_kept = ff_grad(gate, others_core, 1, hn_all, hnc_all, 4)
    gate_xa = swap(gate_a, "head", 1)
    down_send, down_kept = ff_grad(act, others_core, 0, dy_all, dyc_all, 2)
    down_near = swap(down_send, "row", 1)
    up_a, up_b, up_near, up_kept = ff_grad(up, others_core, 2, hn_all, hnc_all, 4)
    dhn_came, gate_b, gate_kept, gate_near, down_kept, up_a, up_b, up_near, up_kept = tie(
        (dhn_came, gate_b, gate_kept, gate_near, down_kept, up_a, up_b, up_near, up_kept)
    )

    grad_hidden, go_send, go_own, proj_away, proj_mine, gain_two = hidden_grad(
        att_order, place, dhn_own, dhn_came, hidden, dy_own, gain_mlp, w_out
    )
    (gate_near,) = after(go_send, gate_near)
    gate_send = join(gate_near, gate_xa)
    go_send, go_own, proj_away, gate_send = tie((go_send, go_own, proj_away, gate_send))
    go_oth = swap(go_send, "head", 1)
    proj_core = swap(proj_away, "ffn", 1)
    gate_came = swap(gate_send, "row", 1)
    (gate_b,) = after(go_send, gate_b)
    gate_xb = swap(gate_b, "head", 1)
    out_send, out_kept = bucket_grad(
        proj_mine, proj_core, (att_came, att_own), (came_core, att_core)
    )
    out_y = swap(out_send, "ffn", 2)
    up_xa = swap(after(out_send, up_a)[0], "head", 1)
    go_oth, out_kept = tie((go_oth, out_kept))

    def backward(pairs, lse):
        return attend_backward(
            place, query, keys, mixed, lse, go_own, go_oth, att_own, att_oth, cosine, sine, pairs
        )

    pairs = HEADS // 4
    d_a, fa_own, fa_oth = backward((0, pairs // 2), log_sums)
    out_kept, down_kept, gate_kept = after(d_a, out_kept, down_kept, gate_kept)
    out_send, out_kept = fold(out_kept, out_y)
    out_x = swap(out_send, "head", 1)
    down_send, down_kept = fold(down_kept, down_near)
    down_mid = swap(down_send, "row", 2)
    gate_kept = join(gate_kept, gate_xb)
    d_a, out_kept, down_kept, gate_kept, log_sums = tie(
        (d_a, out_kept, down_kept, gate_kept, log_sums)
    )
    core_a = swap(d_a, "ffn", 1)
    xn_core = swap(after(out_kept, xn_away)[0], "ffn", 1)
    d_b, fb_own, fb_oth = backward((pairs // 2, pairs), log_sums)
    gate_kept, up_near = after(d_b, gate_kept, up_near)
    gate_send, gate_kept = fold(gate_kept, gate_came)
    up_send = join(up_near, up_xa)
    d_b, gate_kept, up_send = tie((d_b, gate_kept, up_send))
    core_b = swap(d_b, "ffn", 1)
    up_xb = swap(after(gate_kept, up_b)[0], "head", 1)
    up_came = swap(up_send, "row", 1)
    (d_a,) = after(gate_kept, d_a)
    before = bucket_grad(xn_mine, xn_core, (d_a,), (core_a,), 0, packed_cols)
    core_b, *before = tie((core_b, *before))
    y_send, kept = bucket_grad(
        xn_mine, xn_core, (d_b,), (core_b,), packed_cols // 2, packed_cols, before
    )
    y_came = swap(y_send, "ffn", 2)
    d_a, d_b = after(y_send, d_a, d_b)
    back_send, share_own, gains = shares(
        d_a, d_b, fa_oth, fb_oth, qkv_w, x_own, x_oth, gain_two
    )
    gate_send, out_kept, act, others, up_kept, down_kept = after(
        back_send, gate_send, out_kept, act, others, up_kept, down_kept
    )
    out_send, out_kept = bucket_near(row, out_kept, out_x)
    out_near = swap(out_send, "row", 1)
    gains = gains + swap(gains, "head", 1)
    gains, back_send = tie((gains, back_send))
    back_came = swap(back_send, "head", 1)
    up_kept, down_kept = after(gains, up_kept, down_kept)
    up_send, up_kept = fold_three(up_kept, up_xb, up_came)
    gate_far = swap(gate_send, "row", 2)
    units = w_down.shape[0]
    far_send = low(matmul(act[rows:], down_w[0]) + matmul(others[rows:span, :units], down_w[1]))
    gains, down_kept, gate_kept, out_kept = after(far_send, gains, down_kept, gate_kept, out_kept)
    gains = gains + swap(gains, "ffn", 1)
    down_send, down_kept = fold(down_kept, down_mid)
    out_send, out_kept = fold_rows(out_kept, out_near)
    out_far = swap(out_send, "row", 2)
    sum_gate = high(gate_kept) + high(gate_far)
    kept, up_send, down_send, sum_gate, gains, out_send = tie(
        (kept, up_send, down_send, sum_gate, gains, out_send)
    )

    near_send, kept = bucket_near(row, kept, y_came)
    near_came = swap(near_send, "row", 1)
    gains, far_send, out_kept, up_send, down_send = after(
        near_send, gains, far_send, out_kept, up_send, down_send
    )
    gains = gains + swap(gains, "ffn", 2)
    (far_send,) = after(gains, far_send)
    far_came = swap(far_send, "ffn", 2)
    up_far = swap(up_send, "row", 2)
    qkv_send, kept = fold_rows(kept, near_came)
    qkv_far = swap(qkv_send, "row", 2)
    share_own, down_kept, up_kept, out_kept, residual, gains, down_send = after(
        qkv_send,
        share_own,
        down_kept,
        up_kept,
        out_kept,
        hidden + down_own,
        gains,
        down_send,
    )
    down_x = swap(down_send, "head", 1)
    gains = gains + swap(gains, "row", 1)
    gains_far = swap(gains, "row", 2)
    (share_own,) = after(gains, share_own)
    grad_in, grad_first = input_grad(
        place, share_own, back_came, grad_hidden, x_own, gain_attn, fa_own, fb_own
    )
    sum_up = high(up_kept) + high(up_far)
    out_sum = high(out_kept) + high(out_far)
    output = low(residual + high(far_came))[None]
    (down_kept,) = after(output, down_kept)
    sum_down = high(down_kept) + high(down_x)
    gains = gains + gains_far
    kept, grad_in, sum_up, sum_down, out_sum, output, gains = tie(
        (kept, grad_in, sum_up, sum_down, out_sum, output, gains)
    )
    sum_qkv = high(kept) + high(qkv_far)
    return (
        output,
        grad_in[None],
        grad_first[None],
        gains[0],
        sum_qkv,
        out_sum.T,
        gains[1],
        sum_gate.T,
        sum_up.T,
        sum_down,
    )


def solution(mesh):
    in_specs = (
        P(("ffn", "row"), "head", None),
        P(("ffn", "row"), "head", None),
        P(("ffn", "row")),
        P(),
        P(),
        P(),
        P(),
        P(None, "ffn"),
        P(None, "ffn"),
        P("ffn", None),
        P(("ffn", "row"), "head", None),
    )
    out_specs = (
        P(("ffn", "row"), "head", None),
        P(("ffn", "row"), "head", None),
        P(("ffn", "row"), "head", None),
        P(),
        P(("ffn", "row"), "head"),
        P("head", ("ffn", "row")),
        P(),
        P(("head", "row"), "ffn"),
        P(("head", "row"), "ffn"),
        P("ffn", ("head", "row")),
    )
    body = two_groups if mesh.shape["head"] == 2 and mesh.shape["ffn"] == 4 else any_groups
    return jax.shard_map(
        body, mesh=mesh, in_specs=in_specs, out_specs=out_specs, check_vma=False
    )
```

```python
import functools

import jax
import jax.numpy as jnp
from jax import lax
from jax.experimental import pallas as pl
from jax.experimental.pallas import tpu as pltpu
from jax.sharding import PartitionSpec as P

HEADS = 16
HD = 64
MIN_LEN = 512
STEP = 256


eps = 1e-06


def rms_scale(values):
    return lax.rsqrt(jnp.mean(values * values, axis=-1, keepdims=True) + eps)


def matmul(left, right):
    return jnp.dot(left, right, preferred_element_type=jnp.float32)


def inner_rows(left, right):
    return lax.dot_general(
        left, right, (((0,), (0,)), ((), ())), preferred_element_type=jnp.float32
    )


def against(left, right):
    return lax.dot_general(
        left, right, (((1,), (1,)), ((), ())), preferred_element_type=jnp.float32
    )


def swap(values, axis, mask):
    size = lax.axis_size(axis)
    return lax.ppermute(values, axis, [(i, i ^ mask) for i in range(size)])


def bits_of(axis):
    size = lax.axis_size(axis)
    return [1 << b for b in range(size.bit_length() - 2, -1, -1)]


def halve(values, dim, axis, mask):
    bit = (lax.axis_index(axis) // mask) % 2
    away = lax.dynamic_index_in_dim(values, 1 - bit, dim, keepdims=False)
    kept = lax.dynamic_index_in_dim(values, bit, dim, keepdims=False)
    came = swap(away.astype(jnp.bfloat16), axis, mask)
    return kept.astype(jnp.float32) + came.astype(jnp.float32)


def total(values, axes):
    for axis in axes:
        for mask in reversed(bits_of(axis)):
            values = values + swap(values, axis, mask)
    return values


def rotary(positions, head_size):
    half_size = head_size // 2
    inverse = jnp.exp(
        -jnp.log(10000.0) * jnp.arange(half_size, dtype=jnp.float32) * 2.0 / head_size
    )
    angles = positions.astype(jnp.float32)[:, None] * inverse[None, :]
    return (jnp.cos(angles), jnp.sin(angles))


def rotate(vectors, cosine, sine, sign):
    half_size = vectors.shape[-1] // 2
    first_half = vectors[..., :half_size]
    second_half = vectors[..., half_size:]
    cos_rows = cosine[:, None, :]
    sin_rows = sign * sine[:, None, :]
    return jnp.concatenate(
        [
            first_half * cos_rows - second_half * sin_rows,
            second_half * cos_rows + first_half * sin_rows,
        ],
        axis=-1,
    )


def masked_scores(q_rows, keys, q_pos, k_pos, valid):
    raw = jnp.einsum("qhe,khe->hqk", q_rows, keys, preferred_element_type=jnp.float32)
    allowed = (k_pos[None, :] <= q_pos[:, None]) & (k_pos[None, :] < valid)
    return jnp.where(allowed[None], 0.125 * raw, -1e30)


def scan_forward(query, keys, mixed, positions, valid, block_rows):
    count = query.shape[0] // block_rows

    def step(carry, index):
        start = index * block_rows
        q_rows = lax.dynamic_slice_in_dim(query, start, block_rows, 0)
        q_pos = lax.dynamic_slice_in_dim(positions, start, block_rows, 0)
        scores = masked_scores(q_rows, keys, q_pos, positions, valid)
        top = jnp.max(scores, axis=-1, keepdims=True)
        expo = jnp.exp(scores - top)
        total_w = jnp.sum(expo, axis=-1, keepdims=True)
        weights = expo / total_w
        result = jnp.einsum(
            "hqk,khe->qhe", weights.astype(jnp.bfloat16), mixed, preferred_element_type=jnp.float32
        )
        return (carry, (result.astype(jnp.bfloat16), top + jnp.log(total_w)))

    _, (outs, log_sums) = lax.scan(step, 0, jnp.arange(count, dtype=jnp.int32))
    return (outs.reshape(query.shape), log_sums)


def scan_backward(query, keys, mixed, positions, valid, log_sums, grad_out, block_rows):
    count = query.shape[0] // block_rows
    zeros = jnp.zeros(keys.shape, jnp.float32)

    def step(carry, index):
        key_sum, value_sum = carry
        start = index * block_rows
        q_rows = lax.dynamic_slice_in_dim(query, start, block_rows, 0)
        q_pos = lax.dynamic_slice_in_dim(positions, start, block_rows, 0)
        g_rows = lax.dynamic_slice_in_dim(grad_out, start, block_rows, 0)
        scores = masked_scores(q_rows, keys, q_pos, positions, valid)
        weights = jnp.exp(scores - log_sums[index])
        grad_w = jnp.einsum("qhe,khe->hqk", g_rows, mixed, preferred_element_type=jnp.float32)
        delta = jnp.sum(weights * grad_w, axis=-1, keepdims=True)
        grad_s = (weights * (grad_w - delta)).astype(jnp.bfloat16)
        grad_q = 0.125 * jnp.einsum(
            "hqk,khe->qhe", grad_s, keys, preferred_element_type=jnp.float32
        )
        key_sum = key_sum + 0.125 * jnp.einsum(
            "hqk,qhe->khe", grad_s, q_rows, preferred_element_type=jnp.float32
        )
        value_sum = value_sum + jnp.einsum(
            "hqk,qhe->khe", weights.astype(jnp.bfloat16), g_rows, preferred_element_type=jnp.float32
        )
        return ((key_sum, value_sum), grad_q)

    (grad_keys, grad_mixed), grad_query = lax.scan(
        step, (zeros, zeros), jnp.arange(count, dtype=jnp.int32)
    )
    return (grad_query.reshape(query.shape), grad_keys, grad_mixed)


def any_groups(
    inputs,
    first_values,
    lengths,
    gain_attn,
    w_qkv,
    w_out,
    gain_mlp,
    w_gate,
    w_up,
    w_down,
    cotangent,
):
    rows = inputs.shape[1]
    width = inputs.shape[2]
    groups = lax.axis_size("head")
    shards = lax.axis_size("ffn")
    heads_here = HEADS // groups
    span_rows = rows * groups
    block_rows = span_rows // max(1, span_rows // 512)
    head_pos = lax.axis_index("head")
    valid_len = lengths[0]
    packed_cols = heads_here * 3 * HD
    out_cols = heads_here * HD
    hidden_here = w_gate.shape[1]

    owners = [head_pos ^ m for m in range(groups)]
    x_all = [inputs[0]] + [swap(inputs[0], "head", m) for m in range(1, groups)]
    early = []
    for m in range(groups):
        piece = lax.dynamic_slice_in_dim(first_values[0], owners[m] * out_cols, out_cols, 1)
        early.append(swap(piece, "head", m) if m else piece)
    far = range(2, shards, 2)
    grad_rows = jnp.concatenate([cotangent[0]] + [swap(cotangent[0], "ffn", m) for m in far], 0)
    gate_w = jnp.concatenate([w_gate, swap(w_gate, "ffn", 1)], 1)
    up_w = jnp.concatenate([w_up, swap(w_up, "ffn", 1)], 1)
    down_w = jnp.concatenate([w_down, swap(w_down, "ffn", 1)], 0)
    w_heads = lax.dynamic_slice_in_dim(w_qkv, head_pos * packed_cols, packed_cols, 1)
    out_w = jnp.concatenate(
        [lax.dynamic_slice_in_dim(w_out, o * out_cols, out_cols, 0) for o in owners], 0
    )

    positions = jnp.concatenate([o * rows + jnp.arange(rows, dtype=jnp.int32) for o in owners])
    cosine, sine = rotary(positions, HD)
    normed, scaled, queries, key_list, mixes = [], [], [], [], []
    rows_in = inputs[0].astype(jnp.float32)
    scale_one = rms_scale(rows_in)
    for m in range(groups):
        block = x_all[m].astype(jnp.float32)
        scale = rms_scale(block)
        scaled.append(block * scale)
        normed.append((block * scale * gain_attn).astype(jnp.bfloat16))
        packed = matmul(normed[m], w_heads).astype(jnp.bfloat16)
        packed = packed.reshape(rows, heads_here, 3, HD).astype(jnp.float32)
        part = slice(m * rows, (m + 1) * rows)
        queries.append(rotate(packed[:, :, 0], cosine[part], sine[part], 1.0))
        key_list.append(rotate(packed[:, :, 1], cosine[part], sine[part], 1.0))
        value = early[m].reshape(rows, heads_here, HD).astype(jnp.float32)
        mixes.append(0.5 * (packed[:, :, 2] + value))
    query = jnp.concatenate(queries, 0).astype(jnp.bfloat16)
    keys = jnp.concatenate(key_list, 0).astype(jnp.bfloat16)
    mixed = jnp.concatenate(mixes, 0).astype(jnp.bfloat16)
    attended, log_sums = scan_forward(query, keys, mixed, positions, valid_len, block_rows)
    attended = attended.reshape(groups, rows, out_cols)
    att_own = jnp.concatenate(
        [attended[0]] + [swap(attended[m], "head", m) for m in range(1, groups)], 1
    )
    hidden = rows_in + matmul(att_own, out_w)
    scale_two = rms_scale(hidden)
    normed_two = (hidden * scale_two * gain_mlp).astype(jnp.bfloat16)

    mlp_rows = [normed_two] + [swap(normed_two, "ffn", m) for m in far]
    grad_list = [grad_rows[i * rows : (i + 1) * rows] for i in range(len(mlp_rows))]
    actives, grad_gates, grad_ups, downs, grad_normed_list = [], [], [], [], []
    for i, block in enumerate(mlp_rows):
        gate_rows = matmul(block, gate_w)
        up_rows = matmul(block, up_w)
        sigmoid_gate = jax.nn.sigmoid(gate_rows)
        silu_gate = gate_rows * sigmoid_gate
        grad_active = against(grad_list[i], down_w)
        actives.append((silu_gate * up_rows).astype(jnp.bfloat16))
        grad_gates.append(
            (
                grad_active * up_rows * sigmoid_gate * (1.0 + gate_rows * (1.0 - sigmoid_gate))
            ).astype(jnp.bfloat16)
        )
        grad_ups.append((grad_active * silu_gate).astype(jnp.bfloat16))
        grad_normed_list.append(against(grad_gates[i], gate_w) + against(grad_ups[i], up_w))
        downs.append(matmul(actives[i], down_w))
    grad_normed_two = grad_normed_list[0]
    for i, m in enumerate(far):
        came = swap(grad_normed_list[i + 1].astype(jnp.bfloat16), "ffn", m)
        grad_normed_two = grad_normed_two + came.astype(jnp.float32)
    down_rows = downs[0]
    for i, m in enumerate(far):
        down_rows = down_rows + swap(downs[i + 1].astype(jnp.bfloat16), "ffn", m).astype(jnp.float32)
    output = (hidden + down_rows).astype(jnp.bfloat16)[None]

    all_rows = jnp.concatenate(mlp_rows, 0)
    ff_sums = []
    for left, right in (
        (grad_rows, jnp.concatenate(actives, 0)),
        (all_rows, jnp.concatenate(grad_gates, 0)),
        (all_rows, jnp.concatenate(grad_ups, 0)),
    ):
        away = inner_rows(left, right[:, hidden_here:]).astype(jnp.bfloat16)
        part = inner_rows(left, right[:, :hidden_here])
        part = (part + swap(away, "ffn", 1).astype(jnp.float32)).astype(jnp.bfloat16)
        steps = [("head", b) for b in bits_of("head")] + [("row", b) for b in bits_of("row")]
        part = part.reshape([2] * len(steps) + [-1, hidden_here])
        order = [s for s in steps if s[0] == "head"] + [s for s in reversed(steps) if s[0] == "row"]
        left_steps = list(steps)
        for s in order:
            part = halve(part, left_steps.index(s), *s)
            left_steps.remove(s)
            if left_steps:
                part = part.astype(jnp.bfloat16)
        ff_sums.append(part)
    sum_down, sum_gate, sum_up = ff_sums

    grad_y = cotangent[0].astype(jnp.float32)
    grad_gain_two = jnp.sum(grad_normed_two * hidden * scale_two, axis=0)
    weighted_two = grad_normed_two * gain_mlp
    cube_two = scale_two * scale_two * scale_two
    grad_hidden = (
        grad_y
        + scale_two * weighted_two
        - hidden * cube_two * jnp.mean(weighted_two * hidden, axis=-1, keepdims=True)
    )
    grad_proj = grad_hidden.astype(jnp.bfloat16)
    grad_att = against(grad_proj, out_w).astype(jnp.bfloat16)
    grad_att = jnp.concatenate(
        [
            swap(grad_att[:, m * out_cols : (m + 1) * out_cols], "head", m)
            if m
            else grad_att[:, :out_cols]
            for m in range(groups)
        ],
        0,
    ).reshape(span_rows, heads_here, HD)

    def over_buckets(part):
        steps = [("ffn", b) for b in bits_of("ffn")] + [("row", b) for b in bits_of("row")]
        part = part.astype(jnp.bfloat16).reshape([2] * len(steps) + [-1, part.shape[1]])
        order = [s for s in reversed(steps) if s[0] == "ffn"] + [
            s for s in reversed(steps) if s[0] == "row"
        ]
        left_steps = list(steps)
        for s in order:
            part = halve(part, left_steps.index(s), *s)
            left_steps.remove(s)
            if left_steps:
                part = part.astype(jnp.bfloat16)
        return part

    part = over_buckets(inner_rows(grad_proj, att_own))
    sum_out = part[:, :out_cols]
    for m in range(1, groups):
        came = swap(part[:, m * out_cols : (m + 1) * out_cols].astype(jnp.bfloat16), "head", m)
        sum_out = sum_out + came.astype(jnp.float32)

    grad_query, grad_keys, grad_mixed = scan_backward(
        query, keys, mixed, positions, valid_len, log_sums, grad_att, block_rows
    )
    grad_packed = jnp.stack(
        [
            rotate(grad_query, cosine, sine, -1.0),
            rotate(grad_keys, cosine, sine, -1.0),
            0.5 * grad_mixed,
        ],
        axis=2,
    )
    grad_packed = grad_packed.astype(jnp.bfloat16).reshape(span_rows, packed_cols)
    grad_early = (0.5 * grad_mixed).astype(jnp.bfloat16).reshape(span_rows, out_cols)
    firsts = [grad_early[m * rows : (m + 1) * rows] for m in range(groups)]
    firsts = [swap(firsts[m], "head", m) if m else firsts[0] for m in range(groups)]
    grad_first = jnp.zeros((rows, width), jnp.bfloat16)
    for m in range(groups):
        grad_first = lax.dynamic_update_slice_in_dim(grad_first, firsts[m], owners[m] * out_cols, 1)
    shares = [
        against(grad_packed[m * rows : (m + 1) * rows], w_heads) for m in range(groups)
    ]
    grad_gain_one = sum(jnp.sum(shares[m] * scaled[m], axis=0) for m in range(groups))
    grad_normed = shares[0]
    for m in range(1, groups):
        grad_normed = grad_normed + swap(shares[m].astype(jnp.bfloat16), "head", m).astype(jnp.float32)
    sum_qkv = over_buckets(inner_rows(jnp.concatenate(normed, 0), grad_packed))
    weighted_one = grad_normed * gain_attn
    cube_one = scale_one * scale_one * scale_one
    grad_in = (
        grad_hidden
        + scale_one * weighted_one
        - rows_in * cube_one * jnp.mean(weighted_one * rows_in, axis=-1, keepdims=True)
    )
    gains = total(jnp.stack([grad_gain_one, grad_gain_two]), ("ffn", "head", "row"))
    return (
        output,
        grad_in[None],
        grad_first[None],
        gains[0],
        sum_qkv,
        sum_out.T,
        gains[1],
        sum_gate,
        sum_up,
        sum_down.T,
    )


SCALE = 4.5e8
COSTS = {}
SITES = {}


def site_cost(name, usual):
    count = SITES.get(name, 0)
    SITES[name] = count + 1
    return int(SCALE * COSTS.get(name + str(count), usual))


def low(values):
    return values.astype(jnp.bfloat16)


def high(values):
    return values.astype(jnp.float32)


def on_chip(body, outs, scalars, arrays, name, scratch=(), aliases=None, limit=3, cost=1.0, away=(), far=()):
    inside = pl.BlockSpec(memory_space=pltpu.VMEM)
    outside = pl.BlockSpec(memory_space=pl.ANY)
    return pl.pallas_call(
        body,
        out_shape=jax.tree.unflatten(
            jax.tree.structure(outs),
            [
                pltpu.HBM(o.shape, o.dtype) if i in away else o
                for i, o in enumerate(jax.tree.leaves(outs))
            ],
        ),
        in_specs=[pl.BlockSpec(memory_space=pltpu.SMEM)] * len(scalars)
        + [outside if i in far else inside for i in range(len(arrays))],
        out_specs=jax.tree.unflatten(
            jax.tree.structure(outs),
            [
                outside if i in away else inside
                for i in range(len(jax.tree.leaves(outs)))
            ],
        ),
        scratch_shapes=list(scratch),
        input_output_aliases=aliases or {},
        cost_estimate=pl.CostEstimate(
            flops=site_cost(name, cost), transcendentals=0, bytes_accessed=1
        ),
        compiler_params=pltpu.CompilerParams(vmem_limit_bytes=limit << 20),
        name=name,
    )(*scalars, *arrays)


def shape16(*dims):
    return jax.ShapeDtypeStruct(dims, jnp.bfloat16)


def shape32(*dims):
    return jax.ShapeDtypeStruct(dims, jnp.float32)


def spans(total):
    return [(a, min(a + STEP, total)) for a in range(0, total, STEP)]


def turn(values):
    lane = lax.broadcasted_iota(jnp.int32, values.shape, 1)
    return jnp.where(
        lane % HD < HD // 2, pltpu.roll(values, 2 * HD - HD // 2, 1), pltpu.roll(values, HD // 2, 1)
    )


def allowed_keys(a, b, valid):
    size = b - a
    down = lax.broadcasted_iota(jnp.int32, (size, size), 0)
    across = lax.broadcasted_iota(jnp.int32, (size, size), 1)
    allowed = down <= across
    if b > MIN_LEN:
        allowed = allowed & (down < valid - a)
    return allowed


def columns(index, size):
    return pl.ds(pl.multiple_of(index * size, size), size)


def forward_body(
    place, q_ref, k_ref, raw_ref, early_own, early_oth,
    own_far, oth_far, v_far, lse_out, att_own, att_oth, v_out, flipped, att, sems,
):
    rows = early_own.shape[0]
    span = 2 * rows
    wide = 2 * HD
    valid = place[1]
    bf = jnp.bfloat16
    first = lax.broadcasted_iota(jnp.int32, (1, wide), 1) < HD
    flipped[:, HD:, :] = jnp.ones((2, 16, span), bf)

    def copies(p):
        cols = columns(p, wide)
        return [
            pltpu.make_async_copy(near.at[:, cols], far.at[:, cols], sems.at[i, p])
            for i, (near, far) in enumerate(
                ((v_out, v_far), (att_oth, oth_far), (att_own, own_far))
            )
        ]

    def pair(p, _):
        cols = columns(p, wide)
        for m, early in enumerate((early_own, early_oth)):
            here = columns(place[0] ^ m, rows)
            v_out[here, cols] = low(0.5 * (high(raw_ref[here, cols]) + high(early[:, cols])))
        copies(p)[0].start()
        turned = v_out[:, cols].T
        for e in range(2):
            flipped[e, :HD, :] = turned[e * HD : (e + 1) * HD, :]
        for a, b in spans(span):
            q = q_ref[a:b, cols] * jnp.asarray(0.125, bf)
            allowed = allowed_keys(a, b, valid)
            for e in range(2):
                qe = jnp.where(first == (e == 0), q, jnp.zeros_like(q))
                diag = jnp.where(allowed, against(k_ref[a:b, cols], qe), -1e30)
                top = jnp.max(diag, axis=0, keepdims=True)
                if a:
                    past = against(k_ref[:a, cols], qe)
                    top = jnp.maximum(top, jnp.max(past, axis=0, keepdims=True))
                out = matmul(flipped[e, :, a:b], low(jnp.exp(diag - top)))
                if a:
                    out = out + matmul(flipped[e, :, :a], low(jnp.exp(past - top)))
                amount = out[HD : HD + 1, :]
                att[e * HD : (e + 1) * HD, a:b] = out[:HD, :] / amount
                lse_out[p, e : e + 1, a:b] = top + jnp.log(amount)
        result = low(att[...].T)
        upper = place[0] == 0
        att_own[:, cols] = jnp.where(upper, result[:rows, :], result[rows:, :])
        att_oth[:, cols] = jnp.where(upper, result[rows:, :], result[:rows, :])
        for copy in copies(p)[1:]:
            copy.start()
        return 0

    lax.fori_loop(0, lse_out.shape[0], pair, 0)
    for p in range(lse_out.shape[0]):
        for copy in copies(p):
            copy.wait()


def attend_forward(place, query, keys, raw, early_own, early_oth):
    span, cols = query.shape
    rows = span // 2
    heads = cols // HD
    out = shape16(rows, cols)
    natural = shape16(span, cols)
    return on_chip(
        forward_body,
        (out, out, natural, shape32(heads // 2, 2, span)),
        (place,),
        (query, keys, raw, early_own, early_oth),
        "attend_forward",
        cost=9.0,
        limit=6,
        away=(0, 1, 2),
        scratch=(
            pltpu.VMEM(out.shape, jnp.bfloat16),
            pltpu.VMEM(out.shape, jnp.bfloat16),
            pltpu.VMEM(natural.shape, jnp.bfloat16),
            pltpu.VMEM((2, HD + 16, span), jnp.bfloat16),
            pltpu.VMEM((2 * HD, span), jnp.float32),
            pltpu.SemaphoreType.DMA((3, heads // 2)),
        ),
    )


def backward_body(
    start, place, q_far, k_far, v_far, lse_ref, go_own, go_oth, att_own, att_oth, cos_ref, sin_ref,
    d_out, f_own, f_oth, q_ref, k_ref, v_ref, sems, grad, prod, turned_k, dq, dk, dv,
):
    rows = go_own.shape[0]
    span = 2 * rows
    valid = place[1]
    wide = 2 * HD
    bf = jnp.bfloat16
    first = lax.broadcasted_iota(jnp.int32, (1, wide), 1) < HD
    eighth = jnp.asarray(0.125, bf)
    count = f_own.shape[1] // wide

    def copies(i):
        there = columns(i + start, wide)
        here = columns(i, wide)
        return [
            pltpu.make_async_copy(away.at[:, there], near.at[:, here], sems.at[n, i])
            for n, (away, near) in enumerate(((q_far, q_ref), (k_far, k_ref), (v_far, v_ref)))
        ]

    for i in range(count):
        for copy in copies(i):
            copy.start()

    def pair(i, _):
        p = i + start
        cols = columns(p, wide)
        near = columns(i, wide)
        for copy in copies(i):
            copy.wait()
        for m, (go, att) in enumerate(((go_own, att_own), (go_oth, att_oth))):
            here = columns(place[0] ^ m, rows)
            grad[here, :] = go[:, cols]
            prod[here, :] = high(go[:, cols]) * high(att[:, cols])
        flat = prod[...].T
        deltas = [jnp.sum(flat[e * HD : (e + 1) * HD, :], axis=0, keepdims=True) for e in range(2)]
        turned_k[...] = (k_ref[:, near] * eighth).T
        for n, (a, b) in enumerate(spans(span)):
            allowed = allowed_keys(a, b, valid)
            q = q_ref[a:b, near] * eighth
            g = grad[a:b, :]
            parts = ((a, b), (0, a)) if a else ((a, b),)
            sums = {}
            for e in range(2):
                mine = first == (e == 0)
                qe = jnp.where(mine, q, jnp.zeros_like(q))
                ge = jnp.where(mine, g, jnp.zeros_like(g))
                for lo, hi in parts:
                    scores = against(k_ref[lo:hi, near], qe)
                    if lo == a:
                        scores = jnp.where(allowed, scores, -1e30)
                    weights = jnp.exp(scores - lse_ref[p, e : e + 1, a:b])
                    grad_w = against(v_ref[lo:hi, near], ge)
                    grad_s = low(weights * (grad_w - deltas[e][:, a:b]))
                    dv_here = matmul(low(weights), ge)
                    dk_here = matmul(grad_s, qe)
                    dq_here = matmul(turned_k[e * HD : (e + 1) * HD, lo:hi], grad_s)
                    if (lo, "v") in sums:
                        dv_here = dv_here + sums[lo, "v"]
                        dk_here = dk_here + sums[lo, "k"]
                    sums[lo, "v"], sums[lo, "k"] = dv_here, dk_here
                    sums[lo, e] = dq_here
            for e in range(2):
                dq[e * HD : (e + 1) * HD, a:b] = sums[a, e] + sums[0, e] if a else sums[a, e]
            dv[a:b, :] = sums[a, "v"]
            dk[a:b, :] = sums[a, "k"]
            if a:
                dv[:a, :] += sums[0, "v"]
                dk[:a, :] += sums[0, "k"]
        prod[...] = dq[...].T
        for m, f_out in enumerate((f_own, f_oth)):
            here = columns(place[0] ^ m, rows)
            cosine = cos_ref[here, :]
            sine = sin_ref[here, :]
            gv = low(0.5 * dv[here, :])
            gk = dk[here, :]
            gk = low(pltpu.roll(gk * cosine - turn(gk) * sine, HD, 1))
            gq = prod[here, :]
            gq = low(gq * cosine - turn(gq) * sine)
            part = slice(m * rows, (m + 1) * rows)
            base = i * 3 * wide
            d_out[part, pl.ds(pl.multiple_of(base, wide), wide)] = jnp.where(first, gq, gk)
            d_out[part, pl.ds(pl.multiple_of(base + wide, wide), wide)] = jnp.where(first, gv, gq)
            d_out[part, pl.ds(pl.multiple_of(base + 2 * wide, wide), wide)] = jnp.where(first, gk, gv)
            f_out[:, columns(i, wide)] = gv
        return 0

    lax.fori_loop(0, count, pair, 0)


def attend_backward(place, q, k, v, lse, go_own, go_oth, att_own, att_oth, cosine, sine, pairs):
    span = q.shape[0]
    rows = span // 2
    wide = 2 * HD
    cols = wide * (pairs[1] - pairs[0])
    return on_chip(
        functools.partial(backward_body, pairs[0]),
        (shape16(span, 3 * cols), shape16(rows, cols), shape16(rows, cols)),
        (place,),
        (q, k, v, lse, go_own, go_oth, att_own, att_oth, cosine, sine),
        "attend_backward",
        cost=7.5,
        limit=6,
        far=(0, 1, 2),
        scratch=(
            pltpu.VMEM((span, cols), jnp.bfloat16),
            pltpu.VMEM((span, cols), jnp.bfloat16),
            pltpu.VMEM((span, cols), jnp.bfloat16),
            pltpu.SemaphoreType.DMA((3, pairs[1] - pairs[0])),
            pltpu.VMEM((span, wide), jnp.bfloat16),
            pltpu.VMEM((span, wide), jnp.float32),
            pltpu.VMEM((wide, span), jnp.bfloat16),
            pltpu.VMEM((wide, span), jnp.float32),
            pltpu.VMEM((span, wide), jnp.float32),
            pltpu.VMEM((span, wide), jnp.float32),
        ),
    )


def row_blocks(rows, body, size=64):
    def step(c, _):
        body(columns(c, size))
        return 0

    lax.fori_loop(0, rows // size, step, 0)


def tables(span, inverse, sign):
    def body(inverse, sign, cos_ref, sin_ref):
        def rows(part):
            shape = (64, inverse.shape[1])
            place = part.start + lax.broadcasted_iota(jnp.int32, shape, 0)
            angles = place.astype(jnp.float32) * inverse[...]
            cos_ref[part, :] = jnp.cos(angles)
            sin_ref[part, :] = jnp.sin(angles) * sign[...]

        row_blocks(span, rows)

    out = shape32(span, inverse.shape[1])
    return on_chip(body, (out, out), (), (inverse, sign), "tables", cost=1.0)


def project_body(block, order, place, x_ref, gain_ref, w_ref, cos_ref, sin_ref, *refs):
    away_far, mine_far, q_far, k_far, q_out, k_out, v_out = refs[-12:-5]
    xn, away, mine, packed, sems = refs[-5:]
    rows = x_ref.shape[0]
    wide = 2 * HD
    x = high(x_ref[...])
    xn[...] = low(x * rms_scale(x) * gain_ref[...])
    arrange_halves(order, (xn,), away, mine)
    there = slice(block * rows, (block + 1) * rows)
    here = columns(place[0] ^ block, rows)
    copies = [
        pltpu.make_async_copy(away, away_far.at[there, :], sems.at[0]),
        pltpu.make_async_copy(mine, mine_far.at[there, :], sems.at[1]),
        pltpu.make_async_copy(q_out.at[here, :], q_far.at[here, :], sems.at[2]),
        pltpu.make_async_copy(k_out.at[here, :], k_far.at[here, :], sems.at[3]),
    ]
    for copy in copies[:2]:
        copy.start()
    cols = w_ref.shape[1] // 3
    for i in range(3):
        part = slice(i * cols, (i + 1) * cols)
        packed[:, part] = low(matmul(xn[...], w_ref[:, part]))
    cosine = cos_ref[here, :]
    sine = sin_ref[here, :]
    first = lax.broadcasted_iota(jnp.int32, (1, wide), 1) < HD

    def pair(p, _):
        to = columns(p, wide)
        x0, x1, x2 = [high(packed[:, columns(3 * p + i, wide)]) for i in range(3)]
        q = jnp.where(first, x0, x1)
        k = pltpu.roll(jnp.where(first, x2, x0), HD, 1)
        q_out[here, to] = low(q * cosine + turn(q) * sine)
        k_out[here, to] = low(k * cosine + turn(k) * sine)
        v_out[here, to] = low(jnp.where(first, x1, x2))
        return 0

    lax.fori_loop(0, q_out.shape[1] // wide, pair, 0)
    for copy in copies[2:]:
        copy.start()
    for copy in copies:
        copy.wait()


def project(order, place, x, gain, w, cosine, sine, before=()):
    rows, width = x.shape
    inside = pl.BlockSpec(memory_space=pltpu.VMEM)
    outside = pl.BlockSpec(memory_space=pl.ANY)
    scalar = pl.BlockSpec(memory_space=pltpu.SMEM)
    part = (2 * rows, width // 2)
    natural = (2 * rows, w.shape[1] // 3)
    far = [part, part, natural, natural]
    return pl.pallas_call(
        functools.partial(project_body, 1 if before else 0),
        out_shape=tuple(pltpu.HBM(f, jnp.bfloat16) for f in far) + (shape16(*natural),) * 3,
        in_specs=[scalar] * 2 + [inside] * 5 + ([outside] * 4 + [inside] * 3 if before else []),
        out_specs=(outside,) * 4 + (inside,) * 3,
        scratch_shapes=[
            pltpu.VMEM((rows, width), jnp.bfloat16),
            pltpu.VMEM((rows, width // 2), jnp.bfloat16),
            pltpu.VMEM((rows, width // 2), jnp.bfloat16),
            pltpu.VMEM((rows, w.shape[1]), jnp.bfloat16),
            pltpu.SemaphoreType.DMA((4,)),
        ],
        input_output_aliases={7 + i: i for i in range(len(before))},
        cost_estimate=pl.CostEstimate(
            flops=site_cost("project", 3.0), transcendentals=0, bytes_accessed=1
        ),
        compiler_params=pltpu.CompilerParams(vmem_limit_bytes=8 << 20),
        name="project",
    )(order, place, x, gain, w, cosine, sine, *before)


def arrange(order, blocks, out):
    rows = blocks[0].shape[0]
    size = out.shape[1] // order.shape[0]
    for i in range(order.shape[0]):
        for b, block in enumerate(blocks):
            out[b * rows : (b + 1) * rows, i * size : (i + 1) * size] = block[:, columns(order[i], size)]


def finish(place, x, att_own, att_came, w, gain):
    def body(
        place, x_far, own_far, came_far, w_far, gain_ref,
        hidden_far, hn_ref, hidden_ref, w_ref, att_ref, x_ref, sems,
    ):
        cols = own_far.shape[1]
        x_load = pltpu.make_async_copy(x_far, x_ref, sems.at[5])
        x_load.start()
        loads = []
        for m, far in enumerate((own_far, came_far)):
            there = columns(place[0] ^ m, cols)
            loads.append(pltpu.make_async_copy(far, att_ref.at[m], sems.at[3 + m]))
            loads.append(pltpu.make_async_copy(w_far.at[there, :], w_ref.at[m], sems.at[m]))
        for load in loads:
            load.start()
        x_load.wait()
        hidden = high(x_ref[...])
        for m in range(2):
            loads[2 * m].wait()
            loads[2 * m + 1].wait()
            hidden = hidden + matmul(att_ref[m], w_ref[m])
        hidden_ref[...] = hidden
        copy = pltpu.make_async_copy(hidden_ref, hidden_far, sems.at[2])
        copy.start()
        hn_ref[...] = low(hidden * rms_scale(hidden) * gain_ref[...])
        copy.wait()

    rows, width = x.shape
    return on_chip(
        body,
        (shape32(rows, width), shape16(rows, width)),
        (place,),
        (x, pltpu.with_memory_space_constraint(att_own, pltpu.HBM), att_came, w, gain),
        "finish",
        cost=3.0,
        limit=8,
        away=(0,),
        far=(0, 1, 2, 3),
        scratch=(
            pltpu.VMEM((rows, width), jnp.float32),
            pltpu.VMEM((2, width // 2, width), jnp.bfloat16),
            pltpu.VMEM((2, rows, width // 2), jnp.bfloat16),
            pltpu.VMEM((rows, width), jnp.bfloat16),
            pltpu.SemaphoreType.DMA((6,)),
        ),
    )


def reorder(order, *blocks):
    rows, cols = blocks[0].shape

    def body(order, *refs):
        arrange(order, refs[:-1], refs[-1])

    return on_chip(body, shape16(rows * len(blocks), cols), (order,), blocks, "reorder", cost=0.9)


def arrange_halves(order, blocks, away, mine):
    rows = blocks[0].shape[0]
    count = order.shape[0] // 2
    size = mine.shape[1] // count
    for half, out in enumerate((away, mine)):
        for i in range(count):
            for b, block in enumerate(blocks):
                out[b * rows : (b + 1) * rows, i * size : (i + 1) * size] = block[
                    :, columns(order[half * count + i], size)
                ]


def reorder_halves(order, *blocks):
    rows, cols = blocks[0].shape

    def body(order, *refs):
        arrange_halves(order, refs[:-2], *refs[-2:])

    part = shape16(rows * len(blocks), cols // 2)
    return on_chip(body, (part, part), (order,), blocks, "reorder_halves", cost=0.9)


def feed_rows(hn, grads, gate_w, up_w, mine, other, base):
    rows = hn.shape[0]
    units = gate_w[0].shape[0]
    here = slice(base, base + rows)
    total_hn = None
    for s in range(2):
        gate = against(hn[...], gate_w[s][...])
        up = against(hn[...], up_w[s][...])
        grad = high(grads[s][...])
        sig = 1.0 / (1.0 + jnp.exp(-gate))
        silu = gate * sig
        results = (silu * up, grad * up * sig * (1.0 + gate * (1.0 - sig)), grad * silu)
        for i, result in enumerate(results):
            if s == 0:
                mine[i][here, :] = low(result)
            else:
                other[2 * i * rows + base : 2 * i * rows + base + rows, :units] = low(result)
    for s in range(2):
        for i, w in ((1, gate_w[s]), (2, up_w[s])):
            if s == 0:
                share = matmul(mine[i][here, :], w[...])
            else:
                share = matmul(other[2 * i * rows + base : 2 * i * rows + base + rows, :units], w[...])
            total_hn = share if total_hn is None else total_hn + share
    return total_hn


def feed_own_body(order, hn, dy_own, dy_oth, wg0, wg1, wu0, wu1, wd0, wd1, *refs):
    rows = hn.shape[0]
    outs, grads = refs[:9], refs[9:]
    mine, other, dhn, down = outs[:3], outs[3], outs[4], outs[5]
    for grad, w in zip(grads, (wd0, wd1)):
        grad[...] = low(against(dy_own[...], w[...]))
    dhn[...] = feed_rows(hn, grads, (wg0, wg1), (wu0, wu1), mine, other, 0)
    down[...] = matmul(mine[0][:rows, :], wd0[...]) + matmul(other[:rows, : wd1.shape[0]], wd1[...])
    for grad, w in zip(outs[6:8], (wd0, wd1)):
        grad[...] = low(against(dy_oth[...], w[...]))
    arrange(order, (dy_own, dy_oth), outs[8])


def feed_oth_body(order, hn_own, hn, g0, g1, wg0, wg1, wu0, wu1, *refs):
    outs = refs[4:]
    outs[4][...] = low(
        feed_rows(hn, (g0, g1), (wg0, wg1), (wu0, wu1), outs[:3], outs[3], hn.shape[0])
    )
    arrange(order, (hn_own, hn), outs[5])


def feed_own(order, hn, dy_own, dy_oth, gate_w, up_w, down_w):
    rows, width = hn.shape
    units = gate_w[0].shape[0]
    part = shape16(2 * rows, units)
    other = shape16(6 * rows, -(-units // 128) * 128)
    return on_chip(
        feed_own_body,
        (part,) * 3
        + (other,)
        + (shape32(rows, width),) * 2
        + (shape16(rows, units),) * 2
        + (shape16(2 * rows, width),),
        (order,),
        (hn, dy_own, dy_oth, *gate_w, *up_w, *down_w),
        "feed_own",
        limit=15,
        cost=11.0,
        scratch=(pltpu.VMEM((rows, units), jnp.bfloat16),) * 2,
    )


def feed_oth(order, hn_own, hn, grads, gate_w, up_w, parts):
    rows, width = hn.shape
    return on_chip(
        feed_oth_body,
        tuple(shape16(*part.shape) for part in parts)
        + (shape16(rows, width), shape16(2 * rows, width)),
        (order,),
        (hn_own, hn, *grads, *gate_w, *up_w, *parts),
        "feed_oth",
        aliases={9 + i: i for i in range(4)},
        limit=14,
        cost=7.0,
    )


def ff_grad(left, left_core, index, right, right_core, pieces):
    rows, units = left.shape
    size = right.shape[1] // pieces
    half = right.shape[1] // 2

    def body(left, left_core, right, right_core, *outs):
        for i in range(2):
            part = slice(i * half, (i + 1) * half)
            sums = low(
                inner_rows(left[...], right[:, part])
                + inner_rows(left_core[index * rows : (index + 1) * rows, :units], right_core[:, part])
            )
            for j in range(pieces // 2):
                outs[i * pieces // 2 + j][...] = sums[:, j * size : (j + 1) * size]

    part = shape16(units, size)
    return on_chip(
        body, (part,) * pieces, (), (left, left_core, right, right_core), "ff_grad", cost=2.7
    )


def join(first, second):
    def body(first, second, out):
        out[...] = low(high(first[...]) + high(second[...]))

    return on_chip(body, shape16(*first.shape), (), (first, second), "join", cost=0.3)


def fold_three(first, second, third):
    mid = first.shape[1] // 2

    def body(first, second, third, away, rest):
        for out, part in ((away, slice(0, mid)), (rest, slice(mid, 2 * mid))):
            out[...] = low(high(first[:, part]) + high(second[:, part]) + high(third[:, part]))

    part = shape16(first.shape[0], mid)
    return on_chip(body, (part, part), (), (first, second, third), "fold_three", cost=0.3)


def fold(kept, came):
    mid = kept.shape[1] // 2

    def body(kept, came, away, rest):
        away[...] = low(high(kept[:, :mid]) + high(came[:, :mid]))
        rest[...] = low(high(kept[:, mid:]) + high(came[:, mid:]))

    part = shape16(kept.shape[0], mid)
    return on_chip(body, (part, part), (), (kept, came), "fold", cost=0.3)


def fold_rows(kept, came):
    mid = kept.shape[0] // 2

    def body(kept, came, away, rest):
        away[...] = low(high(kept[:mid, :]) + high(came[:mid, :]))
        rest[...] = low(high(kept[mid:, :]) + high(came[mid:, :]))

    part = shape16(mid, kept.shape[1])
    return on_chip(body, (part, part), (), (kept, came), "fold_rows", cost=0.3)


def hidden_grad_body(order, place, dhn_own, dhn_came, hidden_far, dy_ref, gain_ref, w_far,
    grad_ref, send_ref, own_ref, away_ref, mine_ref, gains_ref, proj, hidden_ref, w_ref, sems,
):
    cols = send_ref.shape[1]
    loads = [pltpu.make_async_copy(hidden_far, hidden_ref, sems.at[2])]
    for m in (1, 0):
        there = columns(place[0] ^ m, cols)
        loads.append(pltpu.make_async_copy(w_far.at[there, :], w_ref.at[m], sems.at[m]))
    for load in loads:
        load.start()
    loads[0].wait()
    hidden = hidden_ref[...]
    scale = rms_scale(hidden)
    dhn = dhn_own[...] + high(dhn_came[...])
    gains_ref[...] = jnp.sum(dhn * hidden * scale, axis=0, keepdims=True)
    weighted = dhn * gain_ref[...]
    mean = jnp.mean(weighted * hidden, axis=-1, keepdims=True)
    grad = high(dy_ref[...]) + scale * weighted - hidden * (scale * scale * scale * mean)
    grad_ref[...] = grad
    proj[...] = low(grad)
    loads[1].wait()
    send_ref[...] = low(against(proj[...], w_ref[1]))
    loads[2].wait()
    own_ref[...] = low(against(proj[...], w_ref[0]))
    arrange_halves(order, (proj,), away_ref, mine_ref)


def hidden_grad(order, place, dhn_own, dhn_came, hidden, dy, gain, w):
    rows, width = hidden.shape
    part = shape16(rows, width // 2)
    return on_chip(
        hidden_grad_body,
        (shape32(rows, width), part, part, part, part, shape32(1, width)),
        (order, place),
        (dhn_own, dhn_came, hidden, dy, gain, w),
        "hidden_grad",
        cost=2.2,
        limit=9,
        far=(2, 5),
        scratch=(
            pltpu.VMEM((rows, width), jnp.bfloat16),
            pltpu.VMEM((rows, width), jnp.float32),
            pltpu.VMEM((2, width // 2, width), jnp.bfloat16),
            pltpu.SemaphoreType.DMA((3,)),
        ),
    )


def bucket_grad(left, left_core, rights, rights_core, place=0, total_cols=None, before=()):
    mid = left.shape[1] // 2
    cols = rights[0].shape[1]
    count = len(rights)

    def body(left, left_core, *refs):
        for i in range(count):
            part = slice(place + i * cols, place + (i + 1) * cols)
            for half, out in enumerate(refs[-2:]):
                cut = slice(half * mid, (half + 1) * mid)
                out[:, part] = low(
                    inner_rows(left[:, cut], refs[i][...])
                    + inner_rows(left_core[:, cut], refs[count + i][...])
                )

    full = shape16(mid, total_cols or cols * count)
    return on_chip(
        body,
        (full, full),
        (),
        (left, left_core, *rights, *rights_core, *before),
        "bucket_grad",
        aliases={2 + 2 * count + i: i for i in range(len(before))},
        cost=1.5,
    )


def bucket_near(row, kept, came):
    quarter, cols = kept.shape
    size = quarter // 4

    def body(row, kept, came, away, rest):
        near = row[0] & 1
        for i in range(2):
            here = pl.ds(pl.multiple_of(i * 2 * size + near * size, size), size)
            there = pl.ds(pl.multiple_of(i * 2 * size + (1 - near) * size, size), size)
            part = slice(i * size, (i + 1) * size)
            away[part, :] = low(high(kept[there, :]) + high(came[there, :]))
            rest[part, :] = low(high(kept[here, :]) + high(came[here, :]))

    half = shape16(2 * size, cols)
    return on_chip(body, (half, half), (row,), (kept, came), "bucket_near", cost=0.3)


def shares_body(d_a, d_b, fa, fb, w_ref, x_own, x_oth, gain_two, send_ref, own_ref, gains_ref):
    rows, width = x_own.shape
    cut = d_a.shape[1]
    sums = None
    for m, x_ref in ((1, x_oth), (0, x_own)):
        part = slice(m * rows, (m + 1) * rows)
        share = against(d_a[part, :], w_ref[:, :cut]) + against(d_b[part, :], w_ref[:, cut:])
        if m:
            send_ref[:, :width] = low(share)
        else:
            own_ref[...] = share
        x = high(x_ref[...])
        here = jnp.sum(share * (x * rms_scale(x)), axis=0, keepdims=True)
        sums = here if sums is None else sums + here
    send_ref[:, width : width + fa.shape[1]] = fa[...]
    send_ref[:, width + fa.shape[1] :] = fb[...]
    gains_ref[0:1, :] = sums
    gains_ref[1:2, :] = gain_two[...]


def shares(d_a, d_b, fa, fb, w, x_own, x_oth, gain_two):
    rows, width = x_own.shape
    return on_chip(
        shares_body,
        (shape16(rows, width + 2 * fa.shape[1]), shape32(rows, width), shape32(2, width)),
        (),
        (d_a, d_b, fa, fb, w, x_own, x_oth, gain_two),
        "shares",
        cost=2.3,
    )


def input_grad_body(place, share_ref, came_ref, grad_ref, x_ref, gain_ref, fa, fb, out_ref, first_ref):
    width = x_ref.shape[1]
    x = high(x_ref[...])
    scale = rms_scale(x)
    weighted = (share_ref[...] + high(came_ref[:, :width])) * gain_ref[...]
    mean = jnp.mean(weighted * x, axis=-1, keepdims=True)
    out_ref[...] = grad_ref[...] + scale * weighted - x * (scale * scale * scale * mean)
    cols = fa.shape[1]
    own = 2 * place[0]
    oth = 2 - own
    first_ref[:, columns(own, cols)] = fa[...]
    first_ref[:, columns(own + 1, cols)] = fb[...]
    first_ref[:, columns(oth, cols)] = came_ref[:, width : width + cols]
    first_ref[:, columns(oth + 1, cols)] = came_ref[:, width + cols :]


def input_grad(place, share, came, grad_hidden, x, gain, fa, fb):
    return on_chip(
        input_grad_body,
        (shape32(*x.shape), shape16(*x.shape)),
        (place,),
        (share, came, grad_hidden, x, gain, fa, fb),
        "input_grad",
        cost=2.0,
        limit=6,
    )


def after(first, *values):
    return lax.optimization_barrier((first, *values))[1:]


def two_groups(
    inputs,
    first_values,
    lengths,
    gain_attn,
    w_qkv,
    w_out,
    gain_mlp,
    w_gate,
    w_up,
    w_down,
    cotangent,
):
    SITES.clear()
    rows = inputs.shape[1]
    width = inputs.shape[2]
    span = 2 * rows
    out_cols = HEADS // 2 * HD
    packed_cols = 3 * out_cols
    mid = width // 2
    h = lax.axis_index("head")
    f = lax.axis_index("ffn")
    r = lax.axis_index("row")
    row_size = lax.axis_size("row")
    place = jnp.stack([h, lengths[0]]).astype(jnp.int32)
    row = r.reshape(1).astype(jnp.int32)
    tie = lax.optimization_barrier
    gain_attn = gain_attn.reshape(1, width)
    gain_mlp = gain_mlp.reshape(1, width)

    x_own = inputs[0]
    x_oth = swap(x_own, "head", 1)
    early_own = lax.dynamic_slice_in_dim(first_values[0], h * out_cols, out_cols, 1)
    early_oth = swap(
        lax.dynamic_slice_in_dim(first_values[0], (1 - h) * out_cols, out_cols, 1), "head", 1
    )
    dy_own = cotangent[0]
    down_core = swap(w_down, "ffn", 1)
    gate_core = swap(w_gate.T, "ffn", 1)
    up_core = swap(w_up.T, "ffn", 1)
    qkv_w = lax.dynamic_slice_in_dim(w_qkv, h * packed_cols, packed_cols, 1)
    half = HD // 2
    inverse = jnp.exp(-jnp.log(10000.0) * jnp.arange(half, dtype=jnp.float32) * 2.0 / HD)
    sign = jnp.where(jnp.arange(2 * HD) % HD < half, -1.0, 1.0)
    cosine, sine = tables(span, jnp.tile(inverse, 4)[None, :], sign[None, :])

    ff_order = jnp.stack([(h ^ a) * row_size + (r ^ b) for a in (1, 0) for b in (3, 1, 2, 0)])
    down_order = jnp.stack([(h ^ a) * row_size + (r ^ b) for b in (3, 1, 2, 0) for a in (1, 0)])
    att_order = jnp.stack(
        [((f ^ a) * row_size + (r & 2 ^ b)) // 2 for a in (3, 1, 2, 0) for b in (2, 0)]
    )

    before = project(att_order, place, x_own, gain_attn, qkv_w, cosine, sine)
    x_oth, before, early_own, down_core, gate_core, up_core = tie(
        (x_oth, before, early_own, down_core, gate_core, up_core)
    )
    xn_away, xn_mine, query, keys, *near = project(
        att_order, place, x_oth, gain_attn, qkv_w, cosine, sine, before
    )
    att_own, att_oth, mixed, log_sums = attend_forward(place, *near, early_own, early_oth)
    att_came = swap(att_oth, "head", 1)
    (dy_send,) = after(near[2], dy_own)
    dy_oth = swap(dy_send, "ffn", 2)
    att_came, dy_oth = tie((att_came, dy_oth))
    down_w = (w_down, down_core)
    gate_w = (w_gate.T, gate_core)
    up_w = (w_up.T, up_core)
    hidden, hn_own = finish(place, x_own, att_own, att_came, w_out, gain_mlp)
    hn_oth = swap(hn_own, "ffn", 2)
    dy_send, dy_oth = after(hn_own, dy_send, dy_oth)
    dyc_own = swap(dy_send, "ffn", 1)
    dyc_oth = swap(dy_oth, "ffn", 1)
    hnc_own = swap(hn_own, "ffn", 1)

    *parts, dhn_own, down_own, dact0, dact1, dy_all = feed_own(
        down_order, hn_own, dy_own, dy_oth, gate_w, up_w, down_w
    )
    hn_oth, parts, dhn_own, down_own, dact0, dact1, dy_all, hnc_own, dyc_own, dyc_oth = tie(
        (hn_oth, parts, dhn_own, down_own, dact0, dact1, dy_all, hnc_own, dyc_own, dyc_oth)
    )
    hnc_oth = swap(hn_oth, "ffn", 1)
    act, gate, up, others, dhn_send, hn_all = feed_oth(
        ff_order, hn_own, hn_oth, (dact0, dact1), gate_w, up_w, parts
    )
    dhn_came = swap(dhn_send, "ffn", 2)
    others_core = swap(others, "ffn", 1)
    own_send, came_send = after(dhn_send, att_own, att_came)
    att_core = swap(own_send, "ffn", 1)
    came_core = swap(came_send, "ffn", 1)
    hnc_oth, dyc_own, dyc_oth = after(dhn_send, hnc_oth, dyc_own, dyc_oth)
    dyc_all = reorder(down_order, dyc_own, dyc_oth)
    hnc_all = reorder(ff_order, hnc_own, hnc_oth)

    gate_a, gate_b, gate_near, gate_kept = ff_grad(gate, others_core, 1, hn_all, hnc_all, 4)
    gate_xa = swap(gate_a, "head", 1)
    down_send, down_kept = ff_grad(act, others_core, 0, dy_all, dyc_all, 2)
    down_near = swap(down_send, "row", 1)
    up_a, up_b, up_near, up_kept = ff_grad(up, others_core, 2, hn_all, hnc_all, 4)
    dhn_came, gate_b, gate_kept, gate_near, down_kept, up_a, up_b, up_near, up_kept = tie(
        (dhn_came, gate_b, gate_kept, gate_near, down_kept, up_a, up_b, up_near, up_kept)
    )

    grad_hidden, go_send, go_own, proj_away, proj_mine, gain_two = hidden_grad(
        att_order, place, dhn_own, dhn_came, hidden, dy_own, gain_mlp, w_out
    )
    (gate_near,) = after(go_send, gate_near)
    gate_send = join(gate_near, gate_xa)
    go_send, go_own, proj_away, gate_send = tie((go_send, go_own, proj_away, gate_send))
    go_oth = swap(go_send, "head", 1)
    proj_core = swap(proj_away, "ffn", 1)
    gate_came = swap(gate_send, "row", 1)
    (gate_b,) = after(go_send, gate_b)
    gate_xb = swap(gate_b, "head", 1)
    out_send, out_kept = bucket_grad(
        proj_mine, proj_core, (att_came, att_own), (came_core, att_core)
    )
    out_y = swap(out_send, "ffn", 2)
    up_xa = swap(after(out_send, up_a)[0], "head", 1)
    go_oth, out_kept = tie((go_oth, out_kept))

    def backward(pairs, lse):
        return attend_backward(
            place, query, keys, mixed, lse, go_own, go_oth, att_own, att_oth, cosine, sine, pairs
        )

    pairs = HEADS // 4
    d_a, fa_own, fa_oth = backward((0, pairs // 2), log_sums)
    out_kept, down_kept, gate_kept = after(d_a, out_kept, down_kept, gate_kept)
    out_send, out_kept = fold(out_kept, out_y)
    out_x = swap(out_send, "head", 1)
    down_send, down_kept = fold(down_kept, down_near)
    down_mid = swap(down_send, "row", 2)
    gate_kept = join(gate_kept, gate_xb)
    d_a, out_kept, down_kept, gate_kept, log_sums = tie(
        (d_a, out_kept, down_kept, gate_kept, log_sums)
    )
    core_a = swap(d_a, "ffn", 1)
    xn_core = swap(after(out_kept, xn_away)[0], "ffn", 1)
    d_b, fb_own, fb_oth = backward((pairs // 2, pairs), log_sums)
    gate_kept, up_near = after(d_b, gate_kept, up_near)
    gate_send, gate_kept = fold(gate_kept, gate_came)
    up_send = join(up_near, up_xa)
    d_b, gate_kept, up_send = tie((d_b, gate_kept, up_send))
    core_b = swap(d_b, "ffn", 1)
    up_xb = swap(after(gate_kept, up_b)[0], "head", 1)
    up_came = swap(up_send, "row", 1)
    (d_a,) = after(gate_kept, d_a)
    before = bucket_grad(xn_mine, xn_core, (d_a,), (core_a,), 0, packed_cols)
    core_b, *before = tie((core_b, *before))
    y_send, kept = bucket_grad(
        xn_mine, xn_core, (d_b,), (core_b,), packed_cols // 2, packed_cols, before
    )
    y_came = swap(y_send, "ffn", 2)
    d_a, d_b = after(y_send, d_a, d_b)
    back_send, share_own, gains = shares(
        d_a, d_b, fa_oth, fb_oth, qkv_w, x_own, x_oth, gain_two
    )
    gate_send, out_kept, act, others, up_kept, down_kept = after(
        back_send, gate_send, out_kept, act, others, up_kept, down_kept
    )
    out_send, out_kept = bucket_near(row, out_kept, out_x)
    out_near = swap(out_send, "row", 1)
    gains = gains + swap(gains, "head", 1)
    gains, back_send = tie((gains, back_send))
    back_came = swap(back_send, "head", 1)
    up_kept, down_kept = after(gains, up_kept, down_kept)
    up_send, up_kept = fold_three(up_kept, up_xb, up_came)
    gate_far = swap(gate_send, "row", 2)
    units = w_down.shape[0]
    far_send = low(matmul(act[rows:], down_w[0]) + matmul(others[rows:span, :units], down_w[1]))
    gains, down_kept, gate_kept, out_kept = after(far_send, gains, down_kept, gate_kept, out_kept)
    gains = gains + swap(gains, "ffn", 1)
    down_send, down_kept = fold(down_kept, down_mid)
    out_send, out_kept = fold_rows(out_kept, out_near)
    out_far = swap(out_send, "row", 2)
    sum_gate = high(gate_kept) + high(gate_far)
    kept, up_send, down_send, sum_gate, gains, out_send = tie(
        (kept, up_send, down_send, sum_gate, gains, out_send)
    )

    near_send, kept = bucket_near(row, kept, y_came)
    near_came = swap(near_send, "row", 1)
    gains, far_send, out_kept, up_send, down_send = after(
        near_send, gains, far_send, out_kept, up_send, down_send
    )
    gains = gains + swap(gains, "ffn", 2)
    (far_send,) = after(gains, far_send)
    far_came = swap(far_send, "ffn", 2)
    up_far = swap(up_send, "row", 2)
    qkv_send, kept = fold_rows(kept, near_came)
    qkv_far = swap(qkv_send, "row", 2)
    share_own, down_kept, up_kept, out_kept, residual, gains, down_send = after(
        qkv_send,
        share_own,
        down_kept,
        up_kept,
        out_kept,
        hidden + down_own,
        gains,
        down_send,
    )
    down_x = swap(down_send, "head", 1)
    gains = gains + swap(gains, "row", 1)
    gains_far = swap(gains, "row", 2)
    (share_own,) = after(gains, share_own)
    grad_in, grad_first = input_grad(
        place, share_own, back_came, grad_hidden, x_own, gain_attn, fa_own, fb_own
    )
    sum_up = high(up_kept) + high(up_far)
    out_sum = high(out_kept) + high(out_far)
    output = low(residual + high(far_came))[None]
    (down_kept,) = after(output, down_kept)
    sum_down = high(down_kept) + high(down_x)
    gains = gains + gains_far
    kept, grad_in, sum_up, sum_down, out_sum, output, gains = tie(
        (kept, grad_in, sum_up, sum_down, out_sum, output, gains)
    )
    sum_qkv = high(kept) + high(qkv_far)
    return (
        output,
        grad_in[None],
        grad_first[None],
        gains[0],
        sum_qkv,
        out_sum.T,
        gains[1],
        sum_gate.T,
        sum_up.T,
        sum_down,
    )


def solution(mesh):
    in_specs = (
        P(("ffn", "row"), "head", None),
        P(("ffn", "row"), "head", None),
        P(("ffn", "row")),
        P(),
        P(),
        P(),
        P(),
        P(None, "ffn"),
        P(None, "ffn"),
        P("ffn", None),
        P(("ffn", "row"), "head", None),
    )
    out_specs = (
        P(("ffn", "row"), "head", None),
        P(("ffn", "row"), "head", None),
        P(("ffn", "row"), "head", None),
        P(),
        P(("ffn", "row"), "head"),
        P("head", ("ffn", "row")),
        P(),
        P(("head", "row"), "ffn"),
        P(("head", "row"), "ffn"),
        P("ffn", ("head", "row")),
    )
    body = two_groups if mesh.shape["head"] == 2 and mesh.shape["ffn"] == 4 else any_groups
    return jax.shard_map(
        body, mesh=mesh, in_specs=in_specs, out_specs=out_specs, check_vma=False
    )
```

```python
import functools

import jax
import jax.numpy as jnp
from jax import lax
from jax.experimental import pallas as pl
from jax.experimental.pallas import tpu as pltpu
from jax.sharding import PartitionSpec as P

HEADS = 16
HD = 64
MIN_LEN = 512
STEP = 256


eps = 1e-06


def rms_scale(values):
    return lax.rsqrt(jnp.mean(values * values, axis=-1, keepdims=True) + eps)


def matmul(left, right):
    return jnp.dot(left, right, preferred_element_type=jnp.float32)


def inner_rows(left, right):
    return lax.dot_general(
        left, right, (((0,), (0,)), ((), ())), preferred_element_type=jnp.float32
    )


def against(left, right):
    return lax.dot_general(
        left, right, (((1,), (1,)), ((), ())), preferred_element_type=jnp.float32
    )


def swap(values, axis, mask):
    size = lax.axis_size(axis)
    return lax.ppermute(values, axis, [(i, i ^ mask) for i in range(size)])


def bits_of(axis):
    size = lax.axis_size(axis)
    return [1 << b for b in range(size.bit_length() - 2, -1, -1)]


def halve(values, dim, axis, mask):
    bit = (lax.axis_index(axis) // mask) % 2
    away = lax.dynamic_index_in_dim(values, 1 - bit, dim, keepdims=False)
    kept = lax.dynamic_index_in_dim(values, bit, dim, keepdims=False)
    came = swap(away.astype(jnp.bfloat16), axis, mask)
    return kept.astype(jnp.float32) + came.astype(jnp.float32)


def total(values, axes):
    for axis in axes:
        for mask in reversed(bits_of(axis)):
            values = values + swap(values, axis, mask)
    return values


def rotary(positions, head_size):
    half_size = head_size // 2
    inverse = jnp.exp(
        -jnp.log(10000.0) * jnp.arange(half_size, dtype=jnp.float32) * 2.0 / head_size
    )
    angles = positions.astype(jnp.float32)[:, None] * inverse[None, :]
    return (jnp.cos(angles), jnp.sin(angles))


def rotate(vectors, cosine, sine, sign):
    half_size = vectors.shape[-1] // 2
    first_half = vectors[..., :half_size]
    second_half = vectors[..., half_size:]
    cos_rows = cosine[:, None, :]
    sin_rows = sign * sine[:, None, :]
    return jnp.concatenate(
        [
            first_half * cos_rows - second_half * sin_rows,
            second_half * cos_rows + first_half * sin_rows,
        ],
        axis=-1,
    )


def masked_scores(q_rows, keys, q_pos, k_pos, valid):
    raw = jnp.einsum("qhe,khe->hqk", q_rows, keys, preferred_element_type=jnp.float32)
    allowed = (k_pos[None, :] <= q_pos[:, None]) & (k_pos[None, :] < valid)
    return jnp.where(allowed[None], 0.125 * raw, -1e30)


def scan_forward(query, keys, mixed, positions, valid, block_rows):
    count = query.shape[0] // block_rows

    def step(carry, index):
        start = index * block_rows
        q_rows = lax.dynamic_slice_in_dim(query, start, block_rows, 0)
        q_pos = lax.dynamic_slice_in_dim(positions, start, block_rows, 0)
        scores = masked_scores(q_rows, keys, q_pos, positions, valid)
        top = jnp.max(scores, axis=-1, keepdims=True)
        expo = jnp.exp(scores - top)
        total_w = jnp.sum(expo, axis=-1, keepdims=True)
        weights = expo / total_w
        result = jnp.einsum(
            "hqk,khe->qhe", weights.astype(jnp.bfloat16), mixed, preferred_element_type=jnp.float32
        )
        return (carry, (result.astype(jnp.bfloat16), top + jnp.log(total_w)))

    _, (outs, log_sums) = lax.scan(step, 0, jnp.arange(count, dtype=jnp.int32))
    return (outs.reshape(query.shape), log_sums)


def scan_backward(query, keys, mixed, positions, valid, log_sums, grad_out, block_rows):
    count = query.shape[0] // block_rows
    zeros = jnp.zeros(keys.shape, jnp.float32)

    def step(carry, index):
        key_sum, value_sum = carry
        start = index * block_rows
        q_rows = lax.dynamic_slice_in_dim(query, start, block_rows, 0)
        q_pos = lax.dynamic_slice_in_dim(positions, start, block_rows, 0)
        g_rows = lax.dynamic_slice_in_dim(grad_out, start, block_rows, 0)
        scores = masked_scores(q_rows, keys, q_pos, positions, valid)
        weights = jnp.exp(scores - log_sums[index])
        grad_w = jnp.einsum("qhe,khe->hqk", g_rows, mixed, preferred_element_type=jnp.float32)
        delta = jnp.sum(weights * grad_w, axis=-1, keepdims=True)
        grad_s = (weights * (grad_w - delta)).astype(jnp.bfloat16)
        grad_q = 0.125 * jnp.einsum(
            "hqk,khe->qhe", grad_s, keys, preferred_element_type=jnp.float32
        )
        key_sum = key_sum + 0.125 * jnp.einsum(
            "hqk,qhe->khe", grad_s, q_rows, preferred_element_type=jnp.float32
        )
        value_sum = value_sum + jnp.einsum(
            "hqk,qhe->khe", weights.astype(jnp.bfloat16), g_rows, preferred_element_type=jnp.float32
        )
        return ((key_sum, value_sum), grad_q)

    (grad_keys, grad_mixed), grad_query = lax.scan(
        step, (zeros, zeros), jnp.arange(count, dtype=jnp.int32)
    )
    return (grad_query.reshape(query.shape), grad_keys, grad_mixed)


def any_groups(
    inputs,
    first_values,
    lengths,
    gain_attn,
    w_qkv,
    w_out,
    gain_mlp,
    w_gate,
    w_up,
    w_down,
    cotangent,
):
    rows = inputs.shape[1]
    width = inputs.shape[2]
    groups = lax.axis_size("head")
    shards = lax.axis_size("ffn")
    heads_here = HEADS // groups
    span_rows = rows * groups
    block_rows = span_rows // max(1, span_rows // 512)
    head_pos = lax.axis_index("head")
    valid_len = lengths[0]
    packed_cols = heads_here * 3 * HD
    out_cols = heads_here * HD
    hidden_here = w_gate.shape[1]

    owners = [head_pos ^ m for m in range(groups)]
    x_all = [inputs[0]] + [swap(inputs[0], "head", m) for m in range(1, groups)]
    early = []
    for m in range(groups):
        piece = lax.dynamic_slice_in_dim(first_values[0], owners[m] * out_cols, out_cols, 1)
        early.append(swap(piece, "head", m) if m else piece)
    far = range(2, shards, 2)
    grad_rows = jnp.concatenate([cotangent[0]] + [swap(cotangent[0], "ffn", m) for m in far], 0)
    gate_w = jnp.concatenate([w_gate, swap(w_gate, "ffn", 1)], 1)
    up_w = jnp.concatenate([w_up, swap(w_up, "ffn", 1)], 1)
    down_w = jnp.concatenate([w_down, swap(w_down, "ffn", 1)], 0)
    w_heads = lax.dynamic_slice_in_dim(w_qkv, head_pos * packed_cols, packed_cols, 1)
    out_w = jnp.concatenate(
        [lax.dynamic_slice_in_dim(w_out, o * out_cols, out_cols, 0) for o in owners], 0
    )

    positions = jnp.concatenate([o * rows + jnp.arange(rows, dtype=jnp.int32) for o in owners])
    cosine, sine = rotary(positions, HD)
    normed, scaled, queries, key_list, mixes = [], [], [], [], []
    rows_in = inputs[0].astype(jnp.float32)
    scale_one = rms_scale(rows_in)
    for m in range(groups):
        block = x_all[m].astype(jnp.float32)
        scale = rms_scale(block)
        scaled.append(block * scale)
        normed.append((block * scale * gain_attn).astype(jnp.bfloat16))
        packed = matmul(normed[m], w_heads).astype(jnp.bfloat16)
        packed = packed.reshape(rows, heads_here, 3, HD).astype(jnp.float32)
        part = slice(m * rows, (m + 1) * rows)
        queries.append(rotate(packed[:, :, 0], cosine[part], sine[part], 1.0))
        key_list.append(rotate(packed[:, :, 1], cosine[part], sine[part], 1.0))
        value = early[m].reshape(rows, heads_here, HD).astype(jnp.float32)
        mixes.append(0.5 * (packed[:, :, 2] + value))
    query = jnp.concatenate(queries, 0).astype(jnp.bfloat16)
    keys = jnp.concatenate(key_list, 0).astype(jnp.bfloat16)
    mixed = jnp.concatenate(mixes, 0).astype(jnp.bfloat16)
    attended, log_sums = scan_forward(query, keys, mixed, positions, valid_len, block_rows)
    attended = attended.reshape(groups, rows, out_cols)
    att_own = jnp.concatenate(
        [attended[0]] + [swap(attended[m], "head", m) for m in range(1, groups)], 1
    )
    hidden = rows_in + matmul(att_own, out_w)
    scale_two = rms_scale(hidden)
    normed_two = (hidden * scale_two * gain_mlp).astype(jnp.bfloat16)

    mlp_rows = [normed_two] + [swap(normed_two, "ffn", m) for m in far]
    grad_list = [grad_rows[i * rows : (i + 1) * rows] for i in range(len(mlp_rows))]
    actives, grad_gates, grad_ups, downs, grad_normed_list = [], [], [], [], []
    for i, block in enumerate(mlp_rows):
        gate_rows = matmul(block, gate_w)
        up_rows = matmul(block, up_w)
        sigmoid_gate = jax.nn.sigmoid(gate_rows)
        silu_gate = gate_rows * sigmoid_gate
        grad_active = against(grad_list[i], down_w)
        actives.append((silu_gate * up_rows).astype(jnp.bfloat16))
        grad_gates.append(
            (
                grad_active * up_rows * sigmoid_gate * (1.0 + gate_rows * (1.0 - sigmoid_gate))
            ).astype(jnp.bfloat16)
        )
        grad_ups.append((grad_active * silu_gate).astype(jnp.bfloat16))
        grad_normed_list.append(against(grad_gates[i], gate_w) + against(grad_ups[i], up_w))
        downs.append(matmul(actives[i], down_w))
    grad_normed_two = grad_normed_list[0]
    for i, m in enumerate(far):
        came = swap(grad_normed_list[i + 1].astype(jnp.bfloat16), "ffn", m)
        grad_normed_two = grad_normed_two + came.astype(jnp.float32)
    down_rows = downs[0]
    for i, m in enumerate(far):
        down_rows = down_rows + swap(downs[i + 1].astype(jnp.bfloat16), "ffn", m).astype(jnp.float32)
    output = (hidden + down_rows).astype(jnp.bfloat16)[None]

    all_rows = jnp.concatenate(mlp_rows, 0)
    ff_sums = []
    for left, right in (
        (grad_rows, jnp.concatenate(actives, 0)),
        (all_rows, jnp.concatenate(grad_gates, 0)),
        (all_rows, jnp.concatenate(grad_ups, 0)),
    ):
        away = inner_rows(left, right[:, hidden_here:]).astype(jnp.bfloat16)
        part = inner_rows(left, right[:, :hidden_here])
        part = (part + swap(away, "ffn", 1).astype(jnp.float32)).astype(jnp.bfloat16)
        steps = [("head", b) for b in bits_of("head")] + [("row", b) for b in bits_of("row")]
        part = part.reshape([2] * len(steps) + [-1, hidden_here])
        order = [s for s in steps if s[0] == "head"] + [s for s in reversed(steps) if s[0] == "row"]
        left_steps = list(steps)
        for s in order:
            part = halve(part, left_steps.index(s), *s)
            left_steps.remove(s)
            if left_steps:
                part = part.astype(jnp.bfloat16)
        ff_sums.append(part)
    sum_down, sum_gate, sum_up = ff_sums

    grad_y = cotangent[0].astype(jnp.float32)
    grad_gain_two = jnp.sum(grad_normed_two * hidden * scale_two, axis=0)
    weighted_two = grad_normed_two * gain_mlp
    cube_two = scale_two * scale_two * scale_two
    grad_hidden = (
        grad_y
        + scale_two * weighted_two
        - hidden * cube_two * jnp.mean(weighted_two * hidden, axis=-1, keepdims=True)
    )
    grad_proj = grad_hidden.astype(jnp.bfloat16)
    grad_att = against(grad_proj, out_w).astype(jnp.bfloat16)
    grad_att = jnp.concatenate(
        [
            swap(grad_att[:, m * out_cols : (m + 1) * out_cols], "head", m)
            if m
            else grad_att[:, :out_cols]
            for m in range(groups)
        ],
        0,
    ).reshape(span_rows, heads_here, HD)

    def over_buckets(part):
        steps = [("ffn", b) for b in bits_of("ffn")] + [("row", b) for b in bits_of("row")]
        part = part.astype(jnp.bfloat16).reshape([2] * len(steps) + [-1, part.shape[1]])
        order = [s for s in reversed(steps) if s[0] == "ffn"] + [
            s for s in reversed(steps) if s[0] == "row"
        ]
        left_steps = list(steps)
        for s in order:
            part = halve(part, left_steps.index(s), *s)
            left_steps.remove(s)
            if left_steps:
                part = part.astype(jnp.bfloat16)
        return part

    part = over_buckets(inner_rows(grad_proj, att_own))
    sum_out = part[:, :out_cols]
    for m in range(1, groups):
        came = swap(part[:, m * out_cols : (m + 1) * out_cols].astype(jnp.bfloat16), "head", m)
        sum_out = sum_out + came.astype(jnp.float32)

    grad_query, grad_keys, grad_mixed = scan_backward(
        query, keys, mixed, positions, valid_len, log_sums, grad_att, block_rows
    )
    grad_packed = jnp.stack(
        [
            rotate(grad_query, cosine, sine, -1.0),
            rotate(grad_keys, cosine, sine, -1.0),
            0.5 * grad_mixed,
        ],
        axis=2,
    )
    grad_packed = grad_packed.astype(jnp.bfloat16).reshape(span_rows, packed_cols)
    grad_early = (0.5 * grad_mixed).astype(jnp.bfloat16).reshape(span_rows, out_cols)
    firsts = [grad_early[m * rows : (m + 1) * rows] for m in range(groups)]
    firsts = [swap(firsts[m], "head", m) if m else firsts[0] for m in range(groups)]
    grad_first = jnp.zeros((rows, width), jnp.bfloat16)
    for m in range(groups):
        grad_first = lax.dynamic_update_slice_in_dim(grad_first, firsts[m], owners[m] * out_cols, 1)
    shares = [
        against(grad_packed[m * rows : (m + 1) * rows], w_heads) for m in range(groups)
    ]
    grad_gain_one = sum(jnp.sum(shares[m] * scaled[m], axis=0) for m in range(groups))
    grad_normed = shares[0]
    for m in range(1, groups):
        grad_normed = grad_normed + swap(shares[m].astype(jnp.bfloat16), "head", m).astype(jnp.float32)
    sum_qkv = over_buckets(inner_rows(jnp.concatenate(normed, 0), grad_packed))
    weighted_one = grad_normed * gain_attn
    cube_one = scale_one * scale_one * scale_one
    grad_in = (
        grad_hidden
        + scale_one * weighted_one
        - rows_in * cube_one * jnp.mean(weighted_one * rows_in, axis=-1, keepdims=True)
    )
    gains = total(jnp.stack([grad_gain_one, grad_gain_two]), ("ffn", "head", "row"))
    return (
        output,
        grad_in[None],
        grad_first[None],
        gains[0],
        sum_qkv,
        sum_out.T,
        gains[1],
        sum_gate,
        sum_up,
        sum_down.T,
    )


SCALE = 4.5e8
COSTS = {}
SITES = {}


def site_cost(name, usual):
    count = SITES.get(name, 0)
    SITES[name] = count + 1
    return int(SCALE * COSTS.get(name + str(count), usual))


def low(values):
    return values.astype(jnp.bfloat16)


def high(values):
    return values.astype(jnp.float32)


def on_chip(body, outs, scalars, arrays, name, scratch=(), aliases=None, limit=3, cost=1.0, away=(), far=()):
    inside = pl.BlockSpec(memory_space=pltpu.VMEM)
    outside = pl.BlockSpec(memory_space=pl.ANY)
    return pl.pallas_call(
        body,
        out_shape=jax.tree.unflatten(
            jax.tree.structure(outs),
            [
                pltpu.HBM(o.shape, o.dtype) if i in away else o
                for i, o in enumerate(jax.tree.leaves(outs))
            ],
        ),
        in_specs=[pl.BlockSpec(memory_space=pltpu.SMEM)] * len(scalars)
        + [outside if i in far else inside for i in range(len(arrays))],
        out_specs=jax.tree.unflatten(
            jax.tree.structure(outs),
            [
                outside if i in away else inside
                for i in range(len(jax.tree.leaves(outs)))
            ],
        ),
        scratch_shapes=list(scratch),
        input_output_aliases=aliases or {},
        cost_estimate=pl.CostEstimate(
            flops=site_cost(name, cost), transcendentals=0, bytes_accessed=1
        ),
        compiler_params=pltpu.CompilerParams(vmem_limit_bytes=limit << 20),
        name=name,
    )(*scalars, *arrays)


def shape16(*dims):
    return jax.ShapeDtypeStruct(dims, jnp.bfloat16)


def shape32(*dims):
    return jax.ShapeDtypeStruct(dims, jnp.float32)


def spans(total):
    return [(a, min(a + STEP, total)) for a in range(0, total, STEP)]


def turn(values):
    lane = lax.broadcasted_iota(jnp.int32, values.shape, 1)
    return jnp.where(
        lane % HD < HD // 2, pltpu.roll(values, 2 * HD - HD // 2, 1), pltpu.roll(values, HD // 2, 1)
    )


def allowed_keys(a, b, valid):
    size = b - a
    down = lax.broadcasted_iota(jnp.int32, (size, size), 0)
    across = lax.broadcasted_iota(jnp.int32, (size, size), 1)
    allowed = down <= across
    if b > MIN_LEN:
        allowed = allowed & (down < valid - a)
    return allowed


def columns(index, size):
    return pl.ds(pl.multiple_of(index * size, size), size)


def forward_body(
    place, q_ref, k_ref, raw_ref, early_own, early_oth,
    own_far, oth_far, v_far, lse_out, att_own, att_oth, v_out, flipped, att, sems,
):
    rows = early_own.shape[0]
    span = 2 * rows
    wide = 2 * HD
    valid = place[1]
    bf = jnp.bfloat16
    first = lax.broadcasted_iota(jnp.int32, (1, wide), 1) < HD
    flipped[:, HD:, :] = jnp.ones((2, 16, span), bf)

    def copies(p):
        cols = columns(p, wide)
        return [
            pltpu.make_async_copy(near.at[:, cols], far.at[:, cols], sems.at[i, p])
            for i, (near, far) in enumerate(
                ((v_out, v_far), (att_oth, oth_far), (att_own, own_far))
            )
        ]

    def pair(p, _):
        cols = columns(p, wide)
        for m, early in enumerate((early_own, early_oth)):
            here = columns(place[0] ^ m, rows)
            v_out[here, cols] = low(0.5 * (high(raw_ref[here, cols]) + high(early[:, cols])))
        copies(p)[0].start()
        turned = v_out[:, cols].T
        for e in range(2):
            flipped[e, :HD, :] = turned[e * HD : (e + 1) * HD, :]
        for a, b in spans(span):
            q = q_ref[a:b, cols] * jnp.asarray(0.125, bf)
            allowed = allowed_keys(a, b, valid)
            for e in range(2):
                qe = jnp.where(first == (e == 0), q, jnp.zeros_like(q))
                diag = jnp.where(allowed, against(k_ref[a:b, cols], qe), -1e30)
                top = jnp.max(diag, axis=0, keepdims=True)
                if a:
                    past = against(k_ref[:a, cols], qe)
                    top = jnp.maximum(top, jnp.max(past, axis=0, keepdims=True))
                out = matmul(flipped[e, :, a:b], low(jnp.exp(diag - top)))
                if a:
                    out = out + matmul(flipped[e, :, :a], low(jnp.exp(past - top)))
                amount = out[HD : HD + 1, :]
                att[e * HD : (e + 1) * HD, a:b] = out[:HD, :] / amount
                lse_out[p, e : e + 1, a:b] = top + jnp.log(amount)
        result = low(att[...].T)
        upper = place[0] == 0
        att_own[:, cols] = jnp.where(upper, result[:rows, :], result[rows:, :])
        att_oth[:, cols] = jnp.where(upper, result[rows:, :], result[:rows, :])
        for copy in copies(p)[1:]:
            copy.start()
        return 0

    lax.fori_loop(0, lse_out.shape[0], pair, 0)
    for p in range(lse_out.shape[0]):
        for copy in copies(p):
            copy.wait()


def attend_forward(place, query, keys, raw, early_own, early_oth):
    span, cols = query.shape
    rows = span // 2
    heads = cols // HD
    out = shape16(rows, cols)
    natural = shape16(span, cols)
    return on_chip(
        forward_body,
        (out, out, natural, shape32(heads // 2, 2, span)),
        (place,),
        (query, keys, raw, early_own, early_oth),
        "attend_forward",
        cost=9.0,
        limit=6,
        away=(0, 1, 2),
        scratch=(
            pltpu.VMEM(out.shape, jnp.bfloat16),
            pltpu.VMEM(out.shape, jnp.bfloat16),
            pltpu.VMEM(natural.shape, jnp.bfloat16),
            pltpu.VMEM((2, HD + 16, span), jnp.bfloat16),
            pltpu.VMEM((2 * HD, span), jnp.float32),
            pltpu.SemaphoreType.DMA((3, heads // 2)),
        ),
    )


def backward_body(
    start, place, q_far, k_far, v_far, lse_ref, go_own, go_oth, att_own, att_oth, cos_ref, sin_ref,
    d_out, f_own, f_oth, q_ref, k_ref, v_ref, sems, grad, prod, turned_k, dq, dk, dv,
):
    rows = go_own.shape[0]
    span = 2 * rows
    valid = place[1]
    wide = 2 * HD
    bf = jnp.bfloat16
    first = lax.broadcasted_iota(jnp.int32, (1, wide), 1) < HD
    eighth = jnp.asarray(0.125, bf)
    count = f_own.shape[1] // wide

    def copies(i):
        there = columns(i + start, wide)
        here = columns(i, wide)
        return [
            pltpu.make_async_copy(away.at[:, there], near.at[:, here], sems.at[n, i])
            for n, (away, near) in enumerate(((q_far, q_ref), (k_far, k_ref), (v_far, v_ref)))
        ]

    for i in range(count):
        for copy in copies(i):
            copy.start()

    def pair(i, _):
        p = i + start
        cols = columns(p, wide)
        near = columns(i, wide)
        for copy in copies(i):
            copy.wait()
        for m, (go, att) in enumerate(((go_own, att_own), (go_oth, att_oth))):
            here = columns(place[0] ^ m, rows)
            grad[here, :] = go[:, cols]
            prod[here, :] = high(go[:, cols]) * high(att[:, cols])
        flat = prod[...].T
        deltas = [jnp.sum(flat[e * HD : (e + 1) * HD, :], axis=0, keepdims=True) for e in range(2)]
        turned_k[...] = (k_ref[:, near] * eighth).T
        for n, (a, b) in enumerate(spans(span)):
            allowed = allowed_keys(a, b, valid)
            q = q_ref[a:b, near] * eighth
            g = grad[a:b, :]
            parts = ((a, b), (0, a)) if a else ((a, b),)
            sums = {}
            for e in range(2):
                mine = first == (e == 0)
                qe = jnp.where(mine, q, jnp.zeros_like(q))
                ge = jnp.where(mine, g, jnp.zeros_like(g))
                for lo, hi in parts:
                    scores = against(k_ref[lo:hi, near], qe)
                    if lo == a:
                        scores = jnp.where(allowed, scores, -1e30)
                    weights = jnp.exp(scores - lse_ref[p, e : e + 1, a:b])
                    grad_w = against(v_ref[lo:hi, near], ge)
                    grad_s = low(weights * (grad_w - deltas[e][:, a:b]))
                    dv_here = matmul(low(weights), ge)
                    dk_here = matmul(grad_s, qe)
                    dq_here = matmul(turned_k[e * HD : (e + 1) * HD, lo:hi], grad_s)
                    if (lo, "v") in sums:
                        dv_here = dv_here + sums[lo, "v"]
                        dk_here = dk_here + sums[lo, "k"]
                    sums[lo, "v"], sums[lo, "k"] = dv_here, dk_here
                    sums[lo, e] = dq_here
            for e in range(2):
                dq[e * HD : (e + 1) * HD, a:b] = sums[a, e] + sums[0, e] if a else sums[a, e]
            dv[a:b, :] = sums[a, "v"]
            dk[a:b, :] = sums[a, "k"]
            if a:
                dv[:a, :] += sums[0, "v"]
                dk[:a, :] += sums[0, "k"]
        prod[...] = dq[...].T
        for m, f_out in enumerate((f_own, f_oth)):
            here = columns(place[0] ^ m, rows)
            cosine = cos_ref[here, :]
            sine = sin_ref[here, :]
            gv = low(0.5 * dv[here, :])
            gk = dk[here, :]
            gk = low(pltpu.roll(gk * cosine - turn(gk) * sine, HD, 1))
            gq = prod[here, :]
            gq = low(gq * cosine - turn(gq) * sine)
            part = slice(m * rows, (m + 1) * rows)
            base = i * 3 * wide
            d_out[part, pl.ds(pl.multiple_of(base, wide), wide)] = jnp.where(first, gq, gk)
            d_out[part, pl.ds(pl.multiple_of(base + wide, wide), wide)] = jnp.where(first, gv, gq)
            d_out[part, pl.ds(pl.multiple_of(base + 2 * wide, wide), wide)] = jnp.where(first, gk, gv)
            f_out[:, columns(i, wide)] = gv
        return 0

    lax.fori_loop(0, count, pair, 0)


def attend_backward(place, q, k, v, lse, go_own, go_oth, att_own, att_oth, cosine, sine, pairs):
    span = q.shape[0]
    rows = span // 2
    wide = 2 * HD
    cols = wide * (pairs[1] - pairs[0])
    return on_chip(
        functools.partial(backward_body, pairs[0]),
        (shape16(span, 3 * cols), shape16(rows, cols), shape16(rows, cols)),
        (place,),
        (q, k, v, lse, go_own, go_oth, att_own, att_oth, cosine, sine),
        "attend_backward",
        cost=7.5,
        limit=6,
        far=(0, 1, 2),
        scratch=(
            pltpu.VMEM((span, cols), jnp.bfloat16),
            pltpu.VMEM((span, cols), jnp.bfloat16),
            pltpu.VMEM((span, cols), jnp.bfloat16),
            pltpu.SemaphoreType.DMA((3, pairs[1] - pairs[0])),
            pltpu.VMEM((span, wide), jnp.bfloat16),
            pltpu.VMEM((span, wide), jnp.float32),
            pltpu.VMEM((wide, span), jnp.bfloat16),
            pltpu.VMEM((wide, span), jnp.float32),
            pltpu.VMEM((span, wide), jnp.float32),
            pltpu.VMEM((span, wide), jnp.float32),
        ),
    )


def row_blocks(rows, body, size=64):
    def step(c, _):
        body(columns(c, size))
        return 0

    lax.fori_loop(0, rows // size, step, 0)


def tables(span, inverse, sign):
    def body(inverse, sign, cos_ref, sin_ref):
        def rows(part):
            shape = (64, inverse.shape[1])
            place = part.start + lax.broadcasted_iota(jnp.int32, shape, 0)
            angles = place.astype(jnp.float32) * inverse[...]
            cos_ref[part, :] = jnp.cos(angles)
            sin_ref[part, :] = jnp.sin(angles) * sign[...]

        row_blocks(span, rows)

    out = shape32(span, inverse.shape[1])
    return on_chip(body, (out, out), (), (inverse, sign), "tables", cost=1.0)


def project_body(block, order, place, x_ref, gain_ref, w_ref, cos_ref, sin_ref, *refs):
    away_far, mine_far, q_far, k_far, q_out, k_out, v_out = refs[-12:-5]
    xn, away, mine, packed, sems = refs[-5:]
    rows = x_ref.shape[0]
    wide = 2 * HD
    x = high(x_ref[...])
    xn[...] = low(x * rms_scale(x) * gain_ref[...])
    arrange_halves(order, (xn,), away, mine)
    there = slice(block * rows, (block + 1) * rows)
    here = columns(place[0] ^ block, rows)
    copies = [
        pltpu.make_async_copy(away, away_far.at[there, :], sems.at[0]),
        pltpu.make_async_copy(mine, mine_far.at[there, :], sems.at[1]),
        pltpu.make_async_copy(q_out.at[here, :], q_far.at[here, :], sems.at[2]),
        pltpu.make_async_copy(k_out.at[here, :], k_far.at[here, :], sems.at[3]),
    ]
    for copy in copies[:2]:
        copy.start()
    cols = w_ref.shape[1] // 3
    for i in range(3):
        part = slice(i * cols, (i + 1) * cols)
        packed[:, part] = low(matmul(xn[...], w_ref[:, part]))
    cosine = cos_ref[here, :]
    sine = sin_ref[here, :]
    first = lax.broadcasted_iota(jnp.int32, (1, wide), 1) < HD

    def pair(p, _):
        to = columns(p, wide)
        x0, x1, x2 = [high(packed[:, columns(3 * p + i, wide)]) for i in range(3)]
        q = jnp.where(first, x0, x1)
        k = pltpu.roll(jnp.where(first, x2, x0), HD, 1)
        q_out[here, to] = low(q * cosine + turn(q) * sine)
        k_out[here, to] = low(k * cosine + turn(k) * sine)
        v_out[here, to] = low(jnp.where(first, x1, x2))
        return 0

    lax.fori_loop(0, q_out.shape[1] // wide, pair, 0)
    for copy in copies[2:]:
        copy.start()
    for copy in copies:
        copy.wait()


def project(order, place, x, gain, w, cosine, sine, before=()):
    rows, width = x.shape
    inside = pl.BlockSpec(memory_space=pltpu.VMEM)
    outside = pl.BlockSpec(memory_space=pl.ANY)
    scalar = pl.BlockSpec(memory_space=pltpu.SMEM)
    part = (2 * rows, width // 2)
    natural = (2 * rows, w.shape[1] // 3)
    far = [part, part, natural, natural]
    return pl.pallas_call(
        functools.partial(project_body, 1 if before else 0),
        out_shape=tuple(pltpu.HBM(f, jnp.bfloat16) for f in far) + (shape16(*natural),) * 3,
        in_specs=[scalar] * 2 + [inside] * 5 + ([outside] * 4 + [inside] * 3 if before else []),
        out_specs=(outside,) * 4 + (inside,) * 3,
        scratch_shapes=[
            pltpu.VMEM((rows, width), jnp.bfloat16),
            pltpu.VMEM((rows, width // 2), jnp.bfloat16),
            pltpu.VMEM((rows, width // 2), jnp.bfloat16),
            pltpu.VMEM((rows, w.shape[1]), jnp.bfloat16),
            pltpu.SemaphoreType.DMA((4,)),
        ],
        input_output_aliases={7 + i: i for i in range(len(before))},
        cost_estimate=pl.CostEstimate(
            flops=site_cost("project", 3.0), transcendentals=0, bytes_accessed=1
        ),
        compiler_params=pltpu.CompilerParams(vmem_limit_bytes=8 << 20),
        name="project",
    )(order, place, x, gain, w, cosine, sine, *before)


def arrange(order, blocks, out):
    rows = blocks[0].shape[0]
    size = out.shape[1] // order.shape[0]
    for i in range(order.shape[0]):
        for b, block in enumerate(blocks):
            out[b * rows : (b + 1) * rows, i * size : (i + 1) * size] = block[:, columns(order[i], size)]


def finish(place, x, att_own, att_came, w, gain):
    def body(
        place, x_far, own_far, came_far, w_far, gain_ref,
        hidden_far, hn_ref, hidden_ref, w_ref, att_ref, x_ref, sems,
    ):
        cols = own_far.shape[1]
        x_load = pltpu.make_async_copy(x_far, x_ref, sems.at[5])
        x_load.start()
        loads = []
        for m, far in enumerate((own_far, came_far)):
            there = columns(place[0] ^ m, cols)
            loads.append(pltpu.make_async_copy(far, att_ref.at[m], sems.at[3 + m]))
            loads.append(pltpu.make_async_copy(w_far.at[there, :], w_ref.at[m], sems.at[m]))
        for load in loads:
            load.start()
        x_load.wait()
        hidden = high(x_ref[...])
        for m in range(2):
            loads[2 * m].wait()
            loads[2 * m + 1].wait()
            hidden = hidden + matmul(att_ref[m], w_ref[m])
        hidden_ref[...] = hidden
        copy = pltpu.make_async_copy(hidden_ref, hidden_far, sems.at[2])
        copy.start()
        hn_ref[...] = low(hidden * rms_scale(hidden) * gain_ref[...])
        copy.wait()

    rows, width = x.shape
    return on_chip(
        body,
        (shape32(rows, width), shape16(rows, width)),
        (place,),
        (x, pltpu.with_memory_space_constraint(att_own, pltpu.HBM), att_came, w, gain),
        "finish",
        cost=3.0,
        limit=8,
        away=(0,),
        far=(0, 1, 2, 3),
        scratch=(
            pltpu.VMEM((rows, width), jnp.float32),
            pltpu.VMEM((2, width // 2, width), jnp.bfloat16),
            pltpu.VMEM((2, rows, width // 2), jnp.bfloat16),
            pltpu.VMEM((rows, width), jnp.bfloat16),
            pltpu.SemaphoreType.DMA((6,)),
        ),
    )


def reorder(order, *blocks):
    rows, cols = blocks[0].shape

    def body(order, *refs):
        arrange(order, refs[:-1], refs[-1])

    return on_chip(body, shape16(rows * len(blocks), cols), (order,), blocks, "reorder", cost=0.9)


def arrange_halves(order, blocks, away, mine):
    rows = blocks[0].shape[0]
    count = order.shape[0] // 2
    size = mine.shape[1] // count
    for half, out in enumerate((away, mine)):
        for i in range(count):
            for b, block in enumerate(blocks):
                out[b * rows : (b + 1) * rows, i * size : (i + 1) * size] = block[
                    :, columns(order[half * count + i], size)
                ]


def reorder_halves(order, *blocks):
    rows, cols = blocks[0].shape

    def body(order, *refs):
        arrange_halves(order, refs[:-2], *refs[-2:])

    part = shape16(rows * len(blocks), cols // 2)
    return on_chip(body, (part, part), (order,), blocks, "reorder_halves", cost=0.9)


def feed_rows(hn, grads, gate_w, up_w, mine, other, base):
    rows = hn.shape[0]
    units = gate_w[0].shape[0]
    here = slice(base, base + rows)
    total_hn = None
    for s in range(2):
        gate = against(hn[...], gate_w[s][...])
        up = against(hn[...], up_w[s][...])
        grad = high(grads[s][...])
        sig = 1.0 / (1.0 + jnp.exp(-gate))
        silu = gate * sig
        results = (silu * up, grad * up * sig * (1.0 + gate * (1.0 - sig)), grad * silu)
        for i, result in enumerate(results):
            if s == 0:
                mine[i][here, :] = low(result)
            else:
                other[2 * i * rows + base : 2 * i * rows + base + rows, :units] = low(result)
    for s in range(2):
        for i, w in ((1, gate_w[s]), (2, up_w[s])):
            if s == 0:
                share = matmul(mine[i][here, :], w[...])
            else:
                share = matmul(other[2 * i * rows + base : 2 * i * rows + base + rows, :units], w[...])
            total_hn = share if total_hn is None else total_hn + share
    return total_hn


def feed_own_body(order, hn, dy_own, dy_oth, wg0, wg1, wu0, wu1, wd0, wd1, *refs):
    rows = hn.shape[0]
    outs, grads = refs[:9], refs[9:]
    mine, other, dhn, down = outs[:3], outs[3], outs[4], outs[5]
    for grad, w in zip(grads, (wd0, wd1)):
        grad[...] = low(against(dy_own[...], w[...]))
    dhn[...] = feed_rows(hn, grads, (wg0, wg1), (wu0, wu1), mine, other, 0)
    down[...] = matmul(mine[0][:rows, :], wd0[...]) + matmul(other[:rows, : wd1.shape[0]], wd1[...])
    for grad, w in zip(outs[6:8], (wd0, wd1)):
        grad[...] = low(against(dy_oth[...], w[...]))
    arrange(order, (dy_own, dy_oth), outs[8])


def feed_oth_body(order, hn_own, hn, g0, g1, wg0, wg1, wu0, wu1, *refs):
    outs = refs[4:]
    outs[4][...] = low(
        feed_rows(hn, (g0, g1), (wg0, wg1), (wu0, wu1), outs[:3], outs[3], hn.shape[0])
    )
    arrange(order, (hn_own, hn), outs[5])


def feed_own(order, hn, dy_own, dy_oth, gate_w, up_w, down_w):
    rows, width = hn.shape
    units = gate_w[0].shape[0]
    part = shape16(2 * rows, units)
    other = shape16(6 * rows, -(-units // 128) * 128)
    return on_chip(
        feed_own_body,
        (part,) * 3
        + (other,)
        + (shape32(rows, width),) * 2
        + (shape16(rows, units),) * 2
        + (shape16(2 * rows, width),),
        (order,),
        (hn, dy_own, dy_oth, *gate_w, *up_w, *down_w),
        "feed_own",
        limit=15,
        cost=11.0,
        scratch=(pltpu.VMEM((rows, units), jnp.bfloat16),) * 2,
    )


def feed_oth(order, hn_own, hn, grads, gate_w, up_w, parts):
    rows, width = hn.shape
    return on_chip(
        feed_oth_body,
        tuple(shape16(*part.shape) for part in parts)
        + (shape16(rows, width), shape16(2 * rows, width)),
        (order,),
        (hn_own, hn, *grads, *gate_w, *up_w, *parts),
        "feed_oth",
        aliases={9 + i: i for i in range(4)},
        limit=14,
        cost=7.0,
    )


def ff_grad(left, left_core, index, right, right_core, pieces):
    rows, units = left.shape
    size = right.shape[1] // pieces
    half = right.shape[1] // 2

    def body(left, left_core, right, right_core, *outs):
        for i in range(2):
            part = slice(i * half, (i + 1) * half)
            sums = low(
                inner_rows(left[...], right[:, part])
                + inner_rows(left_core[index * rows : (index + 1) * rows, :units], right_core[:, part])
            )
            for j in range(pieces // 2):
                outs[i * pieces // 2 + j][...] = sums[:, j * size : (j + 1) * size]

    part = shape16(units, size)
    return on_chip(
        body, (part,) * pieces, (), (left, left_core, right, right_core), "ff_grad", cost=2.7
    )


def join(first, second):
    def body(first, second, out):
        out[...] = low(high(first[...]) + high(second[...]))

    return on_chip(body, shape16(*first.shape), (), (first, second), "join", cost=0.3)


def fold_three(first, second, third):
    mid = first.shape[1] // 2

    def body(first, second, third, away, rest):
        for out, part in ((away, slice(0, mid)), (rest, slice(mid, 2 * mid))):
            out[...] = low(high(first[:, part]) + high(second[:, part]) + high(third[:, part]))

    part = shape16(first.shape[0], mid)
    return on_chip(body, (part, part), (), (first, second, third), "fold_three", cost=0.3)


def fold(kept, came):
    mid = kept.shape[1] // 2

    def body(kept, came, away, rest):
        away[...] = low(high(kept[:, :mid]) + high(came[:, :mid]))
        rest[...] = low(high(kept[:, mid:]) + high(came[:, mid:]))

    part = shape16(kept.shape[0], mid)
    return on_chip(body, (part, part), (), (kept, came), "fold", cost=0.3)


def fold_rows(kept, came):
    mid = kept.shape[0] // 2

    def body(kept, came, away, rest):
        away[...] = low(high(kept[:mid, :]) + high(came[:mid, :]))
        rest[...] = low(high(kept[mid:, :]) + high(came[mid:, :]))

    part = shape16(mid, kept.shape[1])
    return on_chip(body, (part, part), (), (kept, came), "fold_rows", cost=0.3)


def hidden_grad_body(order, place, dhn_own, dhn_came, hidden_far, dy_ref, gain_ref, w_far,
    grad_ref, send_ref, own_ref, away_ref, mine_ref, gains_ref, proj, hidden_ref, w_ref, sems,
):
    cols = send_ref.shape[1]
    loads = [pltpu.make_async_copy(hidden_far, hidden_ref, sems.at[2])]
    for m in (1, 0):
        there = columns(place[0] ^ m, cols)
        loads.append(pltpu.make_async_copy(w_far.at[there, :], w_ref.at[m], sems.at[m]))
    for load in loads:
        load.start()
    loads[0].wait()
    hidden = hidden_ref[...]
    scale = rms_scale(hidden)
    dhn = dhn_own[...] + high(dhn_came[...])
    gains_ref[...] = jnp.sum(dhn * hidden * scale, axis=0, keepdims=True)
    weighted = dhn * gain_ref[...]
    mean = jnp.mean(weighted * hidden, axis=-1, keepdims=True)
    grad = high(dy_ref[...]) + scale * weighted - hidden * (scale * scale * scale * mean)
    grad_ref[...] = grad
    proj[...] = low(grad)
    loads[1].wait()
    send_ref[...] = low(against(proj[...], w_ref[1]))
    loads[2].wait()
    own_ref[...] = low(against(proj[...], w_ref[0]))
    arrange_halves(order, (proj,), away_ref, mine_ref)


def hidden_grad(order, place, dhn_own, dhn_came, hidden, dy, gain, w):
    rows, width = hidden.shape
    part = shape16(rows, width // 2)
    return on_chip(
        hidden_grad_body,
        (shape32(rows, width), part, part, part, part, shape32(1, width)),
        (order, place),
        (dhn_own, dhn_came, hidden, dy, gain, w),
        "hidden_grad",
        cost=2.2,
        limit=9,
        far=(2, 5),
        scratch=(
            pltpu.VMEM((rows, width), jnp.bfloat16),
            pltpu.VMEM((rows, width), jnp.float32),
            pltpu.VMEM((2, width // 2, width), jnp.bfloat16),
            pltpu.SemaphoreType.DMA((3,)),
        ),
    )


def bucket_grad(left, left_core, rights, rights_core, place=0, total_cols=None, before=()):
    mid = left.shape[1] // 2
    cols = rights[0].shape[1]
    count = len(rights)

    def body(left, left_core, *refs):
        for i in range(count):
            part = slice(place + i * cols, place + (i + 1) * cols)
            for half, out in enumerate(refs[-2:]):
                cut = slice(half * mid, (half + 1) * mid)
                out[:, part] = low(
                    inner_rows(left[:, cut], refs[i][...])
                    + inner_rows(left_core[:, cut], refs[count + i][...])
                )

    full = shape16(mid, total_cols or cols * count)
    return on_chip(
        body,
        (full, full),
        (),
        (left, left_core, *rights, *rights_core, *before),
        "bucket_grad",
        aliases={2 + 2 * count + i: i for i in range(len(before))},
        cost=1.5,
    )


def bucket_near(row, kept, came):
    quarter, cols = kept.shape
    size = quarter // 4

    def body(row, kept, came, away, rest):
        near = row[0] & 1
        for i in range(2):
            here = pl.ds(pl.multiple_of(i * 2 * size + near * size, size), size)
            there = pl.ds(pl.multiple_of(i * 2 * size + (1 - near) * size, size), size)
            part = slice(i * size, (i + 1) * size)
            away[part, :] = low(high(kept[there, :]) + high(came[there, :]))
            rest[part, :] = low(high(kept[here, :]) + high(came[here, :]))

    half = shape16(2 * size, cols)
    return on_chip(body, (half, half), (row,), (kept, came), "bucket_near", cost=0.3)


def shares_body(d_a, d_b, fa, fb, w_ref, x_own, x_oth, gain_two, send_ref, own_ref, gains_ref):
    rows, width = x_own.shape
    cut = d_a.shape[1]
    sums = None
    for m, x_ref in ((1, x_oth), (0, x_own)):
        part = slice(m * rows, (m + 1) * rows)
        share = against(d_a[part, :], w_ref[:, :cut]) + against(d_b[part, :], w_ref[:, cut:])
        if m:
            send_ref[:, :width] = low(share)
        else:
            own_ref[...] = share
        x = high(x_ref[...])
        here = jnp.sum(share * (x * rms_scale(x)), axis=0, keepdims=True)
        sums = here if sums is None else sums + here
    send_ref[:, width : width + fa.shape[1]] = fa[...]
    send_ref[:, width + fa.shape[1] :] = fb[...]
    gains_ref[0:1, :] = sums
    gains_ref[1:2, :] = gain_two[...]


def shares(d_a, d_b, fa, fb, w, x_own, x_oth, gain_two):
    rows, width = x_own.shape
    return on_chip(
        shares_body,
        (shape16(rows, width + 2 * fa.shape[1]), shape32(rows, width), shape32(2, width)),
        (),
        (d_a, d_b, fa, fb, w, x_own, x_oth, gain_two),
        "shares",
        cost=2.3,
    )


def input_grad_body(place, share_ref, came_ref, grad_ref, x_ref, gain_ref, fa, fb, out_ref, first_ref):
    width = x_ref.shape[1]
    x = high(x_ref[...])
    scale = rms_scale(x)
    weighted = (share_ref[...] + high(came_ref[:, :width])) * gain_ref[...]
    mean = jnp.mean(weighted * x, axis=-1, keepdims=True)
    out_ref[...] = grad_ref[...] + scale * weighted - x * (scale * scale * scale * mean)
    cols = fa.shape[1]
    own = 2 * place[0]
    oth = 2 - own
    first_ref[:, columns(own, cols)] = fa[...]
    first_ref[:, columns(own + 1, cols)] = fb[...]
    first_ref[:, columns(oth, cols)] = came_ref[:, width : width + cols]
    first_ref[:, columns(oth + 1, cols)] = came_ref[:, width + cols :]


def input_grad(place, share, came, grad_hidden, x, gain, fa, fb):
    return on_chip(
        input_grad_body,
        (shape32(*x.shape), shape16(*x.shape)),
        (place,),
        (share, came, grad_hidden, x, gain, fa, fb),
        "input_grad",
        cost=0.5,
        limit=6,
    )


def after(first, *values):
    return lax.optimization_barrier((first, *values))[1:]


def two_groups(
    inputs,
    first_values,
    lengths,
    gain_attn,
    w_qkv,
    w_out,
    gain_mlp,
    w_gate,
    w_up,
    w_down,
    cotangent,
):
    SITES.clear()
    rows = inputs.shape[1]
    width = inputs.shape[2]
    span = 2 * rows
    out_cols = HEADS // 2 * HD
    packed_cols = 3 * out_cols
    mid = width // 2
    h = lax.axis_index("head")
    f = lax.axis_index("ffn")
    r = lax.axis_index("row")
    row_size = lax.axis_size("row")
    place = jnp.stack([h, lengths[0]]).astype(jnp.int32)
    row = r.reshape(1).astype(jnp.int32)
    tie = lax.optimization_barrier
    gain_attn = gain_attn.reshape(1, width)
    gain_mlp = gain_mlp.reshape(1, width)

    x_own = inputs[0]
    x_oth = swap(x_own, "head", 1)
    early_own = lax.dynamic_slice_in_dim(first_values[0], h * out_cols, out_cols, 1)
    early_oth = swap(
        lax.dynamic_slice_in_dim(first_values[0], (1 - h) * out_cols, out_cols, 1), "head", 1
    )
    dy_own = cotangent[0]
    down_core = swap(w_down, "ffn", 1)
    gate_core = swap(w_gate.T, "ffn", 1)
    up_core = swap(w_up.T, "ffn", 1)
    qkv_w = lax.dynamic_slice_in_dim(w_qkv, h * packed_cols, packed_cols, 1)
    half = HD // 2
    inverse = jnp.exp(-jnp.log(10000.0) * jnp.arange(half, dtype=jnp.float32) * 2.0 / HD)
    sign = jnp.where(jnp.arange(2 * HD) % HD < half, -1.0, 1.0)
    cosine, sine = tables(span, jnp.tile(inverse, 4)[None, :], sign[None, :])

    ff_order = jnp.stack([(h ^ a) * row_size + (r ^ b) for a in (1, 0) for b in (3, 1, 2, 0)])
    down_order = jnp.stack([(h ^ a) * row_size + (r ^ b) for b in (3, 1, 2, 0) for a in (1, 0)])
    att_order = jnp.stack(
        [((f ^ a) * row_size + (r & 2 ^ b)) // 2 for a in (3, 1, 2, 0) for b in (2, 0)]
    )

    before = project(att_order, place, x_own, gain_attn, qkv_w, cosine, sine)
    x_oth, before, early_own, down_core, gate_core, up_core = tie(
        (x_oth, before, early_own, down_core, gate_core, up_core)
    )
    xn_away, xn_mine, query, keys, *near = project(
        att_order, place, x_oth, gain_attn, qkv_w, cosine, sine, before
    )
    att_own, att_oth, mixed, log_sums = attend_forward(place, *near, early_own, early_oth)
    att_came = swap(att_oth, "head", 1)
    (dy_send,) = after(near[2], dy_own)
    dy_oth = swap(dy_send, "ffn", 2)
    att_came, dy_oth = tie((att_came, dy_oth))
    down_w = (w_down, down_core)
    gate_w = (w_gate.T, gate_core)
    up_w = (w_up.T, up_core)
    hidden, hn_own = finish(place, x_own, att_own, att_came, w_out, gain_mlp)
    hn_oth = swap(hn_own, "ffn", 2)
    dy_send, dy_oth = after(hn_own, dy_send, dy_oth)
    dyc_own = swap(dy_send, "ffn", 1)
    dyc_oth = swap(dy_oth, "ffn", 1)
    hnc_own = swap(hn_own, "ffn", 1)

    *parts, dhn_own, down_own, dact0, dact1, dy_all = feed_own(
        down_order, hn_own, dy_own, dy_oth, gate_w, up_w, down_w
    )
    hn_oth, parts, dhn_own, down_own, dact0, dact1, dy_all, hnc_own, dyc_own, dyc_oth = tie(
        (hn_oth, parts, dhn_own, down_own, dact0, dact1, dy_all, hnc_own, dyc_own, dyc_oth)
    )
    hnc_oth = swap(hn_oth, "ffn", 1)
    act, gate, up, others, dhn_send, hn_all = feed_oth(
        ff_order, hn_own, hn_oth, (dact0, dact1), gate_w, up_w, parts
    )
    dhn_came = swap(dhn_send, "ffn", 2)
    others_core = swap(others, "ffn", 1)
    own_send, came_send = after(dhn_send, att_own, att_came)
    att_core = swap(own_send, "ffn", 1)
    came_core = swap(came_send, "ffn", 1)
    hnc_oth, dyc_own, dyc_oth = after(dhn_send, hnc_oth, dyc_own, dyc_oth)
    dyc_all = reorder(down_order, dyc_own, dyc_oth)
    hnc_all = reorder(ff_order, hnc_own, hnc_oth)

    gate_a, gate_b, gate_near, gate_kept = ff_grad(gate, others_core, 1, hn_all, hnc_all, 4)
    gate_xa = swap(gate_a, "head", 1)
    down_send, down_kept = ff_grad(act, others_core, 0, dy_all, dyc_all, 2)
    down_near = swap(down_send, "row", 1)
    up_a, up_b, up_near, up_kept = ff_grad(up, others_core, 2, hn_all, hnc_all, 4)
    dhn_came, gate_b, gate_kept, gate_near, down_kept, up_a, up_b, up_near, up_kept = tie(
        (dhn_came, gate_b, gate_kept, gate_near, down_kept, up_a, up_b, up_near, up_kept)
    )

    grad_hidden, go_send, go_own, proj_away, proj_mine, gain_two = hidden_grad(
        att_order, place, dhn_own, dhn_came, hidden, dy_own, gain_mlp, w_out
    )
    (gate_near,) = after(go_send, gate_near)
    gate_send = join(gate_near, gate_xa)
    go_send, go_own, proj_away, gate_send = tie((go_send, go_own, proj_away, gate_send))
    go_oth = swap(go_send, "head", 1)
    proj_core = swap(proj_away, "ffn", 1)
    gate_came = swap(gate_send, "row", 1)
    (gate_b,) = after(go_send, gate_b)
    gate_xb = swap(gate_b, "head", 1)
    out_send, out_kept = bucket_grad(
        proj_mine, proj_core, (att_came, att_own), (came_core, att_core)
    )
    out_y = swap(out_send, "ffn", 2)
    up_xa = swap(after(out_send, up_a)[0], "head", 1)
    go_oth, out_kept = tie((go_oth, out_kept))

    def backward(pairs, lse):
        return attend_backward(
            place, query, keys, mixed, lse, go_own, go_oth, att_own, att_oth, cosine, sine, pairs
        )

    pairs = HEADS // 4
    d_a, fa_own, fa_oth = backward((0, pairs // 2), log_sums)
    out_kept, down_kept, gate_kept = after(d_a, out_kept, down_kept, gate_kept)
    out_send, out_kept = fold(out_kept, out_y)
    out_x = swap(out_send, "head", 1)
    down_send, down_kept = fold(down_kept, down_near)
    down_mid = swap(down_send, "row", 2)
    gate_kept = join(gate_kept, gate_xb)
    d_a, out_kept, down_kept, gate_kept, log_sums = tie(
        (d_a, out_kept, down_kept, gate_kept, log_sums)
    )
    core_a = swap(d_a, "ffn", 1)
    xn_core = swap(after(out_kept, xn_away)[0], "ffn", 1)
    d_b, fb_own, fb_oth = backward((pairs // 2, pairs), log_sums)
    gate_kept, up_near = after(d_b, gate_kept, up_near)
    gate_send, gate_kept = fold(gate_kept, gate_came)
    up_send = join(up_near, up_xa)
    d_b, gate_kept, up_send = tie((d_b, gate_kept, up_send))
    core_b = swap(d_b, "ffn", 1)
    up_xb = swap(after(gate_kept, up_b)[0], "head", 1)
    up_came = swap(up_send, "row", 1)
    (d_a,) = after(gate_kept, d_a)
    before = bucket_grad(xn_mine, xn_core, (d_a,), (core_a,), 0, packed_cols)
    core_b, *before = tie((core_b, *before))
    y_send, kept = bucket_grad(
        xn_mine, xn_core, (d_b,), (core_b,), packed_cols // 2, packed_cols, before
    )
    y_came = swap(y_send, "ffn", 2)
    d_a, d_b = after(y_send, d_a, d_b)
    back_send, share_own, gains = shares(
        d_a, d_b, fa_oth, fb_oth, qkv_w, x_own, x_oth, gain_two
    )
    gate_send, out_kept, act, others, up_kept, down_kept = after(
        back_send, gate_send, out_kept, act, others, up_kept, down_kept
    )
    out_send, out_kept = bucket_near(row, out_kept, out_x)
    out_near = swap(out_send, "row", 1)
    gains = gains + swap(gains, "head", 1)
    gains, back_send = tie((gains, back_send))
    back_came = swap(back_send, "head", 1)
    up_kept, down_kept = after(gains, up_kept, down_kept)
    up_send, up_kept = fold_three(up_kept, up_xb, up_came)
    gate_far = swap(gate_send, "row", 2)
    units = w_down.shape[0]
    far_send = low(matmul(act[rows:], down_w[0]) + matmul(others[rows:span, :units], down_w[1]))
    gains, down_kept, gate_kept, out_kept = after(far_send, gains, down_kept, gate_kept, out_kept)
    gains = gains + swap(gains, "ffn", 1)
    down_send, down_kept = fold(down_kept, down_mid)
    out_send, out_kept = fold_rows(out_kept, out_near)
    out_far = swap(out_send, "row", 2)
    sum_gate = high(gate_kept) + high(gate_far)
    kept, up_send, down_send, sum_gate, gains, out_send = tie(
        (kept, up_send, down_send, sum_gate, gains, out_send)
    )

    near_send, kept = bucket_near(row, kept, y_came)
    near_came = swap(near_send, "row", 1)
    gains, far_send, out_kept, up_send, down_send = after(
        near_send, gains, far_send, out_kept, up_send, down_send
    )
    gains = gains + swap(gains, "ffn", 2)
    (far_send,) = after(gains, far_send)
    far_came = swap(far_send, "ffn", 2)
    up_far = swap(up_send, "row", 2)
    qkv_send, kept = fold_rows(kept, near_came)
    qkv_far = swap(qkv_send, "row", 2)
    share_own, down_kept, up_kept, out_kept, residual, gains, down_send = after(
        qkv_send,
        share_own,
        down_kept,
        up_kept,
        out_kept,
        hidden + down_own,
        gains,
        down_send,
    )
    down_x = swap(down_send, "head", 1)
    gains = gains + swap(gains, "row", 1)
    gains_far = swap(gains, "row", 2)
    (share_own,) = after(gains, share_own)
    grad_in, grad_first = input_grad(
        place, share_own, back_came, grad_hidden, x_own, gain_attn, fa_own, fb_own
    )
    sum_up = high(up_kept) + high(up_far)
    out_sum = high(out_kept) + high(out_far)
    output = low(residual + high(far_came))[None]
    (down_kept,) = after(output, down_kept)
    sum_down = high(down_kept) + high(down_x)
    gains = gains + gains_far
    kept, grad_in, sum_up, sum_down, out_sum, output, gains = tie(
        (kept, grad_in, sum_up, sum_down, out_sum, output, gains)
    )
    sum_qkv = high(kept) + high(qkv_far)
    return (
        output,
        grad_in[None],
        grad_first[None],
        gains[0],
        sum_qkv,
        out_sum.T,
        gains[1],
        sum_gate.T,
        sum_up.T,
        sum_down,
    )


def solution(mesh):
    in_specs = (
        P(("ffn", "row"), "head", None),
        P(("ffn", "row"), "head", None),
        P(("ffn", "row")),
        P(),
        P(),
        P(),
        P(),
        P(None, "ffn"),
        P(None, "ffn"),
        P("ffn", None),
        P(("ffn", "row"), "head", None),
    )
    out_specs = (
        P(("ffn", "row"), "head", None),
        P(("ffn", "row"), "head", None),
        P(("ffn", "row"), "head", None),
        P(),
        P(("ffn", "row"), "head"),
        P("head", ("ffn", "row")),
        P(),
        P(("head", "row"), "ffn"),
        P(("head", "row"), "ffn"),
        P("ffn", ("head", "row")),
    )
    body = two_groups if mesh.shape["head"] == 2 and mesh.shape["ffn"] == 4 else any_groups
    return jax.shard_map(
        body, mesh=mesh, in_specs=in_specs, out_specs=out_specs, check_vma=False
    )
```
